32 devices in a mesh: dp: 4 (over z), ctx: 2 (over y), head: 4 (over x, core).
Axes of the slice: x: 2, y: 2, z: 4, core: 2. Of those that a mesh axis runs over, the one named last changes fastest.
Arguments:
- tokens: bfloat16 [8, 4096, 1536], P('dp', ('ctx', 'head')), may hold values from -6 to 6
- cotangent: bfloat16 [8, 4096, 1536], P('dp', ('ctx', 'head')), may hold values from -6 to 6
- doc_lengths: int32 [8, 4], P('dp'), may hold values from 1 to 2048, 4096 in all within a row
- qkv_weight: float32 [1536, 12, 3, 128], P('dp', 'head'), may hold values from -0.15625 to 0.15625
- out_weight: float32 [12, 128, 1536], P('head', None, 'dp'), may hold values from -0.15625 to 0.15625
- inner_weight: float32 [1536, 2, 4096], P('dp', None, 'head'), may hold values from -0.15625 to 0.15625
- down_weight: float32 [4096, 1536], P('head', 'dp'), may hold values from -0.09375 to 0.09375
- norm_gains: float32 [2, 1536], replicated, may hold values from 0.5 to 1.5
- head_gain: float32 [128], replicated, may hold values from 0.5 to 1.5
- lambdas: float32 [4, 64], replicated, may hold values from -0.15 to 0.15
- qkv_momentum: float32 [1536, 12, 3, 128], P('dp', 'head'), may hold values from -128 to 128
- out_momentum: float32 [12, 128, 1536], P('head', None, 'dp'), may hold values from -128 to 128
- inner_momentum: float32 [1536, 2, 4096], P('dp', None, 'head'), may hold values from -64 to 64
- down_momentum: float32 [4096, 1536], P('head', 'dp'), may hold values from -64 to 64
- norm_momentum: float32 [2, 1536], replicated, may hold values from -128 to 128
- head_momentum: float32 [128], replicated, may hold values from -384 to 384
- lambda_momentum: float32 [4, 64], replicated, may hold values from -640 to 640
- qkv_variance: float32 [1536, 12, 3, 128], P('dp', 'head'), may hold values from 16.384 to 262.144
- out_variance: float32 [12, 128, 1536], P('head', None, 'dp'), may hold values from 16.384 to 262.144
- inner_variance: float32 [1536, 2, 4096], P('dp', None, 'head'), may hold values from 4.096 to 65.536
- down_variance: float32 [4096, 1536], P('head', 'dp'), may hold values from 4.096 to 65.536
- norm_variance: float32 [2, 1536], replicated, may hold values from 16.384 to 262.144
- head_variance: float32 [128], replicated, may hold values from 147.456 to 2359.296
- lambda_variance: float32 [4, 64], replicated, may hold values from 409.6 to 6553.6
Outputs:
- output: bfloat16 [8, 4096, 1536], P('dp', ('ctx', 'head'))
- input_grad: bfloat16 [8, 4096, 1536], P('dp', ('ctx', 'head'))
- qkv_updated: float32 [1536, 12, 3, 128], P('dp', 'head')
- out_updated: float32 [12, 128, 1536], P('head', None, 'dp')
- inner_updated: float32 [1536, 2, 4096], P('dp', None, 'head')
- down_updated: float32 [4096, 1536], P('head', 'dp')
- norm_updated: float32 [2, 1536], replicated
- head_updated: float32 [128], replicated
- lambda_updated: float32 [4, 64], replicated
- qkv_momentum_new: float32 [1536, 12, 3, 128], P('dp', 'head')
- out_momentum_new: float32 [12, 128, 1536], P('head', None, 'dp')
- inner_momentum_new: float32 [1536, 2, 4096], P('dp', None, 'head')
- down_momentum_new: float32 [4096, 1536], P('head', 'dp')
- norm_momentum_new: float32 [2, 1536], replicated
- head_momentum_new: float32 [128], replicated
- lambda_momentum_new: float32 [4, 64], replicated
- qkv_variance_new: float32 [1536, 12, 3, 128], P('dp', 'head')
- out_variance_new: float32 [12, 128, 1536], P('head', None, 'dp')
- inner_variance_new: float32 [1536, 2, 4096], P('dp', None, 'head')
- down_variance_new: float32 [4096, 1536], P('head', 'dp')
- norm_variance_new: float32 [2, 1536], replicated
- head_variance_new: float32 [128], replicated
- lambda_variance_new: float32 [4, 64], replicated
The draws below stay inside these ranges and needn't reach their ends.
Inputs may be any that keep to these rules, and one draw needn't show every extreme that they name: `doc_lengths`: each row holds the lengths of the 4 documents packed in order into one sequence; they sum to 4096, and the longest is exactly 2048.
All inputs are finite; a program needn't handle non-finite values.
Results may differ from the reference program's by a relative error of at most 0.025.
Values may be sent and summed in bfloat16 or wider, within the bound.
A program may use at most 320 MiB of HBM per device.

```python
import math
import jax
import jax.numpy as jnp
import numpy as np
from jax import lax

D = 1536
FF = 4096
H = 12
HD = 64
LEN = 4096
NDOC = 4
STEP = 10
VD = 128
SEQS = 8
TOKENS = 32768


def block_levels(rng, shape, shards, smallest, high):
    def one(axis_at, blocks):
        draws = jax.random.uniform(jax.random.fold_in(jax.random.fold_in(rng, 6), axis_at), (blocks,), jnp.float32, smallest / len(shards), high / len(shards))
        return jnp.repeat(jnp.exp(draws), shape[axis_at] // blocks).reshape((-1,) + (1,) * (len(shape) - axis_at - 1))

    factor_of = one(*shards[0])
    for cut in shards[1:]:
        factor_of = factor_of * one(*cut)
    return factor_of


def profile(amount, total, most, slope):
    loads = [(1 << 20) // math.isqrt(grade ** slope) + 1 for grade in range(2, amount + 1)]
    rest, given = total - most - (amount - 1), [1] * (amount - 1)
    while rest > 0:
        candidates = [i for i in range(amount - 1) if given[i] < most]
        mass, left = sum([loads[i] for i in candidates]), rest
        for i in candidates:
            more = min(most - given[i], max(1, left * loads[i] // mass), rest)
            given[i] = given[i] + more
            rest = rest - more
    return np.array([most] + given)


def ragged(key, number_of, total, limit, slope):
    if number_of == 2:
        one = jax.random.randint(key, (), max(1, total - limit), min(limit, total - 1) + 1)
        return jnp.stack([one, total - one])
    sizes = jnp.asarray(profile(number_of, total, limit, slope), jnp.int32)
    twos = (number_of - 1) // 2
    source_of, taker = sizes[1:1 + 2 * twos:2], sizes[2:2 + 2 * twos:2]
    slack = jnp.minimum(source_of - 1, limit - taker)
    moved = jax.random.randint(jax.random.fold_in(key, 1), (twos,), 0, 1 << 20) % (slack + 1)
    sizes = sizes.at[1:1 + 2 * twos:2].set(source_of - moved).at[2:2 + 2 * twos:2].set(taker + moved)
    return sizes[jax.random.permutation(jax.random.fold_in(key, 2), number_of)]


def normal_values(rng, dims, deviation, bound, split=(), kind=jnp.bfloat16):
    gain = block_levels(rng, dims, split, -0.22, 0.18) if split else 1.0
    drawn = jax.random.normal(rng, dims, jnp.float32) * deviation * gain
    return jnp.minimum(jnp.maximum(drawn, -bound), bound).astype(kind)


def setup_inputs(seed: int = 0) -> dict:
    splits = jax.random.split(jax.random.key(seed), 25)
    tokens = normal_values(splits[0], (SEQS, LEN, D), 1.0, 6.0, ((0, 4), (1, 8)))
    cotangent = normal_values(splits[1], (SEQS, LEN, D), 1.0, 6.0, ((0, 4), (1, 8)))
    doc_lengths = jax.vmap(lambda own: ragged(own, NDOC, LEN, LEN // 2, 2))(jax.random.split(splits[2], SEQS)).reshape((SEQS, NDOC)).astype(jnp.int32)
    qkv_weight = normal_values(splits[3], (D, H, 3, VD), D ** -0.5, 0.15625, ((0, 4), (1, 4)), jnp.float32)
    out_weight = normal_values(splits[4], (H, VD, D), (H * VD) ** -0.5, 0.15625, ((0, 4), (2, 4)), jnp.float32)
    inner_weight = normal_values(splits[5], (D, 2, FF), D ** -0.5, 0.15625, ((0, 4), (2, 4)), jnp.float32)
    down_weight = normal_values(splits[6], (FF, D), FF ** -0.5, 0.09375, ((0, 4), (1, 4)), jnp.float32)
    norm_gains = jnp.clip(1.0 + 0.1 * jax.random.normal(splits[7], (2, D), jnp.float32), 0.5, 1.5)
    head_gain = jnp.clip(1.0 + 0.1 * jax.random.normal(splits[8], (VD,), jnp.float32), 0.5, 1.5)
    lambdas = jnp.clip(jax.random.uniform(splits[9], (4, HD), jnp.float32, -0.15, 0.15), -0.15, 0.15)
    qkv_momentum = normal_values(splits[10], (D, H, 3, VD), (0.11 * TOKENS ** 0.5), 128.0, ((0, 4), (1, 4)), jnp.float32)
    out_momentum = normal_values(splits[11], (H, VD, D), (0.11 * TOKENS ** 0.5), 128.0, ((0, 4), (2, 4)), jnp.float32)
    inner_momentum = normal_values(splits[12], (D, 2, FF), (0.055 * TOKENS ** 0.5), 64.0, ((0, 4), (2, 4)), jnp.float32)
    down_momentum = normal_values(splits[13], (FF, D), (0.055 * TOKENS ** 0.5), 64.0, ((0, 4), (1, 4)), jnp.float32)
    norm_momentum = normal_values(splits[14], (2, D), (0.11 * TOKENS ** 0.5), 128.0, (), jnp.float32)
    head_momentum = normal_values(splits[15], (VD,), (0.33 * TOKENS ** 0.5), 384.0, (), jnp.float32)
    lambda_momentum = normal_values(splits[16], (4, HD), (0.55 * TOKENS ** 0.5), 640.0, (), jnp.float32)
    qkv_variance = jnp.clip(jnp.exp(math.log(262.144) - 2.7725887 * jax.random.uniform(splits[17], (D, H, 3, VD), jnp.float32) ** block_levels(splits[17], (D, H, 3, VD), ((0, 4), (1, 4)), -0.2, 0.2)), 16.384, 262.144)
    out_variance = jnp.clip(jnp.exp(math.log(262.144) - 2.7725887 * jax.random.uniform(splits[18], (H, VD, D), jnp.float32) ** block_levels(splits[18], (H, VD, D), ((0, 4), (2, 4)), -0.2, 0.2)), 16.384, 262.144)
    inner_variance = jnp.clip(jnp.exp(math.log(65.536) - 2.7725887 * jax.random.uniform(splits[19], (D, 2, FF), jnp.float32) ** block_levels(splits[19], (D, 2, FF), ((0, 4), (2, 4)), -0.2, 0.2)), 4.096, 65.536)
    down_variance = jnp.clip(jnp.exp(math.log(65.536) - 2.7725887 * jax.random.uniform(splits[20], (FF, D), jnp.float32) ** block_levels(splits[20], (FF, D), ((0, 4), (1, 4)), -0.2, 0.2)), 4.096, 65.536)
    norm_variance = jnp.clip(jnp.exp(jax.random.uniform(splits[21], (2, D), jnp.float32, math.log(16.384), math.log(262.144))), 16.384, 262.144)
    head_variance = jnp.clip(jnp.exp(jax.random.uniform(splits[22], (VD,), jnp.float32, math.log(147.456), math.log(2359.296))), 147.456, 2359.296)
    lambda_variance = jnp.clip(jnp.exp(jax.random.uniform(splits[23], (4, HD), jnp.float32, math.log(409.6), math.log(6553.6))), 409.6, 6553.6)
    return dict(tokens=tokens, cotangent=cotangent, doc_lengths=doc_lengths, qkv_weight=qkv_weight, out_weight=out_weight, inner_weight=inner_weight, down_weight=down_weight, norm_gains=norm_gains, head_gain=head_gain, lambdas=lambdas, qkv_momentum=qkv_momentum, out_momentum=out_momentum, inner_momentum=inner_momentum, down_momentum=down_momentum, norm_momentum=norm_momentum, head_momentum=head_momentum, lambda_momentum=lambda_momentum, qkv_variance=qkv_variance, out_variance=out_variance, inner_variance=inner_variance, down_variance=down_variance, norm_variance=norm_variance, head_variance=head_variance, lambda_variance=lambda_variance)


EPS = 1e-05
LAMBDA_INIT = 0.2
SCALE = 0.125
NEG = -1e+30
BETA1 = 0.9
BETA2 = 0.999
ADAM_EPS = 1e-08
DECAY = 0.1
ROPE_BASE = 10000.0

@jax.custom_vjp
def low(v):
    return lax.optimization_barrier(v.astype(jnp.bfloat16)).astype(jnp.float32)

@jax.custom_vjp
def low_back(v):
    return v

def low_keep(v):
    return (low(v), None)

def low_pass(kept, grad):
    return (grad,)

def back_keep(v):
    return (v, None)

def back_low(kept, grad):
    return (low(grad),)
low.defvjp(low_keep, low_pass)
low_back.defvjp(back_keep, back_low)

def matmul(left_side, right_side):
    return jnp.dot(left_side, right_side, preferred_element_type=jnp.float32, precision=lax.Precision.HIGHEST)

def einsum_high(formula, left_side, right_side):
    return jnp.einsum(formula, left_side, right_side, preferred_element_type=jnp.float32, precision=lax.Precision.HIGHEST)

def rms_norm(values, gain_vec):
    return values * lax.rsqrt(lax.optimization_barrier(jnp.mean(values * values, axis=-1, keepdims=True)) + EPS) * gain_vec

def angles(positions):
    half_size = HD // 2
    frequency = ROPE_BASE ** (-jnp.arange(half_size, dtype=jnp.float32) / half_size)
    phases = positions[:, None] * frequency[None, :]
    return (jnp.cos(phases)[:, None, :], jnp.sin(phases)[:, None, :])

def rotary(values, cos_table, sin_table):
    half_size = values.shape[-1] // 2
    leading = values[..., :half_size]
    trailing = values[..., half_size:]
    return jnp.concatenate([leading * cos_table - trailing * sin_table, leading * sin_table + trailing * cos_table], axis=-1)

def rotate_pair(values, cos_table, sin_table):
    return jnp.concatenate([rotary(values[..., :HD], cos_table, sin_table), rotary(values[..., HD:], cos_table, sin_table)], axis=-1)

def layer(tokens_in, parameters, segment, cos_table, sin_table):
    qkv_weight, out_weight, inner_weight, down_weight, norm_gains, head_gain, lambdas = parameters
    length = tokens_in.shape[0]
    normed = low(rms_norm(tokens_in, norm_gains[0]))
    projected = low_back(matmul(normed, low(qkv_weight).reshape(D, H * 3 * VD))).reshape(length, H, 3, VD)
    queries = low(rotate_pair(projected[:, :, 0], cos_table, sin_table))
    keys_all = low(rotate_pair(projected[:, :, 1], cos_table, sin_table))
    values_all = low(projected[:, :, 2])
    lambda_value = jnp.exp(jnp.sum(lambdas[0] * lambdas[1])) - jnp.exp(jnp.sum(lambdas[2] * lambdas[3])) + LAMBDA_INIT
    positions = jnp.arange(length, dtype=jnp.int32)
    block_rows = min(512, length)

    @jax.checkpoint
    def attend(row_start):
        query_block = lax.dynamic_slice_in_dim(queries, row_start, block_rows, 0)
        query_pos = row_start + jnp.arange(block_rows, dtype=jnp.int32)
        query_seg = lax.dynamic_slice_in_dim(segment, row_start, block_rows, 0)
        allowed = (positions[None, :] <= query_pos[:, None]) & (segment[None, :] == query_seg[:, None])
        results = []
        for offset in (0, HD):
            raw_scores = low_back(einsum_high('qhd,khd->hqk', query_block[..., offset:offset + HD], keys_all[..., offset:offset + HD]))
            scores = jnp.where(allowed[None], raw_scores * SCALE, NEG)
            totals = jax.nn.logsumexp(scores, axis=-1, keepdims=True)
            weights_now = low(jnp.where(allowed[None], jnp.exp(scores - totals), 0.0))
            results.append(einsum_high('hqk,khd->qhd', weights_now, values_all))
        return (results[0], results[1])
    starts = jnp.arange(length // block_rows, dtype=jnp.int32) * block_rows
    first_map, second_map = lax.map(attend, starts)
    first_map = first_map.reshape(length, H, VD)
    second_map = second_map.reshape(length, H, VD)
    difference = low_back(first_map - lambda_value * second_map)
    attn_in = low(rms_norm(difference, head_gain * (1.0 - LAMBDA_INIT)))
    attended = matmul(attn_in.reshape(length, H * VD), low(out_weight).reshape(H * VD, D))
    middle = low_back(tokens_in + attended)
    normed_mid = low(rms_norm(middle, norm_gains[1]))
    gate_up = low_back(matmul(normed_mid, low(inner_weight).reshape(D, 2 * FF)))
    gates = gate_up[:, :FF]
    up_part = gate_up[:, FF:]
    hidden = low(gates * jax.nn.sigmoid(gates) * up_part)
    return middle + matmul(hidden, low(down_weight))

def adamw(parameter, momentum, variance, gradient, learn_rate, decay_rate):
    momentum = BETA1 * momentum + (1.0 - BETA1) * gradient
    variance = BETA2 * variance + (1.0 - BETA2) * gradient * gradient
    corrected = momentum / (1.0 - BETA1 ** STEP)
    spread = jnp.sqrt(variance / (1.0 - BETA2 ** STEP))
    return (parameter - learn_rate * (corrected / (spread + ADAM_EPS) + decay_rate * parameter), momentum, variance)

def reference(tokens, cotangent, doc_lengths, qkv_weight, out_weight, inner_weight, down_weight, norm_gains, head_gain, lambdas, qkv_momentum, out_momentum, inner_momentum, down_momentum, norm_momentum, head_momentum, lambda_momentum, qkv_variance, out_variance, inner_variance, down_variance, norm_variance, head_variance, lambda_variance):
    parameters = (qkv_weight, out_weight, inner_weight, down_weight, norm_gains, head_gain, lambdas)
    cos_table, sin_table = angles(jnp.arange(LEN, dtype=jnp.float32))
    bounds = jnp.cumsum(doc_lengths, axis=-1, dtype=jnp.int32)
    position_ids = jnp.arange(LEN, dtype=jnp.int32)

    def one_sequence(carried, inputs):
        tokens_row, cot_row, bound_row = inputs
        segment = lax.optimization_barrier(jnp.sum((position_ids[:, None] >= bound_row[None, :]).astype(jnp.int32), axis=1))

        def apply_layer(values, params_in):
            return layer(values, params_in, segment, cos_table, sin_table)
        result, pullback = jax.vjp(apply_layer, tokens_row.astype(jnp.float32), parameters)
        grad_tokens, grad_params = pullback(cot_row.astype(jnp.float32))
        carried = jax.tree.map(jnp.add, carried, grad_params)
        return (carried, (result.astype(jnp.bfloat16), grad_tokens.astype(jnp.bfloat16)))
    zeros_start = jax.tree.map(jnp.zeros_like, parameters)
    gradients, (output, input_grad) = lax.scan(one_sequence, zeros_start, (tokens, cotangent, bounds))
    momenta = (qkv_momentum, out_momentum, inner_momentum, down_momentum, norm_momentum, head_momentum, lambda_momentum)
    variances = (qkv_variance, out_variance, inner_variance, down_variance, norm_variance, head_variance, lambda_variance)
    learn_rates = (0.5 * D ** (-0.5), 0.5 * (H * VD) ** (-0.5), 0.5 * D ** (-0.5), 0.5 * FF ** (-0.5), 0.4, 0.4, 0.1)
    decay_rates = (DECAY, DECAY, DECAY, DECAY, 0.0, 0.0, 0.0)
    updated = []
    moment_new = []
    variance_new = []
    for item in range(7):
        new_param, new_moment, new_variance = adamw(parameters[item], momenta[item], variances[item], gradients[item], learn_rates[item], decay_rates[item])
        updated.append(new_param)
        moment_new.append(new_moment)
        variance_new.append(new_variance)
    return (output, input_grad, updated[0], updated[1], updated[2], updated[3], updated[4], updated[5], updated[6], moment_new[0], moment_new[1], moment_new[2], moment_new[3], moment_new[4], moment_new[5], moment_new[6], variance_new[0], variance_new[1], variance_new[2], variance_new[3], variance_new[4], variance_new[5], variance_new[6])
```

```python
import functools

import jax
import jax.numpy as jnp
from jax import lax
from jax.experimental import pallas as pl
from jax.experimental.pallas import tpu as pltpu
from jax.sharding import PartitionSpec as P

D = 1536
FF = 4096
H = 12
HD = 64
STEP = 10
VD = 128


EPS = 1e-05
LAMBDA_INIT = 0.2
SCALE = 0.125
NEG = -1e30
BETA1 = 0.9
BETA2 = 0.999
ADAM_EPS = 1e-08
DECAY = 0.1
ROPE_BASE = 10000.0

MIB = 1 << 20
NT = (((1,), (1,)), ((), ()))
TN = (((0,), (0,)), ((), ()))
F32 = jnp.float32
BF16 = jnp.bfloat16


def dot(left, right, dims=(((1,), (0,)), ((), ())), **kw):
    return lax.dot_general(left, right, dims, preferred_element_type=F32, **kw)


def swap(array, bit):
    size = lax.axis_size("head")
    return lax.ppermute(array, "head", [(i, i ^ bit) for i in range(size)])


def gather_chunks(own):
    mate = swap(own, 1)
    far = swap(own, 2)
    return [own, mate, far, swap(far, 1)]


def reduce_chunks(parts):
    near = swap(parts[1], 1)
    far = swap(parts[3], 1)
    far_sum = (parts[2].astype(F32) + far.astype(F32)).astype(BF16)
    across = swap(far_sum, 2)
    return parts[0].astype(F32) + near.astype(F32) + across.astype(F32)


def split_rows(array, count):
    size = array.shape[0] // count
    return [array[i * size : (i + 1) * size] for i in range(count)]


def turn(values, cos_table, sin_table, low_half, sign):
    ahead = pltpu.roll(values, VD - HD // 2, 1)
    behind = pltpu.roll(values, HD // 2, 1)
    rotated = jnp.where(low_half, -ahead, behind)
    return values * cos_table + sign * rotated * sin_table


def low_half_mask(rows):
    lane = lax.broadcasted_iota(jnp.int32, (rows, VD), 1)
    return (lane % HD) < HD // 2


def project_kernel(x_ref, w_ref, cos_ref, sin_ref, q_ref, kv_ref, *, heads):
    rows = x_ref.shape[0]
    mask = low_half_mask(rows)
    cos_table, sin_table = cos_ref[...], sin_ref[...]
    x = x_ref[...]
    for head in range(heads):
        base = head * 3 * VD
        out = dot(x, w_ref[:, base : base + 3 * VD])
        query = turn(out[:, :VD], cos_table, sin_table, mask, 1.0) * SCALE
        key = turn(out[:, VD : 2 * VD], cos_table, sin_table, mask, 1.0)
        q_ref[:, head * VD : (head + 1) * VD] = query.astype(BF16)
        kv_ref[:, head * 2 * VD : head * 2 * VD + VD] = key.astype(BF16)
        kv_ref[:, head * 2 * VD + VD : (head + 1) * 2 * VD] = out[:, 2 * VD :].astype(BF16)


def project(x, weight, cos_table, sin_table):
    rows = x.shape[0]
    heads = weight.shape[1] // (3 * VD)
    tile = min(512, rows)
    return pl.pallas_call(
        functools.partial(project_kernel, heads=heads),
        grid=(rows // tile,),
        in_specs=[
            pl.BlockSpec((tile, D), lambda i: (i, 0)),
            pl.BlockSpec(weight.shape, lambda i: (0, 0)),
            pl.BlockSpec((tile, VD), lambda i: (i, 0)),
            pl.BlockSpec((tile, VD), lambda i: (i, 0)),
        ],
        out_specs=[
            pl.BlockSpec((tile, heads * VD), lambda i: (i, 0)),
            pl.BlockSpec((tile, heads * 2 * VD), lambda i: (i, 0)),
        ],
        out_shape=[
            jax.ShapeDtypeStruct((rows, heads * VD), BF16),
            jax.ShapeDtypeStruct((rows, heads * 2 * VD), BF16),
        ],
        compiler_params=pltpu.CompilerParams(vmem_limit_bytes=40 * MIB),
        cost_estimate=pl.CostEstimate(
            flops=2 * rows * D * weight.shape[1],
            bytes_accessed=2 * (rows * D + weight.size + rows * weight.shape[1]),
            transcendentals=0,
        ),
        name="project",
    )(x, weight, cos_table, sin_table)


def unproject_kernel(dq_ref, own_ref, recv_ref, w_ref, cos_ref, sin_ref, gp_ref, gn_ref, *, heads):
    rows = dq_ref.shape[0]
    mask = low_half_mask(rows)
    cos_table, sin_table = cos_ref[...], sin_ref[...]
    for head in range(heads):
        base = head * 3 * VD
        pair = slice(head * 2 * VD, (head + 1) * 2 * VD)
        both = own_ref[:, pair].astype(F32) + recv_ref[:, pair].astype(F32)
        query = dq_ref[:, head * VD : (head + 1) * VD].astype(F32)
        gp_ref[:, base : base + VD] = turn(query, cos_table, sin_table, mask, -1.0).astype(BF16)
        gp_ref[:, base + VD : base + 2 * VD] = turn(
            both[:, :VD], cos_table, sin_table, mask, -1.0
        ).astype(BF16)
        gp_ref[:, base + 2 * VD : base + 3 * VD] = both[:, VD:].astype(BF16)
    gn_ref[...] = dot(gp_ref[...], w_ref[...], NT).astype(BF16)


def unproject(dq, dkv_own, dkv_recv, weight, cos_table, sin_table):
    rows = dq.shape[0]
    heads = weight.shape[1] // (3 * VD)
    tile = min(512, rows)
    return pl.pallas_call(
        functools.partial(unproject_kernel, heads=heads),
        grid=(rows // tile,),
        in_specs=[
            pl.BlockSpec((tile, heads * VD), lambda i: (i, 0)),
            pl.BlockSpec((tile, heads * 2 * VD), lambda i: (i, 0)),
            pl.BlockSpec((tile, heads * 2 * VD), lambda i: (i, 0)),
            pl.BlockSpec(weight.shape, lambda i: (0, 0)),
            pl.BlockSpec((tile, VD), lambda i: (i, 0)),
            pl.BlockSpec((tile, VD), lambda i: (i, 0)),
        ],
        out_specs=[
            pl.BlockSpec((tile, heads * 3 * VD), lambda i: (i, 0)),
            pl.BlockSpec((tile, D), lambda i: (i, 0)),
        ],
        out_shape=[
            jax.ShapeDtypeStruct((rows, heads * 3 * VD), BF16),
            jax.ShapeDtypeStruct((rows, D), BF16),
        ],
        compiler_params=pltpu.CompilerParams(vmem_limit_bytes=40 * MIB),
        cost_estimate=pl.CostEstimate(
            flops=2 * rows * D * weight.shape[1],
            bytes_accessed=2 * (rows * D + weight.size + 3 * rows * weight.shape[1]),
            transcendentals=0,
        ),
        name="unproject",
    )(dq, dkv_own, dkv_recv, weight, cos_table, sin_table)


class Plan:
    def __init__(self, own_rows, block_len, prev_rows, ndoc):
        self.own_rows = own_rows
        self.block_len = block_len
        self.prev_rows = prev_rows
        self.ndoc = ndoc
        self.bq = min(256, own_rows)
        self.bk = min(512, own_rows)
        self.total = prev_rows + block_len

    def doc_start(self, info, pos):
        start = jnp.zeros_like(pos)
        for item in range(self.ndoc):
            start = jnp.where(pos >= info[2 + item], info[2 + item], start)
        return start

    def query_start(self, info, index):
        per = self.own_rows // self.bq
        chunk = (index // per) ^ info[0]
        return info[1] * self.block_len + chunk * self.own_rows + (index % per) * self.bq

    def key_row(self, info, index):
        per = self.own_rows // self.bk
        blocks = self.block_len // self.bk
        owner = index // blocks
        local = index % blocks
        inside = (((local // per) ^ info[0]) * per + local % per) * self.bk
        base = jnp.where(owner == info[1], self.prev_rows, owner * self.block_len)
        return pl.multiple_of(base + inside, self.bk)

    def ranges(self, info, start):
        last = start + self.bq - 1
        low = self.doc_start(info, start) // self.bk
        high = last // self.bk + 1
        open_from = (self.doc_start(info, last) + self.bk - 1) // self.bk
        first = jnp.minimum(jnp.maximum(open_from, low), high)
        until = jnp.maximum(first, jnp.minimum((start + 1) // self.bk, high))
        return low, first, until, high


def split_halves(q):
    lane = lax.broadcasted_iota(jnp.int32, q.shape, 1)
    zero = jnp.zeros_like(q)
    return jnp.concatenate([jnp.where(lane < HD, q, zero), jnp.where(lane >= HD, q, zero)], axis=0)


def load_keys(plan, info, own_ref, prev_ref, kv_sc):
    @pl.when(pl.program_id(1) == 0)
    def _():
        kv_sc[plan.prev_rows :, :] = own_ref[...]

        @pl.when(info[1] > 0)
        def _():
            kv_sc[: plan.prev_rows, :] = prev_ref[...]


def forward_kernel(
    info,
    lam_ref,
    gain_ref,
    q_ref,
    own_ref,
    prev_ref,
    attn_ref,
    first_ref,
    second_ref,
    lse_ref,
    kv_sc,
    m_sc,
    l_sc,
    acc_sc,
    *,
    plan,
):
    bq, bk = plan.bq, plan.bk
    load_keys(plan, info, own_ref, prev_ref, kv_sc)
    start = plan.query_start(info, pl.program_id(1))
    q2 = split_halves(q_ref[...])
    m_sc[...] = jnp.full_like(m_sc, NEG)
    l_sc[...] = jnp.zeros_like(l_sc)
    acc_sc[...] = jnp.zeros_like(acc_sc)
    low, first, until, high = plan.ranges(info, start)

    def visit(index, masked):
        row = plan.key_row(info, index)
        key = kv_sc[pl.ds(row, bk), :VD]
        value = kv_sc[pl.ds(row, bk), VD:]
        scores = dot(q2, key, NT)
        if masked:
            query_pos = start + lax.broadcasted_iota(jnp.int32, (bq, 1), 0)
            begin = plan.doc_start(info, query_pos)
            key_pos = index * bk + lax.broadcasted_iota(jnp.int32, (bq, bk), 1)
            keep = (key_pos <= query_pos) & (key_pos >= begin)
            scores = jnp.concatenate(
                [jnp.where(keep, scores[:bq], NEG), jnp.where(keep, scores[bq:], NEG)], axis=0
            )
        before = m_sc[...]
        after = jnp.maximum(before, jnp.max(scores, axis=1, keepdims=True))
        weights = jnp.exp(scores - jnp.tile(after, (1, bk // VD)))
        factor = jnp.exp(before - after)
        m_sc[...] = after
        l_sc[...] = l_sc[...] * factor + jnp.sum(weights, axis=1, keepdims=True)
        acc_sc[...] = acc_sc[...] * factor + dot(weights.astype(BF16), value)

    @pl.loop(low, first)
    def _(index):
        visit(index, True)

    @pl.loop(first, until)
    def _(index):
        visit(index, False)

    @pl.loop(until, high)
    def _(index):
        visit(index, True)

    total = l_sc[...]
    maps = acc_sc[...] * (1.0 / total)
    first_map, second_map = maps[:bq], maps[bq:]
    first_ref[...] = first_map
    second_ref[...] = second_map
    difference = first_map - lam_ref[0] * second_map
    scaling = lax.rsqrt(jnp.mean(difference * difference, axis=1, keepdims=True) + EPS)
    attn_ref[...] = (difference * scaling * gain_ref[...]).astype(BF16)
    lse = (m_sc[...] + jnp.log(total)).T
    lse_ref[0, 0:1, :] = lse[0:1, :bq]
    lse_ref[0, 1:2, :] = lse[0:1, bq:]


def attention_cost(plan, heads, per_pair):
    pairs = heads * plan.block_len * plan.block_len * 5 // 8
    return pl.CostEstimate(
        flops=pairs * per_pair,
        bytes_accessed=heads * plan.block_len * VD * 32,
        transcendentals=2 * pairs,
    )


def attend_forward(plan, info, lam, gain, q, kv_own, kv_prev):
    rows = q.shape[0]
    heads = q.shape[1] // VD
    bq = plan.bq
    grid_spec = pltpu.PrefetchScalarGridSpec(
        num_scalar_prefetch=1,
        grid=(heads, rows // bq),
        in_specs=[
            pl.BlockSpec(memory_space=pltpu.SMEM),
            pl.BlockSpec((1, VD), lambda h, i, s: (0, 0)),
            pl.BlockSpec((bq, VD), lambda h, i, s: (i, h)),
            pl.BlockSpec((rows, 2 * VD), lambda h, i, s: (0, h)),
            pl.BlockSpec((plan.prev_rows, 2 * VD), lambda h, i, s: (0, h)),
        ],
        out_specs=[
            pl.BlockSpec((bq, VD), lambda h, i, s: (i, h)),
            pl.BlockSpec((bq, VD), lambda h, i, s: (i, h)),
            pl.BlockSpec((bq, VD), lambda h, i, s: (i, h)),
            pl.BlockSpec((1, 2, bq), lambda h, i, s: (h, 0, i)),
        ],
        scratch_shapes=[
            pltpu.VMEM((plan.total, 2 * VD), BF16),
            pltpu.VMEM((2 * bq, VD), F32),
            pltpu.VMEM((2 * bq, VD), F32),
            pltpu.VMEM((2 * bq, VD), F32),
        ],
    )
    return pl.pallas_call(
        functools.partial(forward_kernel, plan=plan),
        grid_spec=grid_spec,
        out_shape=[
            jax.ShapeDtypeStruct((rows, heads * VD), BF16),
            jax.ShapeDtypeStruct((rows, heads * VD), F32),
            jax.ShapeDtypeStruct((rows, heads * VD), F32),
            jax.ShapeDtypeStruct((heads, 2, rows), F32),
        ],
        compiler_params=pltpu.CompilerParams(vmem_limit_bytes=40 * MIB),
        cost_estimate=attention_cost(plan, heads, 6 * VD),
        name="attend_forward",
    )(info, lam, gain, q, kv_own, kv_prev)


def backward_kernel(
    info,
    lam_ref,
    gain_ref,
    q_ref,
    own_ref,
    prev_ref,
    ga_ref,
    first_ref,
    second_ref,
    lse_ref,
    dq_ref,
    dkv_own_ref,
    dkv_prev_ref,
    sums_ref,
    kv_sc,
    dk_sc,
    dv_sc,
    dqt_sc,
    *,
    plan,
):
    bq, bk = plan.bq, plan.bk
    head, step = pl.program_id(0), pl.program_id(1)
    load_keys(plan, info, own_ref, prev_ref, kv_sc)
    lam = lam_ref[0]

    @pl.when(step == 0)
    def _():
        dk_sc[...] = jnp.zeros_like(dk_sc)
        dv_sc[...] = jnp.zeros_like(dv_sc)

    @pl.when((step == 0) & (head == 0))
    def _():
        sums_ref[...] = jnp.zeros_like(sums_ref)

    upstream = ga_ref[...]
    first_map, second_map = first_ref[...], second_ref[...]
    difference = first_map - lam * second_map
    scaling = lax.rsqrt(jnp.mean(difference * difference, axis=1, keepdims=True) + EPS)
    normal = difference * scaling
    weighted = upstream * gain_ref[...]
    inner_mean = jnp.mean(weighted * normal, axis=1, keepdims=True)
    grad = (scaling * (weighted - normal * inner_mean)).astype(BF16)
    grad_wide = grad.astype(F32)
    second_product = grad_wide * second_map
    sums_ref[0:1, :] += jnp.sum(upstream * normal, axis=0, keepdims=True)
    sums_ref[1:2, :] += jnp.sum(second_product, axis=0, keepdims=True)
    ones = jnp.ones((8, VD), F32)
    delta_first = dot(ones, grad_wide * first_map, NT, precision=lax.Precision.HIGHEST)[0:1]
    delta_second = dot(ones, second_product, NT, precision=lax.Precision.HIGHEST)[0:1]
    lse_first = lse_ref[0, 0:1, :]
    lse_second = lse_ref[0, 1:2, :]

    start = plan.query_start(info, step)
    q2 = split_halves(q_ref[...])
    dqt_sc[...] = jnp.zeros_like(dqt_sc)
    low, first, until, high = plan.ranges(info, start)

    def visit(index, masked):
        row = plan.key_row(info, index)
        key = kv_sc[pl.ds(row, bk), :VD]
        value = kv_sc[pl.ds(row, bk), VD:]
        scores = dot(key, q2, NT)
        base = dot(value, grad, NT)
        prob_first = jnp.exp(scores[:, :bq] - lse_first)
        prob_second = jnp.exp(scores[:, bq:] - lse_second)
        if masked:
            query_pos = start + lax.broadcasted_iota(jnp.int32, (1, bq), 1)
            begin = plan.doc_start(info, query_pos)
            key_pos = index * bk + lax.broadcasted_iota(jnp.int32, (bk, bq), 0)
            keep = (key_pos <= query_pos) & (key_pos >= begin)
            prob_first = jnp.where(keep, prob_first, 0.0)
            prob_second = jnp.where(keep, prob_second, 0.0)
        raw = jnp.concatenate(
            [
                (prob_first * (base - delta_first)).astype(BF16),
                (prob_second * (base - delta_second)).astype(BF16),
            ],
            axis=1,
        )
        dv_sc[pl.ds(row, bk), :] += dot(prob_first.astype(BF16), grad) - lam * dot(
            prob_second.astype(BF16), grad
        )
        dk_sc[pl.ds(row, bk), :] += dot(raw, q2)
        dqt_sc[...] += dot(key, raw, TN)

    @pl.loop(low, first)
    def _(index):
        visit(index, True)

    @pl.loop(first, until)
    def _(index):
        visit(index, False)

    @pl.loop(until, high)
    def _(index):
        visit(index, True)

    dq_t = jnp.concatenate([dqt_sc[:HD, :bq], -lam * dqt_sc[HD:, bq:]], axis=0) * SCALE
    dq_ref[...] = dq_t.T.astype(BF16)

    @pl.when(step == pl.num_programs(1) - 1)
    def _():
        lane = lax.broadcasted_iota(jnp.int32, (1, VD), 1)
        side = jnp.where(lane < HD, 1.0, -lam)
        dkv_own_ref[:, :VD] = (dk_sc[plan.prev_rows :, :] * side).astype(BF16)
        dkv_own_ref[:, VD:] = dv_sc[plan.prev_rows :, :].astype(BF16)
        dkv_prev_ref[:, :VD] = (dk_sc[: plan.prev_rows, :] * side).astype(BF16)
        dkv_prev_ref[:, VD:] = dv_sc[: plan.prev_rows, :].astype(BF16)


def attend_backward(plan, info, lam, gain, q, kv_own, kv_prev, grad_attn, first, second, lse):
    rows = q.shape[0]
    heads = q.shape[1] // VD
    bq = plan.bq
    row_spec = pl.BlockSpec((bq, VD), lambda h, i, s: (i, h))
    own_spec = pl.BlockSpec((rows, 2 * VD), lambda h, i, s: (0, h))
    prev_spec = pl.BlockSpec((plan.prev_rows, 2 * VD), lambda h, i, s: (0, h))
    grid_spec = pltpu.PrefetchScalarGridSpec(
        num_scalar_prefetch=1,
        grid=(heads, rows // bq),
        in_specs=[
            pl.BlockSpec(memory_space=pltpu.SMEM),
            pl.BlockSpec((1, VD), lambda h, i, s: (0, 0)),
            row_spec,
            own_spec,
            prev_spec,
            row_spec,
            row_spec,
            row_spec,
            pl.BlockSpec((1, 2, bq), lambda h, i, s: (h, 0, i)),
        ],
        out_specs=[
            row_spec,
            own_spec,
            prev_spec,
            pl.BlockSpec((8, VD), lambda h, i, s: (0, 0)),
        ],
        scratch_shapes=[
            pltpu.VMEM((plan.total, 2 * VD), BF16),
            pltpu.VMEM((plan.total, VD), F32),
            pltpu.VMEM((plan.total, VD), F32),
            pltpu.VMEM((VD, 2 * bq), F32),
        ],
    )
    return pl.pallas_call(
        functools.partial(backward_kernel, plan=plan),
        grid_spec=grid_spec,
        out_shape=[
            jax.ShapeDtypeStruct((rows, heads * VD), BF16),
            jax.ShapeDtypeStruct((rows, heads * 2 * VD), BF16),
            jax.ShapeDtypeStruct((plan.prev_rows, heads * 2 * VD), BF16),
            jax.ShapeDtypeStruct((8, VD), F32),
        ],
        compiler_params=pltpu.CompilerParams(vmem_limit_bytes=48 * MIB),
        cost_estimate=attention_cost(plan, heads, 16 * VD),
        name="attend_backward",
    )(info, lam, gain, q, kv_own, kv_prev, grad_attn, first, second, lse)


def norm_forward(values, gain_vec):
    scaling = lax.rsqrt(jnp.mean(values * values, axis=-1, keepdims=True) + EPS)
    return (values * scaling * gain_vec, scaling)


def norm_backward(values, scaling, gain_vec, upstream):
    normal = values * scaling
    weighted = upstream * gain_vec
    inner_mean = jnp.mean(weighted * normal, axis=-1, keepdims=True)
    return (scaling * (weighted - normal * inner_mean), jnp.sum(upstream * normal, axis=0))


def adamw(parameter, momentum, variance, gradient, learn_rate, decay_rate):
    momentum = BETA1 * momentum + (1.0 - BETA1) * gradient
    variance = BETA2 * variance + (1.0 - BETA2) * gradient * gradient
    corrected = momentum / (1.0 - BETA1**STEP)
    spread = jnp.sqrt(variance / (1.0 - BETA2**STEP))
    return (
        parameter - learn_rate * (corrected / (spread + ADAM_EPS) + decay_rate * parameter),
        momentum,
        variance,
    )


def send_keys(kv, ctx_count):
    if ctx_count == 2:
        return lax.ppermute(kv, "ctx", [(0, 1)])
    return lax.all_gather(kv, "ctx", axis=0, tiled=True)


def return_keys(grads, ctx_count):
    if ctx_count == 2:
        return lax.ppermute(grads, "ctx", [(1, 0)])
    return lax.psum_scatter(grads, "ctx", scatter_dimension=0, tiled=True)


def reduce_weight(grad, dim, ctx_count):
    share = lax.psum_scatter(grad.astype(BF16), "dp", scatter_dimension=dim, tiled=True)
    if ctx_count == 2:
        other = lax.ppermute(share, "ctx", [(0, 1), (1, 0)])
        return share.astype(F32) + other.astype(F32)
    return lax.psum(share, "ctx").astype(F32)


def on_device(
    tokens,
    cotangent,
    doc_lengths,
    qkv_weight,
    out_weight,
    inner_weight,
    down_weight,
    norm_gains,
    head_gain,
    lambdas,
    qkv_momentum,
    out_momentum,
    inner_momentum,
    down_momentum,
    norm_momentum,
    head_momentum,
    lambda_momentum,
    qkv_variance,
    out_variance,
    inner_variance,
    down_variance,
    norm_variance,
    head_variance,
    lambda_variance,
):
    micro_count, own_rows, _ = tokens.shape
    head_count = lax.axis_size("head")
    ctx_count = lax.axis_size("ctx")
    block_len = own_rows * head_count
    seq_len = block_len * ctx_count
    ctx_index = lax.axis_index("ctx")
    head_index = lax.axis_index("head")
    local_heads = qkv_weight.shape[1]
    ff_local = inner_weight.shape[2]
    ndoc = doc_lengths.shape[1]
    plan = Plan(own_rows, block_len, block_len if ctx_count == 2 else seq_len, ndoc)

    def gather_weight(weight, dim):
        return lax.all_gather(weight.astype(BF16), "dp", axis=dim, tiled=True)

    qkv_low = gather_weight(qkv_weight.reshape(-1, local_heads * 3 * VD), 0)
    out_low = gather_weight(out_weight.reshape(local_heads * VD, -1), 1)
    inner_low = gather_weight(inner_weight.reshape(-1, 2 * ff_local), 0)
    down_low = gather_weight(down_weight, 1)

    first_exp = jnp.exp(jnp.sum(lambdas[0] * lambdas[1]))
    second_exp = jnp.exp(jnp.sum(lambdas[2] * lambdas[3]))
    lambda_value = first_exp - second_exp + LAMBDA_INIT
    lam = lambda_value.reshape(1)
    head_scale = (head_gain * (1.0 - LAMBDA_INIT)).reshape(1, VD)

    chunk = jnp.arange(block_len, dtype=jnp.int32) // own_rows
    position = (
        ctx_index * block_len
        + (chunk ^ head_index) * own_rows
        + jnp.arange(block_len, dtype=jnp.int32) % own_rows
    )
    frequency = ROPE_BASE ** (
        -(jnp.arange(VD, dtype=jnp.int32) % (HD // 2)).astype(F32) / (HD // 2)
    )
    phases = position.astype(F32)[:, None] * frequency[None, :]
    cos_table, sin_table = jnp.cos(phases), jnp.sin(phases)

    def info_of(micro):
        bounds = jnp.cumsum(doc_lengths[micro], dtype=jnp.int32)
        return jnp.concatenate([jnp.stack([head_index, ctx_index]).astype(jnp.int32), bounds])

    micros = range(micro_count)
    infos = [info_of(m) for m in micros]
    own = [tokens[m].astype(F32) for m in micros]
    normed_own = [norm_forward(own[m], norm_gains[0]) for m in micros]
    normed = [jnp.concatenate(gather_chunks(normed_own[m][0].astype(BF16))) for m in micros]
    cot = [jnp.concatenate(gather_chunks(cotangent[m])) for m in micros]

    q, kv, kv_prev = [], [], []
    for m in micros:
        q_m, kv_m = project(normed[m], qkv_low, cos_table, sin_table)
        q.append(q_m)
        kv.append(kv_m)
        kv_prev.append(send_keys(kv_m, ctx_count))

    attn = [
        attend_forward(plan, infos[m], lam, head_scale, q[m], kv[m], kv_prev[m]) for m in micros
    ]
    middle, mid_scaling, normed_mid = [], [], []
    for m in micros:
        attended = reduce_chunks(split_rows(dot(attn[m][0], out_low).astype(BF16), head_count))
        middle.append(own[m] + attended)
        value, scaling = norm_forward(middle[m], norm_gains[1])
        mid_scaling.append(scaling)
        normed_mid.append(jnp.concatenate(gather_chunks(value.astype(BF16))))

    outputs, grad_middle, grad_middle_all = [], [], []
    grad_inner, grad_down = 0.0, 0.0
    gain_mid = 0.0
    for m in micros:
        gate_up = dot(normed_mid[m], inner_low)
        gates, up_part = gate_up[:, :ff_local], gate_up[:, ff_local:]
        sigmoid_gate = jax.nn.sigmoid(gates)
        hidden = (gates * sigmoid_gate * up_part).astype(BF16)
        grad_hidden = dot(cot[m], down_low, NT)
        grad_gate = grad_hidden * up_part * sigmoid_gate * (1.0 + gates * (1.0 - sigmoid_gate))
        grad_up = grad_hidden * gates * sigmoid_gate
        grad_gate_up = jnp.concatenate([grad_gate, grad_up], axis=1).astype(BF16)
        grad_mid = dot(grad_gate_up, inner_low, NT).astype(BF16)
        grad_normed_mid = reduce_chunks(split_rows(grad_mid, head_count))
        grad_mid_norm, gain_part = norm_backward(
            middle[m], mid_scaling[m], norm_gains[1], grad_normed_mid
        )
        gain_mid = gain_mid + gain_part
        grad_middle.append((cotangent[m].astype(F32) + grad_mid_norm).astype(BF16))
        grad_middle_all.append(jnp.concatenate(gather_chunks(grad_middle[m])))
        ffn = dot(hidden, down_low).astype(BF16)
        outputs.append((middle[m] + reduce_chunks(split_rows(ffn, head_count))).astype(BF16))
        grad_inner = grad_inner + dot(normed_mid[m], grad_gate_up, TN)
        grad_down = grad_down + dot(hidden, cot[m], TN)

    inner_share = reduce_weight(grad_inner, 0, ctx_count)
    down_share = reduce_weight(grad_down, 1, ctx_count)

    grad_out, grad_qkv = 0.0, 0.0
    sums = 0.0
    gain_in = 0.0
    input_grads = []
    for m in micros:
        grad_out = grad_out + dot(attn[m][0], grad_middle_all[m], TN)
        grad_attn = dot(grad_middle_all[m], out_low, NT)
        dq, dkv, dkv_prev, part = attend_backward(
            plan,
            infos[m],
            lam,
            head_scale,
            q[m],
            kv[m],
            kv_prev[m],
            grad_attn,
            attn[m][1],
            attn[m][2],
            attn[m][3],
        )
        sums = sums + part
        grad_projected, grad_norm = unproject(
            dq, dkv, return_keys(dkv_prev, ctx_count), qkv_low, cos_table, sin_table
        )
        grad_qkv = grad_qkv + dot(normed[m], grad_projected, TN)
        grad_normed = reduce_chunks(split_rows(grad_norm, head_count))
        grad_in_norm, gain_part = norm_backward(
            own[m], normed_own[m][1], norm_gains[0], grad_normed
        )
        gain_in = gain_in + gain_part
        input_grads.append((grad_middle[m].astype(F32) + grad_in_norm).astype(BF16))

    out_share = reduce_weight(grad_out, 1, ctx_count)
    qkv_share = reduce_weight(grad_qkv, 0, ctx_count)

    lambda_acc = -jnp.sum(sums[1])
    lambda_local = jnp.stack(
        [
            lambda_acc * first_exp * lambdas[1],
            lambda_acc * first_exp * lambdas[0],
            -lambda_acc * second_exp * lambdas[3],
            -lambda_acc * second_exp * lambdas[2],
        ]
    )
    norm_grad, head_grad, lambda_grad = lax.psum(
        (jnp.stack([gain_in, gain_mid]), sums[0] * (1.0 - LAMBDA_INIT), lambda_local),
        ("dp", "ctx", "head"),
    )

    states = [
        adamw(
            qkv_weight,
            qkv_momentum,
            qkv_variance,
            qkv_share.reshape(qkv_weight.shape),
            0.5 * D ** (-0.5),
            DECAY,
        ),
        adamw(
            out_weight,
            out_momentum,
            out_variance,
            out_share.reshape(out_weight.shape),
            0.5 * (H * VD) ** (-0.5),
            DECAY,
        ),
        adamw(
            inner_weight,
            inner_momentum,
            inner_variance,
            inner_share.reshape(inner_weight.shape),
            0.5 * D ** (-0.5),
            DECAY,
        ),
        adamw(
            down_weight, down_momentum, down_variance, down_share, 0.5 * FF ** (-0.5), DECAY
        ),
        adamw(norm_gains, norm_momentum, norm_variance, norm_grad, 0.4, 0.0),
        adamw(head_gain, head_momentum, head_variance, head_grad, 0.4, 0.0),
        adamw(lambdas, lambda_momentum, lambda_variance, lambda_grad, 0.1, 0.0),
    ]
    return (
        jnp.stack(outputs),
        jnp.stack(input_grads),
        *[state[0] for state in states],
        *[state[1] for state in states],
        *[state[2] for state in states],
    )


def solution(mesh):
    activation = P("dp", ("ctx", "head"), None)
    big = (P("dp", "head", None, None), P("head", None, "dp"), P("dp", None, "head"), P("head", "dp"))
    state = big + (P(), P(), P())
    return jax.shard_map(
        on_device,
        mesh=mesh,
        in_specs=(activation, activation, P("dp", None)) + state * 3,
        out_specs=(activation, activation) + state * 3,
        check_vma=False,
    )
```

```python
import functools

import jax
import jax.numpy as jnp
from jax import lax
from jax.experimental import pallas as pl
from jax.experimental.pallas import tpu as pltpu
from jax.sharding import PartitionSpec as P

D = 1536
FF = 4096
H = 12
HD = 64
STEP = 10
VD = 128


EPS = 1e-05
LAMBDA_INIT = 0.2
SCALE = 0.125
NEG = -1e30
BETA1 = 0.9
BETA2 = 0.999
ADAM_EPS = 1e-08
DECAY = 0.1
ROPE_BASE = 10000.0

MIB = 1 << 20
NT = (((1,), (1,)), ((), ()))
TN = (((0,), (0,)), ((), ()))
F32 = jnp.float32
BF16 = jnp.bfloat16


def dot(left, right, dims=(((1,), (0,)), ((), ())), **kw):
    return lax.dot_general(left, right, dims, preferred_element_type=F32, **kw)


def swap(array, bit):
    size = lax.axis_size("head")
    return lax.ppermute(array, "head", [(i, i ^ bit) for i in range(size)])


def gather_chunks(own):
    mate = swap(own, 1)
    far = swap(own, 2)
    return [own, mate, far, swap(far, 1)]


def after(value, *others):
    return lax.optimization_barrier((value, *others))[0]


def chip_sum(keep, mate):
    received = swap(mate, 1)
    rows = keep.shape[0] // 2
    far = (keep[rows:].astype(F32) + received[rows:].astype(F32)).astype(BF16)
    near = keep[:rows].astype(F32) + received[:rows].astype(F32)
    return near, far


def chunk_specs(tile, per, width, count=4):
    return [
        pl.BlockSpec((tile, width), lambda i, *_, r=r: (jnp.clip(i - r * per, 0, per - 1), 0))
        for r in range(count)
    ]


def pick(refs, per, out_ref):
    index = pl.program_id(0) // per
    for r, ref in enumerate(refs):

        @pl.when(index == r)
        def _(ref=ref):
            out_ref[...] = ref[...]


def row_spec(tile, width):
    return pl.BlockSpec((tile, width), lambda i, *_: (i, 0))


def whole_spec(shape):
    return pl.BlockSpec(shape, lambda i, *_: (0,) * len(shape))


def pair_specs(tile, per, width):
    def keep(i, *_):
        chunk = i // per
        return (chunk // 2 * per + jnp.where(chunk % 2 == 0, i % per, per - 1), 0)

    def mate(i, *_):
        chunk = i // per
        hold = jnp.maximum(chunk // 2 * per - 1, 0)
        return (jnp.where(chunk % 2 == 1, chunk // 2 * per + i % per, hold), 0)

    return [pl.BlockSpec((tile, width), keep), pl.BlockSpec((tile, width), mate)]


def pair_shapes(rows, width):
    return [jax.ShapeDtypeStruct((rows // 2, width), BF16)] * 2


def put_pair(value, per, keep_ref, mate_ref):
    even = (pl.program_id(0) // per) % 2 == 0

    @pl.when(even)
    def _():
        keep_ref[...] = value

    @pl.when(jnp.logical_not(even))
    def _():
        mate_ref[...] = value


def cost(flops, moved, transcendentals=0):
    return pl.CostEstimate(
        flops=int(flops), bytes_accessed=int(moved), transcendentals=int(transcendentals)
    )


def turn(values, cos_table, sin_table, low_half, sign):
    ahead = pltpu.roll(values, VD - HD // 2, 1)
    behind = pltpu.roll(values, HD // 2, 1)
    rotated = jnp.where(low_half, -ahead, behind)
    return values * cos_table + sign * rotated * sin_table


def low_half_mask(rows):
    lane = lax.broadcasted_iota(jnp.int32, (rows, VD), 1)
    return (lane % HD) < HD // 2


def project_kernel(*refs, heads, per):
    chunks, (w_ref, cos_ref, sin_ref, x_ref) = refs[:4], refs[4:8]
    q_refs, kv_refs = refs[8 : 8 + heads], refs[8 + heads :]
    pick(chunks, per, x_ref)
    mask = low_half_mask(x_ref.shape[0])
    cos_table, sin_table = cos_ref[...], sin_ref[...]
    out = dot(x_ref[...], w_ref[...])
    for head in range(heads):
        base = head * 3 * VD
        query = turn(out[:, base : base + VD], cos_table, sin_table, mask, 1.0) * SCALE
        key = turn(out[:, base + VD : base + 2 * VD], cos_table, sin_table, mask, 1.0)
        q_refs[head][...] = query.astype(BF16)
        kv_refs[head][:, :VD] = key.astype(BF16)
        kv_refs[head][:, VD:] = out[:, base + 2 * VD : base + 3 * VD].astype(BF16)


def project(chunks, weight, cos_table, sin_table):
    own_rows = chunks[0].shape[0]
    rows = 4 * own_rows
    heads = weight.shape[1] // (3 * VD)
    tile = min(256, own_rows)
    per = own_rows // tile
    out = pl.pallas_call(
        functools.partial(project_kernel, heads=heads, per=per),
        grid=(rows // tile,),
        in_specs=chunk_specs(tile, per, D)
        + [whole_spec(weight.shape), row_spec(tile, VD), row_spec(tile, VD)],
        out_specs=[row_spec(tile, D)]
        + [row_spec(tile, VD)] * heads
        + [row_spec(tile, 2 * VD)] * heads,
        out_shape=[jax.ShapeDtypeStruct((rows, D), BF16)]
        + [jax.ShapeDtypeStruct((rows, VD), BF16)] * heads
        + [jax.ShapeDtypeStruct((rows, 2 * VD), BF16)] * heads,
        compiler_params=pltpu.CompilerParams(vmem_limit_bytes=40 * MIB),
        cost_estimate=cost(
            2 * rows * D * weight.shape[1],
            2 * (2 * rows * D + weight.size + rows * weight.shape[1]),
        ),
        name="project",
    )(*chunks, weight, cos_table, sin_table)
    return out[0], out[1 : 1 + heads], out[1 + heads :]


def unproject_kernel(*refs, heads, per):
    dq_refs, own_refs, recv_refs = refs[:heads], refs[heads : 2 * heads], refs[2 * heads : 3 * heads]
    w_ref, cos_ref, sin_ref, gp_ref, keep_ref, mate_ref = refs[3 * heads :]
    mask = low_half_mask(gp_ref.shape[0])
    cos_table, sin_table = cos_ref[...], sin_ref[...]
    for head in range(heads):
        base = head * 3 * VD
        both = own_refs[head][...].astype(F32) + recv_refs[head][...].astype(F32)
        query = dq_refs[head][...].astype(F32)
        gp_ref[:, base : base + VD] = turn(query, cos_table, sin_table, mask, -1.0).astype(BF16)
        gp_ref[:, base + VD : base + 2 * VD] = turn(
            both[:, :VD], cos_table, sin_table, mask, -1.0
        ).astype(BF16)
        gp_ref[:, base + 2 * VD : base + 3 * VD] = both[:, VD:].astype(BF16)
    put_pair(dot(gp_ref[...], w_ref[...], NT).astype(BF16), per, keep_ref, mate_ref)


def unproject(dq, dkv_own, dkv_recv, weight, cos_table, sin_table):
    rows = dq[0].shape[0]
    heads = len(dq)
    tile = min(256, rows // 4)
    per = rows // 4 // tile
    return pl.pallas_call(
        functools.partial(unproject_kernel, heads=heads, per=per),
        grid=(rows // tile,),
        in_specs=[row_spec(tile, VD)] * heads
        + [row_spec(tile, 2 * VD)] * (2 * heads)
        + [whole_spec(weight.shape), row_spec(tile, VD), row_spec(tile, VD)],
        out_specs=[row_spec(tile, heads * 3 * VD)] + pair_specs(tile, per, D),
        out_shape=[jax.ShapeDtypeStruct((rows, heads * 3 * VD), BF16)] + pair_shapes(rows, D),
        compiler_params=pltpu.CompilerParams(vmem_limit_bytes=40 * MIB),
        cost_estimate=cost(
            2 * rows * D * weight.shape[1],
            2 * (rows * D + weight.size + 3 * rows * weight.shape[1]),
        ),
        name="unproject",
    )(*dq, *dkv_own, *dkv_recv, weight, cos_table, sin_table)


def output_kernel(*refs, heads, per):
    attn_refs = refs[:heads]
    w_ref, all_ref, keep_ref, mate_ref = refs[heads:]
    for head in range(heads):
        all_ref[:, head * VD : (head + 1) * VD] = attn_refs[head][...]
    put_pair(dot(all_ref[...], w_ref[...], NT).astype(BF16), per, keep_ref, mate_ref)


def output_projection(attn, weight):
    rows = attn[0].shape[0]
    heads = len(attn)
    tile = min(256, rows // 4)
    per = rows // 4 // tile
    return pl.pallas_call(
        functools.partial(output_kernel, heads=heads, per=per),
        grid=(rows // tile,),
        in_specs=[row_spec(tile, VD)] * heads + [whole_spec(weight.shape)],
        out_specs=[row_spec(tile, heads * VD)] + pair_specs(tile, per, D),
        out_shape=[jax.ShapeDtypeStruct((rows, heads * VD), BF16)] + pair_shapes(rows, D),
        compiler_params=pltpu.CompilerParams(vmem_limit_bytes=40 * MIB),
        cost_estimate=cost(
            2 * rows * D * weight.shape[1], 2 * (rows * D + weight.size + 2 * rows * heads * VD)
        ),
        name="output_projection",
    )(*attn, weight)


def gate_kernel(*refs, per):
    chunks, (w_ref, x_ref, hidden_ref, by_gate_ref, by_up_ref) = refs[:4], refs[4:]
    pick(chunks, per, x_ref)
    width = hidden_ref.shape[1]
    step = min(512, width)
    x = x_ref[...]
    for base in range(0, width, step):
        cols = slice(base, base + step)
        gate = dot(x, w_ref[:, cols])
        up = dot(x, w_ref[:, width + base : width + base + step])
        share = jax.nn.sigmoid(gate)
        swish = gate * share
        hidden_ref[:, cols] = (swish * up).astype(BF16)
        by_gate_ref[:, cols] = (up * share * (1.0 + gate * (1.0 - share))).astype(BF16)
        by_up_ref[:, cols] = swish.astype(BF16)


def gate_up(chunks, weight):
    own_rows = chunks[0].shape[0]
    rows = 4 * own_rows
    width = weight.shape[1] // 2
    tile = min(256, own_rows)
    per = own_rows // tile
    return pl.pallas_call(
        functools.partial(gate_kernel, per=per),
        grid=(rows // tile,),
        in_specs=chunk_specs(tile, per, D) + [whole_spec(weight.shape)],
        out_specs=[row_spec(tile, D)] + [row_spec(tile, width)] * 3,
        out_shape=[jax.ShapeDtypeStruct((rows, D), BF16)]
        + [jax.ShapeDtypeStruct((rows, width), BF16)] * 3,
        compiler_params=pltpu.CompilerParams(vmem_limit_bytes=48 * MIB),
        cost_estimate=cost(
            2 * rows * D * weight.shape[1], 2 * (2 * rows * D + weight.size + 3 * rows * width)
        ),
        name="gate_up",
    )(*chunks, weight)


def feed_kernel(*refs, per):
    chunks = refs[:4]
    hidden_ref, by_gate_ref, by_up_ref, down_ref, inner_ref = refs[4:9]
    cot_ref, grad_ref, ffn_keep, ffn_mate, mid_keep, mid_mate = refs[9:]
    pick(chunks, per, cot_ref)
    width = hidden_ref.shape[1]
    grad_hidden = dot(cot_ref[...], down_ref[...])
    grad_ref[:, :width] = (grad_hidden * by_gate_ref[...].astype(F32)).astype(BF16)
    grad_ref[:, width:] = (grad_hidden * by_up_ref[...].astype(F32)).astype(BF16)
    put_pair(dot(hidden_ref[...], down_ref[...], NT).astype(BF16), per, ffn_keep, ffn_mate)
    put_pair(dot(grad_ref[...], inner_ref[...], NT).astype(BF16), per, mid_keep, mid_mate)


def feed(chunks, hidden, by_gate, by_up, down, inner):
    own_rows = chunks[0].shape[0]
    rows = 4 * own_rows
    width = hidden.shape[1]
    tile = min(256, own_rows)
    per = own_rows // tile
    return pl.pallas_call(
        functools.partial(feed_kernel, per=per),
        grid=(rows // tile,),
        in_specs=chunk_specs(tile, per, D)
        + [row_spec(tile, width)] * 3
        + [whole_spec(down.shape), whole_spec(inner.shape)],
        out_specs=[row_spec(tile, D), row_spec(tile, 2 * width)]
        + pair_specs(tile, per, D)
        + pair_specs(tile, per, D),
        out_shape=[
            jax.ShapeDtypeStruct((rows, D), BF16),
            jax.ShapeDtypeStruct((rows, 2 * width), BF16),
        ]
        + pair_shapes(rows, D)
        + pair_shapes(rows, D),
        compiler_params=pltpu.CompilerParams(vmem_limit_bytes=56 * MIB),
        cost_estimate=cost(
            8 * rows * D * width, 2 * (4 * rows * D + down.size + inner.size + 5 * rows * width)
        ),
        name="feed",
    )(*chunks, hidden, by_gate, by_up, down, inner)


class Plan:
    def __init__(self, own_rows, block_len, prev_rows, ndoc):
        self.own_rows = own_rows
        self.block_len = block_len
        self.prev_rows = prev_rows
        self.ndoc = ndoc
        self.bq = min(256, own_rows)
        self.bk = min(512, own_rows)
        self.total = prev_rows + block_len

    def doc_start(self, info, pos):
        start = jnp.zeros_like(pos)
        for item in range(self.ndoc):
            start = jnp.where(pos >= info[2 + item], info[2 + item], start)
        return start

    def query_start(self, info, index):
        per = self.own_rows // self.bq
        chunk = (index // per) ^ info[0]
        return info[1] * self.block_len + chunk * self.own_rows + (index % per) * self.bq

    def key_row(self, info, index):
        per = self.own_rows // self.bk
        blocks = self.block_len // self.bk
        owner = index // blocks
        local = index % blocks
        inside = (((local // per) ^ info[0]) * per + local % per) * self.bk
        base = jnp.where(owner == info[1], self.prev_rows, owner * self.block_len)
        return pl.multiple_of(base + inside, self.bk)

    def ranges(self, info, start):
        last = start + self.bq - 1
        low = self.doc_start(info, start) // self.bk
        high = last // self.bk + 1
        open_from = (self.doc_start(info, last) + self.bk - 1) // self.bk
        first = jnp.minimum(jnp.maximum(open_from, low), high)
        until = jnp.maximum(first, jnp.minimum((start + 1) // self.bk, high))
        return low, first, until, high


def split_halves(q):
    lane = lax.broadcasted_iota(jnp.int32, q.shape, 1)
    zero = jnp.zeros_like(q)
    return jnp.concatenate([jnp.where(lane < HD, q, zero), jnp.where(lane >= HD, q, zero)], axis=0)


def load_keys(plan, info, own_ref, prev_ref, kv_sc):
    @pl.when(pl.program_id(0) == 0)
    def _():
        kv_sc[plan.prev_rows :, :] = own_ref[...]

        @pl.when(info[1] > 0)
        def _():
            kv_sc[: plan.prev_rows, :] = prev_ref[...]


def forward_kernel(
    info,
    lam_ref,
    gain_ref,
    q_ref,
    own_ref,
    prev_ref,
    attn_ref,
    first_ref,
    second_ref,
    lse_ref,
    kv_sc,
    m_sc,
    l_sc,
    acc_sc,
    *,
    plan,
):
    bq, bk = plan.bq, plan.bk
    load_keys(plan, info, own_ref, prev_ref, kv_sc)
    start = plan.query_start(info, pl.program_id(0))
    q2 = split_halves(q_ref[...])
    m_sc[...] = jnp.full_like(m_sc, NEG)
    l_sc[...] = jnp.zeros_like(l_sc)
    acc_sc[...] = jnp.zeros_like(acc_sc)
    low, first, until, high = plan.ranges(info, start)

    def visit(index, masked):
        row = plan.key_row(info, index)
        key = kv_sc[pl.ds(row, bk), :VD]
        value = kv_sc[pl.ds(row, bk), VD:]
        scores = dot(q2, key, NT)
        if masked:
            query_pos = start + lax.broadcasted_iota(jnp.int32, (bq, 1), 0)
            begin = plan.doc_start(info, query_pos)
            key_pos = index * bk + lax.broadcasted_iota(jnp.int32, (bq, bk), 1)
            keep = (key_pos <= query_pos) & (key_pos >= begin)
            scores = jnp.concatenate(
                [jnp.where(keep, scores[:bq], NEG), jnp.where(keep, scores[bq:], NEG)], axis=0
            )
        before = m_sc[...]
        after = jnp.maximum(before, jnp.max(scores, axis=1, keepdims=True))
        weights = jnp.exp(scores - jnp.tile(after, (1, bk // VD)))
        factor = jnp.exp(before - after)
        m_sc[...] = after
        l_sc[...] = l_sc[...] * factor + jnp.sum(weights, axis=1, keepdims=True)
        acc_sc[...] = acc_sc[...] * factor + dot(weights.astype(BF16), value)

    @pl.loop(low, first)
    def _(index):
        visit(index, True)

    @pl.loop(first, until)
    def _(index):
        visit(index, False)

    @pl.loop(until, high)
    def _(index):
        visit(index, True)

    total = l_sc[...]
    maps = acc_sc[...] * (1.0 / total)
    first_map, second_map = maps[:bq], maps[bq:]
    first_ref[...] = first_map
    second_ref[...] = second_map
    difference = first_map - lam_ref[0] * second_map
    scaling = lax.rsqrt(jnp.mean(difference * difference, axis=1, keepdims=True) + EPS)
    attn_ref[...] = (difference * scaling * gain_ref[...]).astype(BF16)
    lse = (m_sc[...] + jnp.log(total)).T
    lse_ref[0:1, :] = lse[0:1, :bq]
    lse_ref[1:2, :] = lse[0:1, bq:]


def attention_cost(plan, per_pair, extra=0):
    pairs = plan.block_len * plan.block_len * 5 // 8
    return cost(pairs * per_pair + extra, plan.block_len * VD * 32, 2 * pairs)


def attend_forward(plan, info, lam, gain, q, kv_own, kv_prev):
    rows, bq = plan.block_len, plan.bq
    grid_spec = pltpu.PrefetchScalarGridSpec(
        num_scalar_prefetch=1,
        grid=(rows // bq,),
        in_specs=[
            pl.BlockSpec(memory_space=pltpu.SMEM),
            whole_spec((1, VD)),
            row_spec(bq, VD),
            whole_spec((rows, 2 * VD)),
            whole_spec((plan.prev_rows, 2 * VD)),
        ],
        out_specs=[row_spec(bq, VD)] * 3 + [pl.BlockSpec((2, bq), lambda i, *_: (0, i))],
        scratch_shapes=[
            pltpu.VMEM((plan.total, 2 * VD), BF16),
            pltpu.VMEM((2 * bq, VD), F32),
            pltpu.VMEM((2 * bq, VD), F32),
            pltpu.VMEM((2 * bq, VD), F32),
        ],
    )
    return pl.pallas_call(
        functools.partial(forward_kernel, plan=plan),
        grid_spec=grid_spec,
        out_shape=[
            jax.ShapeDtypeStruct((rows, VD), BF16),
            jax.ShapeDtypeStruct((rows, VD), F32),
            jax.ShapeDtypeStruct((rows, VD), F32),
            jax.ShapeDtypeStruct((2, rows), F32),
        ],
        compiler_params=pltpu.CompilerParams(vmem_limit_bytes=40 * MIB),
        cost_estimate=attention_cost(plan, 6 * VD),
        name="attend_forward",
    )(info, lam, gain, q, kv_own, kv_prev)


def backward_kernel(
    info,
    lam_ref,
    gain_ref,
    q_ref,
    own_ref,
    prev_ref,
    gm_0_ref,
    gm_1_ref,
    gm_2_ref,
    gm_3_ref,
    w_ref,
    first_ref,
    second_ref,
    lse_ref,
    gm_ref,
    dq_ref,
    dkv_own_ref,
    dkv_prev_ref,
    sums_ref,
    kv_sc,
    dk_sc,
    dv_sc,
    dqt_sc,
    *,
    plan,
):
    bq, bk = plan.bq, plan.bk
    step = pl.program_id(0)
    load_keys(plan, info, own_ref, prev_ref, kv_sc)
    lam = lam_ref[0]

    @pl.when(step == 0)
    def _():
        dk_sc[...] = jnp.zeros_like(dk_sc)
        dv_sc[...] = jnp.zeros_like(dv_sc)

        sums_ref[...] = jnp.zeros_like(sums_ref)

    pick((gm_0_ref, gm_1_ref, gm_2_ref, gm_3_ref), plan.own_rows // bq, gm_ref)
    upstream = dot(gm_ref[...], w_ref[...])
    first_map, second_map = first_ref[...], second_ref[...]
    difference = first_map - lam * second_map
    scaling = lax.rsqrt(jnp.mean(difference * difference, axis=1, keepdims=True) + EPS)
    normal = difference * scaling
    weighted = upstream * gain_ref[...]
    inner_mean = jnp.mean(weighted * normal, axis=1, keepdims=True)
    grad = (scaling * (weighted - normal * inner_mean)).astype(BF16)
    grad_wide = grad.astype(F32)
    second_product = grad_wide * second_map
    sums_ref[0:1, :] += jnp.sum(upstream * normal, axis=0, keepdims=True)
    sums_ref[1:2, :] += jnp.sum(second_product, axis=0, keepdims=True)
    ones = jnp.ones((8, VD), F32)
    delta_first = dot(ones, grad_wide * first_map, NT, precision=lax.Precision.HIGHEST)[0:1]
    delta_second = dot(ones, second_product, NT, precision=lax.Precision.HIGHEST)[0:1]
    lse_first = lse_ref[0:1, :]
    lse_second = lse_ref[1:2, :]

    start = plan.query_start(info, step)
    q2 = split_halves(q_ref[...])
    dqt_sc[...] = jnp.zeros_like(dqt_sc)
    low, first, until, high = plan.ranges(info, start)

    def visit(index, masked):
        row = plan.key_row(info, index)
        key = kv_sc[pl.ds(row, bk), :VD]
        value = kv_sc[pl.ds(row, bk), VD:]
        scores = dot(key, q2, NT)
        base = dot(value, grad, NT)
        prob_first = jnp.exp(scores[:, :bq] - lse_first)
        prob_second = jnp.exp(scores[:, bq:] - lse_second)
        if masked:
            query_pos = start + lax.broadcasted_iota(jnp.int32, (1, bq), 1)
            begin = plan.doc_start(info, query_pos)
            key_pos = index * bk + lax.broadcasted_iota(jnp.int32, (bk, bq), 0)
            keep = (key_pos <= query_pos) & (key_pos >= begin)
            prob_first = jnp.where(keep, prob_first, 0.0)
            prob_second = jnp.where(keep, prob_second, 0.0)
        raw = jnp.concatenate(
            [
                (prob_first * (base - delta_first)).astype(BF16),
                (prob_second * (base - delta_second)).astype(BF16),
            ],
            axis=1,
        )
        dv_sc[pl.ds(row, bk), :] += dot(prob_first.astype(BF16), grad) - lam * dot(
            prob_second.astype(BF16), grad
        )
        dk_sc[pl.ds(row, bk), :] += dot(raw, q2)
        dqt_sc[...] += dot(key, raw, TN)

    @pl.loop(low, first)
    def _(index):
        visit(index, True)

    @pl.loop(first, until)
    def _(index):
        visit(index, False)

    @pl.loop(until, high)
    def _(index):
        visit(index, True)

    dq_t = jnp.concatenate([dqt_sc[:HD, :bq], -lam * dqt_sc[HD:, bq:]], axis=0) * SCALE
    dq_ref[...] = dq_t.T.astype(BF16)

    @pl.when(step == pl.num_programs(0) - 1)
    def _():
        lane = lax.broadcasted_iota(jnp.int32, (1, VD), 1)
        side = jnp.where(lane < HD, 1.0, -lam)
        dkv_own_ref[:, :VD] = (dk_sc[plan.prev_rows :, :] * side).astype(BF16)
        dkv_own_ref[:, VD:] = dv_sc[plan.prev_rows :, :].astype(BF16)
        dkv_prev_ref[:, :VD] = (dk_sc[: plan.prev_rows, :] * side).astype(BF16)
        dkv_prev_ref[:, VD:] = dv_sc[: plan.prev_rows, :].astype(BF16)


def attend_backward(plan, info, lam, gain, q, kv_own, kv_prev, gm, weight, head, maps, keep_gm):
    rows, bq = plan.block_len, plan.bq
    first, second, lse = maps
    gm_spec = row_spec(bq, D) if keep_gm else whole_spec((bq, D))
    gm_rows = rows if keep_gm else bq
    grid_spec = pltpu.PrefetchScalarGridSpec(
        num_scalar_prefetch=1,
        grid=(rows // bq,),
        in_specs=[
            pl.BlockSpec(memory_space=pltpu.SMEM),
            whole_spec((1, VD)),
            row_spec(bq, VD),
            whole_spec((rows, 2 * VD)),
            whole_spec((plan.prev_rows, 2 * VD)),
        ]
        + chunk_specs(bq, plan.own_rows // bq, D)
        + [
            pl.BlockSpec((D, VD), lambda i, *_: (0, head)),
            row_spec(bq, VD),
            row_spec(bq, VD),
            pl.BlockSpec((2, bq), lambda i, *_: (0, i)),
        ],
        out_specs=[
            gm_spec,
            row_spec(bq, VD),
            whole_spec((rows, 2 * VD)),
            whole_spec((plan.prev_rows, 2 * VD)),
            whole_spec((8, VD)),
        ],
        scratch_shapes=[
            pltpu.VMEM((plan.total, 2 * VD), BF16),
            pltpu.VMEM((plan.total, VD), F32),
            pltpu.VMEM((plan.total, VD), F32),
            pltpu.VMEM((VD, 2 * bq), F32),
        ],
    )
    return pl.pallas_call(
        functools.partial(backward_kernel, plan=plan),
        grid_spec=grid_spec,
        out_shape=[
            jax.ShapeDtypeStruct((gm_rows, D), BF16),
            jax.ShapeDtypeStruct((rows, VD), BF16),
            jax.ShapeDtypeStruct((rows, 2 * VD), BF16),
            jax.ShapeDtypeStruct((plan.prev_rows, 2 * VD), BF16),
            jax.ShapeDtypeStruct((8, VD), F32),
        ],
        compiler_params=pltpu.CompilerParams(vmem_limit_bytes=48 * MIB),
        cost_estimate=attention_cost(plan, 16 * VD, 2 * rows * D * VD),
        name="attend_backward",
    )(info, lam, gain, q, kv_own, kv_prev, *gm, weight, first, second, lse)


def norm_forward(values, gain_vec):
    scaling = lax.rsqrt(jnp.mean(values * values, axis=-1, keepdims=True) + EPS)
    return (values * scaling * gain_vec, scaling)


def norm_backward(values, scaling, gain_vec, upstream):
    normal = values * scaling
    weighted = upstream * gain_vec
    inner_mean = jnp.mean(weighted * normal, axis=-1, keepdims=True)
    return (scaling * (weighted - normal * inner_mean), jnp.sum(upstream * normal, axis=0))


def adamw(parameter, momentum, variance, gradient, learn_rate, decay_rate):
    momentum = BETA1 * momentum + (1.0 - BETA1) * gradient
    variance = BETA2 * variance + (1.0 - BETA2) * gradient * gradient
    corrected = momentum / (1.0 - BETA1**STEP)
    spread = jnp.sqrt(variance / (1.0 - BETA2**STEP))
    return (
        parameter - learn_rate * (corrected / (spread + ADAM_EPS) + decay_rate * parameter),
        momentum,
        variance,
    )


def send_keys(kv, ctx_count):
    if ctx_count == 2:
        return lax.ppermute(kv, "ctx", [(0, 1)])
    return lax.all_gather(kv, "ctx", axis=0, tiled=True)


def return_keys(grads, ctx_count):
    if ctx_count == 2:
        return lax.ppermute(grads, "ctx", [(1, 0)])
    return lax.psum_scatter(grads, "ctx", scatter_dimension=0, tiled=True)


def scatter_weight(grad, *others):
    grad = after(grad.astype(BF16), *others)
    return lax.psum_scatter(grad, "dp", scatter_dimension=0, tiled=True)


def sum_blocks(share, ctx_count):
    if ctx_count == 2:
        other = lax.ppermute(share, "ctx", [(0, 1), (1, 0)])
        return share.astype(F32) + other.astype(F32)
    return lax.psum(share, "ctx").astype(F32)


def on_device(
    tokens,
    cotangent,
    doc_lengths,
    qkv_weight,
    out_weight,
    inner_weight,
    down_weight,
    norm_gains,
    head_gain,
    lambdas,
    qkv_momentum,
    out_momentum,
    inner_momentum,
    down_momentum,
    norm_momentum,
    head_momentum,
    lambda_momentum,
    qkv_variance,
    out_variance,
    inner_variance,
    down_variance,
    norm_variance,
    head_variance,
    lambda_variance,
):
    micro_count, own_rows, _ = tokens.shape
    head_count = lax.axis_size("head")
    ctx_count = lax.axis_size("ctx")
    block_len = own_rows * head_count
    seq_len = block_len * ctx_count
    ctx_index = lax.axis_index("ctx")
    head_index = lax.axis_index("head")
    local_heads = qkv_weight.shape[1]
    ff_local = inner_weight.shape[2]
    ndoc = doc_lengths.shape[1]
    plan = Plan(own_rows, block_len, block_len if ctx_count == 2 else seq_len, ndoc)

    def gather_weight(shard):
        return lax.all_gather(shard.astype(BF16), "dp", axis=0, tiled=True)

    qkv_low = gather_weight(qkv_weight.reshape(-1, local_heads * 3 * VD))
    out_t = gather_weight(out_weight.reshape(local_heads * VD, -1).T)
    inner_low = gather_weight(inner_weight.reshape(-1, 2 * ff_local))
    down_t = gather_weight(down_weight.T)

    first_exp = jnp.exp(jnp.sum(lambdas[0] * lambdas[1]))
    second_exp = jnp.exp(jnp.sum(lambdas[2] * lambdas[3]))
    lambda_value = first_exp - second_exp + LAMBDA_INIT
    lam = lambda_value.reshape(1)
    head_scale = (head_gain * (1.0 - LAMBDA_INIT)).reshape(1, VD)

    chunk = jnp.arange(block_len, dtype=jnp.int32) // own_rows
    position = (
        ctx_index * block_len
        + (chunk ^ head_index) * own_rows
        + jnp.arange(block_len, dtype=jnp.int32) % own_rows
    )
    frequency = ROPE_BASE ** (
        -(jnp.arange(VD, dtype=jnp.int32) % (HD // 2)).astype(F32) / (HD // 2)
    )
    phases = position.astype(F32)[:, None] * frequency[None, :]
    cos_table, sin_table = jnp.cos(phases), jnp.sin(phases)

    def info_of(micro):
        bounds = jnp.cumsum(doc_lengths[micro], dtype=jnp.int32)
        return jnp.concatenate([jnp.stack([head_index, ctx_index]).astype(jnp.int32), bounds])

    micros = range(micro_count)
    heads = range(local_heads)
    infos = [info_of(m) for m in micros]
    own = [tokens[m].astype(F32) for m in micros]
    normed_own = [norm_forward(own[m], norm_gains[0]) for m in micros]
    normed = [gather_chunks(normed_own[m][0].astype(BF16)) for m in micros]
    cot = [
        gather_chunks(after(cotangent[m], *[normed[n][2] for n in micros])) for m in micros
    ]

    normed_all, q, kv, kv_prev = [], [], [], []
    for m in micros:
        chunks = after(normed[m], normed[-1]) if m == 0 else normed[m]
        all_m, q_m, kv_m = project(chunks, qkv_low, cos_table, sin_table)
        normed_all.append(all_m)
        q.append(q_m)
        kv.append(kv_m)
        kv_prev.append([send_keys(kv_m[h], ctx_count) for h in heads])

    maps, attn_all, middle, mid_scaling, normed_mid, mid_own = [], [], [], [], [], []
    far_sums = []
    for m in micros:
        outs = []
        for h in heads:
            query = q[m][h]
            if m == 0 and h == 0:
                query = after(query, kv[-1], out_t)
            elif m == 0 and h == 1:
                query = after(query, outs[0], cot[0][2])
            elif m > 0 and h == 0:
                query = after(query, far_sums[m - 1], cot[m][2])
            elif m > 0 and h == local_heads - 1:
                query = after(query, outs[h - 1], mid_own[m - 1])
            else:
                query = after(query, outs[h - 1])
            outs.append(
                attend_forward(plan, infos[m], lam, head_scale, query, kv[m][h], kv_prev[m][h])
            )
        maps.append([out[1:] for out in outs])
        all_m, keep, mate = output_projection([out[0] for out in outs], out_t)
        attn_all.append(all_m)
        near, far = chip_sum(keep, mate)
        far_sums.append(far)
        middle.append(own[m] + near + swap(far, 2).astype(F32))
        value, scaling = norm_forward(middle[m], norm_gains[1])
        mid_scaling.append(scaling)
        mid_own.append(value.astype(BF16))
        normed_mid.append(gather_chunks(mid_own[m]))

    grad_middle, gm_chunks, ffn_pairs, grads_inner, grads_down = [], [], [], [], []
    gain_mid = 0.0
    waits = [far_sums[-1]]
    for m in micros:
        x_all, hidden, by_gate, by_up = gate_up(after(normed_mid[m], *waits), inner_low)
        if m == 0:
            waits = mid_own[1:]
        else:
            grads_inner[m - 1] = grads_inner[m - 1](hidden)
            waits = [grad_middle[m - 1], grads_inner[m - 1]]
        cot_all, grad_gate_up, ffn_keep, ffn_mate, mid_keep, mid_mate = feed(
            after(cot[m], *waits), hidden, by_gate, by_up, down_t, inner_low
        )
        ffn_pairs.append((ffn_keep, ffn_mate))
        near, far = chip_sum(mid_keep, mid_mate)
        waits = [far]
        grad_normed_mid = near + swap(far, 2).astype(F32)
        grad_mid_norm, gain_part = norm_backward(
            middle[m], mid_scaling[m], norm_gains[1], grad_normed_mid
        )
        gain_mid = gain_mid + gain_part
        grad_middle.append((cotangent[m].astype(F32) + grad_mid_norm).astype(BF16))
        gm_chunks.append(gather_chunks(grad_middle[m]))
        grads_inner.append(
            lambda other, x=x_all, g=grad_gate_up: dot(after(x, other), g, TN)
        )
        grads_down.append(lambda other, x=cot_all, g=hidden: dot(after(x, other), g, TN))

    grad_inner = grads_inner[-1](far)
    for m in micros[:-1]:
        grad_inner = grad_inner + grads_inner[m]
    grad_down = grads_down[0](grad_inner)
    for m in micros[1:]:
        grad_down = grad_down + grads_down[m](grad_inner)
    feed_part = scatter_weight(
        jnp.concatenate([grad_inner.astype(BF16), grad_down.astype(BF16)], axis=1)
    )

    sums = 0.0
    last = (grad_down,)
    dqs, dkvs, recvs, gm_alls = [], [], [], []
    far_ffn, across_ffn, outputs = [], [], []
    for m in micros:
        dq, dkv, recv = [], [], []
        for h in heads:
            if m == 0 and h == 1:
                last += (grad_middle[-1],)
            if m == 1 and h == 0:
                last += (far_ffn[0],)
            if m == 1 and h == 1:
                last += (far_ffn[1],)
            if m == 1 and h == 2:
                last += (recv[0], far_in[0], across_ffn[0])
            gm_out, dq_h, dkv_h, dkv_prev, part = attend_backward(
                plan,
                infos[m],
                lam,
                head_scale,
                after(q[m][h], *last),
                kv[m][h],
                kv_prev[m][h],
                gm_chunks[m],
                out_t,
                h,
                maps[m][h],
                h == 0,
            )
            last = (dq_h,)
            if h == 0:
                gm_alls.append(gm_out)
            sums = sums + part
            dq.append(dq_h)
            dkv.append(dkv_h)
            recv.append(return_keys(dkv_prev, ctx_count))
            if m == 1 and h == 0:
                back = unproject(
                    after(dqs[0], *last), dkvs[0], recvs[0], qkv_low, cos_table, sin_table
                )
                grads_projected = [back[0]]
                near_in, far_in = [[value] for value in chip_sum(*back[1:])]
                last = (back[0],)
        dqs.append(dq)
        dkvs.append(dkv)
        recvs.append(recv)
        if m == 0:
            for n in micros:
                keep, mate = ffn_pairs[n]
                near, far = chip_sum(keep, after(mate, *[gm_chunks[k][2] for k in micros]))
                far_ffn.append(far)
                across_ffn.append(swap(far, 2))
                outputs.append(
                    (middle[n] + near + across_ffn[n].astype(F32)).astype(BF16)
                )

    grad_out = 0.0
    for m in micros:
        grad_out = grad_out + dot(after(gm_alls[m], *last), attn_all[m], TN)
    grad_qkv = dot(normed_all[0], after(grads_projected[0], grad_out, recvs[-1][1], across_ffn[1]), TN)
    back = unproject(
        after(dqs[-1], grad_qkv), dkvs[-1], recvs[-1], qkv_low, cos_table, sin_table
    )
    grads_projected.append(back[0])
    near, far = chip_sum(*back[1:])
    near_in.append(near)
    far_in.append(far)
    across_in = [swap(far_in[m], 2) for m in micros]
    grad_qkv = grad_qkv + dot(normed_all[-1], after(back[0], far, across_in[0]), TN)
    grad_last = jnp.concatenate([grad_qkv.astype(BF16), grad_out.astype(BF16)], axis=1)
    last_part = scatter_weight(grad_last, feed_part)
    last_share = sum_blocks(last_part, ctx_count)
    feed_share = sum_blocks(feed_part, ctx_count)
    inner_share = feed_share[:, : inner_low.shape[1]]
    down_share = feed_share[:, inner_low.shape[1] :]
    qkv_share = last_share[:, : qkv_low.shape[1]]
    out_share = last_share[:, qkv_low.shape[1] :]

    gain_in = 0.0
    input_grads = []
    for m in micros:
        grad_in_norm, gain_part = norm_backward(
            own[m],
            normed_own[m][1],
            norm_gains[0],
            near_in[m] + across_in[m].astype(F32),
        )
        gain_in = gain_in + gain_part
        input_grads.append((grad_middle[m].astype(F32) + grad_in_norm).astype(BF16))

    lambda_acc = -jnp.sum(sums[1])
    lambda_local = jnp.stack(
        [
            lambda_acc * first_exp * lambdas[1],
            lambda_acc * first_exp * lambdas[0],
            -lambda_acc * second_exp * lambdas[3],
            -lambda_acc * second_exp * lambdas[2],
        ]
    )
    norm_grad, head_grad, lambda_grad = lax.psum(
        (jnp.stack([gain_in, gain_mid]), sums[0] * (1.0 - LAMBDA_INIT), lambda_local),
        ("dp", "ctx", "head"),
    )

    states = [
        adamw(
            qkv_weight,
            qkv_momentum,
            qkv_variance,
            qkv_share.reshape(qkv_weight.shape),
            0.5 * D ** (-0.5),
            DECAY,
        ),
        adamw(
            out_weight,
            out_momentum,
            out_variance,
            out_share.T.reshape(out_weight.shape),
            0.5 * (H * VD) ** (-0.5),
            DECAY,
        ),
        adamw(
            inner_weight,
            inner_momentum,
            inner_variance,
            inner_share.reshape(inner_weight.shape),
            0.5 * D ** (-0.5),
            DECAY,
        ),
        adamw(
            down_weight, down_momentum, down_variance, down_share.T, 0.5 * FF ** (-0.5), DECAY
        ),
        adamw(norm_gains, norm_momentum, norm_variance, norm_grad, 0.4, 0.0),
        adamw(head_gain, head_momentum, head_variance, head_grad, 0.4, 0.0),
        adamw(lambdas, lambda_momentum, lambda_variance, lambda_grad, 0.1, 0.0),
    ]
    return (
        jnp.stack(outputs),
        jnp.stack(input_grads),
        *[state[0] for state in states],
        *[state[1] for state in states],
        *[state[2] for state in states],
    )


def solution(mesh):
    activation = P("dp", ("ctx", "head"), None)
    big = (P("dp", "head", None, None), P("head", None, "dp"), P("dp", None, "head"), P("head", "dp"))
    state = big + (P(), P(), P())
    return jax.shard_map(
        on_device,
        mesh=mesh,
        in_specs=(activation, activation, P("dp", None)) + state * 3,
        out_specs=(activation, activation) + state * 3,
        check_vma=False,
    )
```

```python
import functools

import jax
import jax.numpy as jnp
from jax import lax
from jax.experimental import pallas as pl
from jax.experimental.pallas import tpu as pltpu
from jax.sharding import PartitionSpec as P

D = 1536
FF = 4096
H = 12
HD = 64
STEP = 10
VD = 128


EPS = 1e-05
LAMBDA_INIT = 0.2
SCALE = 0.125
NEG = -1e30
BETA1 = 0.9
BETA2 = 0.999
ADAM_EPS = 1e-08
DECAY = 0.1
ROPE_BASE = 10000.0

MIB = 1 << 20
NT = (((1,), (1,)), ((), ()))
TN = (((0,), (0,)), ((), ()))
F32 = jnp.float32
BF16 = jnp.bfloat16


def dot(left, right, dims=(((1,), (0,)), ((), ())), **kw):
    return lax.dot_general(left, right, dims, preferred_element_type=F32, **kw)


def swap(array, bit):
    size = lax.axis_size("head")
    return lax.ppermute(array, "head", [(i, i ^ bit) for i in range(size)])


def split_rows(array, count):
    size = array.shape[0] // count
    return [array[i * size : (i + 1) * size] for i in range(count)]


class Gather:
    def __init__(self, own):
        parts = 2 if own.shape[0] % 512 == 0 else 1
        self.own = own
        self.mate = swap(own, 1)
        self.far = [swap(part, 2) for part in split_rows(own, parts)]
        self.far_mate = None

    def pieces(self):
        if self.far_mate is None:
            self.far_mate = [swap(part, 1) for part in self.far]
        return [self.own, self.mate, *self.far, *self.far_mate]


class Reduce:
    def __init__(self, keep, mate):
        received = swap(mate, 1)
        rows = keep.shape[0] // 2
        parts = 2 if rows % 512 == 0 else 1
        total = keep.astype(F32) + received.astype(F32)
        self.near = keep[:rows].astype(F32) + received[:rows].astype(F32)
        self.sent = [part.astype(BF16) for part in split_rows(total[rows:], parts)]
        self.send()

    def send(self, *others):
        self.across = [swap(part, 2) for part in after(self.sent, *others)]

    def value(self):
        return self.near + jnp.concatenate(self.across).astype(F32)


def after(value, *others):
    return lax.optimization_barrier((value, *others))[0]


def together(result, *slots):
    values = lax.optimization_barrier((result, *[array[i] for array, i in slots]))
    for (array, i), value in zip(slots, values[1:]):
        array[i] = value
    return values[0]


def slots_of(array, *wanted):
    return [(array, i) for i in (wanted or range(len(array))) if i < len(array)]


def butterfly(array):
    for axis in ("head", "ctx", "dp"):
        size = lax.axis_size(axis)
        bit = 1
        while bit < size:
            array = array + lax.ppermute(array, axis, [(i, i ^ bit) for i in range(size)])
            bit *= 2
    return array


def chunk_specs(tile, pieces):
    specs, start = [], 0
    for piece in pieces:
        count = piece.shape[0] // tile
        specs.append(
            pl.BlockSpec(
                (tile, piece.shape[1]),
                lambda i, *_, a=start, n=count: (jnp.clip(i - a, 0, n - 1), 0),
            )
        )
        start += count
    return specs


def chunk_ends(tile, pieces):
    ends, start = [], 0
    for piece in pieces:
        start += piece.shape[0] // tile
        ends.append(start)
    return ends


def pick(refs, ends, out_ref):
    index = pl.program_id(0)
    start = 0
    for ref, end in zip(refs, ends):

        @pl.when((index >= start) & (index < end))
        def _(ref=ref):
            out_ref[...] = ref[...]

        start = end


def columns_spec(rows, width, index):
    return pl.BlockSpec((rows, width), lambda i, *_: (0, index))


def row_spec(tile, width):
    return pl.BlockSpec((tile, width), lambda i, *_: (i, 0))


def whole_spec(shape):
    return pl.BlockSpec(shape, lambda i, *_: (0,) * len(shape))


def pair_specs(tile, per, width):
    def keep(i, *_):
        chunk = i // per
        return (chunk // 2 * per + jnp.where(chunk % 2 == 0, i % per, per - 1), 0)

    def mate(i, *_):
        chunk = i // per
        hold = jnp.maximum(chunk // 2 * per - 1, 0)
        return (jnp.where(chunk % 2 == 1, chunk // 2 * per + i % per, hold), 0)

    return [pl.BlockSpec((tile, width), keep), pl.BlockSpec((tile, width), mate)]


def pair_shapes(rows, width):
    return [jax.ShapeDtypeStruct((rows // 2, width), BF16)] * 2


def put_pair(value, per, keep_ref, mate_ref):
    even = (pl.program_id(0) // per) % 2 == 0

    @pl.when(even)
    def _():
        keep_ref[...] = value

    @pl.when(jnp.logical_not(even))
    def _():
        mate_ref[...] = value


def cost(flops, moved, transcendentals=0):
    return pl.CostEstimate(
        flops=int(flops), bytes_accessed=int(moved), transcendentals=int(transcendentals)
    )


def turn(values, cos_table, sin_table, low_half, sign):
    ahead = pltpu.roll(values, VD - HD // 2, 1)
    behind = pltpu.roll(values, HD // 2, 1)
    rotated = jnp.where(low_half, -ahead, behind)
    return values * cos_table + sign * rotated * sin_table


def low_half_mask(rows):
    lane = lax.broadcasted_iota(jnp.int32, (rows, VD), 1)
    return (lane % HD) < HD // 2


def project_kernel(*refs, heads, ends):
    count = len(ends)
    w_ref, cos_ref, sin_ref, x_ref = refs[count : count + 4]
    q_refs, kv_refs = refs[count + 4 : count + 4 + heads], refs[count + 4 + heads :]
    pick(refs[:count], ends, x_ref)
    mask = low_half_mask(x_ref.shape[0])
    cos_table, sin_table = cos_ref[...], sin_ref[...]
    out = dot(x_ref[...], w_ref[...])
    for head in range(heads):
        base = head * 3 * VD
        query = turn(out[:, base : base + VD], cos_table, sin_table, mask, 1.0) * SCALE
        key = turn(out[:, base + VD : base + 2 * VD], cos_table, sin_table, mask, 1.0)
        q_refs[head][...] = query.astype(BF16)
        kv_refs[head][:, :VD] = key.astype(BF16)
        kv_refs[head][:, VD:] = out[:, base + 2 * VD : base + 3 * VD].astype(BF16)


def project(chunks, weight, cos_table, sin_table):
    own_rows = chunks[0].shape[0]
    rows = 4 * own_rows
    heads = weight.shape[1] // (3 * VD)
    tile = min(256, own_rows)
    out = pl.pallas_call(
        functools.partial(project_kernel, heads=heads, ends=chunk_ends(tile, chunks)),
        grid=(rows // tile,),
        in_specs=chunk_specs(tile, chunks)
        + [whole_spec(weight.shape), row_spec(tile, VD), row_spec(tile, VD)],
        out_specs=[row_spec(tile, D)]
        + [row_spec(tile, VD)] * heads
        + [row_spec(tile, 2 * VD)] * heads,
        out_shape=[jax.ShapeDtypeStruct((rows, D), BF16)]
        + [jax.ShapeDtypeStruct((rows, VD), BF16)] * heads
        + [jax.ShapeDtypeStruct((rows, 2 * VD), BF16)] * heads,
        compiler_params=pltpu.CompilerParams(vmem_limit_bytes=40 * MIB),
        cost_estimate=cost(
            2 * rows * D * weight.shape[1],
            2 * (2 * rows * D + weight.size + rows * weight.shape[1]),
        ),
        name="project",
    )(*chunks, weight, cos_table, sin_table)
    return out[0], out[1 : 1 + heads], out[1 + heads :]


def unproject_kernel(*refs, heads, per):
    dq_refs, own_refs, recv_refs = refs[:heads], refs[heads : 2 * heads], refs[2 * heads : 3 * heads]
    w_ref, cos_ref, sin_ref, gp_ref, keep_ref, mate_ref = refs[3 * heads :]
    mask = low_half_mask(gp_ref.shape[0])
    cos_table, sin_table = cos_ref[...], sin_ref[...]
    for head in range(heads):
        base = head * 3 * VD
        both = own_refs[head][...].astype(F32) + recv_refs[head][...].astype(F32)
        query = dq_refs[head][...].astype(F32)
        gp_ref[:, base : base + VD] = turn(query, cos_table, sin_table, mask, -1.0).astype(BF16)
        gp_ref[:, base + VD : base + 2 * VD] = turn(
            both[:, :VD], cos_table, sin_table, mask, -1.0
        ).astype(BF16)
        gp_ref[:, base + 2 * VD : base + 3 * VD] = both[:, VD:].astype(BF16)
    put_pair(dot(gp_ref[...], w_ref[...], NT).astype(BF16), per, keep_ref, mate_ref)


def unproject(dq, dkv_own, dkv_recv, weight, cos_table, sin_table):
    rows = dq[0].shape[0]
    heads = len(dq)
    tile = min(256, rows // 4)
    per = rows // 4 // tile
    return pl.pallas_call(
        functools.partial(unproject_kernel, heads=heads, per=per),
        grid=(rows // tile,),
        in_specs=[row_spec(tile, VD)] * heads
        + [row_spec(tile, 2 * VD)] * (2 * heads)
        + [whole_spec(weight.shape), row_spec(tile, VD), row_spec(tile, VD)],
        out_specs=[row_spec(tile, heads * 3 * VD)] + pair_specs(tile, per, D),
        out_shape=[jax.ShapeDtypeStruct((rows, heads * 3 * VD), BF16)] + pair_shapes(rows, D),
        compiler_params=pltpu.CompilerParams(vmem_limit_bytes=40 * MIB),
        cost_estimate=cost(
            2 * rows * D * weight.shape[1],
            2 * (rows * D + weight.size + 3 * rows * weight.shape[1]),
        ),
        name="unproject",
    )(*dq, *dkv_own, *dkv_recv, weight, cos_table, sin_table)


def output_kernel(*refs, heads, per):
    attn_refs = refs[:heads]
    w_ref, all_ref, keep_ref, mate_ref = refs[heads:]
    for head in range(heads):
        all_ref[:, head * VD : (head + 1) * VD] = attn_refs[head][...]
    put_pair(dot(all_ref[...], w_ref[...], NT).astype(BF16), per, keep_ref, mate_ref)


def output_projection(attn, weight):
    rows = attn[0].shape[0]
    heads = len(attn)
    tile = min(256, rows // 4)
    per = rows // 4 // tile
    return pl.pallas_call(
        functools.partial(output_kernel, heads=heads, per=per),
        grid=(rows // tile,),
        in_specs=[row_spec(tile, VD)] * heads + [whole_spec(weight.shape)],
        out_specs=[row_spec(tile, heads * VD)] + pair_specs(tile, per, D),
        out_shape=[jax.ShapeDtypeStruct((rows, heads * VD), BF16)] + pair_shapes(rows, D),
        compiler_params=pltpu.CompilerParams(vmem_limit_bytes=40 * MIB),
        cost_estimate=cost(
            2 * rows * D * weight.shape[1], 2 * (rows * D + weight.size + 2 * rows * heads * VD)
        ),
        name="output_projection",
    )(*attn, weight)


def gate_kernel(*refs, ends):
    count = len(ends)
    w_ref, x_ref, hidden_ref, by_gate_ref, by_up_ref = refs[count:]
    pick(refs[:count], ends, x_ref)
    width = hidden_ref.shape[1]
    step = min(512, width)
    x = x_ref[...]
    for base in range(0, width, step):
        cols = slice(base, base + step)
        gate = dot(x, w_ref[:, cols])
        up = dot(x, w_ref[:, width + base : width + base + step])
        share = jax.nn.sigmoid(gate)
        swish = gate * share
        hidden_ref[:, cols] = (swish * up).astype(BF16)
        by_gate_ref[:, cols] = (up * share * (1.0 + gate * (1.0 - share))).astype(BF16)
        by_up_ref[:, cols] = swish.astype(BF16)


def gate_up(chunks, weights, width):
    own_rows = chunks[0].shape[0]
    rows = 4 * own_rows
    tile = min(256, own_rows)
    return pl.pallas_call(
        functools.partial(gate_kernel, ends=chunk_ends(tile, chunks)),
        grid=(rows // tile,),
        in_specs=chunk_specs(tile, chunks) + [columns_spec(D, 2 * width, 0)],
        out_specs=[row_spec(tile, D)] + [row_spec(tile, width)] * 3,
        out_shape=[jax.ShapeDtypeStruct((rows, D), BF16)]
        + [jax.ShapeDtypeStruct((rows, width), BF16)] * 3,
        compiler_params=pltpu.CompilerParams(vmem_limit_bytes=48 * MIB),
        cost_estimate=cost(4 * rows * D * width, 2 * (2 * rows * D + 2 * D * width + 3 * rows * width)),
        name="gate_up",
    )(*chunks, weights)


def feed_kernel(*refs, ends, per):
    count = len(ends)
    hidden_ref, by_gate_ref, by_up_ref, down_ref, inner_ref = refs[count : count + 5]
    cot_ref, grad_ref, ffn_keep, ffn_mate, mid_keep, mid_mate = refs[count + 5 :]
    pick(refs[:count], ends, cot_ref)
    width = hidden_ref.shape[1]
    grad_hidden = dot(cot_ref[...], down_ref[...])
    grad_ref[:, :width] = (grad_hidden * by_gate_ref[...].astype(F32)).astype(BF16)
    grad_ref[:, width:] = (grad_hidden * by_up_ref[...].astype(F32)).astype(BF16)
    put_pair(dot(hidden_ref[...], down_ref[...], NT).astype(BF16), per, ffn_keep, ffn_mate)
    put_pair(dot(grad_ref[...], inner_ref[...], NT).astype(BF16), per, mid_keep, mid_mate)


def feed(chunks, hidden, by_gate, by_up, weights):
    own_rows = chunks[0].shape[0]
    rows = 4 * own_rows
    width = hidden.shape[1]
    tile = min(256, own_rows)
    per = own_rows // tile
    return pl.pallas_call(
        functools.partial(feed_kernel, ends=chunk_ends(tile, chunks), per=per),
        grid=(rows // tile,),
        in_specs=chunk_specs(tile, chunks)
        + [row_spec(tile, width)] * 3
        + [columns_spec(D, width, 2), columns_spec(D, 2 * width, 0)],
        out_specs=[row_spec(tile, D), row_spec(tile, 2 * width)]
        + pair_specs(tile, per, D)
        + pair_specs(tile, per, D),
        out_shape=[
            jax.ShapeDtypeStruct((rows, D), BF16),
            jax.ShapeDtypeStruct((rows, 2 * width), BF16),
        ]
        + pair_shapes(rows, D)
        + pair_shapes(rows, D),
        compiler_params=pltpu.CompilerParams(vmem_limit_bytes=56 * MIB),
        cost_estimate=cost(8 * rows * D * width, 2 * (4 * rows * D + 3 * D * width + 5 * rows * width)),
        name="feed",
    )(*chunks, hidden, by_gate, by_up, weights, weights)


class Plan:
    def __init__(self, own_rows, block_len, prev_rows, ndoc):
        self.own_rows = own_rows
        self.block_len = block_len
        self.prev_rows = prev_rows
        self.ndoc = ndoc
        self.bq = min(256, own_rows)
        self.bk = min(512, own_rows)
        self.total = prev_rows + block_len

    def doc_start(self, info, pos):
        start = jnp.zeros_like(pos)
        for item in range(self.ndoc):
            start = jnp.where(pos >= info[2 + item], info[2 + item], start)
        return start

    def query_start(self, info, index):
        per = self.own_rows // self.bq
        chunk = (index // per) ^ info[0]
        return info[1] * self.block_len + chunk * self.own_rows + (index % per) * self.bq

    def key_row(self, info, index):
        per = self.own_rows // self.bk
        blocks = self.block_len // self.bk
        owner = index // blocks
        local = index % blocks
        inside = (((local // per) ^ info[0]) * per + local % per) * self.bk
        base = jnp.where(owner == info[1], self.prev_rows, owner * self.block_len)
        return pl.multiple_of(base + inside, self.bk)

    def ranges(self, info, start):
        last = start + self.bq - 1
        low = self.doc_start(info, start) // self.bk
        high = last // self.bk + 1
        open_from = (self.doc_start(info, last) + self.bk - 1) // self.bk
        first = jnp.minimum(jnp.maximum(open_from, low), high)
        until = jnp.maximum(first, jnp.minimum((start + 1) // self.bk, high))
        return low, first, until, high


def split_halves(q):
    lane = lax.broadcasted_iota(jnp.int32, q.shape, 1)
    zero = jnp.zeros_like(q)
    return jnp.concatenate([jnp.where(lane < HD, q, zero), jnp.where(lane >= HD, q, zero)], axis=0)


def load_keys(plan, info, own_ref, prev_ref, kv_sc):
    @pl.when(pl.program_id(0) == 0)
    def _():
        kv_sc[plan.prev_rows :, :] = own_ref[...]

        @pl.when(info[1] > 0)
        def _():
            kv_sc[: plan.prev_rows, :] = prev_ref[...]


def forward_kernel(
    info,
    lam_ref,
    gain_ref,
    q_ref,
    own_ref,
    prev_ref,
    attn_ref,
    first_ref,
    second_ref,
    lse_ref,
    kv_sc,
    m_sc,
    l_sc,
    acc_sc,
    *,
    plan,
):
    bq, bk = plan.bq, plan.bk
    load_keys(plan, info, own_ref, prev_ref, kv_sc)
    start = plan.query_start(info, pl.program_id(0))
    q2 = split_halves(q_ref[...])
    m_sc[...] = jnp.full_like(m_sc, NEG)
    l_sc[...] = jnp.zeros_like(l_sc)
    acc_sc[...] = jnp.zeros_like(acc_sc)
    low, first, until, high = plan.ranges(info, start)

    def visit(index, masked):
        row = plan.key_row(info, index)
        key = kv_sc[pl.ds(row, bk), :VD]
        value = kv_sc[pl.ds(row, bk), VD:]
        scores = dot(q2, key, NT)
        if masked:
            query_pos = start + lax.broadcasted_iota(jnp.int32, (bq, 1), 0)
            begin = plan.doc_start(info, query_pos)
            key_pos = index * bk + lax.broadcasted_iota(jnp.int32, (bq, bk), 1)
            keep = (key_pos <= query_pos) & (key_pos >= begin)
            scores = jnp.concatenate(
                [jnp.where(keep, scores[:bq], NEG), jnp.where(keep, scores[bq:], NEG)], axis=0
            )
        before = m_sc[...]
        after = jnp.maximum(before, jnp.max(scores, axis=1, keepdims=True))
        weights = jnp.exp(scores - jnp.tile(after, (1, bk // VD)))
        factor = jnp.exp(before - after)
        m_sc[...] = after
        l_sc[...] = l_sc[...] * factor + jnp.sum(weights, axis=1, keepdims=True)
        acc_sc[...] = acc_sc[...] * factor + dot(weights.astype(BF16), value)

    @pl.loop(low, first)
    def _(index):
        visit(index, True)

    @pl.loop(first, until)
    def _(index):
        visit(index, False)

    @pl.loop(until, high)
    def _(index):
        visit(index, True)

    total = l_sc[...]
    maps = acc_sc[...] * (1.0 / total)
    first_map, second_map = maps[:bq], maps[bq:]
    first_ref[...] = first_map
    second_ref[...] = second_map
    difference = first_map - lam_ref[0] * second_map
    scaling = lax.rsqrt(jnp.mean(difference * difference, axis=1, keepdims=True) + EPS)
    attn_ref[...] = (difference * scaling * gain_ref[...]).astype(BF16)
    lse = (m_sc[...] + jnp.log(total)).T
    lse_ref[0:1, :] = lse[0:1, :bq]
    lse_ref[1:2, :] = lse[0:1, bq:]


def attention_cost(plan, per_pair, extra=0):
    pairs = plan.block_len * plan.block_len * 5 // 8
    return cost(pairs * per_pair + extra, plan.block_len * VD * 32, 2 * pairs)


def attend_forward(plan, info, lam, gain, q, kv_own, kv_prev):
    rows, bq = plan.block_len, plan.bq
    grid_spec = pltpu.PrefetchScalarGridSpec(
        num_scalar_prefetch=1,
        grid=(rows // bq,),
        in_specs=[
            pl.BlockSpec(memory_space=pltpu.SMEM),
            whole_spec((1, VD)),
            row_spec(bq, VD),
            whole_spec((rows, 2 * VD)),
            whole_spec((plan.prev_rows, 2 * VD)),
        ],
        out_specs=[row_spec(bq, VD)] * 3 + [pl.BlockSpec((2, bq), lambda i, *_: (0, i))],
        scratch_shapes=[
            pltpu.VMEM((plan.total, 2 * VD), BF16),
            pltpu.VMEM((2 * bq, VD), F32),
            pltpu.VMEM((2 * bq, VD), F32),
            pltpu.VMEM((2 * bq, VD), F32),
        ],
    )
    return pl.pallas_call(
        functools.partial(forward_kernel, plan=plan),
        grid_spec=grid_spec,
        out_shape=[
            jax.ShapeDtypeStruct((rows, VD), BF16),
            jax.ShapeDtypeStruct((rows, VD), F32),
            jax.ShapeDtypeStruct((rows, VD), F32),
            jax.ShapeDtypeStruct((2, rows), F32),
        ],
        compiler_params=pltpu.CompilerParams(vmem_limit_bytes=40 * MIB),
        cost_estimate=attention_cost(plan, 6 * VD),
        name="attend_forward",
    )(info, lam, gain, q, kv_own, kv_prev)


def backward_kernel(
    info,
    lam_ref,
    gain_ref,
    q_ref,
    own_ref,
    prev_ref,
    *refs,
    plan,
    ends,
):
    count = len(ends)
    backward_body(
        plan, ends, refs[:count], info, lam_ref, gain_ref, q_ref, own_ref, prev_ref, *refs[count:]
    )


def backward_body(
    plan,
    ends,
    gm_refs,
    info,
    lam_ref,
    gain_ref,
    q_ref,
    own_ref,
    prev_ref,
    w_ref,
    first_ref,
    second_ref,
    lse_ref,
    gm_ref,
    dq_ref,
    dkv_own_ref,
    dkv_prev_ref,
    sums_ref,
    kv_sc,
    dk_sc,
    dv_sc,
    dqt_sc,
):
    bq, bk = plan.bq, plan.bk
    step = pl.program_id(0)
    load_keys(plan, info, own_ref, prev_ref, kv_sc)
    lam = lam_ref[0]

    @pl.when(step == 0)
    def _():
        dk_sc[...] = jnp.zeros_like(dk_sc)
        dv_sc[...] = jnp.zeros_like(dv_sc)

        sums_ref[...] = jnp.zeros_like(sums_ref)

    pick(gm_refs, ends, gm_ref)
    upstream = dot(gm_ref[...], w_ref[...])
    first_map, second_map = first_ref[...], second_ref[...]
    difference = first_map - lam * second_map
    scaling = lax.rsqrt(jnp.mean(difference * difference, axis=1, keepdims=True) + EPS)
    normal = difference * scaling
    weighted = upstream * gain_ref[...]
    inner_mean = jnp.mean(weighted * normal, axis=1, keepdims=True)
    grad = (scaling * (weighted - normal * inner_mean)).astype(BF16)
    grad_wide = grad.astype(F32)
    second_product = grad_wide * second_map
    sums_ref[0:1, :] += jnp.sum(upstream * normal, axis=0, keepdims=True)
    sums_ref[1:2, :] += jnp.sum(second_product, axis=0, keepdims=True)
    ones = jnp.ones((8, VD), F32)
    delta_first = dot(ones, grad_wide * first_map, NT, precision=lax.Precision.HIGHEST)[0:1]
    delta_second = dot(ones, second_product, NT, precision=lax.Precision.HIGHEST)[0:1]
    lse_first = lse_ref[0:1, :]
    lse_second = lse_ref[1:2, :]

    start = plan.query_start(info, step)
    q2 = split_halves(q_ref[...])
    dqt_sc[...] = jnp.zeros_like(dqt_sc)
    low, first, until, high = plan.ranges(info, start)

    def visit(index, masked):
        row = plan.key_row(info, index)
        key = kv_sc[pl.ds(row, bk), :VD]
        value = kv_sc[pl.ds(row, bk), VD:]
        scores = dot(key, q2, NT)
        base = dot(value, grad, NT)
        prob_first = jnp.exp(scores[:, :bq] - lse_first)
        prob_second = jnp.exp(scores[:, bq:] - lse_second)
        if masked:
            query_pos = start + lax.broadcasted_iota(jnp.int32, (1, bq), 1)
            begin = plan.doc_start(info, query_pos)
            key_pos = index * bk + lax.broadcasted_iota(jnp.int32, (bk, bq), 0)
            keep = (key_pos <= query_pos) & (key_pos >= begin)
            prob_first = jnp.where(keep, prob_first, 0.0)
            prob_second = jnp.where(keep, prob_second, 0.0)
        raw = jnp.concatenate(
            [
                (prob_first * (base - delta_first)).astype(BF16),
                (prob_second * (base - delta_second)).astype(BF16),
            ],
            axis=1,
        )
        dv_sc[pl.ds(row, bk), :] += dot(prob_first.astype(BF16), grad) - lam * dot(
            prob_second.astype(BF16), grad
        )
        dk_sc[pl.ds(row, bk), :] += dot(raw, q2)
        dqt_sc[...] += dot(key, raw, TN)

    @pl.loop(low, first)
    def _(index):
        visit(index, True)

    @pl.loop(first, until)
    def _(index):
        visit(index, False)

    @pl.loop(until, high)
    def _(index):
        visit(index, True)

    dq_t = jnp.concatenate([dqt_sc[:HD, :bq], -lam * dqt_sc[HD:, bq:]], axis=0) * SCALE
    dq_ref[...] = dq_t.T.astype(BF16)

    @pl.when(step == pl.num_programs(0) - 1)
    def _():
        lane = lax.broadcasted_iota(jnp.int32, (1, VD), 1)
        side = jnp.where(lane < HD, 1.0, -lam)
        dkv_own_ref[:, :VD] = (dk_sc[plan.prev_rows :, :] * side).astype(BF16)
        dkv_own_ref[:, VD:] = dv_sc[plan.prev_rows :, :].astype(BF16)
        dkv_prev_ref[:, :VD] = (dk_sc[: plan.prev_rows, :] * side).astype(BF16)
        dkv_prev_ref[:, VD:] = dv_sc[: plan.prev_rows, :].astype(BF16)


def attend_backward(plan, info, lam, gain, q, kv_own, kv_prev, gm, weight, head, maps, keep_gm):
    rows, bq = plan.block_len, plan.bq
    first, second, lse = maps
    gm_spec = row_spec(bq, D) if keep_gm else whole_spec((bq, D))
    gm_rows = rows if keep_gm else bq
    grid_spec = pltpu.PrefetchScalarGridSpec(
        num_scalar_prefetch=1,
        grid=(rows // bq,),
        in_specs=[
            pl.BlockSpec(memory_space=pltpu.SMEM),
            whole_spec((1, VD)),
            row_spec(bq, VD),
            whole_spec((rows, 2 * VD)),
            whole_spec((plan.prev_rows, 2 * VD)),
        ]
        + chunk_specs(bq, gm)
        + [
            pl.BlockSpec((D, VD), lambda i, *_: (0, head)),
            row_spec(bq, VD),
            row_spec(bq, VD),
            pl.BlockSpec((2, bq), lambda i, *_: (0, i)),
        ],
        out_specs=[
            gm_spec,
            row_spec(bq, VD),
            whole_spec((rows, 2 * VD)),
            whole_spec((plan.prev_rows, 2 * VD)),
            whole_spec((8, VD)),
        ],
        scratch_shapes=[
            pltpu.VMEM((plan.total, 2 * VD), BF16),
            pltpu.VMEM((plan.total, VD), F32),
            pltpu.VMEM((plan.total, VD), F32),
            pltpu.VMEM((VD, 2 * bq), F32),
        ],
    )
    return pl.pallas_call(
        functools.partial(backward_kernel, plan=plan, ends=chunk_ends(bq, gm)),
        grid_spec=grid_spec,
        out_shape=[
            jax.ShapeDtypeStruct((gm_rows, D), BF16),
            jax.ShapeDtypeStruct((rows, VD), BF16),
            jax.ShapeDtypeStruct((rows, 2 * VD), BF16),
            jax.ShapeDtypeStruct((plan.prev_rows, 2 * VD), BF16),
            jax.ShapeDtypeStruct((8, VD), F32),
        ],
        compiler_params=pltpu.CompilerParams(vmem_limit_bytes=48 * MIB),
        cost_estimate=attention_cost(plan, 16 * VD, 2 * rows * D * VD),
        name="attend_backward",
    )(info, lam, gain, q, kv_own, kv_prev, *gm, weight, first, second, lse)


def norm_forward(values, gain_vec):
    scaling = lax.rsqrt(jnp.mean(values * values, axis=-1, keepdims=True) + EPS)
    return (values * scaling * gain_vec, scaling)


def norm_backward(values, scaling, gain_vec, upstream):
    normal = values * scaling
    weighted = upstream * gain_vec
    inner_mean = jnp.mean(weighted * normal, axis=-1, keepdims=True)
    return (scaling * (weighted - normal * inner_mean), jnp.sum(upstream * normal, axis=0))


def adamw(parameter, momentum, variance, gradient, learn_rate, decay_rate):
    momentum = BETA1 * momentum + (1.0 - BETA1) * gradient
    variance = BETA2 * variance + (1.0 - BETA2) * gradient * gradient
    corrected = momentum / (1.0 - BETA1**STEP)
    spread = jnp.sqrt(variance / (1.0 - BETA2**STEP))
    return (
        parameter - learn_rate * (corrected / (spread + ADAM_EPS) + decay_rate * parameter),
        momentum,
        variance,
    )


def send_keys(kv, ctx_count):
    if ctx_count == 2:
        return lax.ppermute(kv, "ctx", [(0, 1)])
    return lax.all_gather(kv, "ctx", axis=0, tiled=True)


def return_keys(grads, ctx_count):
    if ctx_count == 2:
        return lax.ppermute(grads, "ctx", [(1, 0)])
    return lax.psum_scatter(grads, "ctx", scatter_dimension=0, tiled=True)


def scatter_weight(grad, *others):
    grad = after(grad.astype(BF16), *others)
    return lax.psum_scatter(grad, "dp", scatter_dimension=0, tiled=True)


def sum_blocks(share, ctx_count):
    if ctx_count == 2:
        other = lax.ppermute(share, "ctx", [(0, 1), (1, 0)])
        return share.astype(F32) + other.astype(F32)
    return lax.psum(share, "ctx").astype(F32)


def on_device(
    tokens,
    cotangent,
    doc_lengths,
    qkv_weight,
    out_weight,
    inner_weight,
    down_weight,
    norm_gains,
    head_gain,
    lambdas,
    qkv_momentum,
    out_momentum,
    inner_momentum,
    down_momentum,
    norm_momentum,
    head_momentum,
    lambda_momentum,
    qkv_variance,
    out_variance,
    inner_variance,
    down_variance,
    norm_variance,
    head_variance,
    lambda_variance,
):
    micro_count, own_rows, _ = tokens.shape
    head_count = lax.axis_size("head")
    ctx_count = lax.axis_size("ctx")
    block_len = own_rows * head_count
    seq_len = block_len * ctx_count
    ctx_index = lax.axis_index("ctx")
    head_index = lax.axis_index("head")
    local_heads = qkv_weight.shape[1]
    ff_local = inner_weight.shape[2]
    ndoc = doc_lengths.shape[1]
    plan = Plan(own_rows, block_len, block_len if ctx_count == 2 else seq_len, ndoc)

    def gather_weight(shard):
        return lax.all_gather(shard.astype(BF16), "dp", axis=0, tiled=True)

    qkv_low = gather_weight(qkv_weight.reshape(-1, local_heads * 3 * VD))
    out_t = gather_weight(out_weight.reshape(local_heads * VD, -1).T)
    feed_low = gather_weight(
        jnp.concatenate(
            [
                inner_weight.reshape(-1, 2 * ff_local).astype(BF16),
                down_weight.astype(BF16).T,
            ],
            axis=1,
        )
    )

    first_exp = jnp.exp(jnp.sum(lambdas[0] * lambdas[1]))
    second_exp = jnp.exp(jnp.sum(lambdas[2] * lambdas[3]))
    lambda_value = first_exp - second_exp + LAMBDA_INIT
    lam = lambda_value.reshape(1)
    head_scale = (head_gain * (1.0 - LAMBDA_INIT)).reshape(1, VD)

    chunk = jnp.arange(block_len, dtype=jnp.int32) // own_rows
    position = (
        ctx_index * block_len
        + (chunk ^ head_index) * own_rows
        + jnp.arange(block_len, dtype=jnp.int32) % own_rows
    )
    frequency = ROPE_BASE ** (
        -(jnp.arange(VD, dtype=jnp.int32) % (HD // 2)).astype(F32) / (HD // 2)
    )
    phases = position.astype(F32)[:, None] * frequency[None, :]
    cos_table, sin_table = jnp.cos(phases), jnp.sin(phases)

    def info_of(micro):
        bounds = jnp.cumsum(doc_lengths[micro], dtype=jnp.int32)
        return jnp.concatenate([jnp.stack([head_index, ctx_index]).astype(jnp.int32), bounds])

    micros = range(micro_count)
    heads = range(local_heads)
    infos = [info_of(m) for m in micros]
    own = [tokens[m].astype(F32) for m in micros]
    normed_own = [norm_forward(own[m], norm_gains[0]) for m in micros]
    cot_own = [cotangent[m] for m in micros]
    normed = []
    for m in micros:
        value = normed_own[m][0].astype(BF16)
        if m > 0:
            value = after(value, cos_table, sin_table, *infos, *cot_own, lam, head_scale)
        normed.append(Gather(value))
    normed_all, q, kv, kv_prev, cot = [], [], [], [], []
    for m in micros:
        pieces = after(normed[m].pieces(), *normed[-1].far)
        result = project(pieces, qkv_low, cos_table, sin_table)
        if m == 0:
            cot.append(Gather(after(cot_own[0], qkv_low)))
        else:
            result = together(result, *slots_of(cot[0].far, 0))
            cot.append(Gather(after(cot_own[1], result[2], *cot[0].far)))
        normed_all.append(result[0])
        q.append(result[1])
        kv.append(result[2])
        kv_prev.append([send_keys(result[2][h], ctx_count) for h in heads])

    def attend(m, h, before, beside):
        out = attend_forward(
            plan, infos[m], lam, head_scale, after(q[m][h], *before), kv[m][h], kv_prev[m][h]
        )
        return together(out, *beside)

    mid = []

    def finish_attention(m):
        middle = own[m] + attended[m].value()
        value, scaling = norm_forward(middle, norm_gains[1])
        mid.append((middle, scaling, Gather(value.astype(BF16))))

    maps, attn_all, attended = [], [], []
    for m in micros:
        outs = []
        for h in heads:
            if m == 0:
                before = [out_t, kv[-1]] if h == 0 else [outs[-1]]
                beside = [
                    slots_of(cot[0].far, 1),
                    slots_of(cot[1].far, 0),
                    slots_of(cot[1].far, 1),
                ][h]
            elif h == 0:
                before = [*attended[0].sent, *cot[0].pieces(), *cot[1].pieces()]
                beside = slots_of(attended[0].across) + slots_of(kv_prev[m], 1)
            else:
                before = [outs[-1], mid[0][2].own]
                beside = slots_of(mid[0][2].far, h - 1) + slots_of(kv_prev[m], h + 1)
            outs.append(attend(m, h, before, beside))
            if m > 0 and h == 0:
                finish_attention(0)
        maps.append([out[1:] for out in outs])
        result = output_projection([out[0] for out in outs], out_t)
        if m == 0:
            result = together(result, *slots_of(kv_prev[1], 0))
        attn_all.append(result[0])
        attended.append(Reduce(*result[1:]))

    grad_middle, gm, gain_mid = [], [], []

    def finish_feed(m, reduced):
        middle, scaling, _ = mid[m]
        grad_norm, part = norm_backward(middle, scaling, norm_gains[1], reduced.value())
        grad_middle.append((cot_own[m].astype(F32) + grad_norm).astype(BF16))
        gm.append(Gather(grad_middle[m]))
        gain_mid.append(part)

    def weight_grad(left, right, before, beside, total=None):
        result = dot(after(left, *before), right, TN)
        if total is not None:
            result = (total + result).astype(BF16)
        return together(result, *beside)

    first_gates = gate_up(after(mid[0][2].pieces(), *attended[1].sent), feed_low, ff_local)
    first_gates = together(first_gates, *slots_of(attended[1].across, 0))
    first_feed = feed(cot[0].pieces(), *first_gates[1:], feed_low)
    first_feed = together(first_feed, *slots_of(attended[1].across, 1))
    finish_attention(1)
    reduced_mid = [Reduce(*first_feed[4:])]
    grad_inner = weight_grad(
        first_gates[0],
        first_feed[1],
        [mid[1][2].own, *reduced_mid[0].sent],
        slots_of(mid[1][2].far, 0),
    )
    grad_down = weight_grad(
        first_feed[0], first_gates[1], [grad_inner], slots_of(mid[1][2].far, 1)
    )
    reduced_mid[0].send(*mid[1][2].far)
    second_gates = gate_up(after(mid[1][2].pieces(), grad_down), feed_low, ff_local)
    second_gates = together(second_gates, *slots_of(reduced_mid[0].across))
    finish_feed(0, reduced_mid[0])
    second_feed = feed(after(cot[1].pieces(), gm[0].own), *second_gates[1:], feed_low)
    second_feed = together(second_feed, *slots_of(gm[0].far))
    reduced_mid.append(Reduce(*second_feed[4:]))
    grad_inner = weight_grad(
        second_gates[0],
        second_feed[1],
        reduced_mid[1].sent,
        slots_of(reduced_mid[1].across, 0),
        grad_inner,
    )
    grad_down = weight_grad(
        second_feed[0],
        second_gates[1],
        [grad_inner],
        slots_of(reduced_mid[1].across, 1),
        grad_down,
    )
    feed_grad = jnp.concatenate([grad_inner, grad_down], axis=1)
    feed_part = scatter_weight(feed_grad)
    finish_feed(1, reduced_mid[1])
    ffn_pairs = [first_feed[2:4], second_feed[2:4]]

    dqs, dkvs, recvs, gm_alls = [], [], [], []

    def attend_back(m, h, before, beside):
        out = attend_backward(
            plan,
            infos[m],
            lam,
            head_scale,
            after(q[m][h], *before),
            kv[m][h],
            kv_prev[m][h],
            gm[m].pieces(),
            out_t,
            h,
            maps[m][h],
            h == 0,
        )
        out = together(out, *beside)
        if h == 0:
            gm_alls.append(out[0])
            dqs.append([])
            dkvs.append([])
            recvs.append([])
        dqs[m].append(out[1])
        dkvs[m].append(out[2])
        recvs[m].append(return_keys(out[3], ctx_count))
        return out[4]

    def unprojected(m, before, beside):
        out = unproject(after(dqs[m], *before), dkvs[m], recvs[m], qkv_low, cos_table, sin_table)
        return together(out, *beside)

    def ffn_sum(m, before):
        keep, mate = ffn_pairs[m]
        return Reduce(keep, after(mate, *before))

    sums = attend_back(0, 0, [gm[1].own, *gm[0].pieces(), feed_grad], slots_of(gm[1].far, 0))
    sums = sums + attend_back(
        0, 1, [dqs[0][-1]], slots_of(gm[1].far, 1) + slots_of(recvs[0], 0)
    )
    ffn = [ffn_sum(0, [dqs[0][-1]])]
    sums = sums + attend_back(
        0,
        2,
        [*ffn[0].sent, *gm[1].pieces()],
        slots_of(ffn[0].across, 0) + slots_of(recvs[0], 1),
    )
    ffn.append(ffn_sum(1, [dqs[0][-1]]))
    sums = sums + attend_back(
        1, 0, [dqs[0][-1]], slots_of(ffn[0].across, 1) + slots_of(recvs[0], 2)
    )
    back = [unprojected(0, [dqs[1][-1], *ffn[1].sent], slots_of(ffn[1].across, 0))]
    reduced_in = [Reduce(*back[0][1:])]
    sums = sums + attend_back(
        1, 1, [back[0][0], *reduced_in[0].sent], slots_of(ffn[1].across, 1)
    )
    sums = sums + attend_back(
        1, 2, [dqs[1][-1]], slots_of(reduced_in[0].across, 0) + slots_of(recvs[1], 0)
    )
    grad_out = weight_grad(gm_alls[0], attn_all[0], [dqs[1][-1]], [])
    grad_out = weight_grad(
        gm_alls[1], attn_all[1], [grad_out], slots_of(reduced_in[0].across, 1), grad_out
    )
    grad_qkv = weight_grad(
        normed_all[0], back[0][0], [grad_out, feed_part], slots_of(recvs[1], 1)
    )
    back.append(unprojected(1, [grad_qkv], []))
    reduced_in.append(Reduce(*back[1][1:]))
    grad_qkv = weight_grad(
        normed_all[1],
        back[1][0],
        reduced_in[1].sent,
        slots_of(reduced_in[1].across, 0),
        grad_qkv,
    )
    last_part = scatter_weight(jnp.concatenate([grad_qkv, grad_out], axis=1), feed_part)
    feed_share = sum_blocks(feed_part, ctx_count)
    inner_share = feed_share[:, : 2 * ff_local]
    down_share = feed_share[:, 2 * ff_local :]
    gain_mid = gain_mid[0] + gain_mid[1]
    outputs = [(mid[m][0] + ffn[m].value()).astype(BF16) for m in micros]

    gain_in = 0.0
    input_grads = []
    for m in micros:
        grad_in_norm, gain_part = norm_backward(
            own[m], normed_own[m][1], norm_gains[0], reduced_in[m].value()
        )
        gain_in = gain_in + gain_part
        input_grads.append((grad_middle[m].astype(F32) + grad_in_norm).astype(BF16))

    lambda_acc = -jnp.sum(sums[1])
    lambda_local = jnp.stack(
        [
            lambda_acc * first_exp * lambdas[1],
            lambda_acc * first_exp * lambdas[0],
            -lambda_acc * second_exp * lambdas[3],
            -lambda_acc * second_exp * lambdas[2],
        ]
    )
    small = butterfly(
        jnp.concatenate(
            [
                gain_in.reshape(-1, VD),
                gain_mid.reshape(-1, VD),
                sums[:1] * (1.0 - LAMBDA_INIT),
                lambda_local.reshape(-1, VD),
            ]
        )
    )
    per = D // VD
    norm_grad = small[: 2 * per].reshape(2, D)
    head_grad = small[2 * per]
    lambda_grad = small[2 * per + 1 :].reshape(lambdas.shape)

    feed_states = [
        adamw(
            inner_weight,
            inner_momentum,
            inner_variance,
            inner_share.reshape(inner_weight.shape),
            0.5 * D ** (-0.5),
            DECAY,
        ),
        adamw(
            down_weight, down_momentum, down_variance, down_share.T, 0.5 * FF ** (-0.5), DECAY
        ),
    ]
    last_share = sum_blocks(after(last_part, feed_states), ctx_count)
    qkv_share = last_share[:, : qkv_low.shape[1]]
    out_share = last_share[:, qkv_low.shape[1] :]

    states = [
        adamw(
            qkv_weight,
            qkv_momentum,
            qkv_variance,
            qkv_share.reshape(qkv_weight.shape),
            0.5 * D ** (-0.5),
            DECAY,
        ),
        adamw(
            out_weight,
            out_momentum,
            out_variance,
            out_share.T.reshape(out_weight.shape),
            0.5 * (H * VD) ** (-0.5),
            DECAY,
        ),
        *feed_states,
        adamw(norm_gains, norm_momentum, norm_variance, norm_grad, 0.4, 0.0),
        adamw(head_gain, head_momentum, head_variance, head_grad, 0.4, 0.0),
        adamw(lambdas, lambda_momentum, lambda_variance, lambda_grad, 0.1, 0.0),
    ]
    return (
        jnp.stack(outputs),
        jnp.stack(input_grads),
        *[state[0] for state in states],
        *[state[1] for state in states],
        *[state[2] for state in states],
    )


def solution(mesh):
    activation = P("dp", ("ctx", "head"), None)
    big = (P("dp", "head", None, None), P("head", None, "dp"), P("dp", None, "head"), P("head", "dp"))
    state = big + (P(), P(), P())
    return jax.shard_map(
        on_device,
        mesh=mesh,
        in_specs=(activation, activation, P("dp", None)) + state * 3,
        out_specs=(activation, activation) + state * 3,
        check_vma=False,
    )
```

```python
import functools

import jax
import jax.numpy as jnp
from jax import lax
from jax.experimental import pallas as pl
from jax.experimental.layout import Layout, with_layout_constraint
from jax.experimental.pallas import tpu as pltpu
from jax.sharding import PartitionSpec as P

D = 1536
FF = 4096
H = 12
HD = 64
STEP = 10
VD = 128


EPS = 1e-05
LAMBDA_INIT = 0.2
SCALE = 0.125
NEG = -1e30
BETA1 = 0.9
BETA2 = 0.999
ADAM_EPS = 1e-08
DECAY = 0.1
ROPE_BASE = 10000.0

MIB = 1 << 20
NT = (((1,), (1,)), ((), ()))
TN = (((0,), (0,)), ((), ()))
F32 = jnp.float32
BF16 = jnp.bfloat16


def dot(left, right, dims=(((1,), (0,)), ((), ())), **kw):
    return lax.dot_general(left, right, dims, preferred_element_type=F32, **kw)


def swap(array, bit):
    size = lax.axis_size("head")
    return lax.ppermute(array, "head", [(i, i ^ bit) for i in range(size)])


def split_rows(array, count):
    size = array.shape[0] // count
    return [array[i * size : (i + 1) * size] for i in range(count)]


class Gather:
    def __init__(self, own):
        parts = 2 if own.shape[0] % 512 == 0 else 1
        self.own = own
        self.mate = swap(own, 1)
        self.far = [swap(part, 2) for part in split_rows(own, parts)]
        self.far_mate = None

    def pieces(self):
        if self.far_mate is None:
            self.far_mate = [swap(part, 1) for part in self.far]
        return [self.own, self.mate, *self.far, *self.far_mate]


class Reduce:
    def __init__(self, keep, mate):
        received = swap(mate, 1)
        rows = keep.shape[0] // 2
        parts = 2 if rows % 512 == 0 else 1
        total = keep.astype(F32) + received.astype(F32)
        self.near = keep[:rows].astype(F32) + received[:rows].astype(F32)
        self.sent = [part.astype(BF16) for part in split_rows(total[rows:], parts)]
        self.send()

    def send(self, *others):
        self.across = [swap(part, 2) for part in after(self.sent, *others)]

    def value(self):
        return self.near + jnp.concatenate(self.across).astype(F32)


def after(value, *others):
    return lax.optimization_barrier((value, *others))[0]


def together(result, *slots):
    values = lax.optimization_barrier((result, *[array[i] for array, i in slots]))
    for (array, i), value in zip(slots, values[1:]):
        array[i] = value
    return values[0]


def slots_of(array, *wanted):
    return [(array, i) for i in (wanted or range(len(array))) if i < len(array)]


def row_major(array):
    return with_layout_constraint(array, Layout(tuple(range(array.ndim))))


def butterfly(array):
    for axis in ("head", "ctx", "dp"):
        size = lax.axis_size(axis)
        bit = 1
        while bit < size:
            array = array + lax.ppermute(array, axis, [(i, i ^ bit) for i in range(size)])
            bit *= 2
    return array


def chunk_specs(tile, pieces):
    specs, start = [], 0
    for piece in pieces:
        count = piece.shape[0] // tile
        specs.append(
            pl.BlockSpec(
                (tile, piece.shape[1]),
                lambda i, *_, a=start, n=count: (jnp.clip(i - a, 0, n - 1), 0),
            )
        )
        start += count
    return specs


def chunk_ends(tile, pieces):
    ends, start = [], 0
    for piece in pieces:
        start += piece.shape[0] // tile
        ends.append(start)
    return ends


def pick(refs, ends, out_ref):
    index = pl.program_id(0)
    start = 0
    for ref, end in zip(refs, ends):

        @pl.when((index >= start) & (index < end))
        def _(ref=ref):
            out_ref[...] = ref[...]

        start = end


def columns_spec(rows, width, index):
    return pl.BlockSpec((rows, width), lambda i, *_: (0, index))


def row_spec(tile, width):
    return pl.BlockSpec((tile, width), lambda i, *_: (i, 0))


def whole_spec(shape):
    return pl.BlockSpec(shape, lambda i, *_: (0,) * len(shape))


def pair_specs(tile, per, width):
    def keep(i, *_):
        chunk = i // per
        return (chunk // 2 * per + jnp.where(chunk % 2 == 0, i % per, per - 1), 0)

    def mate(i, *_):
        chunk = i // per
        hold = jnp.maximum(chunk // 2 * per - 1, 0)
        return (jnp.where(chunk % 2 == 1, chunk // 2 * per + i % per, hold), 0)

    return [pl.BlockSpec((tile, width), keep), pl.BlockSpec((tile, width), mate)]


def pair_shapes(rows, width):
    return [jax.ShapeDtypeStruct((rows // 2, width), BF16)] * 2


def put_pair(value, per, keep_ref, mate_ref):
    even = (pl.program_id(0) // per) % 2 == 0

    @pl.when(even)
    def _():
        keep_ref[...] = value

    @pl.when(jnp.logical_not(even))
    def _():
        mate_ref[...] = value


def cost(flops, moved, transcendentals=0):
    return pl.CostEstimate(
        flops=int(flops), bytes_accessed=int(moved), transcendentals=int(transcendentals)
    )


def turn(values, cos_table, sin_table, low_half, sign):
    ahead = pltpu.roll(values, VD - HD // 2, 1)
    behind = pltpu.roll(values, HD // 2, 1)
    rotated = jnp.where(low_half, -ahead, behind)
    return values * cos_table + sign * rotated * sin_table


def low_half_mask(rows):
    lane = lax.broadcasted_iota(jnp.int32, (rows, VD), 1)
    return (lane % HD) < HD // 2


def side_by_side(w_ref):
    return jnp.concatenate([w_ref[item] for item in range(w_ref.shape[0])], axis=1)


def project_kernel(*refs, heads, ends):
    count = len(ends)
    w_ref, cos_ref, sin_ref, x_ref = refs[count : count + 4]
    q_refs, kv_refs = refs[count + 4 : count + 4 + heads], refs[count + 4 + heads :]
    pick(refs[:count], ends, x_ref)
    mask = low_half_mask(x_ref.shape[0])
    cos_table, sin_table = cos_ref[...], sin_ref[...]
    out = dot(x_ref[...], side_by_side(w_ref))
    for head in range(heads):
        base = head * 3 * VD
        query = turn(out[:, base : base + VD], cos_table, sin_table, mask, 1.0) * SCALE
        key = turn(out[:, base + VD : base + 2 * VD], cos_table, sin_table, mask, 1.0)
        q_refs[head][...] = query.astype(BF16)
        kv_refs[head][:, :VD] = key.astype(BF16)
        kv_refs[head][:, VD:] = out[:, base + 2 * VD : base + 3 * VD].astype(BF16)


def project(chunks, weight, cos_table, sin_table):
    own_rows = chunks[0].shape[0]
    rows = 4 * own_rows
    heads = weight.shape[0] // 3
    tile = min(256, own_rows)
    out = pl.pallas_call(
        functools.partial(project_kernel, heads=heads, ends=chunk_ends(tile, chunks)),
        grid=(rows // tile,),
        in_specs=chunk_specs(tile, chunks)
        + [whole_spec(weight.shape), row_spec(tile, VD), row_spec(tile, VD)],
        out_specs=[row_spec(tile, D)]
        + [row_spec(tile, VD)] * heads
        + [row_spec(tile, 2 * VD)] * heads,
        out_shape=[jax.ShapeDtypeStruct((rows, D), BF16)]
        + [jax.ShapeDtypeStruct((rows, VD), BF16)] * heads
        + [jax.ShapeDtypeStruct((rows, 2 * VD), BF16)] * heads,
        compiler_params=pltpu.CompilerParams(vmem_limit_bytes=60 * MIB),
        cost_estimate=cost(
            2 * rows * weight.size,
            2 * (2 * rows * D + weight.size + rows * 3 * heads * VD),
        ),
        name="project",
    )(*chunks, weight, cos_table, sin_table)
    return out[0], out[1 : 1 + heads], out[1 + heads :]


def unproject_kernel(*refs, heads, per):
    dq_refs, own_refs, recv_refs = refs[:heads], refs[heads : 2 * heads], refs[2 * heads : 3 * heads]
    w_ref, cos_ref, sin_ref, gp_ref, keep_ref, mate_ref = refs[3 * heads :]
    mask = low_half_mask(gp_ref.shape[0])
    cos_table, sin_table = cos_ref[...], sin_ref[...]
    for head in range(heads):
        base = head * 3 * VD
        both = own_refs[head][...].astype(F32) + recv_refs[head][...].astype(F32)
        query = dq_refs[head][...].astype(F32)
        gp_ref[:, base : base + VD] = turn(query, cos_table, sin_table, mask, -1.0).astype(BF16)
        gp_ref[:, base + VD : base + 2 * VD] = turn(
            both[:, :VD], cos_table, sin_table, mask, -1.0
        ).astype(BF16)
        gp_ref[:, base + 2 * VD : base + 3 * VD] = both[:, VD:].astype(BF16)
    put_pair(dot(gp_ref[...], side_by_side(w_ref), NT).astype(BF16), per, keep_ref, mate_ref)


def unproject(dq, dkv_own, dkv_recv, weight, cos_table, sin_table):
    rows = dq[0].shape[0]
    heads = len(dq)
    tile = min(256, rows // 4)
    per = rows // 4 // tile
    return pl.pallas_call(
        functools.partial(unproject_kernel, heads=heads, per=per),
        grid=(rows // tile,),
        in_specs=[row_spec(tile, VD)] * heads
        + [row_spec(tile, 2 * VD)] * (2 * heads)
        + [whole_spec(weight.shape), row_spec(tile, VD), row_spec(tile, VD)],
        out_specs=[row_spec(tile, heads * 3 * VD)] + pair_specs(tile, per, D),
        out_shape=[jax.ShapeDtypeStruct((rows, heads * 3 * VD), BF16)] + pair_shapes(rows, D),
        compiler_params=pltpu.CompilerParams(vmem_limit_bytes=60 * MIB),
        cost_estimate=cost(
            2 * rows * weight.size,
            2 * (rows * D + weight.size + 9 * rows * heads * VD),
        ),
        name="unproject",
    )(*dq, *dkv_own, *dkv_recv, weight, cos_table, sin_table)


def output_kernel(*refs, heads, per):
    attn_refs = refs[:heads]
    w_ref, all_ref, keep_ref, mate_ref = refs[heads:]
    for head in range(heads):
        all_ref[:, head * VD : (head + 1) * VD] = attn_refs[head][...]
    put_pair(dot(all_ref[...], w_ref[...], NT).astype(BF16), per, keep_ref, mate_ref)


def output_projection(attn, weight):
    rows = attn[0].shape[0]
    heads = len(attn)
    tile = min(256, rows // 4)
    per = rows // 4 // tile
    return pl.pallas_call(
        functools.partial(output_kernel, heads=heads, per=per),
        grid=(rows // tile,),
        in_specs=[row_spec(tile, VD)] * heads + [whole_spec(weight.shape)],
        out_specs=[row_spec(tile, heads * VD)] + pair_specs(tile, per, D),
        out_shape=[jax.ShapeDtypeStruct((rows, heads * VD), BF16)] + pair_shapes(rows, D),
        compiler_params=pltpu.CompilerParams(vmem_limit_bytes=60 * MIB),
        cost_estimate=cost(
            2 * rows * D * weight.shape[1], 2 * (rows * D + weight.size + 2 * rows * heads * VD)
        ),
        name="output_projection",
    )(*attn, weight)


def gate_kernel(*refs, ends):
    count = len(ends)
    w_ref, x_ref, hidden_ref, by_gate_ref, by_up_ref = refs[count:]
    pick(refs[:count], ends, x_ref)
    width = hidden_ref.shape[1]
    step = min(512, width)
    x = x_ref[...]
    for base in range(0, width, step):
        cols = slice(base, base + step)
        gate = dot(x, w_ref[:, cols])
        up = dot(x, w_ref[:, width + base : width + base + step])
        share = jax.nn.sigmoid(gate)
        swish = gate * share
        hidden_ref[:, cols] = (swish * up).astype(BF16)
        by_gate_ref[:, cols] = (up * share * (1.0 + gate * (1.0 - share))).astype(BF16)
        by_up_ref[:, cols] = swish.astype(BF16)


def gate_up(chunks, weights, width):
    own_rows = chunks[0].shape[0]
    rows = 4 * own_rows
    tile = min(256, own_rows)
    return pl.pallas_call(
        functools.partial(gate_kernel, ends=chunk_ends(tile, chunks)),
        grid=(rows // tile,),
        in_specs=chunk_specs(tile, chunks) + [columns_spec(D, 2 * width, 0)],
        out_specs=[row_spec(tile, D)] + [row_spec(tile, width)] * 3,
        out_shape=[jax.ShapeDtypeStruct((rows, D), BF16)]
        + [jax.ShapeDtypeStruct((rows, width), BF16)] * 3,
        compiler_params=pltpu.CompilerParams(vmem_limit_bytes=60 * MIB),
        cost_estimate=cost(4 * rows * D * width, 2 * (2 * rows * D + 2 * D * width + 3 * rows * width)),
        name="gate_up",
    )(*chunks, weights)


def feed_kernel(*refs, ends, per):
    count = len(ends)
    hidden_ref, by_gate_ref, by_up_ref, down_ref, inner_ref = refs[count : count + 5]
    cot_ref, grad_ref, ffn_keep, ffn_mate, mid_keep, mid_mate = refs[count + 5 :]
    pick(refs[:count], ends, cot_ref)
    width = hidden_ref.shape[1]
    grad_hidden = dot(cot_ref[...], down_ref[...])
    grad_ref[:, :width] = (grad_hidden * by_gate_ref[...].astype(F32)).astype(BF16)
    grad_ref[:, width:] = (grad_hidden * by_up_ref[...].astype(F32)).astype(BF16)
    put_pair(dot(hidden_ref[...], down_ref[...], NT).astype(BF16), per, ffn_keep, ffn_mate)
    put_pair(dot(grad_ref[...], inner_ref[...], NT).astype(BF16), per, mid_keep, mid_mate)


def feed(chunks, hidden, by_gate, by_up, weights):
    own_rows = chunks[0].shape[0]
    rows = 4 * own_rows
    width = hidden.shape[1]
    tile = min(256, own_rows)
    per = own_rows // tile
    return pl.pallas_call(
        functools.partial(feed_kernel, ends=chunk_ends(tile, chunks), per=per),
        grid=(rows // tile,),
        in_specs=chunk_specs(tile, chunks)
        + [row_spec(tile, width)] * 3
        + [columns_spec(D, width, 2), columns_spec(D, 2 * width, 0)],
        out_specs=[row_spec(tile, D), row_spec(tile, 2 * width)]
        + pair_specs(tile, per, D)
        + pair_specs(tile, per, D),
        out_shape=[
            jax.ShapeDtypeStruct((rows, D), BF16),
            jax.ShapeDtypeStruct((rows, 2 * width), BF16),
        ]
        + pair_shapes(rows, D)
        + pair_shapes(rows, D),
        compiler_params=pltpu.CompilerParams(vmem_limit_bytes=60 * MIB),
        cost_estimate=cost(8 * rows * D * width, 2 * (4 * rows * D + 3 * D * width + 5 * rows * width)),
        name="feed",
    )(*chunks, hidden, by_gate, by_up, weights, weights)


class Plan:
    def __init__(self, own_rows, block_len, prev_rows, ndoc):
        self.own_rows = own_rows
        self.block_len = block_len
        self.prev_rows = prev_rows
        self.ndoc = ndoc
        self.bq = min(256, own_rows)
        self.bk = min(512, own_rows)
        self.total = prev_rows + block_len

    def doc_start(self, info, pos):
        start = jnp.zeros_like(pos)
        for item in range(self.ndoc):
            start = jnp.where(pos >= info[2 + item], info[2 + item], start)
        return start

    def query_start(self, info, index):
        per = self.own_rows // self.bq
        chunk = (index // per) ^ info[0]
        return info[1] * self.block_len + chunk * self.own_rows + (index % per) * self.bq

    def key_row(self, info, index):
        per = self.own_rows // self.bk
        blocks = self.block_len // self.bk
        owner = index // blocks
        local = index % blocks
        inside = (((local // per) ^ info[0]) * per + local % per) * self.bk
        base = jnp.where(owner == info[1], self.prev_rows, owner * self.block_len)
        return pl.multiple_of(base + inside, self.bk)

    def ranges(self, info, start):
        last = start + self.bq - 1
        low = self.doc_start(info, start) // self.bk
        high = last // self.bk + 1
        open_from = (self.doc_start(info, last) + self.bk - 1) // self.bk
        first = jnp.minimum(jnp.maximum(open_from, low), high)
        until = jnp.maximum(first, jnp.minimum((start + 1) // self.bk, high))
        return low, first, until, high


def in_groups(low, high, size, visit):
    count = (high - low) // size

    @pl.loop(0, count)
    def _(group):
        visit(*[low + group * size + item for item in range(size)])

    if size > 1:

        @pl.loop(low + count * size, high)
        def _(index):
            visit(index)


def split_halves(q):
    lane = lax.broadcasted_iota(jnp.int32, q.shape, 1)
    zero = jnp.zeros_like(q)
    return jnp.concatenate([jnp.where(lane < HD, q, zero), jnp.where(lane >= HD, q, zero)], axis=0)


def in_lanes(value):
    high = value.astype(BF16)
    rest = value - high.astype(F32)
    middle = rest.astype(BF16)
    low = (rest - middle.astype(F32)).astype(BF16)
    lane = lax.broadcasted_iota(jnp.int32, value.shape, 1)
    zero = jnp.zeros_like(high)
    return jnp.where(
        lane == 0, high, jnp.where(lane == 1, middle, jnp.where(lane == 2, low, zero))
    )


def load_keys(plan, info, own_ref, prev_ref, kv_sc):
    @pl.when(pl.program_id(0) == 0)
    def _():
        kv_sc[plan.prev_rows :, :] = own_ref[...]

        @pl.when(info[1] > 0)
        def _():
            kv_sc[: plan.prev_rows, :] = prev_ref[...]


def forward_kernel(
    info,
    lam_ref,
    gain_ref,
    q_ref,
    own_ref,
    prev_ref,
    attn_ref,
    first_ref,
    second_ref,
    lse_ref,
    kv_sc,
    m_sc,
    l_sc,
    acc_sc,
    *,
    plan,
):
    bq, bk = plan.bq, plan.bk
    load_keys(plan, info, own_ref, prev_ref, kv_sc)
    start = plan.query_start(info, pl.program_id(0))
    q2 = split_halves(q_ref[...])
    m_sc[...] = jnp.full_like(m_sc, NEG)
    l_sc[...] = jnp.zeros_like(l_sc)
    acc_sc[...] = jnp.zeros_like(acc_sc)
    low, first, until, high = plan.ranges(info, start)

    def visit(index, masked):
        row = plan.key_row(info, index)
        key = kv_sc[pl.ds(row, bk), :VD]
        value = kv_sc[pl.ds(row, bk), VD:]
        scores = dot(q2, key, NT)
        if masked:
            query_pos = start + lax.broadcasted_iota(jnp.int32, (bq, 1), 0)
            begin = plan.doc_start(info, query_pos)
            key_pos = index * bk + lax.broadcasted_iota(jnp.int32, (bq, bk), 1)
            keep = (key_pos <= query_pos) & (key_pos >= begin)
            scores = jnp.concatenate(
                [jnp.where(keep, scores[:bq], NEG), jnp.where(keep, scores[bq:], NEG)], axis=0
            )
        before = m_sc[...]
        after = jnp.maximum(before, jnp.max(scores, axis=1, keepdims=True))
        weights = jnp.exp(scores - jnp.tile(after, (1, bk // VD)))
        factor = jnp.exp(before - after)
        m_sc[...] = after
        l_sc[...] = l_sc[...] * factor + jnp.sum(weights, axis=1, keepdims=True)
        acc_sc[...] = acc_sc[...] * factor + dot(weights.astype(BF16), value)

    @pl.loop(low, first)
    def _(index):
        visit(index, True)

    @pl.loop(first, until)
    def _(index):
        visit(index, False)

    @pl.loop(until, high)
    def _(index):
        visit(index, True)

    total = l_sc[...]
    maps = acc_sc[...] * (1.0 / total)
    first_map, second_map = maps[:bq], maps[bq:]
    first_ref[...] = first_map
    second_ref[...] = second_map
    difference = first_map - lam_ref[0] * second_map
    scaling = lax.rsqrt(jnp.mean(difference * difference, axis=1, keepdims=True) + EPS)
    attn_ref[...] = (difference * scaling * gain_ref[...]).astype(BF16)
    lanes = in_lanes(-(m_sc[...] + jnp.log(total)))
    lse_ref[:, :VD] = lanes[:bq]
    lse_ref[:, VD:] = lanes[bq:]


def attention_cost(plan, per_pair, extra=0):
    pairs = plan.block_len * plan.block_len * 5 // 8
    return cost(pairs * per_pair + extra, plan.block_len * VD * 32, 2 * pairs)


def attend_forward(plan, info, lam, gain, q, kv_own, kv_prev):
    rows, bq = plan.block_len, plan.bq
    grid_spec = pltpu.PrefetchScalarGridSpec(
        num_scalar_prefetch=1,
        grid=(rows // bq,),
        in_specs=[
            pl.BlockSpec(memory_space=pltpu.SMEM),
            whole_spec((1, VD)),
            row_spec(bq, VD),
            whole_spec((rows, 2 * VD)),
            whole_spec((plan.prev_rows, 2 * VD)),
        ],
        out_specs=[row_spec(bq, VD)] * 3 + [row_spec(bq, 2 * VD)],
        scratch_shapes=[
            pltpu.VMEM((plan.total, 2 * VD), BF16),
            pltpu.VMEM((2 * bq, VD), F32),
            pltpu.VMEM((2 * bq, VD), F32),
            pltpu.VMEM((2 * bq, VD), F32),
        ],
    )
    return pl.pallas_call(
        functools.partial(forward_kernel, plan=plan),
        grid_spec=grid_spec,
        out_shape=[
            jax.ShapeDtypeStruct((rows, VD), BF16),
            jax.ShapeDtypeStruct((rows, VD), F32),
            jax.ShapeDtypeStruct((rows, VD), F32),
            jax.ShapeDtypeStruct((rows, 2 * VD), BF16),
        ],
        compiler_params=pltpu.CompilerParams(vmem_limit_bytes=60 * MIB),
        cost_estimate=attention_cost(plan, 6 * VD),
        name="attend_forward",
    )(info, lam, gain, q, kv_own, kv_prev)


def difference_kernel(lam_ref, gain_ref, w_ref, *refs, heads, ends):
    count = len(ends)
    chunks, refs = refs[:count], refs[count:]
    first_refs, second_refs, refs = refs[:heads], refs[heads : 2 * heads], refs[2 * heads :]
    gm_ref, sums_ref, grad_refs = refs[0], refs[1], refs[2:]
    lam = lam_ref[0]

    @pl.when(pl.program_id(0) == 0)
    def _():
        sums_ref[...] = jnp.zeros_like(sums_ref)

    pick(chunks, ends, gm_ref)
    upstream_all = dot(gm_ref[...], w_ref[...])
    for head in range(heads):
        upstream = upstream_all[:, head * VD : (head + 1) * VD]
        first_map, second_map = first_refs[head][...], second_refs[head][...]
        difference = first_map - lam * second_map
        scaling = lax.rsqrt(jnp.mean(difference * difference, axis=1, keepdims=True) + EPS)
        normal = difference * scaling
        weighted = upstream * gain_ref[...]
        inner_mean = jnp.mean(weighted * normal, axis=1, keepdims=True)
        grad = (scaling * (weighted - normal * inner_mean)).astype(BF16)
        grad_wide = grad.astype(F32)
        first_product, second_product = grad_wide * first_map, grad_wide * second_map
        sums_ref[0:1, :] += jnp.sum(upstream * normal, axis=0, keepdims=True)
        sums_ref[1:2, :] += jnp.sum(second_product, axis=0, keepdims=True)
        out = grad_refs[head]
        out[:, :VD] = grad
        for item, product in enumerate((first_product, second_product)):
            total = jnp.sum(product, axis=1, keepdims=True)
            out[:, (item + 1) * VD : (item + 2) * VD] = in_lanes(
                jnp.broadcast_to(-total, product.shape)
            )


def difference_grads(lam, gain, weight, gm, first, second):
    own_rows = gm[0].shape[0]
    rows = 4 * own_rows
    heads = len(first)
    tile = min(256, own_rows)
    return pl.pallas_call(
        functools.partial(difference_kernel, heads=heads, ends=chunk_ends(tile, gm)),
        grid=(rows // tile,),
        in_specs=[pl.BlockSpec(memory_space=pltpu.SMEM), whole_spec((1, VD)), whole_spec(weight.shape)]
        + chunk_specs(tile, gm)
        + [row_spec(tile, VD)] * (2 * heads),
        out_specs=[row_spec(tile, D), whole_spec((8, VD))] + [row_spec(tile, 3 * VD)] * heads,
        out_shape=[jax.ShapeDtypeStruct((rows, D), BF16), jax.ShapeDtypeStruct((8, VD), F32)]
        + [jax.ShapeDtypeStruct((rows, 3 * VD), BF16)] * heads,
        compiler_params=pltpu.CompilerParams(vmem_limit_bytes=60 * MIB),
        cost_estimate=cost(2 * rows * D * heads * VD, 4 * rows * D + 14 * rows * heads * VD),
        name="difference_grads",
    )(lam, gain, weight, *gm, *first, *second)


def backward_kernel(
    info,
    lam_ref,
    q_ref,
    own_ref,
    prev_ref,
    lse_ref,
    grad_ref,
    dq_ref,
    dkv_own_ref,
    dkv_prev_ref,
    kv_sc,
    dk_sc,
    dv_sc,
    dqt_sc,
    *,
    plan,
):
    bq, bk = plan.bq, plan.bk
    step = pl.program_id(0)
    lam = lam_ref[0]

    @pl.when(step == 0)
    def _():
        lane = lax.broadcasted_iota(jnp.int32, (bk, VD), 1)
        ones = jnp.where(lane < 3, 1.0, 0.0).astype(BF16)

        def fill(source, base, rows):
            for start in range(0, rows, bk):
                to = slice(base + start, base + start + bk)
                kv_sc[to, :VD] = source[start : start + bk, :VD]
                kv_sc[to, VD : 2 * VD] = ones
                kv_sc[to, 2 * VD :] = source[start : start + bk, VD:]

        fill(own_ref, plan.prev_rows, plan.block_len)

        @pl.when(info[1] > 0)
        def _():
            fill(prev_ref, 0, plan.prev_rows)

        dk_sc[...] = jnp.zeros_like(dk_sc)
        dv_sc[...] = jnp.zeros_like(dv_sc)

    grad = grad_ref[:, :VD]
    start = plan.query_start(info, step)
    q2 = split_halves(q_ref[...])
    q_wide = jnp.concatenate(
        [q2, jnp.concatenate([lse_ref[:, :VD], lse_ref[:, VD:]], axis=0)], axis=1
    )
    ones = jnp.ones((8, VD), BF16)
    delta_first = dot(ones, grad_ref[:, VD : 2 * VD], NT)[0:1]
    delta_second = dot(ones, grad_ref[:, 2 * VD :], NT)[0:1]
    dqt_sc[...] = jnp.zeros_like(dqt_sc)
    low, _, _, high = plan.ranges(info, start)

    query_pos = start + lax.broadcasted_iota(jnp.int32, (1, bq), 1)
    begin = plan.doc_start(info, query_pos)

    def visit(*indices):
        results = []
        for index in indices:
            row = plan.key_row(info, index)
            key = kv_sc[pl.ds(row, bk), :VD]
            prob = jnp.exp(dot(kv_sc[pl.ds(row, bk), : 2 * VD], q_wide, NT))
            base = dot(kv_sc[pl.ds(row, bk), 2 * VD :], grad, NT)
            key_pos = index * bk + lax.broadcasted_iota(jnp.int32, (bk, bq), 0)
            keep = (key_pos <= query_pos) & (key_pos >= begin)
            prob_first = jnp.where(keep, prob[:, :bq], 0.0)
            prob_second = jnp.where(keep, prob[:, bq:], 0.0)
            raw = jnp.concatenate(
                [
                    (prob_first * (base + delta_first)).astype(BF16),
                    (prob_second * (base + delta_second)).astype(BF16),
                ],
                axis=1,
            )
            value_grad = dot((prob_first - lam * prob_second).astype(BF16), grad)
            results.append((row, value_grad, dot(raw, q2), dot(key, raw, TN)))
        for row, value_grad, key_grad, query_grad in results:
            dv_sc[pl.ds(row, bk), :] += value_grad
            dk_sc[pl.ds(row, bk), :] += key_grad
        dqt_sc[...] += sum(result[3] for result in results)

    in_groups(low, high, 2, visit)

    dq_t = jnp.concatenate([dqt_sc[:HD, :bq], -lam * dqt_sc[HD:, bq:]], axis=0) * SCALE
    dq_ref[...] = dq_t.T.astype(BF16)

    @pl.when(step == pl.num_programs(0) - 1)
    def _():
        lane = lax.broadcasted_iota(jnp.int32, (1, VD), 1)
        side = jnp.where(lane < HD, 1.0, -lam)
        dkv_own_ref[:, :VD] = (dk_sc[plan.prev_rows :, :] * side).astype(BF16)
        dkv_own_ref[:, VD:] = dv_sc[plan.prev_rows :, :].astype(BF16)
        dkv_prev_ref[:, :VD] = (dk_sc[: plan.prev_rows, :] * side).astype(BF16)
        dkv_prev_ref[:, VD:] = dv_sc[: plan.prev_rows, :].astype(BF16)


def attend_backward(plan, info, lam, q, kv_own, kv_prev, lse, grad):
    rows, bq = plan.block_len, plan.bq
    grid_spec = pltpu.PrefetchScalarGridSpec(
        num_scalar_prefetch=1,
        grid=(rows // bq,),
        in_specs=[
            pl.BlockSpec(memory_space=pltpu.SMEM),
            row_spec(bq, VD),
            whole_spec((rows, 2 * VD)),
            whole_spec((plan.prev_rows, 2 * VD)),
            row_spec(bq, 2 * VD),
            row_spec(bq, 3 * VD),
        ],
        out_specs=[
            row_spec(bq, VD),
            whole_spec((rows, 2 * VD)),
            whole_spec((plan.prev_rows, 2 * VD)),
        ],
        scratch_shapes=[
            pltpu.VMEM((plan.total, 3 * VD), BF16),
            pltpu.VMEM((plan.total, VD), F32),
            pltpu.VMEM((plan.total, VD), F32),
            pltpu.VMEM((VD, 2 * bq), F32),
        ],
    )
    return pl.pallas_call(
        functools.partial(backward_kernel, plan=plan),
        grid_spec=grid_spec,
        out_shape=[
            jax.ShapeDtypeStruct((rows, VD), BF16),
            jax.ShapeDtypeStruct((rows, 2 * VD), BF16),
            jax.ShapeDtypeStruct((plan.prev_rows, 2 * VD), BF16),
        ],
        compiler_params=pltpu.CompilerParams(vmem_limit_bytes=60 * MIB),
        cost_estimate=attention_cost(plan, 16 * VD),
        name="attend_backward",
    )(info, lam, q, kv_own, kv_prev, lse, grad)


def norm_forward(values, gain_vec):
    scaling = lax.rsqrt(jnp.mean(values * values, axis=-1, keepdims=True) + EPS)
    return (values * scaling * gain_vec, scaling)


def norm_backward(values, scaling, gain_vec, upstream):
    normal = values * scaling
    weighted = upstream * gain_vec
    inner_mean = jnp.mean(weighted * normal, axis=-1, keepdims=True)
    return (scaling * (weighted - normal * inner_mean), jnp.sum(upstream * normal, axis=0))


def adamw(parameter, momentum, variance, gradient, learn_rate, decay_rate):
    momentum = BETA1 * momentum + (1.0 - BETA1) * gradient
    variance = BETA2 * variance + (1.0 - BETA2) * gradient * gradient
    corrected = momentum / (1.0 - BETA1**STEP)
    spread = jnp.sqrt(variance / (1.0 - BETA2**STEP))
    return (
        parameter - learn_rate * (corrected / (spread + ADAM_EPS) + decay_rate * parameter),
        momentum,
        variance,
    )


def send_keys(kv, ctx_count):
    if ctx_count == 2:
        return lax.ppermute(kv, "ctx", [(0, 1)])
    return lax.all_gather(kv, "ctx", axis=0, tiled=True)


def return_keys(grads, ctx_count):
    if ctx_count == 2:
        return lax.ppermute(grads, "ctx", [(1, 0)])
    return lax.psum_scatter(grads, "ctx", scatter_dimension=0, tiled=True)


def scatter_weight(grad, *others):
    grad = after(grad.astype(BF16), *others)
    return lax.psum_scatter(grad, "dp", scatter_dimension=0, tiled=True)


def sum_blocks(share, ctx_count):
    if ctx_count == 2:
        other = lax.ppermute(share, "ctx", [(0, 1), (1, 0)])
        return share.astype(F32) + other.astype(F32)
    return lax.psum(share, "ctx").astype(F32)


def on_device(
    tokens,
    cotangent,
    doc_lengths,
    qkv_weight,
    out_weight,
    inner_weight,
    down_weight,
    norm_gains,
    head_gain,
    lambdas,
    qkv_momentum,
    out_momentum,
    inner_momentum,
    down_momentum,
    norm_momentum,
    head_momentum,
    lambda_momentum,
    qkv_variance,
    out_variance,
    inner_variance,
    down_variance,
    norm_variance,
    head_variance,
    lambda_variance,
):
    micro_count, own_rows, _ = tokens.shape
    head_count = lax.axis_size("head")
    ctx_count = lax.axis_size("ctx")
    block_len = own_rows * head_count
    seq_len = block_len * ctx_count
    ctx_index = lax.axis_index("ctx")
    head_index = lax.axis_index("head")
    local_heads = qkv_weight.shape[1]
    ff_local = inner_weight.shape[2]
    ndoc = doc_lengths.shape[1]
    plan = Plan(own_rows, block_len, block_len if ctx_count == 2 else seq_len, ndoc)

    def gather_weight(shard):
        return lax.all_gather(shard.astype(BF16), "dp", axis=0, tiled=True)

    def by_part(array):
        return array.transpose(1, 2, 0, 3)

    qkv_low = lax.all_gather(
        row_major(by_part(qkv_weight).astype(BF16)).reshape(local_heads * 3, -1, VD),
        "dp",
        axis=1,
        tiled=True,
    )
    out_t = gather_weight(row_major(out_weight.astype(BF16).reshape(local_heads * VD, -1).T))
    feed_low = gather_weight(
        jnp.concatenate(
            [
                inner_weight.reshape(-1, 2 * ff_local).astype(BF16),
                row_major(down_weight.astype(BF16).T),
            ],
            axis=1,
        )
    )

    first_exp = jnp.exp(jnp.sum(lambdas[0] * lambdas[1]))
    second_exp = jnp.exp(jnp.sum(lambdas[2] * lambdas[3]))
    lambda_value = first_exp - second_exp + LAMBDA_INIT
    lam = lambda_value.reshape(1)
    head_scale = (head_gain * (1.0 - LAMBDA_INIT)).reshape(1, VD)

    chunk = jnp.arange(block_len, dtype=jnp.int32) // own_rows
    position = (
        ctx_index * block_len
        + (chunk ^ head_index) * own_rows
        + jnp.arange(block_len, dtype=jnp.int32) % own_rows
    )
    frequency = ROPE_BASE ** (
        -(jnp.arange(VD, dtype=jnp.int32) % (HD // 2)).astype(F32) / (HD // 2)
    )

    def info_of(micro):
        bounds = jnp.cumsum(doc_lengths[micro], dtype=jnp.int32)
        return jnp.concatenate([jnp.stack([head_index, ctx_index]).astype(jnp.int32), bounds])

    micros = range(micro_count)
    heads = range(local_heads)
    infos = [info_of(m) for m in micros]
    own, normed_own, normed, cot_own = [], [], [], []
    for m in micros:
        rows, cot_rows = tokens[m], cotangent[m]
        if m > 0:
            rows = after(rows, normed[0].own)
        own.append(rows.astype(F32))
        normed_own.append(norm_forward(own[m], norm_gains[0]))
        cot_own.append(cot_rows)
        normed.append(Gather(normed_own[m][0].astype(BF16)))
    position = after(position, normed[-1].own)
    phases = position.astype(F32)[:, None] * frequency[None, :]
    cos_table, sin_table = jnp.cos(phases), jnp.sin(phases)

    normed_all, q, kv, kv_prev, cot = [], [], [], [], []
    for m in micros:
        pieces = after(normed[m].pieces(), *normed[-1].far)
        result = project(pieces, qkv_low, cos_table, sin_table)
        if m == 0:
            cot.append(Gather(after(cot_own[0], qkv_low)))
        else:
            result = together(result, *slots_of(cot[0].far, 0))
            cot.append(Gather(after(cot_own[1], result[2], *cot[0].far)))
        normed_all.append(result[0])
        q.append(result[1])
        kv.append(result[2])
        kv_prev.append([send_keys(result[2][h], ctx_count) for h in heads])

    def attend(m, h, before, beside):
        out = attend_forward(
            plan, infos[m], lam, head_scale, after(q[m][h], *before), kv[m][h], kv_prev[m][h]
        )
        return together(out, *beside)

    mid = []

    def finish_attention(m):
        middle = own[m] + attended[m].value()
        value, scaling = norm_forward(middle, norm_gains[1])
        mid.append((middle, scaling, Gather(value.astype(BF16))))

    maps, attn_all, attended = [], [], []
    for m in micros:
        outs = []
        for h in heads:
            if m == 0:
                before = [out_t, kv[-1]] if h == 0 else [outs[-1]]
                beside = [
                    slots_of(cot[0].far, 1),
                    slots_of(cot[1].far, 0),
                    slots_of(cot[1].far, 1),
                ][h]
            elif h == 0:
                before = [*attended[0].sent, *cot[0].pieces(), *cot[1].pieces()]
                beside = slots_of(attended[0].across) + slots_of(kv_prev[m], 1)
            else:
                before = [outs[-1], mid[0][2].own]
                beside = slots_of(mid[0][2].far, h - 1) + slots_of(kv_prev[m], h + 1)
            outs.append(attend(m, h, before, beside))
            if m > 0 and h == 0:
                finish_attention(0)
        maps.append([out[1:] for out in outs])
        result = output_projection([out[0] for out in outs], out_t)
        if m == 0:
            result = together(result, *slots_of(kv_prev[1], 0))
        attn_all.append(result[0])
        attended.append(Reduce(*result[1:]))

    grad_middle, gm, gain_mid = [], [], []

    def finish_feed(m, reduced):
        middle, scaling, _ = mid[m]
        grad_norm, part = norm_backward(middle, scaling, norm_gains[1], reduced.value())
        grad_middle.append((cot_own[m].astype(F32) + grad_norm).astype(BF16))
        gm.append(Gather(grad_middle[m]))
        gain_mid.append(part)

    def weight_grad(left, right, before, beside, total=None):
        result = dot(after(left, *before), right, TN)
        if total is not None:
            result = (total + result).astype(BF16)
        return together(result, *beside)

    first_gates = gate_up(after(mid[0][2].pieces(), *attended[1].sent), feed_low, ff_local)
    first_gates = together(first_gates, *slots_of(attended[1].across, 0))
    first_feed = feed(cot[0].pieces(), *first_gates[1:], feed_low)
    first_feed = together(first_feed, *slots_of(attended[1].across, 1))
    finish_attention(1)
    reduced_mid = [Reduce(*first_feed[4:])]
    grad_inner = weight_grad(
        first_gates[0],
        first_feed[1],
        [mid[1][2].own, *reduced_mid[0].sent],
        slots_of(mid[1][2].far, 0),
    )
    grad_down = weight_grad(
        first_feed[0], first_gates[1], [grad_inner], slots_of(mid[1][2].far, 1)
    )
    reduced_mid[0].send(*mid[1][2].far)
    second_gates = gate_up(after(mid[1][2].pieces(), grad_down), feed_low, ff_local)
    second_gates = together(second_gates, *slots_of(reduced_mid[0].across))
    finish_feed(0, reduced_mid[0])
    second_feed = feed(after(cot[1].pieces(), gm[0].own), *second_gates[1:], feed_low)
    second_feed = together(second_feed, *slots_of(gm[0].far))
    reduced_mid.append(Reduce(*second_feed[4:]))
    grad_inner = weight_grad(
        second_gates[0],
        second_feed[1],
        reduced_mid[1].sent,
        slots_of(reduced_mid[1].across, 0),
        grad_inner,
    )
    grad_down = weight_grad(
        second_feed[0],
        second_gates[1],
        [grad_inner],
        slots_of(reduced_mid[1].across, 1),
        grad_down,
    )
    feed_grad = jnp.concatenate([grad_inner, grad_down], axis=1)
    feed_part = scatter_weight(row_major(feed_grad))
    finish_feed(1, reduced_mid[1])
    ffn_pairs = [first_feed[2:4], second_feed[2:4]]

    dqs, dkvs, recvs, gm_alls, grads, sums = [], [], [], [], [], 0.0

    def start_back(m, before, beside):
        out = difference_grads(
            lam,
            head_scale,
            out_t,
            after(gm[m].pieces(), *before),
            [part[0] for part in maps[m]],
            [part[1] for part in maps[m]],
        )
        out = together(out, *beside)
        gm_alls.append(out[0])
        grads.append(out[2:])
        dqs.append([])
        dkvs.append([])
        recvs.append([])
        return out[1]

    def attend_back(m, h, before, beside):
        out = attend_backward(
            plan,
            infos[m],
            lam,
            after(q[m][h], *before),
            kv[m][h],
            kv_prev[m][h],
            maps[m][h][2],
            grads[m][h],
        )
        out = together(out, *beside)
        dqs[m].append(out[0])
        dkvs[m].append(out[1])
        recvs[m].append(return_keys(out[2], ctx_count))

    def unprojected(m, before, beside):
        out = unproject(after(dqs[m], *before), dkvs[m], recvs[m], qkv_low, cos_table, sin_table)
        return together(out, *beside)

    def ffn_sum(m, before):
        keep, mate = ffn_pairs[m]
        return Reduce(keep, after(mate, *before))

    sums = start_back(0, [gm[1].own, feed_grad], [])
    attend_back(0, 0, [], slots_of(gm[1].far, 0))
    attend_back(0, 1, [dqs[0][-1]], slots_of(gm[1].far, 1) + slots_of(recvs[0], 0))
    ffn = [ffn_sum(0, [dqs[0][-1]])]
    ffn.append(ffn_sum(1, [dqs[0][-1]]))
    attend_back(
        0,
        2,
        [*ffn[0].sent, *gm[1].pieces()],
        slots_of(ffn[0].across, 0) + slots_of(recvs[0], 1),
    )
    sums = sums + start_back(1, [dqs[0][-1]], slots_of(ffn[0].across, 1))
    attend_back(1, 0, [*ffn[1].sent], slots_of(ffn[1].across, 0) + slots_of(recvs[0], 2))
    back = [unprojected(0, [dqs[1][-1]], slots_of(ffn[1].across, 1))]
    reduced_in = [Reduce(*back[0][1:])]
    attend_back(
        1,
        1,
        [back[0][0], *reduced_in[0].sent],
        slots_of(reduced_in[0].across, 0) + slots_of(recvs[1], 0),
    )
    attend_back(1, 2, [dqs[1][-1]], slots_of(reduced_in[0].across, 1) + slots_of(recvs[1], 1))
    grad_out = weight_grad(gm_alls[0], attn_all[0], [dqs[1][-1]], [])
    grad_out = weight_grad(gm_alls[1], attn_all[1], [grad_out], [], grad_out)
    grad_qkv = weight_grad(
        normed_all[0], back[0][0], [grad_out, feed_part], slots_of(recvs[1], 2)
    )
    back.append(unprojected(1, [grad_qkv], []))
    reduced_in.append(Reduce(*back[1][1:]))
    grad_qkv = weight_grad(
        normed_all[1],
        back[1][0],
        reduced_in[1].sent,
        slots_of(reduced_in[1].across, 0),
        grad_qkv,
    )
    last_part = scatter_weight(
        row_major(jnp.concatenate([grad_qkv, grad_out], axis=1)), feed_part
    )
    feed_share = row_major(sum_blocks(feed_part, ctx_count))
    inner_share = feed_share[:, : 2 * ff_local]
    down_share = feed_share[:, 2 * ff_local :]
    gain_mid = gain_mid[0] + gain_mid[1]
    outputs = [(mid[m][0] + ffn[m].value()).astype(BF16) for m in micros]

    gain_in = 0.0
    input_grads = []
    for m in micros:
        grad_in_norm, gain_part = norm_backward(
            own[m], normed_own[m][1], norm_gains[0], reduced_in[m].value()
        )
        gain_in = gain_in + gain_part
        input_grads.append((grad_middle[m].astype(F32) + grad_in_norm).astype(BF16))

    lambda_acc = -jnp.sum(sums[1])
    lambda_local = jnp.stack(
        [
            lambda_acc * first_exp * lambdas[1],
            lambda_acc * first_exp * lambdas[0],
            -lambda_acc * second_exp * lambdas[3],
            -lambda_acc * second_exp * lambdas[2],
        ]
    )
    small = butterfly(
        jnp.concatenate(
            [
                gain_in.reshape(-1, VD),
                gain_mid.reshape(-1, VD),
                sums[:1] * (1.0 - LAMBDA_INIT),
                lambda_local.reshape(-1, VD),
            ]
        )
    )
    per = D // VD
    norm_grad = small[: 2 * per].reshape(2, D)
    head_grad = small[2 * per]
    lambda_grad = small[2 * per + 1 :].reshape(lambdas.shape)

    feed_states = [
        adamw(
            inner_weight,
            inner_momentum,
            inner_variance,
            row_major(inner_share.reshape(inner_weight.shape)),
            0.5 * D ** (-0.5),
            DECAY,
        ),
        adamw(
            down_weight, down_momentum, down_variance, row_major(down_share.T), 0.5 * FF ** (-0.5), DECAY
        ),
    ]
    output, input_grad = jnp.stack(outputs), jnp.stack(input_grads)
    last_share = row_major(
        sum_blocks(after(last_part, feed_states, output, input_grad, small), ctx_count)
    )
    qkv_width = local_heads * 3 * VD
    qkv_share = row_major(
        last_share[:, :qkv_width].reshape(-1, local_heads, 3, VD).transpose(1, 2, 0, 3)
    )
    out_share = last_share[:, qkv_width:]
    qkv_state = adamw(
        by_part(qkv_weight),
        by_part(qkv_momentum),
        by_part(qkv_variance),
        qkv_share,
        0.5 * D ** (-0.5),
        DECAY,
    )

    states = [
        tuple(part.transpose(2, 0, 1, 3) for part in qkv_state),
        adamw(
            out_weight,
            out_momentum,
            out_variance,
            row_major(out_share.T).reshape(out_weight.shape),
            0.5 * (H * VD) ** (-0.5),
            DECAY,
        ),
        *feed_states,
        adamw(norm_gains, norm_momentum, norm_variance, norm_grad, 0.4, 0.0),
        adamw(head_gain, head_momentum, head_variance, head_grad, 0.4, 0.0),
        adamw(lambdas, lambda_momentum, lambda_variance, lambda_grad, 0.1, 0.0),
    ]
    return (
        output,
        input_grad,
        *[state[0] for state in states],
        *[state[1] for state in states],
        *[state[2] for state in states],
    )


def solution(mesh):
    activation = P("dp", ("ctx", "head"), None)
    big = (P("dp", "head", None, None), P("head", None, "dp"), P("dp", None, "head"), P("head", "dp"))
    state = big + (P(), P(), P())
    return jax.shard_map(
        on_device,
        mesh=mesh,
        in_specs=(activation, activation, P("dp", None)) + state * 3,
        out_specs=(activation, activation) + state * 3,
        check_vma=False,
    )
```

```python
import functools

import jax
import jax.numpy as jnp
from jax import lax
from jax.experimental import pallas as pl
from jax.experimental.layout import Layout, with_layout_constraint
from jax.experimental.pallas import tpu as pltpu
from jax.sharding import PartitionSpec as P

D = 1536
FF = 4096
H = 12
HD = 64
STEP = 10
VD = 128


EPS = 1e-05
LAMBDA_INIT = 0.2
SCALE = 0.125
NEG = -1e30
BETA1 = 0.9
BETA2 = 0.999
ADAM_EPS = 1e-08
DECAY = 0.1
ROPE_BASE = 10000.0

MIB = 1 << 20
NT = (((1,), (1,)), ((), ()))
TN = (((0,), (0,)), ((), ()))
F32 = jnp.float32
BF16 = jnp.bfloat16


def dot(left, right, dims=(((1,), (0,)), ((), ())), **kw):
    return lax.dot_general(left, right, dims, preferred_element_type=F32, **kw)


def swap(array, bit):
    size = lax.axis_size("head")
    return lax.ppermute(array, "head", [(i, i ^ bit) for i in range(size)])


def split_rows(array, count):
    size = array.shape[0] // count
    return [array[i * size : (i + 1) * size] for i in range(count)]


class Gather:
    def __init__(self, own, parts=1):
        parts = parts if own.shape[0] % 512 == 0 else 1
        self.own = own
        self.mate = swap(own, 1)
        self.far = [swap(part, 2) for part in split_rows(own, parts)]
        self.far_mate = None

    def pieces(self):
        if self.far_mate is None:
            self.far_mate = [swap(part, 1) for part in self.far]
        return [self.own, self.mate, *self.far, *self.far_mate]


class Reduce:
    def __init__(self, keep, mate, parts=1):
        received = swap(mate, 1)
        rows = keep.shape[0] // 2
        parts = parts if rows % 512 == 0 else 1
        total = keep.astype(F32) + received.astype(F32)
        self.near = keep[:rows].astype(F32) + received[:rows].astype(F32)
        self.sent = [part.astype(BF16) for part in split_rows(total[rows:], parts)]
        self.send()

    def send(self, *others):
        self.across = [swap(part, 2) for part in after(self.sent, *others)]

    def value(self):
        return self.near + jnp.concatenate(self.across).astype(F32)


def after(value, *others):
    return lax.optimization_barrier((value, *others))[0]


def together(result, *slots):
    values = lax.optimization_barrier((result, *[array[i] for array, i in slots]))
    for (array, i), value in zip(slots, values[1:]):
        array[i] = value
    return values[0]


def slots_of(array, *wanted):
    return [(array, i) for i in (wanted or range(len(array))) if i < len(array)]


def row_major(array):
    return with_layout_constraint(array, Layout(tuple(range(array.ndim))))


def butterfly(array):
    for axis in ("head", "ctx", "dp"):
        size = lax.axis_size(axis)
        bit = 1
        while bit < size:
            array = array + lax.ppermute(array, axis, [(i, i ^ bit) for i in range(size)])
            bit *= 2
    return array


def chunk_specs(tile, pieces):
    specs, start = [], 0
    for piece in pieces:
        count = piece.shape[0] // tile
        specs.append(
            pl.BlockSpec(
                (tile, piece.shape[1]),
                lambda i, *_, a=start, n=count: (jnp.clip(i - a, 0, n - 1), 0),
            )
        )
        start += count
    return specs


def chunk_ends(tile, pieces):
    ends, start = [], 0
    for piece in pieces:
        start += piece.shape[0] // tile
        ends.append(start)
    return ends


def pick(refs, ends, out_ref):
    index = pl.program_id(0)
    start = 0
    for ref, end in zip(refs, ends):

        @pl.when((index >= start) & (index < end))
        def _(ref=ref):
            out_ref[...] = ref[...]

        start = end


def columns_spec(rows, width, index):
    return pl.BlockSpec((rows, width), lambda i, *_: (0, index))


def row_spec(tile, width):
    return pl.BlockSpec((tile, width), lambda i, *_: (i, 0))


def whole_spec(shape):
    return pl.BlockSpec(shape, lambda i, *_: (0,) * len(shape))


def pair_specs(tile, per, width):
    def keep(i, *_):
        chunk = i // per
        return (chunk // 2 * per + jnp.where(chunk % 2 == 0, i % per, per - 1), 0)

    def mate(i, *_):
        chunk = i // per
        hold = jnp.maximum(chunk // 2 * per - 1, 0)
        return (jnp.where(chunk % 2 == 1, chunk // 2 * per + i % per, hold), 0)

    return [pl.BlockSpec((tile, width), keep), pl.BlockSpec((tile, width), mate)]


def pair_shapes(rows, width):
    return [jax.ShapeDtypeStruct((rows // 2, width), BF16)] * 2


def put_pair(value, per, keep_ref, mate_ref):
    even = (pl.program_id(0) // per) % 2 == 0

    @pl.when(even)
    def _():
        keep_ref[...] = value

    @pl.when(jnp.logical_not(even))
    def _():
        mate_ref[...] = value


def cost(flops, moved, transcendentals=0):
    return pl.CostEstimate(
        flops=int(flops), bytes_accessed=int(moved), transcendentals=int(transcendentals)
    )


def turn(values, cos_table, sin_table, low_half, sign):
    ahead = pltpu.roll(values, VD - HD // 2, 1)
    behind = pltpu.roll(values, HD // 2, 1)
    rotated = jnp.where(low_half, -ahead, behind)
    return values * cos_table + sign * rotated * sin_table


def low_half_mask(rows):
    lane = lax.broadcasted_iota(jnp.int32, (rows, VD), 1)
    return (lane % HD) < HD // 2


def side_by_side(w_ref):
    return jnp.concatenate([w_ref[item] for item in range(w_ref.shape[0])], axis=1)


def project_kernel(*refs, heads, ends):
    count = len(ends)
    w_ref, cos_ref, sin_ref, x_ref = refs[count : count + 4]
    q_refs, kv_refs = refs[count + 4 : count + 4 + heads], refs[count + 4 + heads :]
    pick(refs[:count], ends, x_ref)
    mask = low_half_mask(x_ref.shape[0])
    cos_table, sin_table = cos_ref[...], sin_ref[...]
    out = dot(x_ref[...], side_by_side(w_ref))
    for head in range(heads):
        base = head * 3 * VD
        query = turn(out[:, base : base + VD], cos_table, sin_table, mask, 1.0) * SCALE
        key = turn(out[:, base + VD : base + 2 * VD], cos_table, sin_table, mask, 1.0)
        q_refs[head][...] = query.astype(BF16)
        kv_refs[head][:, :VD] = key.astype(BF16)
        kv_refs[head][:, VD:] = out[:, base + 2 * VD : base + 3 * VD].astype(BF16)


def project(chunks, weight, cos_table, sin_table):
    own_rows = chunks[0].shape[0]
    rows = 4 * own_rows
    heads = weight.shape[0] // 3
    tile = min(256, own_rows)
    out = pl.pallas_call(
        functools.partial(project_kernel, heads=heads, ends=chunk_ends(tile, chunks)),
        grid=(rows // tile,),
        in_specs=chunk_specs(tile, chunks)
        + [whole_spec(weight.shape), row_spec(tile, VD), row_spec(tile, VD)],
        out_specs=[row_spec(tile, D)]
        + [row_spec(tile, VD)] * heads
        + [row_spec(tile, 2 * VD)] * heads,
        out_shape=[jax.ShapeDtypeStruct((rows, D), BF16)]
        + [jax.ShapeDtypeStruct((rows, VD), BF16)] * heads
        + [jax.ShapeDtypeStruct((rows, 2 * VD), BF16)] * heads,
        compiler_params=pltpu.CompilerParams(vmem_limit_bytes=40 * MIB),
        cost_estimate=cost(
            2 * rows * weight.size,
            2 * (2 * rows * D + weight.size + rows * 3 * heads * VD),
        ),
        name="project",
    )(*chunks, weight, cos_table, sin_table)
    return out[0], out[1 : 1 + heads], out[1 + heads :]


def unproject_kernel(*refs, heads, per):
    dq_refs, own_refs, recv_refs = refs[:heads], refs[heads : 2 * heads], refs[2 * heads : 3 * heads]
    w_ref, cos_ref, sin_ref, gp_ref, keep_ref, mate_ref = refs[3 * heads :]
    mask = low_half_mask(gp_ref.shape[0])
    cos_table, sin_table = cos_ref[...], sin_ref[...]
    for head in range(heads):
        base = head * 3 * VD
        both = own_refs[head][...].astype(F32) + recv_refs[head][...].astype(F32)
        query = dq_refs[head][...].astype(F32)
        gp_ref[:, base : base + VD] = turn(query, cos_table, sin_table, mask, -1.0).astype(BF16)
        gp_ref[:, base + VD : base + 2 * VD] = turn(
            both[:, :VD], cos_table, sin_table, mask, -1.0
        ).astype(BF16)
        gp_ref[:, base + 2 * VD : base + 3 * VD] = both[:, VD:].astype(BF16)
    put_pair(dot(gp_ref[...], side_by_side(w_ref), NT).astype(BF16), per, keep_ref, mate_ref)


def unproject(dq, dkv_own, dkv_recv, weight, cos_table, sin_table):
    rows = dq[0].shape[0]
    heads = len(dq)
    tile = min(256, rows // 4)
    per = rows // 4 // tile
    return pl.pallas_call(
        functools.partial(unproject_kernel, heads=heads, per=per),
        grid=(rows // tile,),
        in_specs=[row_spec(tile, VD)] * heads
        + [row_spec(tile, 2 * VD)] * (2 * heads)
        + [whole_spec(weight.shape), row_spec(tile, VD), row_spec(tile, VD)],
        out_specs=[row_spec(tile, heads * 3 * VD)] + pair_specs(tile, per, D),
        out_shape=[jax.ShapeDtypeStruct((rows, heads * 3 * VD), BF16)] + pair_shapes(rows, D),
        compiler_params=pltpu.CompilerParams(vmem_limit_bytes=40 * MIB),
        cost_estimate=cost(
            2 * rows * weight.size,
            2 * (rows * D + weight.size + 9 * rows * heads * VD),
        ),
        name="unproject",
    )(*dq, *dkv_own, *dkv_recv, weight, cos_table, sin_table)


def output_kernel(*refs, heads, per):
    attn_refs = refs[:heads]
    w_ref, all_ref, keep_ref, mate_ref = refs[heads:]
    for head in range(heads):
        all_ref[:, head * VD : (head + 1) * VD] = attn_refs[head][...]
    put_pair(dot(all_ref[...], w_ref[...], NT).astype(BF16), per, keep_ref, mate_ref)


def output_projection(attn, weight):
    rows = attn[0].shape[0]
    heads = len(attn)
    tile = min(256, rows // 4)
    per = rows // 4 // tile
    return pl.pallas_call(
        functools.partial(output_kernel, heads=heads, per=per),
        grid=(rows // tile,),
        in_specs=[row_spec(tile, VD)] * heads + [whole_spec(weight.shape)],
        out_specs=[row_spec(tile, heads * VD)] + pair_specs(tile, per, D),
        out_shape=[jax.ShapeDtypeStruct((rows, heads * VD), BF16)] + pair_shapes(rows, D),
        compiler_params=pltpu.CompilerParams(vmem_limit_bytes=40 * MIB),
        cost_estimate=cost(
            2 * rows * D * weight.shape[1], 2 * (rows * D + weight.size + 2 * rows * heads * VD)
        ),
        name="output_projection",
    )(*attn, weight)


def gate_kernel(*refs, ends):
    count = len(ends)
    w_ref, x_ref, hidden_ref, by_gate_ref, by_up_ref = refs[count:]
    pick(refs[:count], ends, x_ref)
    width = hidden_ref.shape[1]
    step = min(512, width)
    x = x_ref[...]
    for base in range(0, width, step):
        cols = slice(base, base + step)
        gate = dot(x, w_ref[:, cols])
        up = dot(x, w_ref[:, width + base : width + base + step])
        share = jax.nn.sigmoid(gate)
        swish = gate * share
        hidden_ref[:, cols] = (swish * up).astype(BF16)
        by_gate_ref[:, cols] = (up * share * (1.0 + gate * (1.0 - share))).astype(BF16)
        by_up_ref[:, cols] = swish.astype(BF16)


def gate_up(chunks, weights, width):
    own_rows = chunks[0].shape[0]
    rows = 4 * own_rows
    tile = min(256, own_rows)
    return pl.pallas_call(
        functools.partial(gate_kernel, ends=chunk_ends(tile, chunks)),
        grid=(rows // tile,),
        in_specs=chunk_specs(tile, chunks) + [columns_spec(D, 2 * width, 0)],
        out_specs=[row_spec(tile, D)] + [row_spec(tile, width)] * 3,
        out_shape=[jax.ShapeDtypeStruct((rows, D), BF16)]
        + [jax.ShapeDtypeStruct((rows, width), BF16)] * 3,
        compiler_params=pltpu.CompilerParams(vmem_limit_bytes=60 * MIB),
        cost_estimate=cost(4 * rows * D * width, 2 * (2 * rows * D + 2 * D * width + 3 * rows * width)),
        name="gate_up",
    )(*chunks, weights)


def feed_kernel(*refs, ends, per):
    count = len(ends)
    hidden_ref, by_gate_ref, by_up_ref, down_ref, inner_ref = refs[count : count + 5]
    cot_ref, grad_ref, ffn_keep, ffn_mate, mid_keep, mid_mate = refs[count + 5 :]
    pick(refs[:count], ends, cot_ref)
    width = hidden_ref.shape[1]
    grad_hidden = dot(cot_ref[...], down_ref[...])
    grad_ref[:, :width] = (grad_hidden * by_gate_ref[...].astype(F32)).astype(BF16)
    grad_ref[:, width:] = (grad_hidden * by_up_ref[...].astype(F32)).astype(BF16)
    put_pair(dot(hidden_ref[...], down_ref[...], NT).astype(BF16), per, ffn_keep, ffn_mate)
    put_pair(dot(grad_ref[...], inner_ref[...], NT).astype(BF16), per, mid_keep, mid_mate)


def feed(chunks, hidden, by_gate, by_up, weights):
    own_rows = chunks[0].shape[0]
    rows = 4 * own_rows
    width = hidden.shape[1]
    tile = min(256, own_rows)
    per = own_rows // tile
    return pl.pallas_call(
        functools.partial(feed_kernel, ends=chunk_ends(tile, chunks), per=per),
        grid=(rows // tile,),
        in_specs=chunk_specs(tile, chunks)
        + [row_spec(tile, width)] * 3
        + [columns_spec(D, width, 2), columns_spec(D, 2 * width, 0)],
        out_specs=[row_spec(tile, D), row_spec(tile, 2 * width)]
        + pair_specs(tile, per, D)
        + pair_specs(tile, per, D),
        out_shape=[
            jax.ShapeDtypeStruct((rows, D), BF16),
            jax.ShapeDtypeStruct((rows, 2 * width), BF16),
        ]
        + pair_shapes(rows, D)
        + pair_shapes(rows, D),
        compiler_params=pltpu.CompilerParams(vmem_limit_bytes=60 * MIB),
        cost_estimate=cost(8 * rows * D * width, 2 * (4 * rows * D + 3 * D * width + 5 * rows * width)),
        name="feed",
    )(*chunks, hidden, by_gate, by_up, weights, weights)


class Plan:
    def __init__(self, own_rows, block_len, prev_rows, ndoc):
        self.own_rows = own_rows
        self.block_len = block_len
        self.prev_rows = prev_rows
        self.ndoc = ndoc
        self.bq = min(256, own_rows)
        self.bk = min(512, own_rows)
        self.total = prev_rows + block_len

    def doc_start(self, info, pos):
        start = jnp.zeros_like(pos)
        for item in range(self.ndoc):
            start = jnp.where(pos >= info[2 + item], info[2 + item], start)
        return start

    def query_start(self, info, index):
        per = self.own_rows // self.bq
        chunk = (index // per) ^ info[0]
        return info[1] * self.block_len + chunk * self.own_rows + (index % per) * self.bq

    def key_row(self, info, index):
        per = self.own_rows // self.bk
        blocks = self.block_len // self.bk
        owner = index // blocks
        local = index % blocks
        inside = (((local // per) ^ info[0]) * per + local % per) * self.bk
        base = jnp.where(owner == info[1], self.prev_rows, owner * self.block_len)
        return pl.multiple_of(base + inside, self.bk)

    def ranges(self, info, start):
        last = start + self.bq - 1
        low = self.doc_start(info, start) // self.bk
        high = last // self.bk + 1
        open_from = (self.doc_start(info, last) + self.bk - 1) // self.bk
        first = jnp.minimum(jnp.maximum(open_from, low), high)
        until = jnp.maximum(first, jnp.minimum((start + 1) // self.bk, high))
        return low, first, until, high


def in_groups(low, high, size, visit):
    count = (high - low) // size

    @pl.loop(0, count)
    def _(group):
        visit(*[low + group * size + item for item in range(size)])

    if size > 1:

        @pl.loop(low + count * size, high)
        def _(index):
            visit(index)


def split_halves(q):
    lane = lax.broadcasted_iota(jnp.int32, q.shape, 1)
    zero = jnp.zeros_like(q)
    return jnp.concatenate([jnp.where(lane < HD, q, zero), jnp.where(lane >= HD, q, zero)], axis=0)


def in_lanes(value):
    high = value.astype(BF16)
    rest = value - high.astype(F32)
    middle = rest.astype(BF16)
    low = (rest - middle.astype(F32)).astype(BF16)
    lane = lax.broadcasted_iota(jnp.int32, value.shape, 1)
    zero = jnp.zeros_like(high)
    return jnp.where(
        lane == 0, high, jnp.where(lane == 1, middle, jnp.where(lane == 2, low, zero))
    )


def load_keys(plan, info, own_ref, prev_ref, kv_sc):
    @pl.when(pl.program_id(0) == 0)
    def _():
        kv_sc[plan.prev_rows :, :] = own_ref[...]

        @pl.when(info[1] > 0)
        def _():
            kv_sc[: plan.prev_rows, :] = prev_ref[...]


def forward_kernel(
    info,
    lam_ref,
    gain_ref,
    q_ref,
    own_ref,
    prev_ref,
    attn_ref,
    first_ref,
    second_ref,
    lse_ref,
    kv_sc,
    m_sc,
    l_sc,
    acc_sc,
    *,
    plan,
):
    bq, bk = plan.bq, plan.bk
    load_keys(plan, info, own_ref, prev_ref, kv_sc)
    start = plan.query_start(info, pl.program_id(0))
    q2 = split_halves(q_ref[...])
    m_sc[...] = jnp.full_like(m_sc, NEG)
    l_sc[...] = jnp.zeros_like(l_sc)
    acc_sc[...] = jnp.zeros_like(acc_sc)
    low, first, until, high = plan.ranges(info, start)

    def visit(index, masked):
        row = plan.key_row(info, index)
        key = kv_sc[pl.ds(row, bk), :VD]
        value = kv_sc[pl.ds(row, bk), VD:]
        scores = dot(q2, key, NT)
        if masked:
            query_pos = start + lax.broadcasted_iota(jnp.int32, (bq, 1), 0)
            begin = plan.doc_start(info, query_pos)
            key_pos = index * bk + lax.broadcasted_iota(jnp.int32, (bq, bk), 1)
            keep = (key_pos <= query_pos) & (key_pos >= begin)
            scores = jnp.concatenate(
                [jnp.where(keep, scores[:bq], NEG), jnp.where(keep, scores[bq:], NEG)], axis=0
            )
        before = m_sc[...]
        after = jnp.maximum(before, jnp.max(scores, axis=1, keepdims=True))
        weights = jnp.exp(scores - jnp.tile(after, (1, bk // VD)))
        factor = jnp.exp(before - after)
        m_sc[...] = after
        l_sc[...] = l_sc[...] * factor + jnp.sum(weights, axis=1, keepdims=True)
        acc_sc[...] = acc_sc[...] * factor + dot(weights.astype(BF16), value)

    @pl.loop(low, first)
    def _(index):
        visit(index, True)

    @pl.loop(first, until)
    def _(index):
        visit(index, False)

    @pl.loop(until, high)
    def _(index):
        visit(index, True)

    total = l_sc[...]
    maps = acc_sc[...] * (1.0 / total)
    first_map, second_map = maps[:bq], maps[bq:]
    first_ref[...] = first_map
    second_ref[...] = second_map
    difference = first_map - lam_ref[0] * second_map
    scaling = lax.rsqrt(jnp.mean(difference * difference, axis=1, keepdims=True) + EPS)
    attn_ref[...] = (difference * scaling * gain_ref[...]).astype(BF16)
    lanes = in_lanes(-(m_sc[...] + jnp.log(total)))
    lse_ref[:, :VD] = lanes[:bq]
    lse_ref[:, VD:] = lanes[bq:]


def attention_cost(plan, per_pair, extra=0):
    pairs = plan.block_len * plan.block_len * 5 // 8
    return cost(pairs * per_pair + extra, plan.block_len * VD * 32, 2 * pairs)


def attend_forward(plan, info, lam, gain, q, kv_own, kv_prev):
    rows, bq = plan.block_len, plan.bq
    grid_spec = pltpu.PrefetchScalarGridSpec(
        num_scalar_prefetch=1,
        grid=(rows // bq,),
        in_specs=[
            pl.BlockSpec(memory_space=pltpu.SMEM),
            whole_spec((1, VD)),
            row_spec(bq, VD),
            whole_spec((rows, 2 * VD)),
            whole_spec((plan.prev_rows, 2 * VD)),
        ],
        out_specs=[row_spec(bq, VD)] * 3 + [row_spec(bq, 2 * VD)],
        scratch_shapes=[
            pltpu.VMEM((plan.total, 2 * VD), BF16),
            pltpu.VMEM((2 * bq, VD), F32),
            pltpu.VMEM((2 * bq, VD), F32),
            pltpu.VMEM((2 * bq, VD), F32),
        ],
    )
    return pl.pallas_call(
        functools.partial(forward_kernel, plan=plan),
        grid_spec=grid_spec,
        out_shape=[
            jax.ShapeDtypeStruct((rows, VD), BF16),
            jax.ShapeDtypeStruct((rows, VD), F32),
            jax.ShapeDtypeStruct((rows, VD), F32),
            jax.ShapeDtypeStruct((rows, 2 * VD), BF16),
        ],
        compiler_params=pltpu.CompilerParams(vmem_limit_bytes=60 * MIB),
        cost_estimate=attention_cost(plan, 6 * VD),
        name="attend_forward",
    )(info, lam, gain, q, kv_own, kv_prev)


def difference_kernel(lam_ref, gain_ref, w_ref, *refs, heads, ends):
    count = len(ends)
    chunks, refs = refs[:count], refs[count:]
    first_refs, second_refs, refs = refs[:heads], refs[heads : 2 * heads], refs[2 * heads :]
    gm_ref, sums_ref, grad_refs = refs[0], refs[1], refs[2:]
    lam = lam_ref[0]

    @pl.when(pl.program_id(0) == 0)
    def _():
        sums_ref[...] = jnp.zeros_like(sums_ref)

    pick(chunks, ends, gm_ref)
    upstream_all = dot(gm_ref[...], w_ref[...])
    for head in range(heads):
        upstream = upstream_all[:, head * VD : (head + 1) * VD]
        first_map, second_map = first_refs[head][...], second_refs[head][...]
        difference = first_map - lam * second_map
        scaling = lax.rsqrt(jnp.mean(difference * difference, axis=1, keepdims=True) + EPS)
        normal = difference * scaling
        weighted = upstream * gain_ref[...]
        inner_mean = jnp.mean(weighted * normal, axis=1, keepdims=True)
        grad = (scaling * (weighted - normal * inner_mean)).astype(BF16)
        grad_wide = grad.astype(F32)
        first_product, second_product = grad_wide * first_map, grad_wide * second_map
        sums_ref[0:1, :] += jnp.sum(upstream * normal, axis=0, keepdims=True)
        sums_ref[1:2, :] += jnp.sum(second_product, axis=0, keepdims=True)
        out = grad_refs[head]
        out[:, :VD] = grad
        for item, product in enumerate((first_product, second_product)):
            total = jnp.sum(product, axis=1, keepdims=True)
            out[:, (item + 1) * VD : (item + 2) * VD] = in_lanes(
                jnp.broadcast_to(-total, product.shape)
            )


def difference_grads(lam, gain, weight, gm, first, second):
    own_rows = gm[0].shape[0]
    rows = 4 * own_rows
    heads = len(first)
    tile = min(256, own_rows)
    return pl.pallas_call(
        functools.partial(difference_kernel, heads=heads, ends=chunk_ends(tile, gm)),
        grid=(rows // tile,),
        in_specs=[pl.BlockSpec(memory_space=pltpu.SMEM), whole_spec((1, VD)), whole_spec(weight.shape)]
        + chunk_specs(tile, gm)
        + [row_spec(tile, VD)] * (2 * heads),
        out_specs=[row_spec(tile, D), whole_spec((8, VD))] + [row_spec(tile, 3 * VD)] * heads,
        out_shape=[jax.ShapeDtypeStruct((rows, D), BF16), jax.ShapeDtypeStruct((8, VD), F32)]
        + [jax.ShapeDtypeStruct((rows, 3 * VD), BF16)] * heads,
        compiler_params=pltpu.CompilerParams(vmem_limit_bytes=60 * MIB),
        cost_estimate=cost(2 * rows * D * heads * VD, 4 * rows * D + 14 * rows * heads * VD),
        name="difference_grads",
    )(lam, gain, weight, *gm, *first, *second)


def backward_kernel(
    info,
    lam_ref,
    q_ref,
    own_ref,
    prev_ref,
    lse_ref,
    grad_ref,
    dq_ref,
    dkv_own_ref,
    dkv_prev_ref,
    kv_sc,
    dk_sc,
    dv_sc,
    dqt_sc,
    *,
    plan,
):
    bq, bk = plan.bq, plan.bk
    step = pl.program_id(0)
    lam = lam_ref[0]

    @pl.when(step == 0)
    def _():
        lane = lax.broadcasted_iota(jnp.int32, (bk, VD), 1)
        ones = jnp.where(lane < 3, 1.0, 0.0).astype(BF16)

        def fill(source, base, rows):
            for start in range(0, rows, bk):
                to = slice(base + start, base + start + bk)
                kv_sc[to, :VD] = source[start : start + bk, :VD]
                kv_sc[to, VD : 2 * VD] = ones
                kv_sc[to, 2 * VD :] = source[start : start + bk, VD:]

        fill(own_ref, plan.prev_rows, plan.block_len)

        @pl.when(info[1] > 0)
        def _():
            fill(prev_ref, 0, plan.prev_rows)

        dk_sc[...] = jnp.zeros_like(dk_sc)
        dv_sc[...] = jnp.zeros_like(dv_sc)

    grad = grad_ref[:, :VD]
    start = plan.query_start(info, step)
    q2 = split_halves(q_ref[...])
    q_wide = jnp.concatenate(
        [q2, jnp.concatenate([lse_ref[:, :VD], lse_ref[:, VD:]], axis=0)], axis=1
    )
    ones = jnp.ones((8, VD), BF16)
    delta_first = dot(ones, grad_ref[:, VD : 2 * VD], NT)[0:1]
    delta_second = dot(ones, grad_ref[:, 2 * VD :], NT)[0:1]
    dqt_sc[...] = jnp.zeros_like(dqt_sc)
    low, _, _, high = plan.ranges(info, start)

    query_pos = start + lax.broadcasted_iota(jnp.int32, (1, bq), 1)
    begin = plan.doc_start(info, query_pos)

    def visit(*indices):
        results = []
        for index in indices:
            row = plan.key_row(info, index)
            key = kv_sc[pl.ds(row, bk), :VD]
            prob = jnp.exp(dot(kv_sc[pl.ds(row, bk), : 2 * VD], q_wide, NT))
            base = dot(kv_sc[pl.ds(row, bk), 2 * VD :], grad, NT)
            key_pos = index * bk + lax.broadcasted_iota(jnp.int32, (bk, bq), 0)
            keep = (key_pos <= query_pos) & (key_pos >= begin)
            prob_first = jnp.where(keep, prob[:, :bq], 0.0)
            prob_second = jnp.where(keep, prob[:, bq:], 0.0)
            raw = jnp.concatenate(
                [
                    (prob_first * (base + delta_first)).astype(BF16),
                    (prob_second * (base + delta_second)).astype(BF16),
                ],
                axis=1,
            )
            value_grad = dot((prob_first - lam * prob_second).astype(BF16), grad)
            results.append((row, value_grad, dot(raw, q2), dot(key, raw, TN)))
        for row, value_grad, key_grad, query_grad in results:
            dv_sc[pl.ds(row, bk), :] += value_grad
            dk_sc[pl.ds(row, bk), :] += key_grad
        dqt_sc[...] += sum(result[3] for result in results)

    in_groups(low, high, 2, visit)

    dq_t = jnp.concatenate([dqt_sc[:HD, :bq], -lam * dqt_sc[HD:, bq:]], axis=0) * SCALE
    dq_ref[...] = dq_t.T.astype(BF16)

    @pl.when(step == pl.num_programs(0) - 1)
    def _():
        lane = lax.broadcasted_iota(jnp.int32, (1, VD), 1)
        side = jnp.where(lane < HD, 1.0, -lam)
        dkv_own_ref[:, :VD] = (dk_sc[plan.prev_rows :, :] * side).astype(BF16)
        dkv_own_ref[:, VD:] = dv_sc[plan.prev_rows :, :].astype(BF16)
        dkv_prev_ref[:, :VD] = (dk_sc[: plan.prev_rows, :] * side).astype(BF16)
        dkv_prev_ref[:, VD:] = dv_sc[: plan.prev_rows, :].astype(BF16)


def attend_backward(plan, info, lam, q, kv_own, kv_prev, lse, grad):
    rows, bq = plan.block_len, plan.bq
    grid_spec = pltpu.PrefetchScalarGridSpec(
        num_scalar_prefetch=1,
        grid=(rows // bq,),
        in_specs=[
            pl.BlockSpec(memory_space=pltpu.SMEM),
            row_spec(bq, VD),
            whole_spec((rows, 2 * VD)),
            whole_spec((plan.prev_rows, 2 * VD)),
            row_spec(bq, 2 * VD),
            row_spec(bq, 3 * VD),
        ],
        out_specs=[
            row_spec(bq, VD),
            whole_spec((rows, 2 * VD)),
            whole_spec((plan.prev_rows, 2 * VD)),
        ],
        scratch_shapes=[
            pltpu.VMEM((plan.total, 3 * VD), BF16),
            pltpu.VMEM((plan.total, VD), F32),
            pltpu.VMEM((plan.total, VD), F32),
            pltpu.VMEM((VD, 2 * bq), F32),
        ],
    )
    return pl.pallas_call(
        functools.partial(backward_kernel, plan=plan),
        grid_spec=grid_spec,
        out_shape=[
            jax.ShapeDtypeStruct((rows, VD), BF16),
            jax.ShapeDtypeStruct((rows, 2 * VD), BF16),
            jax.ShapeDtypeStruct((plan.prev_rows, 2 * VD), BF16),
        ],
        compiler_params=pltpu.CompilerParams(vmem_limit_bytes=60 * MIB),
        cost_estimate=attention_cost(plan, 16 * VD),
        name="attend_backward",
    )(info, lam, q, kv_own, kv_prev, lse, grad)


def norm_forward(values, gain_vec):
    scaling = lax.rsqrt(jnp.mean(values * values, axis=-1, keepdims=True) + EPS)
    return (values * scaling * gain_vec, scaling)


def norm_backward(values, scaling, gain_vec, upstream):
    normal = values * scaling
    weighted = upstream * gain_vec
    inner_mean = jnp.mean(weighted * normal, axis=-1, keepdims=True)
    return (scaling * (weighted - normal * inner_mean), jnp.sum(upstream * normal, axis=0))


def adamw(parameter, momentum, variance, gradient, learn_rate, decay_rate):
    momentum = BETA1 * momentum + (1.0 - BETA1) * gradient
    variance = BETA2 * variance + (1.0 - BETA2) * gradient * gradient
    corrected = momentum / (1.0 - BETA1**STEP)
    spread = jnp.sqrt(variance / (1.0 - BETA2**STEP))
    return (
        parameter - learn_rate * (corrected / (spread + ADAM_EPS) + decay_rate * parameter),
        momentum,
        variance,
    )


def send_keys(kv, ctx_count):
    if ctx_count == 2:
        return lax.ppermute(kv, "ctx", [(0, 1)])
    return lax.all_gather(kv, "ctx", axis=0, tiled=True)


def return_keys(grads, ctx_count):
    if ctx_count == 2:
        return lax.ppermute(grads, "ctx", [(1, 0)])
    return lax.psum_scatter(grads, "ctx", scatter_dimension=0, tiled=True)


def scatter_weight(grad, *others):
    grad = after(grad.astype(BF16), *others)
    return lax.psum_scatter(grad, "dp", scatter_dimension=0, tiled=True)


def sum_blocks(share, ctx_count):
    if ctx_count == 2:
        other = lax.ppermute(share, "ctx", [(0, 1), (1, 0)])
        return share.astype(F32) + other.astype(F32)
    return lax.psum(share, "ctx").astype(F32)


def on_device(
    tokens,
    cotangent,
    doc_lengths,
    qkv_weight,
    out_weight,
    inner_weight,
    down_weight,
    norm_gains,
    head_gain,
    lambdas,
    qkv_momentum,
    out_momentum,
    inner_momentum,
    down_momentum,
    norm_momentum,
    head_momentum,
    lambda_momentum,
    qkv_variance,
    out_variance,
    inner_variance,
    down_variance,
    norm_variance,
    head_variance,
    lambda_variance,
):
    micro_count, own_rows, _ = tokens.shape
    head_count = lax.axis_size("head")
    ctx_count = lax.axis_size("ctx")
    block_len = own_rows * head_count
    seq_len = block_len * ctx_count
    ctx_index = lax.axis_index("ctx")
    head_index = lax.axis_index("head")
    local_heads = qkv_weight.shape[1]
    ff_local = inner_weight.shape[2]
    ndoc = doc_lengths.shape[1]
    plan = Plan(own_rows, block_len, block_len if ctx_count == 2 else seq_len, ndoc)

    def gather_weight(shard):
        return lax.all_gather(shard.astype(BF16), "dp", axis=0, tiled=True)

    def by_part(array):
        return array.transpose(1, 2, 0, 3)

    qkv_low = lax.all_gather(
        row_major(by_part(qkv_weight).astype(BF16)).reshape(local_heads * 3, -1, VD),
        "dp",
        axis=1,
        tiled=True,
    )
    out_t = gather_weight(row_major(out_weight.astype(BF16).reshape(local_heads * VD, -1).T))
    feed_low = gather_weight(
        jnp.concatenate(
            [
                inner_weight.reshape(-1, 2 * ff_local).astype(BF16),
                row_major(down_weight.astype(BF16).T),
            ],
            axis=1,
        )
    )

    first_exp = jnp.exp(jnp.sum(lambdas[0] * lambdas[1]))
    second_exp = jnp.exp(jnp.sum(lambdas[2] * lambdas[3]))
    lambda_value = first_exp - second_exp + LAMBDA_INIT
    lam = lambda_value.reshape(1)
    head_scale = (head_gain * (1.0 - LAMBDA_INIT)).reshape(1, VD)

    chunk = jnp.arange(block_len, dtype=jnp.int32) // own_rows
    position = (
        ctx_index * block_len
        + (chunk ^ head_index) * own_rows
        + jnp.arange(block_len, dtype=jnp.int32) % own_rows
    )
    frequency = ROPE_BASE ** (
        -(jnp.arange(VD, dtype=jnp.int32) % (HD // 2)).astype(F32) / (HD // 2)
    )

    def info_of(micro):
        bounds = jnp.cumsum(doc_lengths[micro], dtype=jnp.int32)
        return jnp.concatenate([jnp.stack([head_index, ctx_index]).astype(jnp.int32), bounds])

    micros = range(micro_count)
    heads = range(local_heads)
    infos = [info_of(m) for m in micros]
    own, normed_own, normed, cot_own = [], [], [], []
    for m in micros:
        rows, cot_rows = tokens[m], cotangent[m]
        if m > 0:
            rows = after(rows, normed[0].own)
        own.append(rows.astype(F32))
        normed_own.append(norm_forward(own[m], norm_gains[0]))
        cot_own.append(cot_rows)
        normed.append(Gather(normed_own[m][0].astype(BF16), 2 if m else 1))
    position = after(position, normed[-1].own)
    phases = position.astype(F32)[:, None] * frequency[None, :]
    cos_table, sin_table = jnp.cos(phases), jnp.sin(phases)

    normed_all, q, kv, kv_prev, cot = [], [], [], [], []
    for m in micros:
        pieces = normed[m].pieces()
        if m == 0:
            pieces = after(pieces, normed[1].far[0])
        result = project(pieces, qkv_low, cos_table, sin_table)
        if m == 0:
            result = together(result, *slots_of(normed[1].far, 1))
            cot.append(Gather(after(cot_own[0], qkv_low, normed[1].far[-1])))
        else:
            cot.append(Gather(after(cot_own[1], result[2], *cot[0].far), 2))
        normed_all.append(result[0])
        q.append(result[1])
        kv.append(result[2])
        kv_prev.append([send_keys(result[2][h], ctx_count) for h in heads])

    def attend(m, h, before, beside):
        out = attend_forward(
            plan, infos[m], lam, head_scale, after(q[m][h], *before), kv[m][h], kv_prev[m][h]
        )
        return together(out, *beside)

    mid = []

    def finish_attention(m):
        middle = own[m] + attended[m].value()
        value, scaling = norm_forward(middle, norm_gains[1])
        mid.append((middle, scaling, Gather(value.astype(BF16), 2)))

    maps, attn_all, attended = [], [], []
    for m in micros:
        outs = []
        for h in heads:
            if m == 0:
                before = [out_t, kv[-1]] if h == 0 else [outs[-1]]
                beside = [
                    slots_of(cot[0].far, 0),
                    slots_of(cot[1].far, 0),
                    slots_of(cot[1].far, 1),
                ][h]
            elif h == 0:
                before = [*attended[0].sent, *cot[0].pieces(), *cot[1].pieces()]
                beside = slots_of(attended[0].across) + slots_of(kv_prev[m], 1)
            else:
                before = [outs[-1], mid[0][2].own]
                beside = slots_of(mid[0][2].far, h - 1) + slots_of(kv_prev[m], h + 1)
            outs.append(attend(m, h, before, beside))
            if m > 0 and h == 0:
                finish_attention(0)
        maps.append([out[1:] for out in outs])
        result = output_projection([out[0] for out in outs], out_t)
        if m == 0:
            result = together(result, *slots_of(kv_prev[1], 0))
        attn_all.append(result[0])
        attended.append(Reduce(*result[1:], 2 if m else 1))

    grad_middle, gm, gain_mid = [], [], []

    def finish_feed(m, reduced):
        middle, scaling, _ = mid[m]
        grad_norm, part = norm_backward(middle, scaling, norm_gains[1], reduced.value())
        grad_middle.append((cot_own[m].astype(F32) + grad_norm).astype(BF16))
        gm.append(Gather(grad_middle[m], 2 if m else 1))
        gain_mid.append(part)

    def weight_grad(left, right, before, beside, total=None):
        result = dot(after(left, *before), right, TN)
        if total is not None:
            result = (total + result).astype(BF16)
        return together(result, *beside)

    first_gates = gate_up(after(mid[0][2].pieces(), *attended[1].sent), feed_low, ff_local)
    first_gates = together(first_gates, *slots_of(attended[1].across, 0))
    first_feed = feed(cot[0].pieces(), *first_gates[1:], feed_low)
    first_feed = together(first_feed, *slots_of(attended[1].across, 1))
    finish_attention(1)
    reduced_mid = [Reduce(*first_feed[4:])]
    grad_inner = weight_grad(
        first_gates[0],
        first_feed[1],
        [mid[1][2].own, *reduced_mid[0].sent],
        slots_of(mid[1][2].far, 0),
    )
    grad_down = weight_grad(
        first_feed[0], first_gates[1], [grad_inner], slots_of(mid[1][2].far, 1)
    )
    reduced_mid[0].send(*mid[1][2].far)
    second_gates = gate_up(after(mid[1][2].pieces(), grad_down), feed_low, ff_local)
    second_gates = together(second_gates, *slots_of(reduced_mid[0].across))
    finish_feed(0, reduced_mid[0])
    second_feed = feed(after(cot[1].pieces(), gm[0].own), *second_gates[1:], feed_low)
    second_feed = together(second_feed, *slots_of(gm[0].far))
    reduced_mid.append(Reduce(*second_feed[4:], 2))
    grad_inner = weight_grad(
        second_gates[0],
        second_feed[1],
        reduced_mid[1].sent,
        slots_of(reduced_mid[1].across, 0),
        grad_inner,
    )
    grad_down = weight_grad(
        second_feed[0],
        second_gates[1],
        [grad_inner],
        slots_of(reduced_mid[1].across, 1),
        grad_down,
    )
    feed_grad = jnp.concatenate([grad_inner, grad_down], axis=1)
    feed_part = scatter_weight(row_major(feed_grad))
    finish_feed(1, reduced_mid[1])
    ffn_pairs = [first_feed[2:4], second_feed[2:4]]

    dqs, dkvs, recvs, gm_alls, grads, sums = [], [], [], [], [], 0.0

    def start_back(m, before, beside):
        out = difference_grads(
            lam,
            head_scale,
            out_t,
            after(gm[m].pieces(), *before),
            [part[0] for part in maps[m]],
            [part[1] for part in maps[m]],
        )
        out = together(out, *beside)
        gm_alls.append(out[0])
        grads.append(out[2:])
        dqs.append([])
        dkvs.append([])
        recvs.append([])
        return out[1]

    def attend_back(m, h, before, beside):
        out = attend_backward(
            plan,
            infos[m],
            lam,
            after(q[m][h], *before),
            kv[m][h],
            kv_prev[m][h],
            maps[m][h][2],
            grads[m][h],
        )
        out = together(out, *beside)
        dqs[m].append(out[0])
        dkvs[m].append(out[1])
        recvs[m].append(return_keys(out[2], ctx_count))

    def unprojected(m, before, beside):
        out = unproject(after(dqs[m], *before), dkvs[m], recvs[m], qkv_low, cos_table, sin_table)
        return together(out, *beside)

    def ffn_sum(m, before):
        keep, mate = ffn_pairs[m]
        return Reduce(keep, after(mate, *before), 2)

    sums = start_back(0, [gm[1].own, feed_grad], [])
    attend_back(0, 0, [], slots_of(gm[1].far, 0))
    attend_back(0, 1, [dqs[0][-1]], slots_of(gm[1].far, 1) + slots_of(recvs[0], 0))
    ffn = [ffn_sum(0, [dqs[0][-1]])]
    ffn.append(ffn_sum(1, [dqs[0][-1]]))
    attend_back(
        0,
        2,
        [*ffn[0].sent, *gm[1].pieces()],
        slots_of(ffn[0].across, 0) + slots_of(recvs[0], 1),
    )
    sums = sums + start_back(1, [dqs[0][-1]], slots_of(ffn[0].across, 1))
    grad_out = weight_grad(gm_alls[0], attn_all[0], [grads[1][0]], [])
    grad_out = weight_grad(gm_alls[1], attn_all[1], [grad_out], [], grad_out)
    attend_back(
        1, 0, [*ffn[1].sent, grad_out], slots_of(ffn[1].across, 0) + slots_of(recvs[0], 2)
    )
    back = [unprojected(0, [dqs[1][-1]], slots_of(ffn[1].across, 1))]
    reduced_in = [Reduce(*back[0][1:], 2)]
    attend_back(
        1,
        1,
        [back[0][0], *reduced_in[0].sent],
        slots_of(reduced_in[0].across, 0) + slots_of(recvs[1], 0),
    )
    attend_back(1, 2, [dqs[1][-1]], slots_of(reduced_in[0].across, 1) + slots_of(recvs[1], 1))
    out_part = scatter_weight(row_major(grad_out), feed_part)
    grad_qkv = weight_grad(normed_all[0], back[0][0], [dqs[1][-1], out_part], slots_of(recvs[1], 2))
    back.append(unprojected(1, [grad_qkv], []))
    reduced_in.append(Reduce(*back[1][1:], 2))
    grad_qkv = weight_grad(
        normed_all[1],
        back[1][0],
        reduced_in[1].sent,
        slots_of(reduced_in[1].across, 0),
        grad_qkv,
    )
    last_part = scatter_weight(row_major(grad_qkv), out_part)
    out_share = sum_blocks(out_part, ctx_count)
    feed_share = row_major(sum_blocks(feed_part, ctx_count))
    inner_share = feed_share[:, : 2 * ff_local]
    down_share = feed_share[:, 2 * ff_local :]
    gain_mid = gain_mid[0] + gain_mid[1]
    outputs = [(mid[m][0] + ffn[m].value()).astype(BF16) for m in micros]

    gain_in = 0.0
    input_grads = []
    for m in micros:
        grad_in_norm, gain_part = norm_backward(
            own[m], normed_own[m][1], norm_gains[0], reduced_in[m].value()
        )
        gain_in = gain_in + gain_part
        input_grads.append((grad_middle[m].astype(F32) + grad_in_norm).astype(BF16))

    lambda_acc = -jnp.sum(sums[1])
    lambda_local = jnp.stack(
        [
            lambda_acc * first_exp * lambdas[1],
            lambda_acc * first_exp * lambdas[0],
            -lambda_acc * second_exp * lambdas[3],
            -lambda_acc * second_exp * lambdas[2],
        ]
    )
    small = butterfly(
        jnp.concatenate(
            [
                gain_in.reshape(-1, VD),
                gain_mid.reshape(-1, VD),
                sums[:1] * (1.0 - LAMBDA_INIT),
                lambda_local.reshape(-1, VD),
            ]
        )
    )
    per = D // VD
    norm_grad = small[: 2 * per].reshape(2, D)
    head_grad = small[2 * per]
    lambda_grad = small[2 * per + 1 :].reshape(lambdas.shape)

    feed_states = [
        adamw(
            inner_weight,
            inner_momentum,
            inner_variance,
            row_major(inner_share.reshape(inner_weight.shape)),
            0.5 * D ** (-0.5),
            DECAY,
        ),
        adamw(
            down_weight, down_momentum, down_variance, row_major(down_share.T), 0.5 * FF ** (-0.5), DECAY
        ),
    ]
    out_state = adamw(
        out_weight,
        out_momentum,
        out_variance,
        row_major(out_share.T).reshape(out_weight.shape),
        0.5 * (H * VD) ** (-0.5),
        DECAY,
    )
    output, input_grad = jnp.stack(outputs), jnp.stack(input_grads)
    qkv_share = sum_blocks(
        after(last_part, feed_states, out_state, output, input_grad, small), ctx_count
    )
    qkv_share = row_major(
        row_major(qkv_share).reshape(-1, local_heads, 3, VD).transpose(1, 2, 0, 3)
    )
    qkv_state = adamw(
        by_part(qkv_weight),
        by_part(qkv_momentum),
        by_part(qkv_variance),
        qkv_share,
        0.5 * D ** (-0.5),
        DECAY,
    )

    states = [
        tuple(part.transpose(2, 0, 1, 3) for part in qkv_state),
        out_state,
        *feed_states,
        adamw(norm_gains, norm_momentum, norm_variance, norm_grad, 0.4, 0.0),
        adamw(head_gain, head_momentum, head_variance, head_grad, 0.4, 0.0),
        adamw(lambdas, lambda_momentum, lambda_variance, lambda_grad, 0.1, 0.0),
    ]
    return (
        output,
        input_grad,
        *[state[0] for state in states],
        *[state[1] for state in states],
        *[state[2] for state in states],
    )


def solution(mesh):
    activation = P("dp", ("ctx", "head"), None)
    big = (P("dp", "head", None, None), P("head", None, "dp"), P("dp", None, "head"), P("head", "dp"))
    state = big + (P(), P(), P())
    return jax.shard_map(
        on_device,
        mesh=mesh,
        in_specs=(activation, activation, P("dp", None)) + state * 3,
        out_specs=(activation, activation) + state * 3,
        check_vma=False,
    )
```

```python
import functools

import jax
import jax.numpy as jnp
from jax import lax
from jax.experimental import pallas as pl
from jax.experimental.layout import Layout, with_layout_constraint
from jax.experimental.pallas import tpu as pltpu
from jax.sharding import PartitionSpec as P

D = 1536
FF = 4096
H = 12
HD = 64
STEP = 10
VD = 128


EPS = 1e-05
LAMBDA_INIT = 0.2
SCALE = 0.125
NEG = -1e30
BETA1 = 0.9
BETA2 = 0.999
ADAM_EPS = 1e-08
DECAY = 0.1
ROPE_BASE = 10000.0

MIB = 1 << 20
NT = (((1,), (1,)), ((), ()))
TN = (((0,), (0,)), ((), ()))
F32 = jnp.float32
BF16 = jnp.bfloat16
MESH = pl.DeviceIdType.MESH


def dot(left, right, dims=(((1,), (0,)), ((), ())), **kw):
    return lax.dot_general(left, right, dims, preferred_element_type=F32, **kw)


def swap(array, bit):
    size = lax.axis_size("head")
    return lax.ppermute(array, "head", [(i, i ^ bit) for i in range(size)])


def split_rows(array, count):
    size = array.shape[0] // count
    return [array[i * size : (i + 1) * size] for i in range(count)]


class Gather:
    def __init__(self, own, parts=1):
        parts = parts if own.shape[0] % 512 == 0 else 1
        self.own = own
        self.mate = swap(own, 1)
        self.far = [swap(part, 2) for part in split_rows(own, parts)]
        self.far_mate = None

    def pieces(self):
        if self.far_mate is None:
            self.far_mate = [swap(part, 1) for part in self.far]
        return [self.own, self.mate, *self.far, *self.far_mate]

    def mate_first(self):
        own, mate, *rest = self.pieces()
        count = len(self.far)
        return [mate, *rest[count:], own, *rest[:count]]


class Reduce:
    def __init__(self, keep, received, parts=1):
        rows = keep.shape[0] // 2
        parts = parts if rows % 512 == 0 else 1
        total = keep.astype(F32) + received.astype(F32)
        self.near = keep[:rows].astype(F32) + received[:rows].astype(F32)
        self.sent = [part.astype(BF16) for part in split_rows(total[rows:], parts)]
        self.send()

    def send(self, *others):
        self.across = [swap(part, 2) for part in after(self.sent, *others)]

    def value(self):
        return self.near + jnp.concatenate(self.across).astype(F32)


def after(value, *others):
    return lax.optimization_barrier((value, *others))[0]


def together(result, *slots):
    values = lax.optimization_barrier((result, *[array[i] for array, i in slots]))
    for (array, i), value in zip(slots, values[1:]):
        array[i] = value
    return values[0]


def slots_of(array, *wanted):
    return [(array, i) for i in (wanted or range(len(array))) if i < len(array)]


def row_major(array):
    return with_layout_constraint(array, Layout(tuple(range(array.ndim))))


def butterfly(array):
    for axis in ("head", "ctx", "dp"):
        size = lax.axis_size(axis)
        bit = 1
        while bit < size:
            array = array + lax.ppermute(array, axis, [(i, i ^ bit) for i in range(size)])
            bit *= 2
    return array


def chunk_specs(tile, pieces):
    specs, start = [], 0
    for piece in pieces:
        count = piece.shape[0] // tile
        specs.append(
            pl.BlockSpec(
                (tile, piece.shape[1]),
                lambda i, *_, a=start, n=count: (jnp.clip(i - a, 0, n - 1), 0),
            )
        )
        start += count
    return specs


def chunk_ends(tile, pieces):
    ends, start = [], 0
    for piece in pieces:
        start += piece.shape[0] // tile
        ends.append(start)
    return ends


def pick(refs, ends, out_ref):
    index = pl.program_id(0)
    start = 0
    for ref, end in zip(refs, ends):

        @pl.when((index >= start) & (index < end))
        def _(ref=ref):
            out_ref[...] = ref[...]

        start = end


def columns_spec(rows, width, index):
    return pl.BlockSpec((rows, width), lambda i, *_: (0, index))


def row_spec(tile, width):
    return pl.BlockSpec((tile, width), lambda i, *_: (i, 0))


def whole_spec(shape):
    return pl.BlockSpec(shape, lambda i, *_: (0,) * len(shape))


def mate_first_spec(tile, per, width):
    return pl.BlockSpec(
        (tile, width), lambda i, *_: ((2 * (i // per) + 1) % 5 * per + i % per, 0)
    )


def exchange_specs(tile, per, width):
    half = 2 * per
    return [
        pl.BlockSpec((tile, width), lambda i, *_: (i // half * (i - half), 0)),
        pl.BlockSpec(memory_space=pl.ANY),
    ]


def exchange_shapes(rows, width):
    return [jax.ShapeDtypeStruct((rows // 2, width), BF16)] * 2


def exchange_scratch(tile, per, width):
    half = 2 * per
    return [
        pltpu.VMEM((half, tile, width), BF16),
        pltpu.SemaphoreType.DMA((half,)),
        pltpu.SemaphoreType.DMA((half,)),
    ]


def mate_index():
    me = lax.axis_index("head")
    return me + 1 - 2 * (me % 2)


def meet_mate():
    @pl.when(pl.program_id(0) == 0)
    def _():
        barrier = pltpu.get_barrier_semaphore()
        pl.semaphore_signal(
            barrier, inc=1, device_id={"head": mate_index()}, device_id_type=MESH
        )
        pl.semaphore_wait(barrier, 1)


def exchange(value, per, keep_ref, received_ref, sent_sc, send_sem, recv_sem):
    step = pl.program_id(0)
    half = 2 * per
    tile = value.shape[0]

    def copy(slot):
        return pltpu.make_async_remote_copy(
            src_ref=sent_sc.at[slot],
            dst_ref=received_ref.at[pl.ds(pl.multiple_of(slot * tile, tile), tile)],
            send_sem=send_sem.at[slot],
            recv_sem=recv_sem.at[slot],
            device_id={"head": mate_index()},
            device_id_type=MESH,
        )

    @pl.when(step < half)
    def _():
        sent_sc[step] = value
        copy(step).start()

    @pl.when(step >= half)
    def _():
        keep_ref[...] = value

    @pl.when(step == 2 * half - 1)
    def _():
        for slot in range(half):
            copy(slot).wait()


def cost(flops, moved, transcendentals=0):
    return pl.CostEstimate(
        flops=int(flops), bytes_accessed=int(moved), transcendentals=int(transcendentals)
    )


def turn(values, cos_table, sin_table, low_half, sign):
    ahead = pltpu.roll(values, VD - HD // 2, 1)
    behind = pltpu.roll(values, HD // 2, 1)
    rotated = jnp.where(low_half, -ahead, behind)
    return values * cos_table + sign * rotated * sin_table


def low_half_mask(rows):
    lane = lax.broadcasted_iota(jnp.int32, (rows, VD), 1)
    return (lane % HD) < HD // 2


def side_by_side(w_ref):
    return jnp.concatenate([w_ref[item] for item in range(w_ref.shape[0])], axis=1)


def project_kernel(*refs, heads, ends):
    count = len(ends)
    w_ref, cos_ref, sin_ref, x_ref = refs[count : count + 4]
    q_refs, kv_refs = refs[count + 4 : count + 4 + heads], refs[count + 4 + heads :]
    pick(refs[:count], ends, x_ref)
    mask = low_half_mask(x_ref.shape[0])
    cos_table, sin_table = cos_ref[...], sin_ref[...]
    out = dot(x_ref[...], side_by_side(w_ref))
    for head in range(heads):
        base = head * 3 * VD
        query = turn(out[:, base : base + VD], cos_table, sin_table, mask, 1.0) * SCALE
        key = turn(out[:, base + VD : base + 2 * VD], cos_table, sin_table, mask, 1.0)
        q_refs[head][...] = query.astype(BF16)
        kv_refs[head][:, :VD] = key.astype(BF16)
        kv_refs[head][:, VD:] = out[:, base + 2 * VD : base + 3 * VD].astype(BF16)


def project(chunks, weight, cos_table, sin_table):
    own_rows = chunks[0].shape[0]
    rows = 4 * own_rows
    heads = weight.shape[0] // 3
    tile = min(256, own_rows)
    out = pl.pallas_call(
        functools.partial(project_kernel, heads=heads, ends=chunk_ends(tile, chunks)),
        grid=(rows // tile,),
        in_specs=chunk_specs(tile, chunks)
        + [whole_spec(weight.shape), row_spec(tile, VD), row_spec(tile, VD)],
        out_specs=[row_spec(tile, D)]
        + [row_spec(tile, VD)] * heads
        + [row_spec(tile, 2 * VD)] * heads,
        out_shape=[jax.ShapeDtypeStruct((rows, D), BF16)]
        + [jax.ShapeDtypeStruct((rows, VD), BF16)] * heads
        + [jax.ShapeDtypeStruct((rows, 2 * VD), BF16)] * heads,
        compiler_params=pltpu.CompilerParams(vmem_limit_bytes=40 * MIB),
        cost_estimate=cost(
            2 * rows * weight.size,
            2 * (2 * rows * D + weight.size + rows * 3 * heads * VD),
        ),
        name="project",
    )(*chunks, weight, cos_table, sin_table)
    return out[0], out[1 : 1 + heads], out[1 + heads :]


def unproject_kernel(*refs, heads, per):
    dq_refs, own_refs, recv_refs = refs[:heads], refs[heads : 2 * heads], refs[2 * heads : 3 * heads]
    w_ref, cos_ref, sin_ref, gp_ref, keep_ref, received_ref, *scratch = refs[3 * heads :]
    meet_mate()
    mask = low_half_mask(gp_ref.shape[0])
    cos_table, sin_table = cos_ref[...], sin_ref[...]
    for head in range(heads):
        base = head * 3 * VD
        both = own_refs[head][...].astype(F32) + recv_refs[head][...].astype(F32)
        query = dq_refs[head][...].astype(F32)
        gp_ref[:, base : base + VD] = turn(query, cos_table, sin_table, mask, -1.0).astype(BF16)
        gp_ref[:, base + VD : base + 2 * VD] = turn(
            both[:, :VD], cos_table, sin_table, mask, -1.0
        ).astype(BF16)
        gp_ref[:, base + 2 * VD : base + 3 * VD] = both[:, VD:].astype(BF16)
    value = dot(gp_ref[...], side_by_side(w_ref), NT).astype(BF16)
    exchange(value, per, keep_ref, received_ref, *scratch)


def unproject(dq, dkv_own, dkv_recv, weight, cos_table, sin_table):
    rows = dq[0].shape[0]
    heads = len(dq)
    tile = min(256, rows // 4)
    per = rows // 4 // tile
    return pl.pallas_call(
        functools.partial(unproject_kernel, heads=heads, per=per),
        grid=(rows // tile,),
        in_specs=[mate_first_spec(tile, per, VD)] * heads
        + [mate_first_spec(tile, per, 2 * VD)] * (2 * heads)
        + [whole_spec(weight.shape), mate_first_spec(tile, per, VD), mate_first_spec(tile, per, VD)],
        out_specs=[mate_first_spec(tile, per, heads * 3 * VD)] + exchange_specs(tile, per, D),
        scratch_shapes=exchange_scratch(tile, per, D),
        out_shape=[jax.ShapeDtypeStruct((rows, heads * 3 * VD), BF16)] + exchange_shapes(rows, D),
        compiler_params=pltpu.CompilerParams(
            vmem_limit_bytes=40 * MIB, collective_id=3, has_side_effects=True
        ),
        cost_estimate=cost(
            2 * rows * weight.size,
            2 * (rows * D + weight.size + 9 * rows * heads * VD),
        ),
        name="unproject",
    )(*dq, *dkv_own, *dkv_recv, weight, cos_table, sin_table)


def output_kernel(*refs, heads, per):
    attn_refs = refs[:heads]
    w_ref, all_ref, keep_ref, received_ref, *scratch = refs[heads:]
    meet_mate()
    for head in range(heads):
        all_ref[:, head * VD : (head + 1) * VD] = attn_refs[head][...]
    value = dot(all_ref[...], w_ref[...], NT).astype(BF16)
    exchange(value, per, keep_ref, received_ref, *scratch)


def output_projection(attn, weight):
    rows = attn[0].shape[0]
    heads = len(attn)
    tile = min(256, rows // 4)
    per = rows // 4 // tile
    return pl.pallas_call(
        functools.partial(output_kernel, heads=heads, per=per),
        grid=(rows // tile,),
        in_specs=[mate_first_spec(tile, per, VD)] * heads + [whole_spec(weight.shape)],
        out_specs=[mate_first_spec(tile, per, heads * VD)] + exchange_specs(tile, per, D),
        scratch_shapes=exchange_scratch(tile, per, D),
        out_shape=[jax.ShapeDtypeStruct((rows, heads * VD), BF16)] + exchange_shapes(rows, D),
        compiler_params=pltpu.CompilerParams(
            vmem_limit_bytes=40 * MIB, collective_id=1, has_side_effects=True
        ),
        cost_estimate=cost(
            2 * rows * D * weight.shape[1], 2 * (rows * D + weight.size + 2 * rows * heads * VD)
        ),
        name="output_projection",
    )(*attn, weight)


def gate_kernel(*refs, ends, cot_ends):
    count, cot_count = len(ends), len(cot_ends)
    chunks, cot_chunks = refs[:count], refs[count : count + cot_count]
    w_ref, x_ref, cot_ref, hidden_ref, by_gate_ref, by_up_ref = refs[count + cot_count :]
    pick(chunks, ends, x_ref)
    pick(cot_chunks, cot_ends, cot_ref)
    width = hidden_ref.shape[1]
    step = min(512, width)
    x = x_ref[...]
    for base in range(0, width, step):
        cols = slice(base, base + step)
        gate = dot(x, w_ref[:, cols])
        up = dot(x, w_ref[:, width + base : width + base + step])
        share = jax.nn.sigmoid(gate)
        swish = gate * share
        hidden_ref[:, cols] = (swish * up).astype(BF16)
        by_gate_ref[:, cols] = (up * share * (1.0 + gate * (1.0 - share))).astype(BF16)
        by_up_ref[:, cols] = swish.astype(BF16)


def gate_up(chunks, cot_chunks, weights, width):
    own_rows = chunks[0].shape[0]
    rows = 4 * own_rows
    tile = min(256, own_rows)
    return pl.pallas_call(
        functools.partial(
            gate_kernel, ends=chunk_ends(tile, chunks), cot_ends=chunk_ends(tile, cot_chunks)
        ),
        grid=(rows // tile,),
        in_specs=chunk_specs(tile, chunks)
        + chunk_specs(tile, cot_chunks)
        + [columns_spec(D, 2 * width, 0)],
        out_specs=[row_spec(tile, D)] * 2 + [row_spec(tile, width)] * 3,
        out_shape=[jax.ShapeDtypeStruct((rows, D), BF16)] * 2
        + [jax.ShapeDtypeStruct((rows, width), BF16)] * 3,
        compiler_params=pltpu.CompilerParams(vmem_limit_bytes=60 * MIB),
        cost_estimate=cost(
            4 * rows * D * width, 2 * (4 * rows * D + 2 * D * width + 3 * rows * width)
        ),
        name="gate_up",
    )(*chunks, *cot_chunks, weights)


def feed_kernel(
    cot_ref,
    hidden_ref,
    by_gate_ref,
    by_up_ref,
    down_ref,
    inner_ref,
    grad_ref,
    ffn_keep,
    ffn_received,
    mid_keep,
    mid_received,
    *scratch,
    per,
):
    meet_mate()
    width = hidden_ref.shape[1]
    grad_hidden = dot(cot_ref[...], down_ref[...])
    grad_ref[:, :width] = (grad_hidden * by_gate_ref[...].astype(F32)).astype(BF16)
    grad_ref[:, width:] = (grad_hidden * by_up_ref[...].astype(F32)).astype(BF16)
    middle = dot(grad_ref[...], inner_ref[...], NT).astype(BF16)
    exchange(middle, per, mid_keep, mid_received, *scratch[3:])
    output = dot(hidden_ref[...], down_ref[...], NT).astype(BF16)
    exchange(output, per, ffn_keep, ffn_received, *scratch[:3])


def feed(cot, hidden, by_gate, by_up, weights):
    rows, width = hidden.shape
    tile = min(256, rows // 4)
    per = rows // 4 // tile
    return pl.pallas_call(
        functools.partial(feed_kernel, per=per),
        grid=(rows // tile,),
        in_specs=[row_spec(tile, D)]
        + [row_spec(tile, width)] * 3
        + [columns_spec(D, width, 2), columns_spec(D, 2 * width, 0)],
        out_specs=[row_spec(tile, 2 * width)]
        + exchange_specs(tile, per, D)
        + exchange_specs(tile, per, D),
        out_shape=[jax.ShapeDtypeStruct((rows, 2 * width), BF16)]
        + exchange_shapes(rows, D)
        + exchange_shapes(rows, D),
        scratch_shapes=exchange_scratch(tile, per, D) + exchange_scratch(tile, per, D),
        compiler_params=pltpu.CompilerParams(
            vmem_limit_bytes=60 * MIB, collective_id=2, has_side_effects=True
        ),
        cost_estimate=cost(
            8 * rows * D * width, 2 * (3 * rows * D + 3 * D * width + 5 * rows * width)
        ),
        name="feed",
    )(cot, hidden, by_gate, by_up, weights, weights)


class Plan:
    def __init__(self, own_rows, block_len, prev_rows, ndoc):
        self.own_rows = own_rows
        self.block_len = block_len
        self.prev_rows = prev_rows
        self.ndoc = ndoc
        self.bq = min(256, own_rows)
        self.bk = min(512, own_rows)
        self.total = prev_rows + block_len

    def doc_start(self, info, pos):
        start = jnp.zeros_like(pos)
        for item in range(self.ndoc):
            start = jnp.where(pos >= info[2 + item], info[2 + item], start)
        return start

    def query_start(self, info, index):
        per = self.own_rows // self.bq
        chunk = (index // per) ^ info[0]
        return info[1] * self.block_len + chunk * self.own_rows + (index % per) * self.bq

    def key_row(self, info, index):
        per = self.own_rows // self.bk
        blocks = self.block_len // self.bk
        owner = index // blocks
        local = index % blocks
        inside = (((local // per) ^ info[0]) * per + local % per) * self.bk
        base = jnp.where(owner == info[1], self.prev_rows, owner * self.block_len)
        return pl.multiple_of(base + inside, self.bk)

    def ranges(self, info, start):
        last = start + self.bq - 1
        low = self.doc_start(info, start) // self.bk
        high = last // self.bk + 1
        open_from = (self.doc_start(info, last) + self.bk - 1) // self.bk
        first = jnp.minimum(jnp.maximum(open_from, low), high)
        until = jnp.maximum(first, jnp.minimum((start + 1) // self.bk, high))
        return low, first, until, high


def in_groups(low, high, size, visit):
    count = (high - low) // size

    @pl.loop(0, count)
    def _(group):
        visit(*[low + group * size + item for item in range(size)])

    if size > 1:

        @pl.loop(low + count * size, high)
        def _(index):
            visit(index)


def split_halves(q):
    lane = lax.broadcasted_iota(jnp.int32, q.shape, 1)
    zero = jnp.zeros_like(q)
    return jnp.concatenate([jnp.where(lane < HD, q, zero), jnp.where(lane >= HD, q, zero)], axis=0)


def in_lanes(value):
    high = value.astype(BF16)
    rest = value - high.astype(F32)
    middle = rest.astype(BF16)
    low = (rest - middle.astype(F32)).astype(BF16)
    lane = lax.broadcasted_iota(jnp.int32, value.shape, 1)
    zero = jnp.zeros_like(high)
    return jnp.where(
        lane == 0, high, jnp.where(lane == 1, middle, jnp.where(lane == 2, low, zero))
    )


def load_keys(plan, info, own_ref, prev_ref, kv_sc):
    @pl.when(pl.program_id(0) == 0)
    def _():
        kv_sc[plan.prev_rows :, :] = own_ref[...]

        @pl.when(info[1] > 0)
        def _():
            kv_sc[: plan.prev_rows, :] = prev_ref[...]


def forward_kernel(
    info,
    lam_ref,
    gain_ref,
    q_ref,
    own_ref,
    prev_ref,
    attn_ref,
    first_ref,
    second_ref,
    lse_ref,
    kv_sc,
    m_sc,
    l_sc,
    acc_sc,
    *,
    plan,
):
    bq, bk = plan.bq, plan.bk
    load_keys(plan, info, own_ref, prev_ref, kv_sc)
    start = plan.query_start(info, pl.program_id(0))
    q2 = split_halves(q_ref[...])
    m_sc[...] = jnp.full_like(m_sc, NEG)
    l_sc[...] = jnp.zeros_like(l_sc)
    acc_sc[...] = jnp.zeros_like(acc_sc)
    low, first, until, high = plan.ranges(info, start)

    def visit(index, masked):
        row = plan.key_row(info, index)
        key = kv_sc[pl.ds(row, bk), :VD]
        value = kv_sc[pl.ds(row, bk), VD:]
        scores = dot(q2, key, NT)
        if masked:
            query_pos = start + lax.broadcasted_iota(jnp.int32, (bq, 1), 0)
            begin = plan.doc_start(info, query_pos)
            key_pos = index * bk + lax.broadcasted_iota(jnp.int32, (bq, bk), 1)
            keep = (key_pos <= query_pos) & (key_pos >= begin)
            scores = jnp.concatenate(
                [jnp.where(keep, scores[:bq], NEG), jnp.where(keep, scores[bq:], NEG)], axis=0
            )
        before = m_sc[...]
        after = jnp.maximum(before, jnp.max(scores, axis=1, keepdims=True))
        weights = jnp.exp(scores - jnp.tile(after, (1, bk // VD)))
        factor = jnp.exp(before - after)
        m_sc[...] = after
        l_sc[...] = l_sc[...] * factor + jnp.sum(weights, axis=1, keepdims=True)
        acc_sc[...] = acc_sc[...] * factor + dot(weights.astype(BF16), value)

    @pl.loop(low, first)
    def _(index):
        visit(index, True)

    @pl.loop(first, until)
    def _(index):
        visit(index, False)

    @pl.loop(until, high)
    def _(index):
        visit(index, True)

    total = l_sc[...]
    maps = acc_sc[...] * (1.0 / total)
    first_map, second_map = maps[:bq], maps[bq:]
    first_ref[...] = first_map
    second_ref[...] = second_map
    difference = first_map - lam_ref[0] * second_map
    scaling = lax.rsqrt(jnp.mean(difference * difference, axis=1, keepdims=True) + EPS)
    attn_ref[...] = (difference * scaling * gain_ref[...]).astype(BF16)
    lanes = in_lanes(-(m_sc[...] + jnp.log(total)))
    lse_ref[:, :VD] = lanes[:bq]
    lse_ref[:, VD:] = lanes[bq:]


def attention_cost(plan, per_pair, extra=0):
    pairs = plan.block_len * plan.block_len * 5 // 8
    return cost(pairs * per_pair + extra, plan.block_len * VD * 32, 2 * pairs)


def attend_forward(plan, info, lam, gain, q, kv_own, kv_prev):
    rows, bq = plan.block_len, plan.bq
    grid_spec = pltpu.PrefetchScalarGridSpec(
        num_scalar_prefetch=1,
        grid=(rows // bq,),
        in_specs=[
            pl.BlockSpec(memory_space=pltpu.SMEM),
            whole_spec((1, VD)),
            row_spec(bq, VD),
            whole_spec((rows, 2 * VD)),
            whole_spec((plan.prev_rows, 2 * VD)),
        ],
        out_specs=[row_spec(bq, VD)] * 3 + [row_spec(bq, 2 * VD)],
        scratch_shapes=[
            pltpu.VMEM((plan.total, 2 * VD), BF16),
            pltpu.VMEM((2 * bq, VD), F32),
            pltpu.VMEM((2 * bq, VD), F32),
            pltpu.VMEM((2 * bq, VD), F32),
        ],
    )
    return pl.pallas_call(
        functools.partial(forward_kernel, plan=plan),
        grid_spec=grid_spec,
        out_shape=[
            jax.ShapeDtypeStruct((rows, VD), BF16),
            jax.ShapeDtypeStruct((rows, VD), F32),
            jax.ShapeDtypeStruct((rows, VD), F32),
            jax.ShapeDtypeStruct((rows, 2 * VD), BF16),
        ],
        compiler_params=pltpu.CompilerParams(vmem_limit_bytes=60 * MIB),
        cost_estimate=attention_cost(plan, 6 * VD),
        name="attend_forward",
    )(info, lam, gain, q, kv_own, kv_prev)


def difference_kernel(lam_ref, gain_ref, w_ref, *refs, heads, ends):
    count = len(ends)
    chunks, refs = refs[:count], refs[count:]
    first_refs, second_refs, refs = refs[:heads], refs[heads : 2 * heads], refs[2 * heads :]
    gm_ref, sums_ref, grad_refs = refs[0], refs[1], refs[2:]
    lam = lam_ref[0]

    @pl.when(pl.program_id(0) == 0)
    def _():
        sums_ref[...] = jnp.zeros_like(sums_ref)

    pick(chunks, ends, gm_ref)
    upstream_all = dot(gm_ref[...], w_ref[...])
    for head in range(heads):
        upstream = upstream_all[:, head * VD : (head + 1) * VD]
        first_map, second_map = first_refs[head][...], second_refs[head][...]
        difference = first_map - lam * second_map
        scaling = lax.rsqrt(jnp.mean(difference * difference, axis=1, keepdims=True) + EPS)
        normal = difference * scaling
        weighted = upstream * gain_ref[...]
        inner_mean = jnp.mean(weighted * normal, axis=1, keepdims=True)
        grad = (scaling * (weighted - normal * inner_mean)).astype(BF16)
        grad_wide = grad.astype(F32)
        first_product, second_product = grad_wide * first_map, grad_wide * second_map
        sums_ref[0:1, :] += jnp.sum(upstream * normal, axis=0, keepdims=True)
        sums_ref[1:2, :] += jnp.sum(second_product, axis=0, keepdims=True)
        out = grad_refs[head]
        out[:, :VD] = grad
        for item, product in enumerate((first_product, second_product)):
            total = jnp.sum(product, axis=1, keepdims=True)
            out[:, (item + 1) * VD : (item + 2) * VD] = in_lanes(
                jnp.broadcast_to(-total, product.shape)
            )


def difference_grads(lam, gain, weight, gm, first, second):
    own_rows = gm[0].shape[0]
    rows = 4 * own_rows
    heads = len(first)
    tile = min(256, own_rows)
    return pl.pallas_call(
        functools.partial(difference_kernel, heads=heads, ends=chunk_ends(tile, gm)),
        grid=(rows // tile,),
        in_specs=[pl.BlockSpec(memory_space=pltpu.SMEM), whole_spec((1, VD)), whole_spec(weight.shape)]
        + chunk_specs(tile, gm)
        + [row_spec(tile, VD)] * (2 * heads),
        out_specs=[row_spec(tile, D), whole_spec((8, VD))] + [row_spec(tile, 3 * VD)] * heads,
        out_shape=[jax.ShapeDtypeStruct((rows, D), BF16), jax.ShapeDtypeStruct((8, VD), F32)]
        + [jax.ShapeDtypeStruct((rows, 3 * VD), BF16)] * heads,
        compiler_params=pltpu.CompilerParams(vmem_limit_bytes=60 * MIB),
        cost_estimate=cost(2 * rows * D * heads * VD, 4 * rows * D + 14 * rows * heads * VD),
        name="difference_grads",
    )(lam, gain, weight, *gm, *first, *second)


def backward_kernel(
    info,
    lam_ref,
    q_ref,
    own_ref,
    prev_ref,
    lse_ref,
    grad_ref,
    dq_ref,
    dkv_own_ref,
    dkv_prev_ref,
    kv_sc,
    dk_sc,
    dv_sc,
    dqt_sc,
    *,
    plan,
):
    bq, bk = plan.bq, plan.bk
    step = pl.program_id(0)
    lam = lam_ref[0]

    @pl.when(step == 0)
    def _():
        lane = lax.broadcasted_iota(jnp.int32, (bk, VD), 1)
        ones = jnp.where(lane < 3, 1.0, 0.0).astype(BF16)

        def fill(source, base, rows):
            for start in range(0, rows, bk):
                to = slice(base + start, base + start + bk)
                kv_sc[to, :VD] = source[start : start + bk, :VD]
                kv_sc[to, VD : 2 * VD] = ones
                kv_sc[to, 2 * VD :] = source[start : start + bk, VD:]

        fill(own_ref, plan.prev_rows, plan.block_len)

        @pl.when(info[1] > 0)
        def _():
            fill(prev_ref, 0, plan.prev_rows)

        dk_sc[...] = jnp.zeros_like(dk_sc)
        dv_sc[...] = jnp.zeros_like(dv_sc)

    grad = grad_ref[:, :VD]
    start = plan.query_start(info, step)
    q2 = split_halves(q_ref[...])
    q_wide = jnp.concatenate(
        [q2, jnp.concatenate([lse_ref[:, :VD], lse_ref[:, VD:]], axis=0)], axis=1
    )
    ones = jnp.ones((8, VD), BF16)
    delta_first = dot(ones, grad_ref[:, VD : 2 * VD], NT)[0:1]
    delta_second = dot(ones, grad_ref[:, 2 * VD :], NT)[0:1]
    dqt_sc[...] = jnp.zeros_like(dqt_sc)
    low, _, _, high = plan.ranges(info, start)

    query_pos = start + lax.broadcasted_iota(jnp.int32, (1, bq), 1)
    begin = plan.doc_start(info, query_pos)

    def visit(*indices):
        results = []
        for index in indices:
            row = plan.key_row(info, index)
            key = kv_sc[pl.ds(row, bk), :VD]
            prob = jnp.exp(dot(kv_sc[pl.ds(row, bk), : 2 * VD], q_wide, NT))
            base = dot(kv_sc[pl.ds(row, bk), 2 * VD :], grad, NT)
            key_pos = index * bk + lax.broadcasted_iota(jnp.int32, (bk, bq), 0)
            keep = (key_pos <= query_pos) & (key_pos >= begin)
            prob_first = jnp.where(keep, prob[:, :bq], 0.0)
            prob_second = jnp.where(keep, prob[:, bq:], 0.0)
            raw = jnp.concatenate(
                [
                    (prob_first * (base + delta_first)).astype(BF16),
                    (prob_second * (base + delta_second)).astype(BF16),
                ],
                axis=1,
            )
            value_grad = dot((prob_first - lam * prob_second).astype(BF16), grad)
            results.append((row, value_grad, dot(raw, q2), dot(key, raw, TN)))
        for row, value_grad, key_grad, query_grad in results:
            dv_sc[pl.ds(row, bk), :] += value_grad
            dk_sc[pl.ds(row, bk), :] += key_grad
        dqt_sc[...] += sum(result[3] for result in results)

    in_groups(low, high, 2, visit)

    dq_t = jnp.concatenate([dqt_sc[:HD, :bq], -lam * dqt_sc[HD:, bq:]], axis=0) * SCALE
    dq_ref[...] = dq_t.T.astype(BF16)

    @pl.when(step == pl.num_programs(0) - 1)
    def _():
        lane = lax.broadcasted_iota(jnp.int32, (1, VD), 1)
        side = jnp.where(lane < HD, 1.0, -lam)
        dkv_own_ref[:, :VD] = (dk_sc[plan.prev_rows :, :] * side).astype(BF16)
        dkv_own_ref[:, VD:] = dv_sc[plan.prev_rows :, :].astype(BF16)
        dkv_prev_ref[:, :VD] = (dk_sc[: plan.prev_rows, :] * side).astype(BF16)
        dkv_prev_ref[:, VD:] = dv_sc[: plan.prev_rows, :].astype(BF16)


def attend_backward(plan, info, lam, q, kv_own, kv_prev, lse, grad):
    rows, bq = plan.block_len, plan.bq
    grid_spec = pltpu.PrefetchScalarGridSpec(
        num_scalar_prefetch=1,
        grid=(rows // bq,),
        in_specs=[
            pl.BlockSpec(memory_space=pltpu.SMEM),
            row_spec(bq, VD),
            whole_spec((rows, 2 * VD)),
            whole_spec((plan.prev_rows, 2 * VD)),
            row_spec(bq, 2 * VD),
            row_spec(bq, 3 * VD),
        ],
        out_specs=[
            row_spec(bq, VD),
            whole_spec((rows, 2 * VD)),
            whole_spec((plan.prev_rows, 2 * VD)),
        ],
        scratch_shapes=[
            pltpu.VMEM((plan.total, 3 * VD), BF16),
            pltpu.VMEM((plan.total, VD), F32),
            pltpu.VMEM((plan.total, VD), F32),
            pltpu.VMEM((VD, 2 * bq), F32),
        ],
    )
    return pl.pallas_call(
        functools.partial(backward_kernel, plan=plan),
        grid_spec=grid_spec,
        out_shape=[
            jax.ShapeDtypeStruct((rows, VD), BF16),
            jax.ShapeDtypeStruct((rows, 2 * VD), BF16),
            jax.ShapeDtypeStruct((plan.prev_rows, 2 * VD), BF16),
        ],
        compiler_params=pltpu.CompilerParams(vmem_limit_bytes=60 * MIB),
        cost_estimate=attention_cost(plan, 16 * VD),
        name="attend_backward",
    )(info, lam, q, kv_own, kv_prev, lse, grad)


def norm_forward(values, gain_vec):
    scaling = lax.rsqrt(jnp.mean(values * values, axis=-1, keepdims=True) + EPS)
    return (values * scaling * gain_vec, scaling)


def norm_backward(values, scaling, gain_vec, upstream):
    normal = values * scaling
    weighted = upstream * gain_vec
    inner_mean = jnp.mean(weighted * normal, axis=-1, keepdims=True)
    return (scaling * (weighted - normal * inner_mean), jnp.sum(upstream * normal, axis=0))


def adamw(parameter, momentum, variance, gradient, learn_rate, decay_rate):
    momentum = BETA1 * momentum + (1.0 - BETA1) * gradient
    variance = BETA2 * variance + (1.0 - BETA2) * gradient * gradient
    corrected = momentum / (1.0 - BETA1**STEP)
    spread = jnp.sqrt(variance / (1.0 - BETA2**STEP))
    return (
        parameter - learn_rate * (corrected / (spread + ADAM_EPS) + decay_rate * parameter),
        momentum,
        variance,
    )


def send_keys(kv, ctx_count):
    if ctx_count == 2:
        return lax.ppermute(kv, "ctx", [(0, 1)])
    return lax.all_gather(kv, "ctx", axis=0, tiled=True)


def return_keys(grads, ctx_count):
    if ctx_count == 2:
        return lax.ppermute(grads, "ctx", [(1, 0)])
    return lax.psum_scatter(grads, "ctx", scatter_dimension=0, tiled=True)


def scatter_weight(grad, *others):
    grad = after(grad.astype(BF16), *others)
    return lax.psum_scatter(grad, "dp", scatter_dimension=0, tiled=True)


def sum_blocks(share, ctx_count):
    if ctx_count == 2:
        other = lax.ppermute(share, "ctx", [(0, 1), (1, 0)])
        return share.astype(F32) + other.astype(F32)
    return lax.psum(share, "ctx").astype(F32)


def on_device(
    tokens,
    cotangent,
    doc_lengths,
    qkv_weight,
    out_weight,
    inner_weight,
    down_weight,
    norm_gains,
    head_gain,
    lambdas,
    qkv_momentum,
    out_momentum,
    inner_momentum,
    down_momentum,
    norm_momentum,
    head_momentum,
    lambda_momentum,
    qkv_variance,
    out_variance,
    inner_variance,
    down_variance,
    norm_variance,
    head_variance,
    lambda_variance,
):
    micro_count, own_rows, _ = tokens.shape
    head_count = lax.axis_size("head")
    ctx_count = lax.axis_size("ctx")
    block_len = own_rows * head_count
    seq_len = block_len * ctx_count
    ctx_index = lax.axis_index("ctx")
    head_index = lax.axis_index("head")
    local_heads = qkv_weight.shape[1]
    ff_local = inner_weight.shape[2]
    ndoc = doc_lengths.shape[1]
    plan = Plan(own_rows, block_len, block_len if ctx_count == 2 else seq_len, ndoc)

    def gather_weight(shard):
        return lax.all_gather(shard.astype(BF16), "dp", axis=0, tiled=True)

    def by_part(array):
        return array.transpose(1, 2, 0, 3)

    qkv_low = lax.all_gather(
        row_major(by_part(qkv_weight).astype(BF16)).reshape(local_heads * 3, -1, VD),
        "dp",
        axis=1,
        tiled=True,
    )
    out_t = gather_weight(row_major(out_weight.astype(BF16).reshape(local_heads * VD, -1).T))
    feed_low = gather_weight(
        jnp.concatenate(
            [
                inner_weight.reshape(-1, 2 * ff_local).astype(BF16),
                row_major(down_weight.astype(BF16).T),
            ],
            axis=1,
        )
    )

    first_exp = jnp.exp(jnp.sum(lambdas[0] * lambdas[1]))
    second_exp = jnp.exp(jnp.sum(lambdas[2] * lambdas[3]))
    lambda_value = first_exp - second_exp + LAMBDA_INIT
    lam = lambda_value.reshape(1)
    head_scale = (head_gain * (1.0 - LAMBDA_INIT)).reshape(1, VD)

    chunk = jnp.arange(block_len, dtype=jnp.int32) // own_rows
    position = (
        ctx_index * block_len
        + (chunk ^ head_index) * own_rows
        + jnp.arange(block_len, dtype=jnp.int32) % own_rows
    )
    frequency = ROPE_BASE ** (
        -(jnp.arange(VD, dtype=jnp.int32) % (HD // 2)).astype(F32) / (HD // 2)
    )

    def info_of(micro):
        bounds = jnp.cumsum(doc_lengths[micro], dtype=jnp.int32)
        return jnp.concatenate([jnp.stack([head_index, ctx_index]).astype(jnp.int32), bounds])

    micros = range(micro_count)
    heads = range(local_heads)
    infos = [info_of(m) for m in micros]
    own, normed_own, normed, cot_own = [], [], [], []
    for m in micros:
        rows, cot_rows = tokens[m], cotangent[m]
        if m > 0:
            rows = after(rows, normed[0].own)
        own.append(rows.astype(F32))
        normed_own.append(norm_forward(own[m], norm_gains[0]))
        cot_own.append(cot_rows)
        normed.append(Gather(normed_own[m][0].astype(BF16), 2 if m else 1))
    position = after(position, normed[-1].own)
    phases = position.astype(F32)[:, None] * frequency[None, :]
    cos_table, sin_table = jnp.cos(phases), jnp.sin(phases)

    normed_all, q, kv, kv_prev, cot = [], [], [], [], []
    for m in micros:
        pieces = normed[m].pieces()
        if m == 0:
            pieces = after(pieces, normed[1].far[0])
        result = project(pieces, qkv_low, cos_table, sin_table)
        if m == 0:
            result = together(result, *slots_of(normed[1].far, 1))
            cot.append(Gather(after(cot_own[0], qkv_low, normed[1].far[-1])))
        else:
            cot.append(Gather(after(cot_own[1], result[2], *cot[0].far), 2))
        normed_all.append(result[0])
        q.append(result[1])
        kv.append(result[2])
        kv_prev.append([send_keys(result[2][h], ctx_count) for h in heads])

    def attend(m, h, before, beside):
        out = attend_forward(
            plan, infos[m], lam, head_scale, after(q[m][h], *before), kv[m][h], kv_prev[m][h]
        )
        return together(out, *beside)

    mid = []

    def finish_attention(m):
        middle = own[m] + attended[m].value()
        value, scaling = norm_forward(middle, norm_gains[1])
        mid.append((middle, scaling, Gather(value.astype(BF16), 2)))

    maps, attn_all, attended = [], [], []
    for m in micros:
        outs = []
        for h in heads:
            if m == 0:
                before = [out_t, kv[-1]] if h == 0 else [outs[-1]]
                beside = [
                    slots_of(cot[0].far, 0),
                    slots_of(cot[1].far, 0),
                    slots_of(cot[1].far, 1),
                ][h]
            elif h == 0:
                before = [*attended[0].sent, *cot[0].pieces(), *cot[1].pieces()]
                beside = slots_of(attended[0].across) + slots_of(kv_prev[m], 1)
            else:
                before = [outs[-1], mid[0][2].own]
                beside = slots_of(mid[0][2].far, h - 1) + slots_of(kv_prev[m], h + 1)
            outs.append(attend(m, h, before, beside))
            if m > 0 and h == 0:
                finish_attention(0)
        maps.append([out[1:] for out in outs])
        result = output_projection([out[0] for out in outs], out_t)
        if m == 0:
            result = together(result, *slots_of(kv_prev[1], 0))
        attn_all.append(result[0])
        attended.append(Reduce(*result[1:], 2 if m else 1))

    grad_middle, gm, gain_mid = [], [], []

    def finish_feed(m, reduced):
        middle, scaling, _ = mid[m]
        grad_norm, part = norm_backward(middle, scaling, norm_gains[1], reduced.value())
        grad_middle.append((cot_own[m].astype(F32) + grad_norm).astype(BF16))
        gm.append(Gather(grad_middle[m], 2 if m else 1))
        gain_mid.append(part)

    def weight_grad(left, right, before, beside, total=None):
        result = dot(after(left, *before), right, TN)
        if total is not None:
            result = (total + result).astype(BF16)
        return together(result, *beside)

    first_gates = gate_up(
        after(mid[0][2].mate_first(), *attended[1].sent), cot[0].mate_first(), feed_low, ff_local
    )
    first_gates = together(first_gates, *slots_of(attended[1].across, 0))
    first_feed = feed(*first_gates[1:], feed_low)
    first_feed = together(first_feed, *slots_of(attended[1].across, 1))
    finish_attention(1)
    reduced_mid = [Reduce(*first_feed[3:])]
    grad_inner = weight_grad(
        first_gates[0],
        first_feed[0],
        [mid[1][2].own, *reduced_mid[0].sent],
        slots_of(mid[1][2].far, 0),
    )
    grad_down = weight_grad(
        first_gates[1], first_gates[2], [grad_inner], slots_of(mid[1][2].far, 1)
    )
    reduced_mid[0].send(*mid[1][2].far)
    second_gates = gate_up(
        after(mid[1][2].mate_first(), grad_down), cot[1].mate_first(), feed_low, ff_local
    )
    second_gates = together(second_gates, *slots_of(reduced_mid[0].across))
    finish_feed(0, reduced_mid[0])
    second_feed = feed(after(second_gates[1], gm[0].own), *second_gates[2:], feed_low)
    second_feed = together(second_feed, *slots_of(gm[0].far))
    reduced_mid.append(Reduce(*second_feed[3:], 2))
    grad_inner = weight_grad(
        second_gates[0],
        second_feed[0],
        reduced_mid[1].sent,
        slots_of(reduced_mid[1].across, 0),
        grad_inner,
    )
    grad_down = weight_grad(
        second_gates[1],
        second_gates[2],
        [grad_inner],
        slots_of(reduced_mid[1].across, 1),
        grad_down,
    )
    feed_grad = jnp.concatenate([grad_inner, grad_down], axis=1)
    feed_part = scatter_weight(row_major(feed_grad))
    finish_feed(1, reduced_mid[1])
    ffn_pairs = [first_feed[1:3], second_feed[1:3]]

    dqs, dkvs, recvs, gm_alls, grads, sums = [], [], [], [], [], 0.0

    def start_back(m, before, beside):
        out = difference_grads(
            lam,
            head_scale,
            out_t,
            after(gm[m].pieces(), *before),
            [part[0] for part in maps[m]],
            [part[1] for part in maps[m]],
        )
        out = together(out, *beside)
        gm_alls.append(out[0])
        grads.append(out[2:])
        dqs.append([])
        dkvs.append([])
        recvs.append([])
        return out[1]

    def attend_back(m, h, before, beside):
        out = attend_backward(
            plan,
            infos[m],
            lam,
            after(q[m][h], *before),
            kv[m][h],
            kv_prev[m][h],
            maps[m][h][2],
            grads[m][h],
        )
        out = together(out, *beside)
        dqs[m].append(out[0])
        dkvs[m].append(out[1])
        recvs[m].append(return_keys(out[2], ctx_count))

    def unprojected(m, before, beside):
        out = unproject(after(dqs[m], *before), dkvs[m], recvs[m], qkv_low, cos_table, sin_table)
        return together(out, *beside)

    def ffn_sum(m, before):
        keep, received = ffn_pairs[m]
        return Reduce(keep, after(received, *before), 2)

    sums = start_back(0, [gm[1].own, feed_grad], [])
    attend_back(0, 0, [], slots_of(gm[1].far, 0))
    attend_back(0, 1, [dqs[0][-1]], slots_of(gm[1].far, 1) + slots_of(recvs[0], 0))
    ffn = [ffn_sum(0, [dqs[0][-1]])]
    ffn.append(ffn_sum(1, [dqs[0][-1]]))
    attend_back(
        0,
        2,
        [*ffn[0].sent, *gm[1].pieces()],
        slots_of(ffn[0].across, 0) + slots_of(recvs[0], 1),
    )
    sums = sums + start_back(1, [dqs[0][-1]], slots_of(ffn[0].across, 1))
    grad_out = weight_grad(gm_alls[0], attn_all[0], [grads[1][0]], [])
    grad_out = weight_grad(gm_alls[1], attn_all[1], [grad_out], [], grad_out)
    attend_back(
        1, 0, [*ffn[1].sent, grad_out], slots_of(ffn[1].across, 0) + slots_of(recvs[0], 2)
    )
    back = [unprojected(0, [dqs[1][-1]], slots_of(ffn[1].across, 1))]
    reduced_in = [Reduce(*back[0][1:], 2)]
    attend_back(
        1,
        1,
        [back[0][0], *reduced_in[0].sent],
        slots_of(reduced_in[0].across, 0) + slots_of(recvs[1], 0),
    )
    attend_back(1, 2, [dqs[1][-1]], slots_of(reduced_in[0].across, 1) + slots_of(recvs[1], 1))
    out_part = scatter_weight(row_major(grad_out), feed_part)
    grad_qkv = weight_grad(normed_all[0], back[0][0], [dqs[1][-1], out_part], slots_of(recvs[1], 2))
    back.append(unprojected(1, [grad_qkv], []))
    reduced_in.append(Reduce(*back[1][1:], 2))
    grad_qkv = weight_grad(
        normed_all[1],
        back[1][0],
        reduced_in[1].sent,
        slots_of(reduced_in[1].across, 0),
        grad_qkv,
    )
    last_part = scatter_weight(row_major(grad_qkv), out_part)
    out_share = sum_blocks(out_part, ctx_count)
    feed_share = row_major(sum_blocks(feed_part, ctx_count))
    inner_share = feed_share[:, : 2 * ff_local]
    down_share = feed_share[:, 2 * ff_local :]
    gain_mid = gain_mid[0] + gain_mid[1]
    outputs = [(mid[m][0] + ffn[m].value()).astype(BF16) for m in micros]

    gain_in = 0.0
    input_grads = []
    for m in micros:
        grad_in_norm, gain_part = norm_backward(
            own[m], normed_own[m][1], norm_gains[0], reduced_in[m].value()
        )
        gain_in = gain_in + gain_part
        input_grads.append((grad_middle[m].astype(F32) + grad_in_norm).astype(BF16))

    lambda_acc = -jnp.sum(sums[1])
    lambda_local = jnp.stack(
        [
            lambda_acc * first_exp * lambdas[1],
            lambda_acc * first_exp * lambdas[0],
            -lambda_acc * second_exp * lambdas[3],
            -lambda_acc * second_exp * lambdas[2],
        ]
    )
    small = butterfly(
        jnp.concatenate(
            [
                gain_in.reshape(-1, VD),
                gain_mid.reshape(-1, VD),
                sums[:1] * (1.0 - LAMBDA_INIT),
                lambda_local.reshape(-1, VD),
            ]
        )
    )
    per = D // VD
    norm_grad = small[: 2 * per].reshape(2, D)
    head_grad = small[2 * per]
    lambda_grad = small[2 * per + 1 :].reshape(lambdas.shape)

    feed_states = [
        adamw(
            inner_weight,
            inner_momentum,
            inner_variance,
            row_major(inner_share.reshape(inner_weight.shape)),
            0.5 * D ** (-0.5),
            DECAY,
        ),
        adamw(
            down_weight, down_momentum, down_variance, row_major(down_share.T), 0.5 * FF ** (-0.5), DECAY
        ),
    ]
    out_state = adamw(
        out_weight,
        out_momentum,
        out_variance,
        row_major(out_share.T).reshape(out_weight.shape),
        0.5 * (H * VD) ** (-0.5),
        DECAY,
    )
    output, input_grad = jnp.stack(outputs), jnp.stack(input_grads)
    qkv_share = sum_blocks(
        after(last_part, feed_states, out_state, output, input_grad, small), ctx_count
    )
    qkv_share = row_major(
        row_major(qkv_share).reshape(-1, local_heads, 3, VD).transpose(1, 2, 0, 3)
    )
    qkv_state = adamw(
        by_part(qkv_weight),
        by_part(qkv_momentum),
        by_part(qkv_variance),
        qkv_share,
        0.5 * D ** (-0.5),
        DECAY,
    )

    states = [
        tuple(part.transpose(2, 0, 1, 3) for part in qkv_state),
        out_state,
        *feed_states,
        adamw(norm_gains, norm_momentum, norm_variance, norm_grad, 0.4, 0.0),
        adamw(head_gain, head_momentum, head_variance, head_grad, 0.4, 0.0),
        adamw(lambdas, lambda_momentum, lambda_variance, lambda_grad, 0.1, 0.0),
    ]
    return (
        output,
        input_grad,
        *[state[0] for state in states],
        *[state[1] for state in states],
        *[state[2] for state in states],
    )


def solution(mesh):
    activation = P("dp", ("ctx", "head"), None)
    big = (P("dp", "head", None, None), P("head", None, "dp"), P("dp", None, "head"), P("head", "dp"))
    state = big + (P(), P(), P())
    return jax.shard_map(
        on_device,
        mesh=mesh,
        in_specs=(activation, activation, P("dp", None)) + state * 3,
        out_specs=(activation, activation) + state * 3,
        check_vma=False,
    )
```

```python
import functools

import jax
import jax.numpy as jnp
from jax import lax
from jax.experimental import pallas as pl
from jax.experimental.layout import Layout, with_layout_constraint
from jax.experimental.pallas import tpu as pltpu
from jax.sharding import PartitionSpec as P

D = 1536
FF = 4096
H = 12
HD = 64
STEP = 10
VD = 128


EPS = 1e-05
LAMBDA_INIT = 0.2
SCALE = 0.125
NEG = -1e30
BETA1 = 0.9
BETA2 = 0.999
ADAM_EPS = 1e-08
DECAY = 0.1
ROPE_BASE = 10000.0

MIB = 1 << 20
NT = (((1,), (1,)), ((), ()))
TN = (((0,), (0,)), ((), ()))
F32 = jnp.float32
BF16 = jnp.bfloat16
MESH = pl.DeviceIdType.MESH


def dot(left, right, dims=(((1,), (0,)), ((), ())), **kw):
    return lax.dot_general(left, right, dims, preferred_element_type=F32, **kw)


def swap(array, bit):
    size = lax.axis_size("head")
    return lax.ppermute(array, "head", [(i, i ^ bit) for i in range(size)])


def split_rows(array, count):
    size = array.shape[0] // count
    return [array[i * size : (i + 1) * size] for i in range(count)]


class Gather:
    def __init__(self, own, parts=1):
        parts = parts if own.shape[0] % 512 == 0 else 1
        self.own = own
        self.mate = swap(own, 1)
        self.far = [swap(part, 2) for part in split_rows(own, parts)]
        self.far_mate = None

    def pieces(self):
        if self.far_mate is None:
            self.far_mate = [swap(part, 1) for part in self.far]
        return [self.own, self.mate, *self.far, *self.far_mate]

    def mate_first(self):
        own, mate, *rest = self.pieces()
        count = len(self.far)
        return [mate, *rest[count:], own, *rest[:count]]


class Reduce:
    def __init__(self, keep, received, parts=1):
        rows = keep.shape[0] // 2
        parts = parts if rows % 512 == 0 else 1
        total = keep.astype(F32) + received.astype(F32)
        self.near = keep[:rows].astype(F32) + received[:rows].astype(F32)
        self.sent = [part.astype(BF16) for part in split_rows(total[rows:], parts)]
        self.send()

    def send(self, *others):
        self.across = [swap(part, 2) for part in after(self.sent, *others)]

    def value(self):
        return self.near + jnp.concatenate(self.across).astype(F32)


def after(value, *others):
    return lax.optimization_barrier((value, *others))[0]


def together(result, *slots):
    values = lax.optimization_barrier((result, *[array[i] for array, i in slots]))
    for (array, i), value in zip(slots, values[1:]):
        array[i] = value
    return values[0]


def slots_of(array, *wanted):
    return [(array, i) for i in (wanted or range(len(array))) if i < len(array)]


def row_major(array):
    return with_layout_constraint(array, Layout(tuple(range(array.ndim))))


def butterfly(array):
    for axis in ("head", "ctx", "dp"):
        size = lax.axis_size(axis)
        bit = 1
        while bit < size:
            array = array + lax.ppermute(array, axis, [(i, i ^ bit) for i in range(size)])
            bit *= 2
    return array


def chunk_specs(tile, pieces):
    specs, start = [], 0
    for piece in pieces:
        count = piece.shape[0] // tile
        specs.append(
            pl.BlockSpec(
                (tile, piece.shape[1]),
                lambda i, *_, a=start, n=count: (jnp.clip(i - a, 0, n - 1), 0),
            )
        )
        start += count
    return specs


def chunk_ends(tile, pieces):
    ends, start = [], 0
    for piece in pieces:
        start += piece.shape[0] // tile
        ends.append(start)
    return ends


def pick(refs, ends, out_ref):
    index = pl.program_id(0)
    start = 0
    for ref, end in zip(refs, ends):

        @pl.when((index >= start) & (index < end))
        def _(ref=ref):
            out_ref[...] = ref[...]

        start = end


def row_spec(tile, width):
    return pl.BlockSpec((tile, width), lambda i, *_: (i, 0))


def whole_spec(shape):
    return pl.BlockSpec(shape, lambda i, *_: (0,) * len(shape))


def mate_first_spec(tile, per, width):
    return pl.BlockSpec(
        (tile, width), lambda i, *_: ((2 * (i // per) + 1) % 5 * per + i % per, 0)
    )


def exchange_specs(tile, per, width):
    half = 2 * per
    return [
        pl.BlockSpec((tile, width), lambda i, *_: (i // half * (i - half), 0)),
        pl.BlockSpec(memory_space=pl.ANY),
    ]


def exchange_shapes(rows, width):
    return [jax.ShapeDtypeStruct((rows // 2, width), BF16)] * 2


def exchange_scratch(tile, per, width):
    half = 2 * per
    return [
        pltpu.VMEM((half, tile, width), BF16),
        pltpu.SemaphoreType.DMA((half,)),
        pltpu.SemaphoreType.DMA((half,)),
    ]


def mate_index():
    me = lax.axis_index("head")
    return me + 1 - 2 * (me % 2)


def meet_mate():
    @pl.when(pl.program_id(0) == 0)
    def _():
        barrier = pltpu.get_barrier_semaphore()
        pl.semaphore_signal(
            barrier, inc=1, device_id={"head": mate_index()}, device_id_type=MESH
        )
        pl.semaphore_wait(barrier, 1)


def exchange(value, per, keep_ref, received_ref, sent_sc, send_sem, recv_sem):
    step = pl.program_id(0)
    half = 2 * per
    tile = value.shape[0]

    def copy(slot):
        return pltpu.make_async_remote_copy(
            src_ref=sent_sc.at[slot],
            dst_ref=received_ref.at[pl.ds(pl.multiple_of(slot * tile, tile), tile)],
            send_sem=send_sem.at[slot],
            recv_sem=recv_sem.at[slot],
            device_id={"head": mate_index()},
            device_id_type=MESH,
        )

    @pl.when(step < half)
    def _():
        sent_sc[step] = value
        copy(step).start()

    @pl.when(step >= half)
    def _():
        keep_ref[...] = value

    @pl.when(step == 2 * half - 1)
    def _():
        for slot in range(half):
            copy(slot).wait()


def cost(flops, moved, transcendentals=0):
    return pl.CostEstimate(
        flops=int(flops), bytes_accessed=int(moved), transcendentals=int(transcendentals)
    )


def turn(values, cos_table, sin_table, low_half, sign):
    ahead = pltpu.roll(values, VD - HD // 2, 1)
    behind = pltpu.roll(values, HD // 2, 1)
    rotated = jnp.where(low_half, -ahead, behind)
    return values * cos_table + sign * rotated * sin_table


def low_half_mask(rows):
    lane = lax.broadcasted_iota(jnp.int32, (rows, VD), 1)
    return (lane % HD) < HD // 2


def side_by_side(w_refs):
    return jnp.concatenate(
        [w_ref[item] for w_ref in w_refs for item in range(w_ref.shape[0])], axis=1
    )


def project_kernel(*refs, heads, ends):
    count = len(ends)
    chunks, w_refs, refs = refs[:count], refs[count : count + heads], refs[count + heads :]
    cos_ref, sin_ref, refs = refs[0], refs[1], refs[2:]
    if count > 1:
        x_ref, refs = refs[0], refs[1:]
        pick(chunks, ends, x_ref)
    else:
        x_ref = chunks[0]
    q_refs, kv_refs = refs[:heads], refs[heads:]
    mask = low_half_mask(x_ref.shape[0])
    cos_table, sin_table = cos_ref[...], sin_ref[...]
    out = dot(x_ref[...], side_by_side(w_refs))
    for head in range(heads):
        base = head * 3 * VD
        query = turn(out[:, base : base + VD], cos_table, sin_table, mask, 1.0) * SCALE
        key = turn(out[:, base + VD : base + 2 * VD], cos_table, sin_table, mask, 1.0)
        q_refs[head][...] = query.astype(BF16)
        kv_refs[head][:, :VD] = key.astype(BF16)
        kv_refs[head][:, VD:] = out[:, base + 2 * VD : base + 3 * VD].astype(BF16)


def project(chunks, weights, cos_table, sin_table):
    rows = cos_table.shape[0]
    heads = len(weights)
    tile = min(256, rows // 4)
    gathered = len(chunks) > 1
    out = pl.pallas_call(
        functools.partial(project_kernel, heads=heads, ends=chunk_ends(tile, chunks)),
        grid=(rows // tile,),
        in_specs=chunk_specs(tile, chunks)
        + [whole_spec(weight.shape) for weight in weights]
        + [row_spec(tile, VD), row_spec(tile, VD)],
        out_specs=[row_spec(tile, D)] * gathered
        + [row_spec(tile, VD)] * heads
        + [row_spec(tile, 2 * VD)] * heads,
        out_shape=[jax.ShapeDtypeStruct((rows, D), BF16)] * gathered
        + [jax.ShapeDtypeStruct((rows, VD), BF16)] * heads
        + [jax.ShapeDtypeStruct((rows, 2 * VD), BF16)] * heads,
        compiler_params=pltpu.CompilerParams(vmem_limit_bytes=60 * MIB),
        cost_estimate=cost(
            6 * rows * D * heads * VD, 2 * (2 * rows * D + 3 * heads * VD * (D + rows))
        ),
        name="project",
    )(*chunks, *weights, cos_table, sin_table)
    x = out[0] if gathered else chunks[0]
    out = out[gathered:]
    return x, out[:heads], out[heads:]


def unproject_kernel(*refs, heads, per):
    dq_refs, own_refs, recv_refs = refs[:heads], refs[heads : 2 * heads], refs[2 * heads : 3 * heads]
    w_refs, refs = refs[3 * heads : 4 * heads], refs[4 * heads :]
    cos_ref, sin_ref, gp_ref, keep_ref, received_ref, *scratch = refs
    meet_mate()
    mask = low_half_mask(gp_ref.shape[0])
    cos_table, sin_table = cos_ref[...], sin_ref[...]
    for head in range(heads):
        base = head * 3 * VD
        both = own_refs[head][...].astype(F32) + recv_refs[head][...].astype(F32)
        query = dq_refs[head][...].astype(F32)
        gp_ref[:, base : base + VD] = turn(query, cos_table, sin_table, mask, -1.0).astype(BF16)
        gp_ref[:, base + VD : base + 2 * VD] = turn(
            both[:, :VD], cos_table, sin_table, mask, -1.0
        ).astype(BF16)
        gp_ref[:, base + 2 * VD : base + 3 * VD] = both[:, VD:].astype(BF16)
    value = dot(gp_ref[...], side_by_side(w_refs), NT).astype(BF16)
    exchange(value, per, keep_ref, received_ref, *scratch)


def unproject(dq, dkv_own, dkv_recv, weights, cos_table, sin_table):
    rows = dq[0].shape[0]
    heads = len(dq)
    tile = min(256, rows // 4)
    per = rows // 4 // tile
    return pl.pallas_call(
        functools.partial(unproject_kernel, heads=heads, per=per),
        grid=(rows // tile,),
        in_specs=[mate_first_spec(tile, per, VD)] * heads
        + [mate_first_spec(tile, per, 2 * VD)] * (2 * heads)
        + [*[whole_spec(weight.shape) for weight in weights], mate_first_spec(tile, per, VD), mate_first_spec(tile, per, VD)],
        out_specs=[mate_first_spec(tile, per, heads * 3 * VD)] + exchange_specs(tile, per, D),
        scratch_shapes=exchange_scratch(tile, per, D),
        out_shape=[jax.ShapeDtypeStruct((rows, heads * 3 * VD), BF16)] + exchange_shapes(rows, D),
        compiler_params=pltpu.CompilerParams(
            vmem_limit_bytes=60 * MIB, collective_id=3, has_side_effects=True
        ),
        cost_estimate=cost(
            6 * rows * D * heads * VD,
            2 * (rows * D + 3 * D * heads * VD + 9 * rows * heads * VD),
        ),
        name="unproject",
    )(*dq, *dkv_own, *dkv_recv, *weights, cos_table, sin_table)


def output_kernel(*refs, heads, per):
    attn_refs = refs[:heads]
    w_ref, all_ref, keep_ref, received_ref, *scratch = refs[heads:]
    meet_mate()
    for head in range(heads):
        all_ref[:, head * VD : (head + 1) * VD] = attn_refs[head][...]
    value = dot(all_ref[...], w_ref[...], NT).astype(BF16)
    exchange(value, per, keep_ref, received_ref, *scratch)


def output_projection(attn, weight):
    rows = attn[0].shape[0]
    heads = len(attn)
    tile = min(256, rows // 4)
    per = rows // 4 // tile
    return pl.pallas_call(
        functools.partial(output_kernel, heads=heads, per=per),
        grid=(rows // tile,),
        in_specs=[mate_first_spec(tile, per, VD)] * heads + [whole_spec(weight.shape)],
        out_specs=[mate_first_spec(tile, per, heads * VD)] + exchange_specs(tile, per, D),
        scratch_shapes=exchange_scratch(tile, per, D),
        out_shape=[jax.ShapeDtypeStruct((rows, heads * VD), BF16)] + exchange_shapes(rows, D),
        compiler_params=pltpu.CompilerParams(
            vmem_limit_bytes=40 * MIB, collective_id=1, has_side_effects=True
        ),
        cost_estimate=cost(
            2 * rows * D * weight.shape[1], 2 * (rows * D + weight.size + 2 * rows * heads * VD)
        ),
        name="output_projection",
    )(*attn, weight)


def gate_kernel(*refs, ends, cot_ends):
    count, cot_count = len(ends), len(cot_ends)
    chunks, cot_chunks = refs[:count], refs[count : count + cot_count]
    w_ref, x_ref, cot_ref, hidden_ref, by_gate_ref, by_up_ref = refs[count + cot_count :]
    pick(chunks, ends, x_ref)
    pick(cot_chunks, cot_ends, cot_ref)
    width = hidden_ref.shape[1]
    step = min(512, width)
    x = x_ref[...]
    for base in range(0, width, step):
        cols = slice(base, base + step)
        gate = dot(x, w_ref[:, cols])
        up = dot(x, w_ref[:, width + base : width + base + step])
        share = jax.nn.sigmoid(gate)
        swish = gate * share
        hidden_ref[:, cols] = (swish * up).astype(BF16)
        by_gate_ref[:, cols] = (up * share * (1.0 + gate * (1.0 - share))).astype(BF16)
        by_up_ref[:, cols] = swish.astype(BF16)


def gate_up(chunks, cot_chunks, weights, width):
    own_rows = chunks[0].shape[0]
    rows = 4 * own_rows
    tile = min(256, own_rows)
    return pl.pallas_call(
        functools.partial(
            gate_kernel, ends=chunk_ends(tile, chunks), cot_ends=chunk_ends(tile, cot_chunks)
        ),
        grid=(rows // tile,),
        in_specs=chunk_specs(tile, chunks)
        + chunk_specs(tile, cot_chunks)
        + [whole_spec(weights.shape)],
        out_specs=[row_spec(tile, D)] * 2 + [row_spec(tile, width)] * 3,
        out_shape=[jax.ShapeDtypeStruct((rows, D), BF16)] * 2
        + [jax.ShapeDtypeStruct((rows, width), BF16)] * 3,
        compiler_params=pltpu.CompilerParams(vmem_limit_bytes=60 * MIB),
        cost_estimate=cost(
            4 * rows * D * width, 2 * (4 * rows * D + 2 * D * width + 3 * rows * width)
        ),
        name="gate_up",
    )(*chunks, *cot_chunks, weights)


def feed_kernel(
    cot_ref,
    hidden_ref,
    by_gate_ref,
    by_up_ref,
    down_ref,
    inner_ref,
    grad_ref,
    ffn_keep,
    ffn_received,
    mid_keep,
    mid_received,
    *scratch,
    per,
):
    meet_mate()
    width = hidden_ref.shape[1]
    grad_hidden = dot(cot_ref[...], down_ref[...])
    grad_ref[:, :width] = (grad_hidden * by_gate_ref[...].astype(F32)).astype(BF16)
    grad_ref[:, width:] = (grad_hidden * by_up_ref[...].astype(F32)).astype(BF16)
    middle = dot(grad_ref[...], inner_ref[...], NT).astype(BF16)
    exchange(middle, per, mid_keep, mid_received, *scratch[3:])
    output = dot(hidden_ref[...], down_ref[...], NT).astype(BF16)
    exchange(output, per, ffn_keep, ffn_received, *scratch[:3])


def feed(cot, hidden, by_gate, by_up, down, inner):
    rows, width = hidden.shape
    tile = min(256, rows // 4)
    per = rows // 4 // tile
    return pl.pallas_call(
        functools.partial(feed_kernel, per=per),
        grid=(rows // tile,),
        in_specs=[row_spec(tile, D)]
        + [row_spec(tile, width)] * 3
        + [whole_spec(down.shape), whole_spec(inner.shape)],
        out_specs=[row_spec(tile, 2 * width)]
        + exchange_specs(tile, per, D)
        + exchange_specs(tile, per, D),
        out_shape=[jax.ShapeDtypeStruct((rows, 2 * width), BF16)]
        + exchange_shapes(rows, D)
        + exchange_shapes(rows, D),
        scratch_shapes=exchange_scratch(tile, per, D) + exchange_scratch(tile, per, D),
        compiler_params=pltpu.CompilerParams(
            vmem_limit_bytes=60 * MIB, collective_id=2, has_side_effects=True
        ),
        cost_estimate=cost(
            8 * rows * D * width, 2 * (3 * rows * D + 3 * D * width + 5 * rows * width)
        ),
        name="feed",
    )(cot, hidden, by_gate, by_up, down, inner)


class Plan:
    def __init__(self, own_rows, block_len, prev_rows, ndoc):
        self.own_rows = own_rows
        self.block_len = block_len
        self.prev_rows = prev_rows
        self.ndoc = ndoc
        self.bq = min(256, own_rows)
        self.bk = min(512, own_rows)
        self.total = prev_rows + block_len

    def doc_start(self, info, pos):
        start = jnp.zeros_like(pos)
        for item in range(self.ndoc):
            start = jnp.where(pos >= info[2 + item], info[2 + item], start)
        return start

    def query_start(self, info, index):
        per = self.own_rows // self.bq
        chunk = (index // per) ^ info[0]
        return info[1] * self.block_len + chunk * self.own_rows + (index % per) * self.bq

    def key_row(self, info, index):
        per = self.own_rows // self.bk
        blocks = self.block_len // self.bk
        owner = index // blocks
        local = index % blocks
        inside = (((local // per) ^ info[0]) * per + local % per) * self.bk
        base = jnp.where(owner == info[1], self.prev_rows, owner * self.block_len)
        return pl.multiple_of(base + inside, self.bk)

    def ranges(self, info, start):
        last = start + self.bq - 1
        low = self.doc_start(info, start) // self.bk
        high = last // self.bk + 1
        open_from = (self.doc_start(info, last) + self.bk - 1) // self.bk
        first = jnp.minimum(jnp.maximum(open_from, low), high)
        until = jnp.maximum(first, jnp.minimum((start + 1) // self.bk, high))
        return low, first, until, high


def in_groups(low, high, size, visit):
    count = (high - low) // size

    @pl.loop(0, count)
    def _(group):
        visit(*[low + group * size + item for item in range(size)])

    if size > 1:

        @pl.loop(low + count * size, high)
        def _(index):
            visit(index)


def split_halves(q):
    lane = lax.broadcasted_iota(jnp.int32, q.shape, 1)
    zero = jnp.zeros_like(q)
    return jnp.concatenate([jnp.where(lane < HD, q, zero), jnp.where(lane >= HD, q, zero)], axis=0)


def in_lanes(value):
    high = value.astype(BF16)
    rest = value - high.astype(F32)
    middle = rest.astype(BF16)
    low = (rest - middle.astype(F32)).astype(BF16)
    lane = lax.broadcasted_iota(jnp.int32, value.shape, 1)
    zero = jnp.zeros_like(high)
    return jnp.where(
        lane == 0, high, jnp.where(lane == 1, middle, jnp.where(lane == 2, low, zero))
    )


def load_keys(plan, info, own_ref, prev_ref, kv_sc):
    @pl.when(pl.program_id(0) == 0)
    def _():
        kv_sc[plan.prev_rows :, :] = own_ref[...]

        @pl.when(info[1] > 0)
        def _():
            kv_sc[: plan.prev_rows, :] = prev_ref[...]


def forward_kernel(
    info,
    lam_ref,
    gain_ref,
    q_ref,
    own_ref,
    prev_ref,
    attn_ref,
    first_ref,
    second_ref,
    lse_ref,
    kv_sc,
    m_sc,
    l_sc,
    acc_sc,
    *,
    plan,
):
    bq, bk = plan.bq, plan.bk
    load_keys(plan, info, own_ref, prev_ref, kv_sc)
    start = plan.query_start(info, pl.program_id(0))
    q2 = split_halves(q_ref[...])
    m_sc[...] = jnp.full_like(m_sc, NEG)
    l_sc[...] = jnp.zeros_like(l_sc)
    acc_sc[...] = jnp.zeros_like(acc_sc)
    low, first, until, high = plan.ranges(info, start)

    def visit(index, masked):
        row = plan.key_row(info, index)
        key = kv_sc[pl.ds(row, bk), :VD]
        value = kv_sc[pl.ds(row, bk), VD:]
        scores = dot(q2, key, NT)
        if masked:
            query_pos = start + lax.broadcasted_iota(jnp.int32, (bq, 1), 0)
            begin = plan.doc_start(info, query_pos)
            key_pos = index * bk + lax.broadcasted_iota(jnp.int32, (bq, bk), 1)
            keep = (key_pos <= query_pos) & (key_pos >= begin)
            scores = jnp.concatenate(
                [jnp.where(keep, scores[:bq], NEG), jnp.where(keep, scores[bq:], NEG)], axis=0
            )
        before = m_sc[...]
        after = jnp.maximum(before, jnp.max(scores, axis=1, keepdims=True))
        weights = jnp.exp(scores - jnp.tile(after, (1, bk // VD)))
        factor = jnp.exp(before - after)
        m_sc[...] = after
        l_sc[...] = l_sc[...] * factor + jnp.sum(weights, axis=1, keepdims=True)
        acc_sc[...] = acc_sc[...] * factor + dot(weights.astype(BF16), value)

    @pl.loop(low, first)
    def _(index):
        visit(index, True)

    @pl.loop(first, until)
    def _(index):
        visit(index, False)

    @pl.loop(until, high)
    def _(index):
        visit(index, True)

    total = l_sc[...]
    maps = acc_sc[...] * (1.0 / total)
    first_map, second_map = maps[:bq], maps[bq:]
    first_ref[...] = first_map
    second_ref[...] = second_map
    difference = first_map - lam_ref[0] * second_map
    scaling = lax.rsqrt(jnp.mean(difference * difference, axis=1, keepdims=True) + EPS)
    attn_ref[...] = (difference * scaling * gain_ref[...]).astype(BF16)
    lanes = in_lanes(-(m_sc[...] + jnp.log(total)))
    lse_ref[:, :VD] = lanes[:bq]
    lse_ref[:, VD:] = lanes[bq:]


def attention_cost(plan, per_pair, extra=0):
    pairs = plan.block_len * plan.block_len * 5 // 8
    return cost(pairs * per_pair + extra, plan.block_len * VD * 32, 2 * pairs)


def attend_forward(plan, info, lam, gain, q, kv_own, kv_prev):
    rows, bq = plan.block_len, plan.bq
    grid_spec = pltpu.PrefetchScalarGridSpec(
        num_scalar_prefetch=1,
        grid=(rows // bq,),
        in_specs=[
            pl.BlockSpec(memory_space=pltpu.SMEM),
            whole_spec((1, VD)),
            row_spec(bq, VD),
            whole_spec((rows, 2 * VD)),
            whole_spec((plan.prev_rows, 2 * VD)),
        ],
        out_specs=[row_spec(bq, VD)] * 3 + [row_spec(bq, 2 * VD)],
        scratch_shapes=[
            pltpu.VMEM((plan.total, 2 * VD), BF16),
            pltpu.VMEM((2 * bq, VD), F32),
            pltpu.VMEM((2 * bq, VD), F32),
            pltpu.VMEM((2 * bq, VD), F32),
        ],
    )
    return pl.pallas_call(
        functools.partial(forward_kernel, plan=plan),
        grid_spec=grid_spec,
        out_shape=[
            jax.ShapeDtypeStruct((rows, VD), BF16),
            jax.ShapeDtypeStruct((rows, VD), F32),
            jax.ShapeDtypeStruct((rows, VD), F32),
            jax.ShapeDtypeStruct((rows, 2 * VD), BF16),
        ],
        compiler_params=pltpu.CompilerParams(vmem_limit_bytes=60 * MIB),
        cost_estimate=attention_cost(plan, 6 * VD),
        name="attend_forward",
    )(info, lam, gain, q, kv_own, kv_prev)


def difference_kernel(lam_ref, gain_ref, w_ref, *refs, heads, ends):
    count = len(ends)
    chunks, refs = refs[:count], refs[count:]
    first_refs, second_refs, refs = refs[:heads], refs[heads : 2 * heads], refs[2 * heads :]
    gm_ref, sums_ref, grad_refs = refs[0], refs[1], refs[2:]
    lam = lam_ref[0]

    @pl.when(pl.program_id(0) == 0)
    def _():
        sums_ref[...] = jnp.zeros_like(sums_ref)

    pick(chunks, ends, gm_ref)
    upstream_all = dot(gm_ref[...], w_ref[...])
    for head in range(heads):
        upstream = upstream_all[:, head * VD : (head + 1) * VD]
        first_map, second_map = first_refs[head][...], second_refs[head][...]
        difference = first_map - lam * second_map
        scaling = lax.rsqrt(jnp.mean(difference * difference, axis=1, keepdims=True) + EPS)
        normal = difference * scaling
        weighted = upstream * gain_ref[...]
        inner_mean = jnp.mean(weighted * normal, axis=1, keepdims=True)
        grad = (scaling * (weighted - normal * inner_mean)).astype(BF16)
        grad_wide = grad.astype(F32)
        first_product, second_product = grad_wide * first_map, grad_wide * second_map
        sums_ref[0:1, :] += jnp.sum(upstream * normal, axis=0, keepdims=True)
        sums_ref[1:2, :] += jnp.sum(second_product, axis=0, keepdims=True)
        out = grad_refs[head]
        out[:, :VD] = grad
        for item, product in enumerate((first_product, second_product)):
            total = jnp.sum(product, axis=1, keepdims=True)
            out[:, (item + 1) * VD : (item + 2) * VD] = in_lanes(
                jnp.broadcast_to(-total, product.shape)
            )


def difference_grads(lam, gain, weight, gm, first, second):
    own_rows = gm[0].shape[0]
    rows = 4 * own_rows
    heads = len(first)
    tile = min(256, own_rows)
    return pl.pallas_call(
        functools.partial(difference_kernel, heads=heads, ends=chunk_ends(tile, gm)),
        grid=(rows // tile,),
        in_specs=[pl.BlockSpec(memory_space=pltpu.SMEM), whole_spec((1, VD)), whole_spec(weight.shape)]
        + chunk_specs(tile, gm)
        + [row_spec(tile, VD)] * (2 * heads),
        out_specs=[row_spec(tile, D), whole_spec((8, VD))] + [row_spec(tile, 3 * VD)] * heads,
        out_shape=[jax.ShapeDtypeStruct((rows, D), BF16), jax.ShapeDtypeStruct((8, VD), F32)]
        + [jax.ShapeDtypeStruct((rows, 3 * VD), BF16)] * heads,
        compiler_params=pltpu.CompilerParams(vmem_limit_bytes=60 * MIB),
        cost_estimate=cost(2 * rows * D * heads * VD, 4 * rows * D + 14 * rows * heads * VD),
        name="difference_grads",
    )(lam, gain, weight, *gm, *first, *second)


def backward_kernel(
    info,
    lam_ref,
    q_ref,
    own_ref,
    prev_ref,
    lse_ref,
    grad_ref,
    dq_ref,
    dkv_own_ref,
    dkv_prev_ref,
    kv_sc,
    dk_sc,
    dv_sc,
    dqt_sc,
    *,
    plan,
):
    bq, bk = plan.bq, plan.bk
    step = pl.program_id(0)
    lam = lam_ref[0]

    @pl.when(step == 0)
    def _():
        lane = lax.broadcasted_iota(jnp.int32, (bk, VD), 1)
        ones = jnp.where(lane < 3, 1.0, 0.0).astype(BF16)

        def fill(source, base, rows):
            for start in range(0, rows, bk):
                to = slice(base + start, base + start + bk)
                kv_sc[to, :VD] = source[start : start + bk, :VD]
                kv_sc[to, VD : 2 * VD] = ones
                kv_sc[to, 2 * VD :] = source[start : start + bk, VD:]

        fill(own_ref, plan.prev_rows, plan.block_len)

        @pl.when(info[1] > 0)
        def _():
            fill(prev_ref, 0, plan.prev_rows)

        dk_sc[...] = jnp.zeros_like(dk_sc)
        dv_sc[...] = jnp.zeros_like(dv_sc)

    grad = grad_ref[:, :VD]
    start = plan.query_start(info, step)
    q2 = split_halves(q_ref[...])
    q_wide = jnp.concatenate(
        [q2, jnp.concatenate([lse_ref[:, :VD], lse_ref[:, VD:]], axis=0)], axis=1
    )
    ones = jnp.ones((8, VD), BF16)
    delta_first = dot(ones, grad_ref[:, VD : 2 * VD], NT)[0:1]
    delta_second = dot(ones, grad_ref[:, 2 * VD :], NT)[0:1]
    dqt_sc[...] = jnp.zeros_like(dqt_sc)
    low, _, _, high = plan.ranges(info, start)

    query_pos = start + lax.broadcasted_iota(jnp.int32, (1, bq), 1)
    begin = plan.doc_start(info, query_pos)

    def visit(*indices):
        results = []
        for index in indices:
            row = plan.key_row(info, index)
            key = kv_sc[pl.ds(row, bk), :VD]
            prob = jnp.exp(dot(kv_sc[pl.ds(row, bk), : 2 * VD], q_wide, NT))
            base = dot(kv_sc[pl.ds(row, bk), 2 * VD :], grad, NT)
            key_pos = index * bk + lax.broadcasted_iota(jnp.int32, (bk, bq), 0)
            keep = (key_pos <= query_pos) & (key_pos >= begin)
            prob_first = jnp.where(keep, prob[:, :bq], 0.0)
            prob_second = jnp.where(keep, prob[:, bq:], 0.0)
            raw = jnp.concatenate(
                [
                    (prob_first * (base + delta_first)).astype(BF16),
                    (prob_second * (base + delta_second)).astype(BF16),
                ],
                axis=1,
            )
            value_grad = dot((prob_first - lam * prob_second).astype(BF16), grad)
            results.append((row, value_grad, dot(raw, q2), dot(key, raw, TN)))
        for row, value_grad, key_grad, query_grad in results:
            dv_sc[pl.ds(row, bk), :] += value_grad
            dk_sc[pl.ds(row, bk), :] += key_grad
        dqt_sc[...] += sum(result[3] for result in results)

    in_groups(low, high, 2, visit)

    dq_t = jnp.concatenate([dqt_sc[:HD, :bq], -lam * dqt_sc[HD:, bq:]], axis=0) * SCALE
    dq_ref[...] = dq_t.T.astype(BF16)

    @pl.when(step == pl.num_programs(0) - 1)
    def _():
        lane = lax.broadcasted_iota(jnp.int32, (1, VD), 1)
        side = jnp.where(lane < HD, 1.0, -lam)
        dkv_own_ref[:, :VD] = (dk_sc[plan.prev_rows :, :] * side).astype(BF16)
        dkv_own_ref[:, VD:] = dv_sc[plan.prev_rows :, :].astype(BF16)
        dkv_prev_ref[:, :VD] = (dk_sc[: plan.prev_rows, :] * side).astype(BF16)
        dkv_prev_ref[:, VD:] = dv_sc[: plan.prev_rows, :].astype(BF16)


def attend_backward(plan, info, lam, q, kv_own, kv_prev, lse, grad):
    rows, bq = plan.block_len, plan.bq
    grid_spec = pltpu.PrefetchScalarGridSpec(
        num_scalar_prefetch=1,
        grid=(rows // bq,),
        in_specs=[
            pl.BlockSpec(memory_space=pltpu.SMEM),
            row_spec(bq, VD),
            whole_spec((rows, 2 * VD)),
            whole_spec((plan.prev_rows, 2 * VD)),
            row_spec(bq, 2 * VD),
            row_spec(bq, 3 * VD),
        ],
        out_specs=[
            row_spec(bq, VD),
            whole_spec((rows, 2 * VD)),
            whole_spec((plan.prev_rows, 2 * VD)),
        ],
        scratch_shapes=[
            pltpu.VMEM((plan.total, 3 * VD), BF16),
            pltpu.VMEM((plan.total, VD), F32),
            pltpu.VMEM((plan.total, VD), F32),
            pltpu.VMEM((VD, 2 * bq), F32),
        ],
    )
    return pl.pallas_call(
        functools.partial(backward_kernel, plan=plan),
        grid_spec=grid_spec,
        out_shape=[
            jax.ShapeDtypeStruct((rows, VD), BF16),
            jax.ShapeDtypeStruct((rows, 2 * VD), BF16),
            jax.ShapeDtypeStruct((plan.prev_rows, 2 * VD), BF16),
        ],
        compiler_params=pltpu.CompilerParams(vmem_limit_bytes=60 * MIB),
        cost_estimate=attention_cost(plan, 16 * VD),
        name="attend_backward",
    )(info, lam, q, kv_own, kv_prev, lse, grad)


def norm_forward(values, gain_vec):
    scaling = lax.rsqrt(jnp.mean(values * values, axis=-1, keepdims=True) + EPS)
    return (values * scaling * gain_vec, scaling)


def norm_backward(values, scaling, gain_vec, upstream):
    normal = values * scaling
    weighted = upstream * gain_vec
    inner_mean = jnp.mean(weighted * normal, axis=-1, keepdims=True)
    return (scaling * (weighted - normal * inner_mean), jnp.sum(upstream * normal, axis=0))


def adamw(parameter, momentum, variance, gradient, learn_rate, decay_rate):
    momentum = BETA1 * momentum + (1.0 - BETA1) * gradient
    variance = BETA2 * variance + (1.0 - BETA2) * gradient * gradient
    corrected = momentum / (1.0 - BETA1**STEP)
    spread = jnp.sqrt(variance / (1.0 - BETA2**STEP))
    return (
        parameter - learn_rate * (corrected / (spread + ADAM_EPS) + decay_rate * parameter),
        momentum,
        variance,
    )


def send_keys(kv, ctx_count):
    if ctx_count == 2:
        return lax.ppermute(kv, "ctx", [(0, 1)])
    return lax.all_gather(kv, "ctx", axis=0, tiled=True)


def return_keys(grads, ctx_count):
    if ctx_count == 2:
        return lax.ppermute(grads, "ctx", [(1, 0)])
    return lax.psum_scatter(grads, "ctx", scatter_dimension=0, tiled=True)


def scatter_weight(grad, *others):
    grad = after(grad.astype(BF16), *others)
    return lax.psum_scatter(grad, "dp", scatter_dimension=0, tiled=True)


def sum_blocks(share, ctx_count):
    if ctx_count == 2:
        other = lax.ppermute(share, "ctx", [(0, 1), (1, 0)])
        return share.astype(F32) + other.astype(F32)
    return lax.psum(share, "ctx").astype(F32)


def on_device(
    tokens,
    cotangent,
    doc_lengths,
    qkv_weight,
    out_weight,
    inner_weight,
    down_weight,
    norm_gains,
    head_gain,
    lambdas,
    qkv_momentum,
    out_momentum,
    inner_momentum,
    down_momentum,
    norm_momentum,
    head_momentum,
    lambda_momentum,
    qkv_variance,
    out_variance,
    inner_variance,
    down_variance,
    norm_variance,
    head_variance,
    lambda_variance,
):
    micro_count, own_rows, _ = tokens.shape
    head_count = lax.axis_size("head")
    ctx_count = lax.axis_size("ctx")
    block_len = own_rows * head_count
    seq_len = block_len * ctx_count
    ctx_index = lax.axis_index("ctx")
    head_index = lax.axis_index("head")
    local_heads = qkv_weight.shape[1]
    ff_local = inner_weight.shape[2]
    ndoc = doc_lengths.shape[1]
    plan = Plan(own_rows, block_len, block_len if ctx_count == 2 else seq_len, ndoc)

    def gather_weight(shard):
        return lax.all_gather(shard.astype(BF16), "dp", axis=0, tiled=True)

    def by_part(array):
        return array.transpose(1, 2, 0, 3)

    qkv_parts = row_major(by_part(qkv_weight).astype(BF16))
    qkv_low = [
        lax.all_gather(qkv_parts[h], "dp", axis=1, tiled=True) for h in range(local_heads)
    ]
    out_t = gather_weight(row_major(out_weight.astype(BF16).reshape(local_heads * VD, -1).T))
    inner_low = gather_weight(inner_weight.reshape(-1, 2 * ff_local))
    down_shard = row_major(down_weight.astype(BF16).T)
    down_t = gather_weight(down_shard)

    first_exp = jnp.exp(jnp.sum(lambdas[0] * lambdas[1]))
    second_exp = jnp.exp(jnp.sum(lambdas[2] * lambdas[3]))
    lambda_value = first_exp - second_exp + LAMBDA_INIT
    lam = lambda_value.reshape(1)
    head_scale = (head_gain * (1.0 - LAMBDA_INIT)).reshape(1, VD)

    chunk = jnp.arange(block_len, dtype=jnp.int32) // own_rows
    position = (
        ctx_index * block_len
        + (chunk ^ head_index) * own_rows
        + jnp.arange(block_len, dtype=jnp.int32) % own_rows
    )
    frequency = ROPE_BASE ** (
        -(jnp.arange(VD, dtype=jnp.int32) % (HD // 2)).astype(F32) / (HD // 2)
    )

    def info_of(micro):
        bounds = jnp.cumsum(doc_lengths[micro], dtype=jnp.int32)
        return jnp.concatenate([jnp.stack([head_index, ctx_index]).astype(jnp.int32), bounds])

    micros = range(micro_count)
    heads = range(local_heads)
    infos = [info_of(m) for m in micros]
    own, normed_own, normed, cot_own = [], [], [], []
    for m in micros:
        rows, cot_rows = tokens[m], cotangent[m]
        if m > 0:
            rows = after(rows, normed[0].own)
        own.append(rows.astype(F32))
        normed_own.append(norm_forward(own[m], norm_gains[0]))
        cot_own.append(cot_rows)
        normed.append(Gather(normed_own[m][0].astype(BF16), 2 if m else 1))
    position = after(position, normed[-1].own, down_shard)
    phases = position.astype(F32)[:, None] * frequency[None, :]
    cos_table, sin_table = jnp.cos(phases), jnp.sin(phases)

    normed_all, q, kv, kv_prev, cot = [], [], [], [], []

    def keep_projected(m, result):
        if len(q) == m:
            normed_all.append(result[0])
            q.append([])
            kv.append([])
            kv_prev.append([])
        q[m].extend(result[1])
        kv[m].extend(result[2])
        kv_prev[m].extend([send_keys(part, ctx_count) for part in result[2]])

    for h in heads:
        pieces = normed[0].pieces() if h == 0 else [after(normed_all[0], kv[0][-1])]
        result = project(pieces, qkv_low[h : h + 1], cos_table, sin_table)
        if h == 0:
            result = together(result, *slots_of(normed[1].far, 0))
        elif h == 1:
            result = together(result, *slots_of(normed[1].far, 1))
        keep_projected(0, result)
    cot.append(Gather(after(cot_own[0], *normed[1].far)))

    def attend(m, h, before, beside):
        out = attend_forward(
            plan, infos[m], lam, head_scale, after(q[m][h], *before), kv[m][h], kv_prev[m][h]
        )
        return together(out, *beside)

    mid = []

    def finish_attention(m):
        middle = own[m] + attended[m].value()
        value, scaling = norm_forward(middle, norm_gains[1])
        mid.append((middle, scaling, Gather(value.astype(BF16), 2)))

    maps, attn_all, attended = [], [], []
    for m in micros:
        outs = []
        for h in heads:
            if m == 0:
                before = [kv[0]] if h == 0 else [outs[-1], kv[1], out_t]
                beside = [
                    [],
                    slots_of(cot[-1].far, 0),
                    slots_of(cot[-1].far, 1),
                ][h]
            elif h == 0:
                before = [*attended[0].sent, *cot[0].pieces(), *cot[1].pieces()]
                beside = slots_of(attended[0].across) + slots_of(kv_prev[m], 1)
            else:
                before = [outs[-1], mid[0][2].own]
                beside = slots_of(mid[0][2].far, h - 1) + slots_of(kv_prev[m], h + 1)
            outs.append(attend(m, h, before, beside))
            if m == 0 and h == 0:
                pieces = after(normed[1].pieces(), outs[0])
                result = project(pieces, qkv_low, cos_table, sin_table)
                keep_projected(1, together(result, *slots_of(cot[0].far)))
                cot.append(Gather(after(cot_own[1], *cot[0].far), 2))
            if m > 0 and h == 0:
                finish_attention(0)
        maps.append([out[1:] for out in outs])
        result = output_projection([out[0] for out in outs], out_t)
        if m == 0:
            result = together(result, *slots_of(kv_prev[1], 0))
        attn_all.append(result[0])
        attended.append(Reduce(*result[1:], 2 if m else 1))

    grad_middle, gm, gain_mid = [], [], []

    def finish_feed(m, reduced):
        middle, scaling, _ = mid[m]
        grad_norm, part = norm_backward(middle, scaling, norm_gains[1], reduced.value())
        grad_middle.append((cot_own[m].astype(F32) + grad_norm).astype(BF16))
        gm.append(Gather(grad_middle[m], 2 if m else 1))
        gain_mid.append(part)

    def weight_grad(left, right, before, beside, total=None):
        result = dot(after(left, *before), right, TN)
        if total is not None:
            result = (total + result).astype(BF16)
        return together(result, *beside)

    first_gates = gate_up(
        after(mid[0][2].mate_first(), *attended[1].sent), cot[0].mate_first(), inner_low, ff_local
    )
    first_gates = together(first_gates, *slots_of(attended[1].across, 0))
    first_feed = feed(*first_gates[1:], down_t, inner_low)
    first_feed = together(first_feed, *slots_of(attended[1].across, 1))
    finish_attention(1)
    reduced_mid = [Reduce(*first_feed[3:])]
    grad_inner = weight_grad(
        first_gates[0],
        first_feed[0],
        [mid[1][2].own, *reduced_mid[0].sent],
        slots_of(mid[1][2].far, 0),
    )
    grad_down = weight_grad(
        first_gates[1], first_gates[2], [grad_inner], slots_of(mid[1][2].far, 1)
    )
    reduced_mid[0].send(*mid[1][2].far)
    second_gates = gate_up(
        after(mid[1][2].mate_first(), grad_down), cot[1].mate_first(), inner_low, ff_local
    )
    second_gates = together(second_gates, *slots_of(reduced_mid[0].across))
    finish_feed(0, reduced_mid[0])
    second_feed = feed(after(second_gates[1], gm[0].own), *second_gates[2:], down_t, inner_low)
    second_feed = together(second_feed, *slots_of(gm[0].far))
    reduced_mid.append(Reduce(*second_feed[3:], 2))
    grad_inner = weight_grad(
        second_gates[0],
        second_feed[0],
        reduced_mid[1].sent,
        slots_of(reduced_mid[1].across, 0),
        grad_inner,
    )
    grad_down = weight_grad(
        second_gates[1],
        second_gates[2],
        [grad_inner],
        slots_of(reduced_mid[1].across, 1),
        grad_down,
    )
    feed_grad = jnp.concatenate([grad_inner, grad_down], axis=1)
    feed_part = scatter_weight(row_major(feed_grad))
    finish_feed(1, reduced_mid[1])
    ffn_pairs = [first_feed[1:3], second_feed[1:3]]

    dqs, dkvs, recvs, gm_alls, grads, sums = [], [], [], [], [], 0.0

    def start_back(m, before, beside):
        out = difference_grads(
            lam,
            head_scale,
            out_t,
            after(gm[m].pieces(), *before),
            [part[0] for part in maps[m]],
            [part[1] for part in maps[m]],
        )
        out = together(out, *beside)
        gm_alls.append(out[0])
        grads.append(out[2:])
        dqs.append([])
        dkvs.append([])
        recvs.append([])
        return out[1]

    def attend_back(m, h, before, beside):
        out = attend_backward(
            plan,
            infos[m],
            lam,
            after(q[m][h], *before),
            kv[m][h],
            kv_prev[m][h],
            maps[m][h][2],
            grads[m][h],
        )
        out = together(out, *beside)
        dqs[m].append(out[0])
        dkvs[m].append(out[1])
        recvs[m].append(return_keys(out[2], ctx_count))

    def unprojected(m, before, beside):
        out = unproject(after(dqs[m], *before), dkvs[m], recvs[m], qkv_low, cos_table, sin_table)
        return together(out, *beside)

    def ffn_sum(m, before):
        keep, received = ffn_pairs[m]
        return Reduce(keep, after(received, *before), 2)

    sums = start_back(0, [gm[1].own, feed_grad], [])
    attend_back(0, 0, [], slots_of(gm[1].far, 0))
    attend_back(0, 1, [dqs[0][-1]], slots_of(gm[1].far, 1) + slots_of(recvs[0], 0))
    ffn = [ffn_sum(0, [dqs[0][-1]])]
    ffn.append(ffn_sum(1, [dqs[0][-1]]))
    attend_back(
        0,
        2,
        [*ffn[0].sent, *gm[1].pieces()],
        slots_of(ffn[0].across, 0) + slots_of(recvs[0], 1),
    )
    sums = sums + start_back(1, [dqs[0][-1]], slots_of(ffn[0].across, 1))
    grad_out = weight_grad(gm_alls[0], attn_all[0], [grads[1][0]], [])
    grad_out = weight_grad(gm_alls[1], attn_all[1], [grad_out], [], grad_out)
    attend_back(
        1, 0, [*ffn[1].sent, grad_out], slots_of(ffn[1].across, 0) + slots_of(recvs[0], 2)
    )
    back = [unprojected(0, [dqs[1][-1]], slots_of(ffn[1].across, 1))]
    reduced_in = [Reduce(*back[0][1:], 2)]
    attend_back(
        1,
        1,
        [back[0][0], *reduced_in[0].sent],
        slots_of(reduced_in[0].across, 0) + slots_of(recvs[1], 0),
    )
    attend_back(1, 2, [dqs[1][-1]], slots_of(reduced_in[0].across, 1) + slots_of(recvs[1], 1))
    out_part = scatter_weight(row_major(grad_out), feed_part)
    grad_qkv = weight_grad(normed_all[0], back[0][0], [dqs[1][-1], out_part], slots_of(recvs[1], 2))
    back.append(unprojected(1, [grad_qkv], []))
    reduced_in.append(Reduce(*back[1][1:], 2))
    grad_qkv = weight_grad(
        normed_all[1],
        back[1][0],
        reduced_in[1].sent,
        slots_of(reduced_in[1].across, 0),
        grad_qkv,
    )
    last_part = scatter_weight(row_major(grad_qkv), out_part)
    out_share = sum_blocks(out_part, ctx_count)
    feed_share = row_major(sum_blocks(feed_part, ctx_count))
    inner_share = feed_share[:, : 2 * ff_local]
    down_share = feed_share[:, 2 * ff_local :]
    gain_mid = gain_mid[0] + gain_mid[1]
    outputs = [(mid[m][0] + ffn[m].value()).astype(BF16) for m in micros]

    gain_in = 0.0
    input_grads = []
    for m in micros:
        grad_in_norm, gain_part = norm_backward(
            own[m], normed_own[m][1], norm_gains[0], reduced_in[m].value()
        )
        gain_in = gain_in + gain_part
        input_grads.append((grad_middle[m].astype(F32) + grad_in_norm).astype(BF16))

    lambda_acc = -jnp.sum(sums[1])
    lambda_local = jnp.stack(
        [
            lambda_acc * first_exp * lambdas[1],
            lambda_acc * first_exp * lambdas[0],
            -lambda_acc * second_exp * lambdas[3],
            -lambda_acc * second_exp * lambdas[2],
        ]
    )
    small = butterfly(
        jnp.concatenate(
            [
                gain_in.reshape(-1, VD),
                gain_mid.reshape(-1, VD),
                sums[:1] * (1.0 - LAMBDA_INIT),
                lambda_local.reshape(-1, VD),
            ]
        )
    )
    per = D // VD
    norm_grad = small[: 2 * per].reshape(2, D)
    head_grad = small[2 * per]
    lambda_grad = small[2 * per + 1 :].reshape(lambdas.shape)

    feed_states = [
        adamw(
            inner_weight,
            inner_momentum,
            inner_variance,
            row_major(inner_share.reshape(inner_weight.shape)),
            0.5 * D ** (-0.5),
            DECAY,
        ),
        adamw(
            down_weight, down_momentum, down_variance, row_major(down_share.T), 0.5 * FF ** (-0.5), DECAY
        ),
    ]
    out_state = adamw(
        out_weight,
        out_momentum,
        out_variance,
        row_major(out_share.T).reshape(out_weight.shape),
        0.5 * (H * VD) ** (-0.5),
        DECAY,
    )
    output, input_grad = jnp.stack(outputs), jnp.stack(input_grads)
    qkv_share = sum_blocks(
        after(last_part, feed_states, out_state, output, input_grad), ctx_count
    )
    qkv_share = row_major(
        row_major(qkv_share).reshape(-1, local_heads, 3, VD).transpose(1, 2, 0, 3)
    )
    qkv_state = adamw(
        by_part(qkv_weight),
        by_part(qkv_momentum),
        by_part(qkv_variance),
        qkv_share,
        0.5 * D ** (-0.5),
        DECAY,
    )

    states = [
        tuple(part.transpose(2, 0, 1, 3) for part in qkv_state),
        out_state,
        *feed_states,
        adamw(norm_gains, norm_momentum, norm_variance, norm_grad, 0.4, 0.0),
        adamw(head_gain, head_momentum, head_variance, head_grad, 0.4, 0.0),
        adamw(lambdas, lambda_momentum, lambda_variance, lambda_grad, 0.1, 0.0),
    ]
    return (
        output,
        input_grad,
        *[state[0] for state in states],
        *[state[1] for state in states],
        *[state[2] for state in states],
    )


def solution(mesh):
    activation = P("dp", ("ctx", "head"), None)
    big = (P("dp", "head", None, None), P("head", None, "dp"), P("dp", None, "head"), P("head", "dp"))
    state = big + (P(), P(), P())
    return jax.shard_map(
        on_device,
        mesh=mesh,
        in_specs=(activation, activation, P("dp", None)) + state * 3,
        out_specs=(activation, activation) + state * 3,
        check_vma=False,
    )
```

```python
import functools

import jax
import jax.numpy as jnp
from jax import lax
from jax.experimental import pallas as pl
from jax.experimental.layout import Layout, with_layout_constraint
from jax.experimental.pallas import tpu as pltpu
from jax.sharding import PartitionSpec as P

D = 1536
FF = 4096
H = 12
HD = 64
STEP = 10
VD = 128


EPS = 1e-05
LAMBDA_INIT = 0.2
SCALE = 0.125
NEG = -1e30
BETA1 = 0.9
BETA2 = 0.999
ADAM_EPS = 1e-08
DECAY = 0.1
ROPE_BASE = 10000.0

MIB = 1 << 20
NT = (((1,), (1,)), ((), ()))
TN = (((0,), (0,)), ((), ()))
F32 = jnp.float32
BF16 = jnp.bfloat16
MESH = pl.DeviceIdType.MESH


def dot(left, right, dims=(((1,), (0,)), ((), ())), **kw):
    return lax.dot_general(left, right, dims, preferred_element_type=F32, **kw)


def swap(array, bit):
    size = lax.axis_size("head")
    return lax.ppermute(array, "head", [(i, i ^ bit) for i in range(size)])


def split_rows(array, count):
    size = array.shape[0] // count
    return [array[i * size : (i + 1) * size] for i in range(count)]


class Gather:
    def __init__(self, own, parts=1):
        parts = parts if own.shape[0] % 512 == 0 else 1
        self.own = own
        self.mate = swap(own, 1)
        self.far = [swap(part, 2) for part in split_rows(own, parts)]
        self.far_mate = None

    def pieces(self):
        if self.far_mate is None:
            self.far_mate = [swap(part, 1) for part in self.far]
        return [self.own, self.mate, *self.far, *self.far_mate]

    def mate_first(self):
        own, mate, *rest = self.pieces()
        count = len(self.far)
        return [mate, *rest[count:], own, *rest[:count]]


class Reduce:
    def __init__(self, keep, received, parts=1):
        rows = keep.shape[0] // 2
        parts = parts if rows % 512 == 0 else 1
        total = keep.astype(F32) + received.astype(F32)
        self.near = keep[:rows].astype(F32) + received[:rows].astype(F32)
        self.sent = [part.astype(BF16) for part in split_rows(total[rows:], parts)]
        self.send()

    def send(self, *others):
        self.across = [swap(part, 2) for part in after(self.sent, *others)]

    def value(self):
        return self.near + jnp.concatenate(self.across).astype(F32)


def after(value, *others):
    return lax.optimization_barrier((value, *others))[0]


def together(result, *slots):
    values = lax.optimization_barrier((result, *[array[i] for array, i in slots]))
    for (array, i), value in zip(slots, values[1:]):
        array[i] = value
    return values[0]


def slots_of(array, *wanted):
    return [(array, i) for i in (wanted or range(len(array))) if i < len(array)]


def row_major(array):
    return with_layout_constraint(array, Layout(tuple(range(array.ndim))))


def butterfly(array):
    for axis in ("head", "ctx", "dp"):
        size = lax.axis_size(axis)
        bit = 1
        while bit < size:
            array = array + lax.ppermute(array, axis, [(i, i ^ bit) for i in range(size)])
            bit *= 2
    return array


def chunk_specs(tile, pieces):
    specs, start = [], 0
    for piece in pieces:
        count = piece.shape[0] // tile
        specs.append(
            pl.BlockSpec(
                (tile, piece.shape[1]),
                lambda i, *_, a=start, n=count: (jnp.clip(i - a, 0, n - 1), 0),
            )
        )
        start += count
    return specs


def chunk_ends(tile, pieces):
    ends, start = [], 0
    for piece in pieces:
        start += piece.shape[0] // tile
        ends.append(start)
    return ends


def pick(refs, ends, out_ref):
    index = pl.program_id(0)
    start = 0
    for ref, end in zip(refs, ends):

        @pl.when((index >= start) & (index < end))
        def _(ref=ref):
            out_ref[...] = ref[...]

        start = end


def row_spec(tile, width):
    return pl.BlockSpec((tile, width), lambda i, *_: (i, 0))


def whole_spec(shape):
    return pl.BlockSpec(shape, lambda i, *_: (0,) * len(shape))


def mate_first_spec(tile, per, width):
    return pl.BlockSpec(
        (tile, width), lambda i, *_: ((2 * (i // per) + 1) % 5 * per + i % per, 0)
    )


def exchange_specs(tile, per, width):
    half = 2 * per
    return [
        pl.BlockSpec((tile, width), lambda i, *_: (i // half * (i - half), 0)),
        pl.BlockSpec(memory_space=pl.ANY),
    ]


def exchange_shapes(rows, width):
    return [jax.ShapeDtypeStruct((rows // 2, width), BF16)] * 2


def exchange_scratch(tile, per, width):
    half = 2 * per
    return [
        pltpu.VMEM((half, tile, width), BF16),
        pltpu.SemaphoreType.DMA((half,)),
        pltpu.SemaphoreType.DMA((half,)),
    ]


def mate_index():
    me = lax.axis_index("head")
    return me + 1 - 2 * (me % 2)


def meet_mate():
    @pl.when(pl.program_id(0) == 0)
    def _():
        barrier = pltpu.get_barrier_semaphore()
        pl.semaphore_signal(
            barrier, inc=1, device_id={"head": mate_index()}, device_id_type=MESH
        )
        pl.semaphore_wait(barrier, 1)


def exchange(value, per, keep_ref, received_ref, sent_sc, send_sem, recv_sem):
    step = pl.program_id(0)
    half = 2 * per
    tile = value.shape[0]

    def copy(slot):
        return pltpu.make_async_remote_copy(
            src_ref=sent_sc.at[slot],
            dst_ref=received_ref.at[pl.ds(pl.multiple_of(slot * tile, tile), tile)],
            send_sem=send_sem.at[slot],
            recv_sem=recv_sem.at[slot],
            device_id={"head": mate_index()},
            device_id_type=MESH,
        )

    @pl.when(step < half)
    def _():
        sent_sc[step] = value
        copy(step).start()

    @pl.when(step >= half)
    def _():
        keep_ref[...] = value

    @pl.when(step == 2 * half - 1)
    def _():
        for slot in range(half):
            copy(slot).wait()


def cost(flops, moved, transcendentals=0):
    return pl.CostEstimate(
        flops=int(flops), bytes_accessed=int(moved), transcendentals=int(transcendentals)
    )


def turn(values, cos_table, sin_table, low_half, sign):
    ahead = pltpu.roll(values, VD - HD // 2, 1)
    behind = pltpu.roll(values, HD // 2, 1)
    rotated = jnp.where(low_half, -ahead, behind)
    return values * cos_table + sign * rotated * sin_table


def low_half_mask(rows):
    lane = lax.broadcasted_iota(jnp.int32, (rows, VD), 1)
    return (lane % HD) < HD // 2


def side_by_side(w_refs):
    return jnp.concatenate(
        [w_ref[item] for w_ref in w_refs for item in range(w_ref.shape[0])], axis=1
    )


def project_kernel(*refs, heads, groups, ends):
    count = len(ends)
    chunks, w_refs, refs = refs[:count], refs[count : count + groups], refs[count + groups :]
    cos_ref, sin_ref, refs = refs[0], refs[1], refs[2:]
    if count > 1:
        x_ref, refs = refs[0], refs[1:]
        pick(chunks, ends, x_ref)
    else:
        x_ref = chunks[0]
    q_refs, kv_refs = refs[:heads], refs[heads:]
    mask = low_half_mask(x_ref.shape[0])
    cos_table, sin_table = cos_ref[...], sin_ref[...]
    out = dot(x_ref[...], side_by_side(w_refs))
    for head in range(heads):
        base = head * 3 * VD
        query = turn(out[:, base : base + VD], cos_table, sin_table, mask, 1.0) * SCALE
        key = turn(out[:, base + VD : base + 2 * VD], cos_table, sin_table, mask, 1.0)
        q_refs[head][...] = query.astype(BF16)
        kv_refs[head][:, :VD] = key.astype(BF16)
        kv_refs[head][:, VD:] = out[:, base + 2 * VD : base + 3 * VD].astype(BF16)


def project(chunks, weights, cos_table, sin_table):
    rows = cos_table.shape[0]
    heads = sum(weight.shape[0] for weight in weights) // 3
    tile = min(256, rows // 4)
    gathered = len(chunks) > 1
    out = pl.pallas_call(
        functools.partial(
            project_kernel, heads=heads, groups=len(weights), ends=chunk_ends(tile, chunks)
        ),
        grid=(rows // tile,),
        in_specs=chunk_specs(tile, chunks)
        + [whole_spec(weight.shape) for weight in weights]
        + [row_spec(tile, VD), row_spec(tile, VD)],
        out_specs=[row_spec(tile, D)] * gathered
        + [row_spec(tile, VD)] * heads
        + [row_spec(tile, 2 * VD)] * heads,
        out_shape=[jax.ShapeDtypeStruct((rows, D), BF16)] * gathered
        + [jax.ShapeDtypeStruct((rows, VD), BF16)] * heads
        + [jax.ShapeDtypeStruct((rows, 2 * VD), BF16)] * heads,
        compiler_params=pltpu.CompilerParams(vmem_limit_bytes=60 * MIB),
        cost_estimate=cost(
            6 * rows * D * heads * VD, 2 * (2 * rows * D + 3 * heads * VD * (D + rows))
        ),
        name="project",
    )(*chunks, *weights, cos_table, sin_table)
    x = out[0] if gathered else chunks[0]
    out = out[gathered:]
    return x, out[:heads], out[heads:]


def unproject_kernel(*refs, heads, groups, per):
    dq_refs, own_refs, recv_refs = refs[:heads], refs[heads : 2 * heads], refs[2 * heads : 3 * heads]
    w_refs, refs = refs[3 * heads : 3 * heads + groups], refs[3 * heads + groups :]
    cos_ref, sin_ref, kv_ref, keep_ref, received_ref, gp_sc, *scratch = refs
    meet_mate()
    mask = low_half_mask(kv_ref.shape[0])
    cos_table, sin_table = cos_ref[...], sin_ref[...]
    for head in range(heads):
        base = head * 3 * VD
        both = own_refs[head][...].astype(F32) + recv_refs[head][...].astype(F32)
        key = turn(both[:, :VD], cos_table, sin_table, mask, -1.0).astype(BF16)
        value = both[:, VD:].astype(BF16)
        gp_sc[:, base : base + VD] = dq_refs[head][...]
        gp_sc[:, base + VD : base + 2 * VD] = key
        gp_sc[:, base + 2 * VD : base + 3 * VD] = value
        kv_ref[:, head * 2 * VD : head * 2 * VD + VD] = key
        kv_ref[:, head * 2 * VD + VD : (head + 1) * 2 * VD] = value
    value = dot(gp_sc[...], side_by_side(w_refs), NT).astype(BF16)
    exchange(value, per, keep_ref, received_ref, *scratch)


def unproject(dq, dkv_own, dkv_recv, weights, cos_table, sin_table):
    rows = dq[0].shape[0]
    heads = len(dq)
    tile = min(256, rows // 4)
    per = rows // 4 // tile
    return pl.pallas_call(
        functools.partial(unproject_kernel, heads=heads, groups=len(weights), per=per),
        grid=(rows // tile,),
        in_specs=[mate_first_spec(tile, per, VD)] * heads
        + [mate_first_spec(tile, per, 2 * VD)] * (2 * heads)
        + [*[whole_spec(weight.shape) for weight in weights], mate_first_spec(tile, per, VD), mate_first_spec(tile, per, VD)],
        out_specs=[mate_first_spec(tile, per, heads * 2 * VD)] + exchange_specs(tile, per, D),
        scratch_shapes=[pltpu.VMEM((tile, heads * 3 * VD), BF16)] + exchange_scratch(tile, per, D),
        out_shape=[jax.ShapeDtypeStruct((rows, heads * 2 * VD), BF16)] + exchange_shapes(rows, D),
        compiler_params=pltpu.CompilerParams(
            vmem_limit_bytes=60 * MIB, collective_id=3, has_side_effects=True
        ),
        cost_estimate=cost(
            6 * rows * D * heads * VD,
            2 * (rows * D + 3 * D * heads * VD + 9 * rows * heads * VD),
        ),
        name="unproject",
    )(*dq, *dkv_own, *dkv_recv, *weights, cos_table, sin_table)


def output_kernel(*refs, heads, per):
    attn_refs = refs[:heads]
    w_ref, all_ref, keep_ref, received_ref, *scratch = refs[heads:]
    meet_mate()
    for head in range(heads):
        all_ref[:, head * VD : (head + 1) * VD] = attn_refs[head][...]
    value = dot(all_ref[...], w_ref[...], NT).astype(BF16)
    exchange(value, per, keep_ref, received_ref, *scratch)


def output_projection(attn, weight):
    rows = attn[0].shape[0]
    heads = len(attn)
    tile = min(256, rows // 4)
    per = rows // 4 // tile
    return pl.pallas_call(
        functools.partial(output_kernel, heads=heads, per=per),
        grid=(rows // tile,),
        in_specs=[mate_first_spec(tile, per, VD)] * heads + [whole_spec(weight.shape)],
        out_specs=[mate_first_spec(tile, per, heads * VD)] + exchange_specs(tile, per, D),
        scratch_shapes=exchange_scratch(tile, per, D),
        out_shape=[jax.ShapeDtypeStruct((rows, heads * VD), BF16)] + exchange_shapes(rows, D),
        compiler_params=pltpu.CompilerParams(
            vmem_limit_bytes=40 * MIB, collective_id=1, has_side_effects=True
        ),
        cost_estimate=cost(
            2 * rows * D * weight.shape[1], 2 * (rows * D + weight.size + 2 * rows * heads * VD)
        ),
        name="output_projection",
    )(*attn, weight)


def gate_kernel(*refs, ends, cot_ends):
    count, cot_count = len(ends), len(cot_ends)
    chunks, cot_chunks = refs[:count], refs[count : count + cot_count]
    w_ref, x_ref, cot_ref, hidden_ref, by_gate_ref, by_up_ref = refs[count + cot_count :]
    pick(chunks, ends, x_ref)
    pick(cot_chunks, cot_ends, cot_ref)
    width = hidden_ref.shape[1]
    step = min(512, width)
    x = x_ref[...]
    for base in range(0, width, step):
        cols = slice(base, base + step)
        gate = dot(x, w_ref[:, cols])
        up = dot(x, w_ref[:, width + base : width + base + step])
        share = jax.nn.sigmoid(gate)
        swish = gate * share
        hidden_ref[:, cols] = (swish * up).astype(BF16)
        by_gate_ref[:, cols] = (up * share * (1.0 + gate * (1.0 - share))).astype(BF16)
        by_up_ref[:, cols] = swish.astype(BF16)


def gate_up(chunks, cot_chunks, weights, width):
    own_rows = chunks[0].shape[0]
    rows = 4 * own_rows
    tile = min(256, own_rows)
    return pl.pallas_call(
        functools.partial(
            gate_kernel, ends=chunk_ends(tile, chunks), cot_ends=chunk_ends(tile, cot_chunks)
        ),
        grid=(rows // tile,),
        in_specs=chunk_specs(tile, chunks)
        + chunk_specs(tile, cot_chunks)
        + [whole_spec(weights.shape)],
        out_specs=[row_spec(tile, D)] * 2 + [row_spec(tile, width)] * 3,
        out_shape=[jax.ShapeDtypeStruct((rows, D), BF16)] * 2
        + [jax.ShapeDtypeStruct((rows, width), BF16)] * 3,
        compiler_params=pltpu.CompilerParams(vmem_limit_bytes=60 * MIB),
        cost_estimate=cost(
            4 * rows * D * width, 2 * (4 * rows * D + 2 * D * width + 3 * rows * width)
        ),
        name="gate_up",
    )(*chunks, *cot_chunks, weights)


def feed_kernel(
    cot_ref,
    hidden_ref,
    by_gate_ref,
    by_up_ref,
    down_ref,
    inner_ref,
    grad_ref,
    ffn_keep,
    ffn_received,
    mid_keep,
    mid_received,
    *scratch,
    per,
):
    meet_mate()
    width = hidden_ref.shape[1]
    grad_hidden = dot(cot_ref[...], down_ref[...])
    grad_ref[:, :width] = (grad_hidden * by_gate_ref[...].astype(F32)).astype(BF16)
    grad_ref[:, width:] = (grad_hidden * by_up_ref[...].astype(F32)).astype(BF16)
    middle = dot(grad_ref[...], inner_ref[...], NT).astype(BF16)
    exchange(middle, per, mid_keep, mid_received, *scratch[3:])
    output = dot(hidden_ref[...], down_ref[...], NT).astype(BF16)
    exchange(output, per, ffn_keep, ffn_received, *scratch[:3])


def feed(cot, hidden, by_gate, by_up, down, inner):
    rows, width = hidden.shape
    tile = min(256, rows // 4)
    per = rows // 4 // tile
    return pl.pallas_call(
        functools.partial(feed_kernel, per=per),
        grid=(rows // tile,),
        in_specs=[row_spec(tile, D)]
        + [row_spec(tile, width)] * 3
        + [whole_spec(down.shape), whole_spec(inner.shape)],
        out_specs=[row_spec(tile, 2 * width)]
        + exchange_specs(tile, per, D)
        + exchange_specs(tile, per, D),
        out_shape=[jax.ShapeDtypeStruct((rows, 2 * width), BF16)]
        + exchange_shapes(rows, D)
        + exchange_shapes(rows, D),
        scratch_shapes=exchange_scratch(tile, per, D) + exchange_scratch(tile, per, D),
        compiler_params=pltpu.CompilerParams(
            vmem_limit_bytes=60 * MIB, collective_id=2, has_side_effects=True
        ),
        cost_estimate=cost(
            8 * rows * D * width, 2 * (3 * rows * D + 3 * D * width + 5 * rows * width)
        ),
        name="feed",
    )(cot, hidden, by_gate, by_up, down, inner)


class Plan:
    def __init__(self, own_rows, block_len, prev_rows, ndoc):
        self.own_rows = own_rows
        self.block_len = block_len
        self.prev_rows = prev_rows
        self.ndoc = ndoc
        self.bq = min(256, own_rows)
        self.bk = min(512, own_rows)
        self.total = prev_rows + block_len

    def doc_start(self, info, pos):
        start = jnp.zeros_like(pos)
        for item in range(self.ndoc):
            start = jnp.where(pos >= info[2 + item], info[2 + item], start)
        return start

    def query_start(self, info, index):
        per = self.own_rows // self.bq
        chunk = (index // per) ^ info[0]
        return info[1] * self.block_len + chunk * self.own_rows + (index % per) * self.bq

    def key_row(self, info, index):
        per = self.own_rows // self.bk
        blocks = self.block_len // self.bk
        owner = index // blocks
        local = index % blocks
        inside = (((local // per) ^ info[0]) * per + local % per) * self.bk
        base = jnp.where(owner == info[1], self.prev_rows, owner * self.block_len)
        return pl.multiple_of(base + inside, self.bk)

    def ranges(self, info, start):
        last = start + self.bq - 1
        low = self.doc_start(info, start) // self.bk
        high = last // self.bk + 1
        open_from = (self.doc_start(info, last) + self.bk - 1) // self.bk
        first = jnp.minimum(jnp.maximum(open_from, low), high)
        until = jnp.maximum(first, jnp.minimum((start + 1) // self.bk, high))
        return low, first, until, high


def in_groups(low, high, size, visit):
    count = (high - low) // size

    @pl.loop(0, count)
    def _(group):
        visit(*[low + group * size + item for item in range(size)])

    if size > 1:

        @pl.loop(low + count * size, high)
        def _(index):
            visit(index)


def split_halves(q):
    lane = lax.broadcasted_iota(jnp.int32, q.shape, 1)
    zero = jnp.zeros_like(q)
    return jnp.concatenate([jnp.where(lane < HD, q, zero), jnp.where(lane >= HD, q, zero)], axis=0)


def in_lanes(value):
    high = value.astype(BF16)
    rest = value - high.astype(F32)
    middle = rest.astype(BF16)
    low = (rest - middle.astype(F32)).astype(BF16)
    lane = lax.broadcasted_iota(jnp.int32, value.shape, 1)
    zero = jnp.zeros_like(high)
    return jnp.where(
        lane == 0, high, jnp.where(lane == 1, middle, jnp.where(lane == 2, low, zero))
    )


def load_keys(plan, info, own_ref, prev_ref, kv_sc):
    @pl.when(pl.program_id(0) == 0)
    def _():
        kv_sc[plan.prev_rows :, :] = own_ref[...]

        @pl.when(info[1] > 0)
        def _():
            kv_sc[: plan.prev_rows, :] = prev_ref[...]


def forward_kernel(
    info,
    lam_ref,
    gain_ref,
    q_ref,
    own_ref,
    prev_ref,
    attn_ref,
    first_ref,
    second_ref,
    lse_ref,
    kv_sc,
    m_sc,
    l_sc,
    acc_sc,
    *,
    plan,
):
    bq, bk = plan.bq, plan.bk
    load_keys(plan, info, own_ref, prev_ref, kv_sc)
    start = plan.query_start(info, pl.program_id(0))
    q2 = split_halves(q_ref[...])
    m_sc[...] = jnp.full_like(m_sc, NEG)
    l_sc[...] = jnp.zeros_like(l_sc)
    acc_sc[...] = jnp.zeros_like(acc_sc)
    low, first, until, high = plan.ranges(info, start)

    def visit(index, masked):
        row = plan.key_row(info, index)
        key = kv_sc[pl.ds(row, bk), :VD]
        value = kv_sc[pl.ds(row, bk), VD:]
        scores = dot(q2, key, NT)
        if masked:
            query_pos = start + lax.broadcasted_iota(jnp.int32, (bq, 1), 0)
            begin = plan.doc_start(info, query_pos)
            key_pos = index * bk + lax.broadcasted_iota(jnp.int32, (bq, bk), 1)
            keep = (key_pos <= query_pos) & (key_pos >= begin)
            scores = jnp.concatenate(
                [jnp.where(keep, scores[:bq], NEG), jnp.where(keep, scores[bq:], NEG)], axis=0
            )
        before = m_sc[...]
        after = jnp.maximum(before, jnp.max(scores, axis=1, keepdims=True))
        weights = jnp.exp(scores - jnp.tile(after, (1, bk // VD)))
        factor = jnp.exp(before - after)
        m_sc[...] = after
        l_sc[...] = l_sc[...] * factor + jnp.sum(weights, axis=1, keepdims=True)
        acc_sc[...] = acc_sc[...] * factor + dot(weights.astype(BF16), value)

    @pl.loop(low, first)
    def _(index):
        visit(index, True)

    @pl.loop(first, until)
    def _(index):
        visit(index, False)

    @pl.loop(until, high)
    def _(index):
        visit(index, True)

    total = l_sc[...]
    maps = acc_sc[...] * (1.0 / total)
    first_map, second_map = maps[:bq], maps[bq:]
    first_ref[...] = first_map
    second_ref[...] = second_map
    difference = first_map - lam_ref[0] * second_map
    scaling = lax.rsqrt(jnp.mean(difference * difference, axis=1, keepdims=True) + EPS)
    attn_ref[...] = (difference * scaling * gain_ref[...]).astype(BF16)
    lanes = in_lanes(-(m_sc[...] + jnp.log(total)))
    lse_ref[:, :VD] = lanes[:bq]
    lse_ref[:, VD:] = lanes[bq:]


def attention_cost(plan, per_pair, extra=0):
    pairs = plan.block_len * plan.block_len * 5 // 8
    return cost(pairs * per_pair + extra, plan.block_len * VD * 32, 2 * pairs)


def attend_forward(plan, info, lam, gain, q, kv_own, kv_prev):
    rows, bq = plan.block_len, plan.bq
    grid_spec = pltpu.PrefetchScalarGridSpec(
        num_scalar_prefetch=1,
        grid=(rows // bq,),
        in_specs=[
            pl.BlockSpec(memory_space=pltpu.SMEM),
            whole_spec((1, VD)),
            row_spec(bq, VD),
            whole_spec((rows, 2 * VD)),
            whole_spec((plan.prev_rows, 2 * VD)),
        ],
        out_specs=[row_spec(bq, VD)] * 3 + [row_spec(bq, 2 * VD)],
        scratch_shapes=[
            pltpu.VMEM((plan.total, 2 * VD), BF16),
            pltpu.VMEM((2 * bq, VD), F32),
            pltpu.VMEM((2 * bq, VD), F32),
            pltpu.VMEM((2 * bq, VD), F32),
        ],
    )
    return pl.pallas_call(
        functools.partial(forward_kernel, plan=plan),
        grid_spec=grid_spec,
        out_shape=[
            jax.ShapeDtypeStruct((rows, VD), BF16),
            jax.ShapeDtypeStruct((rows, VD), F32),
            jax.ShapeDtypeStruct((rows, VD), F32),
            jax.ShapeDtypeStruct((rows, 2 * VD), BF16),
        ],
        compiler_params=pltpu.CompilerParams(vmem_limit_bytes=60 * MIB),
        cost_estimate=attention_cost(plan, 6 * VD),
        name="attend_forward",
    )(info, lam, gain, q, kv_own, kv_prev)


def difference_kernel(lam_ref, gain_ref, w_ref, *refs, heads, ends):
    count = len(ends)
    chunks, refs = refs[:count], refs[count:]
    first_refs, second_refs, refs = refs[:heads], refs[heads : 2 * heads], refs[2 * heads :]
    gm_ref, sums_ref, grad_refs = refs[0], refs[1], refs[2:]
    lam = lam_ref[0]

    @pl.when(pl.program_id(0) == 0)
    def _():
        sums_ref[...] = jnp.zeros_like(sums_ref)

    pick(chunks, ends, gm_ref)
    upstream_all = dot(gm_ref[...], w_ref[...])
    for head in range(heads):
        upstream = upstream_all[:, head * VD : (head + 1) * VD]
        first_map, second_map = first_refs[head][...], second_refs[head][...]
        difference = first_map - lam * second_map
        scaling = lax.rsqrt(jnp.mean(difference * difference, axis=1, keepdims=True) + EPS)
        normal = difference * scaling
        weighted = upstream * gain_ref[...]
        inner_mean = jnp.mean(weighted * normal, axis=1, keepdims=True)
        grad = (scaling * (weighted - normal * inner_mean)).astype(BF16)
        grad_wide = grad.astype(F32)
        first_product, second_product = grad_wide * first_map, grad_wide * second_map
        sums_ref[0:1, :] += jnp.sum(upstream * normal, axis=0, keepdims=True)
        sums_ref[1:2, :] += jnp.sum(second_product, axis=0, keepdims=True)
        out = grad_refs[head]
        out[:, :VD] = grad
        for item, product in enumerate((first_product, second_product)):
            total = jnp.sum(product, axis=1, keepdims=True)
            out[:, (item + 1) * VD : (item + 2) * VD] = in_lanes(
                jnp.broadcast_to(-total, product.shape)
            )


def difference_grads(lam, gain, weight, gm, first, second):
    own_rows = gm[0].shape[0]
    rows = 4 * own_rows
    heads = len(first)
    tile = min(256, own_rows)
    return pl.pallas_call(
        functools.partial(difference_kernel, heads=heads, ends=chunk_ends(tile, gm)),
        grid=(rows // tile,),
        in_specs=[pl.BlockSpec(memory_space=pltpu.SMEM), whole_spec((1, VD)), whole_spec(weight.shape)]
        + chunk_specs(tile, gm)
        + [row_spec(tile, VD)] * (2 * heads),
        out_specs=[row_spec(tile, D), whole_spec((8, VD))] + [row_spec(tile, 3 * VD)] * heads,
        out_shape=[jax.ShapeDtypeStruct((rows, D), BF16), jax.ShapeDtypeStruct((8, VD), F32)]
        + [jax.ShapeDtypeStruct((rows, 3 * VD), BF16)] * heads,
        compiler_params=pltpu.CompilerParams(vmem_limit_bytes=60 * MIB),
        cost_estimate=cost(2 * rows * D * heads * VD, 4 * rows * D + 14 * rows * heads * VD),
        name="difference_grads",
    )(lam, gain, weight, *gm, *first, *second)


def backward_kernel(
    info,
    lam_ref,
    q_ref,
    own_ref,
    prev_ref,
    lse_ref,
    grad_ref,
    cos_ref,
    sin_ref,
    dq_ref,
    dkv_own_ref,
    dkv_prev_ref,
    kv_sc,
    dk_sc,
    dv_sc,
    dqt_sc,
    *,
    plan,
):
    bq, bk = plan.bq, plan.bk
    step = pl.program_id(0)
    lam = lam_ref[0]

    @pl.when(step == 0)
    def _():
        lane = lax.broadcasted_iota(jnp.int32, (bk, VD), 1)
        ones = jnp.where(lane < 3, 1.0, 0.0).astype(BF16)

        def fill(source, base, rows):
            for start in range(0, rows, bk):
                to = slice(base + start, base + start + bk)
                kv_sc[to, :VD] = source[start : start + bk, :VD]
                kv_sc[to, VD : 2 * VD] = ones
                kv_sc[to, 2 * VD :] = source[start : start + bk, VD:]

        fill(own_ref, plan.prev_rows, plan.block_len)

        @pl.when(info[1] > 0)
        def _():
            fill(prev_ref, 0, plan.prev_rows)

        dk_sc[...] = jnp.zeros_like(dk_sc)
        dv_sc[...] = jnp.zeros_like(dv_sc)

    grad = grad_ref[:, :VD]
    start = plan.query_start(info, step)
    q2 = split_halves(q_ref[...])
    q_wide = jnp.concatenate(
        [q2, jnp.concatenate([lse_ref[:, :VD], lse_ref[:, VD:]], axis=0)], axis=1
    )
    ones = jnp.ones((8, VD), BF16)
    delta_first = dot(ones, grad_ref[:, VD : 2 * VD], NT)[0:1]
    delta_second = dot(ones, grad_ref[:, 2 * VD :], NT)[0:1]
    dqt_sc[...] = jnp.zeros_like(dqt_sc)
    low, _, _, high = plan.ranges(info, start)

    query_pos = start + lax.broadcasted_iota(jnp.int32, (1, bq), 1)
    begin = plan.doc_start(info, query_pos)

    def visit(*indices):
        results = []
        for index in indices:
            row = plan.key_row(info, index)
            key = kv_sc[pl.ds(row, bk), :VD]
            prob = jnp.exp(dot(kv_sc[pl.ds(row, bk), : 2 * VD], q_wide, NT))
            base = dot(kv_sc[pl.ds(row, bk), 2 * VD :], grad, NT)
            key_pos = index * bk + lax.broadcasted_iota(jnp.int32, (bk, bq), 0)
            keep = (key_pos <= query_pos) & (key_pos >= begin)
            prob_first = jnp.where(keep, prob[:, :bq], 0.0)
            prob_second = jnp.where(keep, prob[:, bq:], 0.0)
            raw = jnp.concatenate(
                [
                    (prob_first * (base + delta_first)).astype(BF16),
                    (prob_second * (base + delta_second)).astype(BF16),
                ],
                axis=1,
            )
            value_grad = dot((prob_first - lam * prob_second).astype(BF16), grad)
            results.append((row, value_grad, dot(raw, q2), dot(key, raw, TN)))
        for row, value_grad, key_grad, query_grad in results:
            dv_sc[pl.ds(row, bk), :] += value_grad
            dk_sc[pl.ds(row, bk), :] += key_grad
        dqt_sc[...] += sum(result[3] for result in results)

    in_groups(low, high, 2, visit)

    dq_t = jnp.concatenate([dqt_sc[:HD, :bq], -lam * dqt_sc[HD:, bq:]], axis=0) * SCALE
    dq_ref[...] = turn(
        dq_t.T, cos_ref[...], sin_ref[...], low_half_mask(bq), -1.0
    ).astype(BF16)

    @pl.when(step == pl.num_programs(0) - 1)
    def _():
        lane = lax.broadcasted_iota(jnp.int32, (1, VD), 1)
        side = jnp.where(lane < HD, 1.0, -lam)
        dkv_own_ref[:, :VD] = (dk_sc[plan.prev_rows :, :] * side).astype(BF16)
        dkv_own_ref[:, VD:] = dv_sc[plan.prev_rows :, :].astype(BF16)
        dkv_prev_ref[:, :VD] = (dk_sc[: plan.prev_rows, :] * side).astype(BF16)
        dkv_prev_ref[:, VD:] = dv_sc[: plan.prev_rows, :].astype(BF16)


def attend_backward(plan, info, lam, q, kv_own, kv_prev, lse, grad, cos_table, sin_table):
    rows, bq = plan.block_len, plan.bq
    grid_spec = pltpu.PrefetchScalarGridSpec(
        num_scalar_prefetch=1,
        grid=(rows // bq,),
        in_specs=[
            pl.BlockSpec(memory_space=pltpu.SMEM),
            row_spec(bq, VD),
            whole_spec((rows, 2 * VD)),
            whole_spec((plan.prev_rows, 2 * VD)),
            row_spec(bq, 2 * VD),
            row_spec(bq, 3 * VD),
            row_spec(bq, VD),
            row_spec(bq, VD),
        ],
        out_specs=[
            row_spec(bq, VD),
            whole_spec((rows, 2 * VD)),
            whole_spec((plan.prev_rows, 2 * VD)),
        ],
        scratch_shapes=[
            pltpu.VMEM((plan.total, 3 * VD), BF16),
            pltpu.VMEM((plan.total, VD), F32),
            pltpu.VMEM((plan.total, VD), F32),
            pltpu.VMEM((VD, 2 * bq), F32),
        ],
    )
    return pl.pallas_call(
        functools.partial(backward_kernel, plan=plan),
        grid_spec=grid_spec,
        out_shape=[
            jax.ShapeDtypeStruct((rows, VD), BF16),
            jax.ShapeDtypeStruct((rows, 2 * VD), BF16),
            jax.ShapeDtypeStruct((plan.prev_rows, 2 * VD), BF16),
        ],
        compiler_params=pltpu.CompilerParams(vmem_limit_bytes=60 * MIB),
        cost_estimate=attention_cost(plan, 16 * VD),
        name="attend_backward",
    )(info, lam, q, kv_own, kv_prev, lse, grad, cos_table, sin_table)


def norm_forward(values, gain_vec):
    scaling = lax.rsqrt(jnp.mean(values * values, axis=-1, keepdims=True) + EPS)
    return (values * scaling * gain_vec, scaling)


def norm_backward(values, scaling, gain_vec, upstream):
    normal = values * scaling
    weighted = upstream * gain_vec
    inner_mean = jnp.mean(weighted * normal, axis=-1, keepdims=True)
    return (scaling * (weighted - normal * inner_mean), jnp.sum(upstream * normal, axis=0))


def adamw(parameter, momentum, variance, gradient, learn_rate, decay_rate):
    momentum = BETA1 * momentum + (1.0 - BETA1) * gradient
    variance = BETA2 * variance + (1.0 - BETA2) * gradient * gradient
    corrected = momentum / (1.0 - BETA1**STEP)
    spread = jnp.sqrt(variance / (1.0 - BETA2**STEP))
    return (
        parameter - learn_rate * (corrected / (spread + ADAM_EPS) + decay_rate * parameter),
        momentum,
        variance,
    )


def send_keys(kv, ctx_count):
    if ctx_count == 2:
        return lax.ppermute(kv, "ctx", [(0, 1)])
    return lax.all_gather(kv, "ctx", axis=0, tiled=True)


def return_keys(grads, ctx_count):
    if ctx_count == 2:
        return lax.ppermute(grads, "ctx", [(1, 0)])
    return lax.psum_scatter(grads, "ctx", scatter_dimension=0, tiled=True)


def scatter_weight(grad, *others):
    grad = after(grad.astype(BF16), *others)
    return lax.psum_scatter(grad, "dp", scatter_dimension=0, tiled=True)


def sum_blocks(share, ctx_count):
    if ctx_count == 2:
        other = lax.ppermute(share, "ctx", [(0, 1), (1, 0)])
        return share.astype(F32) + other.astype(F32)
    return lax.psum(share, "ctx").astype(F32)


def on_device(
    tokens,
    cotangent,
    doc_lengths,
    qkv_weight,
    out_weight,
    inner_weight,
    down_weight,
    norm_gains,
    head_gain,
    lambdas,
    qkv_momentum,
    out_momentum,
    inner_momentum,
    down_momentum,
    norm_momentum,
    head_momentum,
    lambda_momentum,
    qkv_variance,
    out_variance,
    inner_variance,
    down_variance,
    norm_variance,
    head_variance,
    lambda_variance,
):
    micro_count, own_rows, _ = tokens.shape
    head_count = lax.axis_size("head")
    ctx_count = lax.axis_size("ctx")
    block_len = own_rows * head_count
    seq_len = block_len * ctx_count
    ctx_index = lax.axis_index("ctx")
    head_index = lax.axis_index("head")
    local_heads = qkv_weight.shape[1]
    ff_local = inner_weight.shape[2]
    ndoc = doc_lengths.shape[1]
    plan = Plan(own_rows, block_len, block_len if ctx_count == 2 else seq_len, ndoc)

    def gather_weight(shard):
        return lax.all_gather(shard.astype(BF16), "dp", axis=0, tiled=True)

    def by_part(array):
        return array.transpose(1, 2, 0, 3)

    qkv_parts = row_major(by_part(qkv_weight).astype(BF16))
    qkv_low = [
        lax.all_gather(part.reshape(-1, *part.shape[2:]), "dp", axis=1, tiled=True)
        for part in (qkv_parts[:1], qkv_parts[1:])
    ]
    out_t = gather_weight(row_major(out_weight.astype(BF16).reshape(local_heads * VD, -1).T))
    inner_low = gather_weight(inner_weight.reshape(-1, 2 * ff_local))
    down_shard = row_major(down_weight.astype(BF16).T)
    down_t = gather_weight(down_shard)

    first_exp = jnp.exp(jnp.sum(lambdas[0] * lambdas[1]))
    second_exp = jnp.exp(jnp.sum(lambdas[2] * lambdas[3]))
    lambda_value = first_exp - second_exp + LAMBDA_INIT
    lam = lambda_value.reshape(1)
    head_scale = (head_gain * (1.0 - LAMBDA_INIT)).reshape(1, VD)

    chunk = jnp.arange(block_len, dtype=jnp.int32) // own_rows
    position = (
        ctx_index * block_len
        + (chunk ^ head_index) * own_rows
        + jnp.arange(block_len, dtype=jnp.int32) % own_rows
    )
    frequency = ROPE_BASE ** (
        -(jnp.arange(VD, dtype=jnp.int32) % (HD // 2)).astype(F32) / (HD // 2)
    )

    def info_of(micro):
        bounds = jnp.cumsum(doc_lengths[micro], dtype=jnp.int32)
        return jnp.concatenate([jnp.stack([head_index, ctx_index]).astype(jnp.int32), bounds])

    micros = range(micro_count)
    heads = range(local_heads)
    infos = [info_of(m) for m in micros]
    own, normed_own, normed, cot_own = [], [], [], []
    for m in micros:
        rows, cot_rows = tokens[m], cotangent[m]
        if m > 0:
            rows = after(rows, normed[0].own)
        own.append(rows.astype(F32))
        normed_own.append(norm_forward(own[m], norm_gains[0]))
        cot_own.append(cot_rows)
        normed.append(Gather(normed_own[m][0].astype(BF16), 2 if m else 1))
    position = after(position, normed[-1].own, down_shard)
    phases = position.astype(F32)[:, None] * frequency[None, :]
    cos_table, sin_table = jnp.cos(phases), jnp.sin(phases)

    normed_all, q, kv, kv_prev, cot = [], [], [], [], []

    def keep_projected(m, result):
        if len(q) == m:
            normed_all.append(result[0])
            q.append([])
            kv.append([])
            kv_prev.append([])
        q[m].extend(result[1])
        kv[m].extend(result[2])
        kv_prev[m].extend([send_keys(part, ctx_count) for part in result[2]])

    normed[0].far[0] = after(normed[0].far[0], cos_table, sin_table, *infos, *cot_own)
    result = project(normed[0].pieces(), qkv_low[:1], cos_table, sin_table)
    keep_projected(0, together(result, *slots_of(normed[1].far, 0)))
    result = project([after(normed_all[0], kv[0][-1])], qkv_low[1:], cos_table, sin_table)
    keep_projected(0, together(result, *slots_of(normed[1].far, 1)))
    cot.append(Gather(after(cot_own[0], *normed[1].far)))

    def attend(m, h, before, beside):
        out = attend_forward(
            plan, infos[m], lam, head_scale, after(q[m][h], *before), kv[m][h], kv_prev[m][h]
        )
        return together(out, *beside)

    mid = []

    def finish_attention(m):
        middle = own[m] + attended[m].value()
        value, scaling = norm_forward(middle, norm_gains[1])
        mid.append((middle, scaling, Gather(value.astype(BF16), 2)))

    maps, attn_all, attended = [], [], []
    for m in micros:
        outs = []
        for h in heads:
            if m == 0:
                before = [kv[0]] if h == 0 else [outs[-1], kv[1], out_t]
                beside = [
                    [],
                    slots_of(cot[-1].far, 0),
                    slots_of(cot[-1].far, 1),
                ][h]
            elif h == 0:
                before = [*attended[0].sent, *cot[0].pieces(), *cot[1].pieces()]
                beside = slots_of(attended[0].across) + slots_of(kv_prev[m], 1)
            else:
                before = [outs[-1], mid[0][2].own]
                beside = slots_of(mid[0][2].far, h - 1) + slots_of(kv_prev[m], h + 1)
            outs.append(attend(m, h, before, beside))
            if m == 0 and h == 0:
                pieces = after(normed[1].pieces(), outs[0])
                result = project(pieces, qkv_low, cos_table, sin_table)
                keep_projected(1, together(result, *slots_of(cot[0].far)))
                cot.append(Gather(after(cot_own[1], *cot[0].far), 2))
            if m > 0 and h == 0:
                finish_attention(0)
        maps.append([out[1:] for out in outs])
        result = output_projection([out[0] for out in outs], out_t)
        if m == 0:
            result = together(result, *slots_of(kv_prev[1], 0))
        attn_all.append(result[0])
        attended.append(Reduce(*result[1:], 2 if m else 1))

    grad_middle, gm, gain_mid = [], [], []

    def finish_feed(m, reduced):
        middle, scaling, _ = mid[m]
        grad_norm, part = norm_backward(middle, scaling, norm_gains[1], reduced.value())
        grad_middle.append((cot_own[m].astype(F32) + grad_norm).astype(BF16))
        gm.append(Gather(grad_middle[m], 2 if m else 1))
        gain_mid.append(part)

    def weight_grad(left, right, before, beside, total=None):
        result = dot(after(left, *before), right, TN)
        if total is not None:
            result = (total + result).astype(BF16)
        return together(result, *beside)

    first_gates = gate_up(
        after(mid[0][2].mate_first(), *attended[1].sent), cot[0].mate_first(), inner_low, ff_local
    )
    first_gates = together(first_gates, *slots_of(attended[1].across, 0))
    first_feed = feed(*first_gates[1:], down_t, inner_low)
    first_feed = together(first_feed, *slots_of(attended[1].across, 1))
    finish_attention(1)
    reduced_mid = [Reduce(*first_feed[3:])]
    grad_inner = weight_grad(
        first_gates[0],
        first_feed[0],
        [mid[1][2].own, *reduced_mid[0].sent],
        slots_of(mid[1][2].far, 0),
    )
    grad_down = weight_grad(
        first_gates[1], first_gates[2], [grad_inner], slots_of(mid[1][2].far, 1)
    )
    reduced_mid[0].send(*mid[1][2].far)
    second_gates = gate_up(
        after(mid[1][2].mate_first(), grad_down), cot[1].mate_first(), inner_low, ff_local
    )
    second_gates = together(second_gates, *slots_of(reduced_mid[0].across))
    finish_feed(0, reduced_mid[0])
    second_feed = feed(after(second_gates[1], gm[0].own), *second_gates[2:], down_t, inner_low)
    second_feed = together(second_feed, *slots_of(gm[0].far))
    reduced_mid.append(Reduce(*second_feed[3:], 2))
    grad_inner = weight_grad(
        second_gates[0],
        second_feed[0],
        reduced_mid[1].sent,
        slots_of(reduced_mid[1].across, 0),
        grad_inner,
    )
    grad_down = weight_grad(
        second_gates[1],
        second_gates[2],
        [grad_inner],
        slots_of(reduced_mid[1].across, 1),
        grad_down,
    )
    inner_part = scatter_weight(row_major(grad_inner))
    down_part = scatter_weight(row_major(grad_down))
    finish_feed(1, reduced_mid[1])
    ffn_pairs = [first_feed[1:3], second_feed[1:3]]

    dqs, dkvs, recvs, gm_alls, grads, sums = [], [], [], [], [], 0.0

    def start_back(m, before, beside):
        out = difference_grads(
            lam,
            head_scale,
            out_t,
            after(gm[m].pieces(), *before),
            [part[0] for part in maps[m]],
            [part[1] for part in maps[m]],
        )
        out = together(out, *beside)
        gm_alls.append(out[0])
        grads.append(out[2:])
        dqs.append([])
        dkvs.append([])
        recvs.append([])
        return out[1]

    def attend_back(m, h, before, beside):
        out = attend_backward(
            plan,
            infos[m],
            lam,
            after(q[m][h], *before),
            kv[m][h],
            kv_prev[m][h],
            maps[m][h][2],
            grads[m][h],
            cos_table,
            sin_table,
        )
        out = together(out, *beside)
        dqs[m].append(out[0])
        dkvs[m].append(out[1])
        recvs[m].append(return_keys(out[2], ctx_count))

    def unprojected(m, before, beside):
        out = unproject(after(dqs[m], *before), dkvs[m], recvs[m], qkv_low, cos_table, sin_table)
        return together(out, *beside)

    def ffn_sum(m, before):
        keep, received = ffn_pairs[m]
        return Reduce(keep, after(received, *before), 2)

    sums = start_back(0, [gm[1].own, grad_down], [])
    attend_back(0, 0, [], slots_of(gm[1].far, 0))
    attend_back(0, 1, [dqs[0][-1]], slots_of(gm[1].far, 1) + slots_of(recvs[0], 0))
    ffn = [ffn_sum(0, [dqs[0][-1]])]
    ffn.append(ffn_sum(1, [dqs[0][-1]]))
    attend_back(
        0,
        2,
        [*ffn[0].sent, *gm[1].pieces()],
        slots_of(ffn[0].across, 0) + slots_of(recvs[0], 1),
    )
    sums = sums + start_back(1, [dqs[0][-1]], slots_of(ffn[0].across, 1))
    grad_out = weight_grad(gm_alls[0], attn_all[0], [grads[1][0]], [])
    grad_out = weight_grad(gm_alls[1], attn_all[1], [grad_out], [], grad_out)
    grad_q = weight_grad(
        normed_all[0], jnp.concatenate(dqs[0], axis=1), [grad_out], []
    )
    attend_back(
        1, 0, [*ffn[1].sent, grad_q], slots_of(ffn[1].across, 0) + slots_of(recvs[0], 2)
    )
    back = [unprojected(0, [dqs[1][-1]], slots_of(ffn[1].across, 1))]
    reduced_in = [Reduce(*back[0][1:], 2)]
    attend_back(
        1,
        1,
        [back[0][0], *reduced_in[0].sent],
        slots_of(reduced_in[0].across, 0) + slots_of(recvs[1], 0),
    )
    attend_back(1, 2, [dqs[1][-1]], slots_of(reduced_in[0].across, 1) + slots_of(recvs[1], 1))
    out_part = scatter_weight(row_major(grad_out), inner_part, down_part)
    grad_kv = weight_grad(normed_all[0], back[0][0], [dqs[1][-1], out_part], [])
    grad_q = weight_grad(
        normed_all[1],
        jnp.concatenate(dqs[1], axis=1),
        [grad_kv],
        slots_of(recvs[1], 2),
        grad_q,
    )
    q_parts = [scatter_weight(row_major(grad_q), out_part)]
    back.append(unprojected(1, [grad_q], slots_of(q_parts, 0)))
    q_part = q_parts[0]
    reduced_in.append(Reduce(*back[1][1:], 2))
    grad_kv = weight_grad(
        normed_all[1],
        back[1][0],
        reduced_in[1].sent,
        [],
        grad_kv,
    )
    kv_part = scatter_weight(row_major(grad_kv), q_part)
    out_share = sum_blocks(out_part, ctx_count)
    inner_share = row_major(sum_blocks(inner_part, ctx_count))
    down_share = row_major(sum_blocks(down_part, ctx_count))
    gain_mid = gain_mid[0] + gain_mid[1]
    outputs = [(mid[m][0] + ffn[m].value()).astype(BF16) for m in micros]

    gain_in = 0.0
    input_grads = []
    for m in micros:
        grad_in_norm, gain_part = norm_backward(
            own[m], normed_own[m][1], norm_gains[0], reduced_in[m].value()
        )
        gain_in = gain_in + gain_part
        input_grads.append((grad_middle[m].astype(F32) + grad_in_norm).astype(BF16))

    lambda_acc = -jnp.sum(sums[1])
    lambda_local = jnp.stack(
        [
            lambda_acc * first_exp * lambdas[1],
            lambda_acc * first_exp * lambdas[0],
            -lambda_acc * second_exp * lambdas[3],
            -lambda_acc * second_exp * lambdas[2],
        ]
    )
    small = jnp.concatenate(
        [
            gain_in.reshape(-1, VD),
            gain_mid.reshape(-1, VD),
            sums[:1] * (1.0 - LAMBDA_INIT),
            lambda_local.reshape(-1, VD),
        ]
    )
    small = butterfly(small)
    per = D // VD
    norm_grad = small[: 2 * per].reshape(2, D)
    head_grad = small[2 * per]
    lambda_grad = small[2 * per + 1 :].reshape(lambdas.shape)

    feed_states = [
        adamw(
            inner_weight,
            inner_momentum,
            inner_variance,
            row_major(inner_share.reshape(inner_weight.shape)),
            0.5 * D ** (-0.5),
            DECAY,
        ),
        adamw(
            down_weight, down_momentum, down_variance, row_major(down_share.T), 0.5 * FF ** (-0.5), DECAY
        ),
    ]
    out_state = adamw(
        out_weight,
        out_momentum,
        out_variance,
        row_major(out_share.T).reshape(out_weight.shape),
        0.5 * (H * VD) ** (-0.5),
        DECAY,
    )
    output, input_grad = jnp.stack(outputs), jnp.stack(input_grads)
    q_share = row_major(sum_blocks(q_part, ctx_count))
    q_share = row_major(q_share.reshape(-1, local_heads, 1, VD).transpose(1, 2, 0, 3))
    kv_share = sum_blocks(
        after(kv_part, feed_states, out_state, output, input_grad, q_share), ctx_count
    )
    kv_share = row_major(
        row_major(kv_share).reshape(-1, local_heads, 2, VD).transpose(1, 2, 0, 3)
    )
    qkv_share = jnp.concatenate([q_share, kv_share], axis=1)
    qkv_state = adamw(
        by_part(qkv_weight),
        by_part(qkv_momentum),
        by_part(qkv_variance),
        qkv_share,
        0.5 * D ** (-0.5),
        DECAY,
    )

    states = [
        tuple(part.transpose(2, 0, 1, 3) for part in qkv_state),
        out_state,
        *feed_states,
        adamw(norm_gains, norm_momentum, norm_variance, norm_grad, 0.4, 0.0),
        adamw(head_gain, head_momentum, head_variance, head_grad, 0.4, 0.0),
        adamw(lambdas, lambda_momentum, lambda_variance, lambda_grad, 0.1, 0.0),
    ]
    return (
        output,
        input_grad,
        *[state[0] for state in states],
        *[state[1] for state in states],
        *[state[2] for state in states],
    )


def solution(mesh):
    activation = P("dp", ("ctx", "head"), None)
    big = (P("dp", "head", None, None), P("head", None, "dp"), P("dp", None, "head"), P("head", "dp"))
    state = big + (P(), P(), P())
    return jax.shard_map(
        on_device,
        mesh=mesh,
        in_specs=(activation, activation, P("dp", None)) + state * 3,
        out_specs=(activation, activation) + state * 3,
        check_vma=False,
    )
```

```python
import functools

import jax
import jax.numpy as jnp
from jax import lax
from jax.experimental import pallas as pl
from jax.experimental.layout import Layout, with_layout_constraint
from jax.experimental.pallas import tpu as pltpu
from jax.sharding import PartitionSpec as P

D = 1536
FF = 4096
H = 12
HD = 64
STEP = 10
VD = 128


EPS = 1e-05
LAMBDA_INIT = 0.2
SCALE = 0.125
NEG = -1e30
BETA1 = 0.9
BETA2 = 0.999
ADAM_EPS = 1e-08
DECAY = 0.1
ROPE_BASE = 10000.0

MIB = 1 << 20
NT = (((1,), (1,)), ((), ()))
TN = (((0,), (0,)), ((), ()))
F32 = jnp.float32
BF16 = jnp.bfloat16
MESH = pl.DeviceIdType.MESH


def dot(left, right, dims=(((1,), (0,)), ((), ())), **kw):
    return lax.dot_general(left, right, dims, preferred_element_type=F32, **kw)


def swap(array, bit):
    size = lax.axis_size("head")
    return lax.ppermute(array, "head", [(i, i ^ bit) for i in range(size)])


def split_rows(array, count):
    size = array.shape[0] // count
    return [array[i * size : (i + 1) * size] for i in range(count)]


class Gather:
    def __init__(self, own, parts=1):
        parts = parts if own.shape[0] % 512 == 0 else 1
        self.own = own
        self.mate = swap(own, 1)
        self.far = [swap(part, 2) for part in split_rows(own, parts)]
        self.far_mate = None

    def pieces(self):
        if self.far_mate is None:
            self.far_mate = [swap(part, 1) for part in self.far]
        return [self.own, self.mate, *self.far, *self.far_mate]

    def mate_first(self):
        own, mate, *rest = self.pieces()
        count = len(self.far)
        return [mate, *rest[count:], own, *rest[:count]]


class Reduce:
    def __init__(self, keep, received, parts=1):
        rows = keep.shape[0] // 2
        parts = parts if rows % 512 == 0 else 1
        total = keep.astype(F32) + received.astype(F32)
        self.near = keep[:rows].astype(F32) + received[:rows].astype(F32)
        self.sent = [part.astype(BF16) for part in split_rows(total[rows:], parts)]
        self.send()

    def send(self, *others):
        self.across = [swap(part, 2) for part in after(self.sent, *others)]

    def value(self):
        return self.near + jnp.concatenate(self.across).astype(F32)


def after(value, *others):
    return lax.optimization_barrier((value, *others))[0]


def together(result, *slots):
    values = lax.optimization_barrier((result, *[array[i] for array, i in slots]))
    for (array, i), value in zip(slots, values[1:]):
        array[i] = value
    return values[0]


def slots_of(array, *wanted):
    return [(array, i) for i in (wanted or range(len(array))) if i < len(array)]


def row_major(array):
    return with_layout_constraint(array, Layout(tuple(range(array.ndim))))


def butterfly(array):
    for axis in ("head", "ctx", "dp"):
        size = lax.axis_size(axis)
        bit = 1
        while bit < size:
            array = array + lax.ppermute(array, axis, [(i, i ^ bit) for i in range(size)])
            bit *= 2
    return array


def chunk_specs(tile, pieces):
    specs, start = [], 0
    for piece in pieces:
        count = piece.shape[0] // tile
        specs.append(
            pl.BlockSpec(
                (tile, piece.shape[1]),
                lambda i, *_, a=start, n=count: (jnp.clip(i - a, 0, n - 1), 0),
            )
        )
        start += count
    return specs


def chunk_ends(tile, pieces):
    ends, start = [], 0
    for piece in pieces:
        start += piece.shape[0] // tile
        ends.append(start)
    return ends


def pick(refs, ends, out_ref):
    index = pl.program_id(0)
    start = 0
    for ref, end in zip(refs, ends):

        @pl.when((index >= start) & (index < end))
        def _(ref=ref):
            out_ref[...] = ref[...]

        start = end


def row_spec(tile, width):
    return pl.BlockSpec((tile, width), lambda i, *_: (i, 0))


def whole_spec(shape):
    return pl.BlockSpec(shape, lambda i, *_: (0,) * len(shape))


def mate_first_spec(tile, per, width):
    return pl.BlockSpec(
        (tile, width), lambda i, *_: ((2 * (i // per) + 1) % 5 * per + i % per, 0)
    )


def exchange_specs(tile, per, width):
    half = 2 * per
    return [
        pl.BlockSpec((tile, width), lambda i, *_: (i // half * (i - half), 0)),
        pl.BlockSpec(memory_space=pl.ANY),
    ]


def exchange_shapes(rows, width):
    return [jax.ShapeDtypeStruct((rows // 2, width), BF16)] * 2


def exchange_scratch(tile, per, width):
    half = 2 * per
    return [
        pltpu.VMEM((half, tile, width), BF16),
        pltpu.SemaphoreType.DMA((half,)),
        pltpu.SemaphoreType.DMA((half,)),
    ]


def mate_index():
    me = lax.axis_index("head")
    return me + 1 - 2 * (me % 2)


def meet_mate():
    @pl.when(pl.program_id(0) == 0)
    def _():
        barrier = pltpu.get_barrier_semaphore()
        pl.semaphore_signal(
            barrier, inc=1, device_id={"head": mate_index()}, device_id_type=MESH
        )
        pl.semaphore_wait(barrier, 1)


def exchange(value, per, keep_ref, received_ref, sent_sc, send_sem, recv_sem):
    step = pl.program_id(0)
    half = 2 * per
    tile = value.shape[0]

    def copy(slot):
        return pltpu.make_async_remote_copy(
            src_ref=sent_sc.at[slot],
            dst_ref=received_ref.at[pl.ds(pl.multiple_of(slot * tile, tile), tile)],
            send_sem=send_sem.at[slot],
            recv_sem=recv_sem.at[slot],
            device_id={"head": mate_index()},
            device_id_type=MESH,
        )

    @pl.when(step < half)
    def _():
        sent_sc[step] = value
        copy(step).start()

    @pl.when(step >= half)
    def _():
        keep_ref[...] = value

    @pl.when(step == 2 * half - 1)
    def _():
        for slot in range(half):
            copy(slot).wait()


def cost(flops, moved, transcendentals=0):
    return pl.CostEstimate(
        flops=int(flops), bytes_accessed=int(moved), transcendentals=int(transcendentals)
    )


def turn(values, cos_table, sin_table, low_half, sign):
    ahead = pltpu.roll(values, VD - HD // 2, 1)
    behind = pltpu.roll(values, HD // 2, 1)
    rotated = jnp.where(low_half, -ahead, behind)
    return values * cos_table + sign * rotated * sin_table


def low_half_mask(rows):
    lane = lax.broadcasted_iota(jnp.int32, (rows, VD), 1)
    return (lane % HD) < HD // 2


def side_by_side(w_refs):
    return jnp.concatenate(
        [w_ref[item] for w_ref in w_refs for item in range(w_ref.shape[0])], axis=1
    )


def project_kernel(*refs, heads, groups, ends):
    count = len(ends)
    chunks, w_refs, refs = refs[:count], refs[count : count + groups], refs[count + groups :]
    cos_ref, sin_ref, refs = refs[0], refs[1], refs[2:]
    if count > 1:
        x_ref, refs = refs[0], refs[1:]
        pick(chunks, ends, x_ref)
    else:
        x_ref = chunks[0]
    q_refs, kv_refs = refs[:heads], refs[heads:]
    mask = low_half_mask(x_ref.shape[0])
    cos_table, sin_table = cos_ref[...], sin_ref[...]
    out = dot(x_ref[...], side_by_side(w_refs))
    for head in range(heads):
        base = head * 3 * VD
        query = turn(out[:, base : base + VD], cos_table, sin_table, mask, 1.0) * SCALE
        key = turn(out[:, base + VD : base + 2 * VD], cos_table, sin_table, mask, 1.0)
        q_refs[head][...] = query.astype(BF16)
        kv_refs[head][:, :VD] = key.astype(BF16)
        kv_refs[head][:, VD:] = out[:, base + 2 * VD : base + 3 * VD].astype(BF16)


def project(chunks, weights, cos_table, sin_table):
    rows = cos_table.shape[0]
    heads = sum(weight.shape[0] for weight in weights) // 3
    tile = min(256, rows // 4)
    gathered = len(chunks) > 1
    out = pl.pallas_call(
        functools.partial(
            project_kernel, heads=heads, groups=len(weights), ends=chunk_ends(tile, chunks)
        ),
        grid=(rows // tile,),
        in_specs=chunk_specs(tile, chunks)
        + [whole_spec(weight.shape) for weight in weights]
        + [row_spec(tile, VD), row_spec(tile, VD)],
        out_specs=[row_spec(tile, D)] * gathered
        + [row_spec(tile, VD)] * heads
        + [row_spec(tile, 2 * VD)] * heads,
        out_shape=[jax.ShapeDtypeStruct((rows, D), BF16)] * gathered
        + [jax.ShapeDtypeStruct((rows, VD), BF16)] * heads
        + [jax.ShapeDtypeStruct((rows, 2 * VD), BF16)] * heads,
        compiler_params=pltpu.CompilerParams(vmem_limit_bytes=60 * MIB),
        cost_estimate=cost(
            6 * rows * D * heads * VD, 2 * (2 * rows * D + 3 * heads * VD * (D + rows))
        ),
        name="project",
    )(*chunks, *weights, cos_table, sin_table)
    x = out[0] if gathered else chunks[0]
    out = out[gathered:]
    return x, out[:heads], out[heads:]


def unproject_kernel(*refs, heads, groups, per):
    dq_refs, own_refs, recv_refs = refs[:heads], refs[heads : 2 * heads], refs[2 * heads : 3 * heads]
    w_refs, refs = refs[3 * heads : 3 * heads + groups], refs[3 * heads + groups :]
    cos_ref, sin_ref, kv_ref, keep_ref, received_ref, gp_sc, *scratch = refs
    meet_mate()
    mask = low_half_mask(kv_ref.shape[0])
    cos_table, sin_table = cos_ref[...], sin_ref[...]
    for head in range(heads):
        base = head * 3 * VD
        both = own_refs[head][...].astype(F32) + recv_refs[head][...].astype(F32)
        key = turn(both[:, :VD], cos_table, sin_table, mask, -1.0).astype(BF16)
        value = both[:, VD:].astype(BF16)
        gp_sc[:, base : base + VD] = dq_refs[head][...]
        gp_sc[:, base + VD : base + 2 * VD] = key
        gp_sc[:, base + 2 * VD : base + 3 * VD] = value
        kv_ref[:, head * 2 * VD : head * 2 * VD + VD] = key
        kv_ref[:, head * 2 * VD + VD : (head + 1) * 2 * VD] = value
    value = dot(gp_sc[...], side_by_side(w_refs), NT).astype(BF16)
    exchange(value, per, keep_ref, received_ref, *scratch)


def unproject(dq, dkv_own, dkv_recv, weights, cos_table, sin_table):
    rows = dq[0].shape[0]
    heads = len(dq)
    tile = min(256, rows // 4)
    per = rows // 4 // tile
    return pl.pallas_call(
        functools.partial(unproject_kernel, heads=heads, groups=len(weights), per=per),
        grid=(rows // tile,),
        in_specs=[mate_first_spec(tile, per, VD)] * heads
        + [mate_first_spec(tile, per, 2 * VD)] * (2 * heads)
        + [*[whole_spec(weight.shape) for weight in weights], mate_first_spec(tile, per, VD), mate_first_spec(tile, per, VD)],
        out_specs=[mate_first_spec(tile, per, heads * 2 * VD)] + exchange_specs(tile, per, D),
        scratch_shapes=[pltpu.VMEM((tile, heads * 3 * VD), BF16)] + exchange_scratch(tile, per, D),
        out_shape=[jax.ShapeDtypeStruct((rows, heads * 2 * VD), BF16)] + exchange_shapes(rows, D),
        compiler_params=pltpu.CompilerParams(
            vmem_limit_bytes=60 * MIB, collective_id=3, has_side_effects=True
        ),
        cost_estimate=cost(
            6 * rows * D * heads * VD,
            2 * (rows * D + 3 * D * heads * VD + 9 * rows * heads * VD),
        ),
        name="unproject",
    )(*dq, *dkv_own, *dkv_recv, *weights, cos_table, sin_table)


def output_kernel(*refs, heads, per):
    attn_refs = refs[:heads]
    w_ref, all_ref, keep_ref, received_ref, *scratch = refs[heads:]
    meet_mate()
    for head in range(heads):
        all_ref[:, head * VD : (head + 1) * VD] = attn_refs[head][...]
    value = dot(all_ref[...], w_ref[...], NT).astype(BF16)
    exchange(value, per, keep_ref, received_ref, *scratch)


def output_projection(attn, weight):
    rows = attn[0].shape[0]
    heads = len(attn)
    tile = min(256, rows // 4)
    per = rows // 4 // tile
    return pl.pallas_call(
        functools.partial(output_kernel, heads=heads, per=per),
        grid=(rows // tile,),
        in_specs=[mate_first_spec(tile, per, VD)] * heads + [whole_spec(weight.shape)],
        out_specs=[mate_first_spec(tile, per, heads * VD)] + exchange_specs(tile, per, D),
        scratch_shapes=exchange_scratch(tile, per, D),
        out_shape=[jax.ShapeDtypeStruct((rows, heads * VD), BF16)] + exchange_shapes(rows, D),
        compiler_params=pltpu.CompilerParams(
            vmem_limit_bytes=40 * MIB, collective_id=1, has_side_effects=True
        ),
        cost_estimate=cost(
            2 * rows * D * weight.shape[1], 2 * (rows * D + weight.size + 2 * rows * heads * VD)
        ),
        name="output_projection",
    )(*attn, weight)


def gate_kernel(*refs, ends, cot_ends):
    count, cot_count = len(ends), len(cot_ends)
    chunks, cot_chunks = refs[:count], refs[count : count + cot_count]
    w_ref, x_ref, cot_ref, hidden_ref, by_gate_ref, by_up_ref = refs[count + cot_count :]
    pick(chunks, ends, x_ref)
    pick(cot_chunks, cot_ends, cot_ref)
    width = hidden_ref.shape[1]
    step = min(512, width)
    x = x_ref[...]
    for base in range(0, width, step):
        cols = slice(base, base + step)
        gate = dot(x, w_ref[:, cols])
        up = dot(x, w_ref[:, width + base : width + base + step])
        share = jax.nn.sigmoid(gate)
        swish = gate * share
        hidden_ref[:, cols] = (swish * up).astype(BF16)
        by_gate_ref[:, cols] = (up * share * (1.0 + gate * (1.0 - share))).astype(BF16)
        by_up_ref[:, cols] = swish.astype(BF16)


def gate_up(chunks, cot_chunks, weights, width):
    own_rows = chunks[0].shape[0]
    rows = 4 * own_rows
    tile = min(256, own_rows)
    return pl.pallas_call(
        functools.partial(
            gate_kernel, ends=chunk_ends(tile, chunks), cot_ends=chunk_ends(tile, cot_chunks)
        ),
        grid=(rows // tile,),
        in_specs=chunk_specs(tile, chunks)
        + chunk_specs(tile, cot_chunks)
        + [whole_spec(weights.shape)],
        out_specs=[row_spec(tile, D)] * 2 + [row_spec(tile, width)] * 3,
        out_shape=[jax.ShapeDtypeStruct((rows, D), BF16)] * 2
        + [jax.ShapeDtypeStruct((rows, width), BF16)] * 3,
        compiler_params=pltpu.CompilerParams(vmem_limit_bytes=60 * MIB),
        cost_estimate=cost(
            4 * rows * D * width, 2 * (4 * rows * D + 2 * D * width + 3 * rows * width)
        ),
        name="gate_up",
    )(*chunks, *cot_chunks, weights)


def feed_kernel(
    cot_ref,
    hidden_ref,
    by_gate_ref,
    by_up_ref,
    down_ref,
    inner_ref,
    grad_ref,
    ffn_keep,
    ffn_received,
    mid_keep,
    mid_received,
    *scratch,
    per,
):
    meet_mate()
    width = hidden_ref.shape[1]
    grad_hidden = dot(cot_ref[...], down_ref[...])
    grad_ref[:, :width] = (grad_hidden * by_gate_ref[...].astype(F32)).astype(BF16)
    grad_ref[:, width:] = (grad_hidden * by_up_ref[...].astype(F32)).astype(BF16)
    middle = dot(grad_ref[...], inner_ref[...], NT).astype(BF16)
    exchange(middle, per, mid_keep, mid_received, *scratch[3:])
    output = dot(hidden_ref[...], down_ref[...], NT).astype(BF16)
    exchange(output, per, ffn_keep, ffn_received, *scratch[:3])


def feed(cot, hidden, by_gate, by_up, down, inner):
    rows, width = hidden.shape
    tile = min(256, rows // 4)
    per = rows // 4 // tile
    return pl.pallas_call(
        functools.partial(feed_kernel, per=per),
        grid=(rows // tile,),
        in_specs=[row_spec(tile, D)]
        + [row_spec(tile, width)] * 3
        + [whole_spec(down.shape), whole_spec(inner.shape)],
        out_specs=[row_spec(tile, 2 * width)]
        + exchange_specs(tile, per, D)
        + exchange_specs(tile, per, D),
        out_shape=[jax.ShapeDtypeStruct((rows, 2 * width), BF16)]
        + exchange_shapes(rows, D)
        + exchange_shapes(rows, D),
        scratch_shapes=exchange_scratch(tile, per, D) + exchange_scratch(tile, per, D),
        compiler_params=pltpu.CompilerParams(
            vmem_limit_bytes=60 * MIB, collective_id=2, has_side_effects=True
        ),
        cost_estimate=cost(
            8 * rows * D * width, 2 * (3 * rows * D + 3 * D * width + 5 * rows * width)
        ),
        name="feed",
    )(cot, hidden, by_gate, by_up, down, inner)


class Plan:
    def __init__(self, own_rows, block_len, prev_rows, ndoc):
        self.own_rows = own_rows
        self.block_len = block_len
        self.prev_rows = prev_rows
        self.ndoc = ndoc
        self.bq = min(256, own_rows)
        self.bk = min(512, own_rows)
        self.total = prev_rows + block_len

    def doc_start(self, info, pos):
        start = jnp.zeros_like(pos)
        for item in range(self.ndoc):
            start = jnp.where(pos >= info[2 + item], info[2 + item], start)
        return start

    def query_start(self, info, index):
        per = self.own_rows // self.bq
        chunk = (index // per) ^ info[0]
        return info[1] * self.block_len + chunk * self.own_rows + (index % per) * self.bq

    def key_row(self, info, index):
        per = self.own_rows // self.bk
        blocks = self.block_len // self.bk
        owner = index // blocks
        local = index % blocks
        inside = (((local // per) ^ info[0]) * per + local % per) * self.bk
        base = jnp.where(owner == info[1], self.prev_rows, owner * self.block_len)
        return pl.multiple_of(base + inside, self.bk)

    def ranges(self, info, start):
        last = start + self.bq - 1
        low = self.doc_start(info, start) // self.bk
        high = last // self.bk + 1
        open_from = (self.doc_start(info, last) + self.bk - 1) // self.bk
        first = jnp.minimum(jnp.maximum(open_from, low), high)
        until = jnp.maximum(first, jnp.minimum((start + 1) // self.bk, high))
        return low, first, until, high


def in_groups(low, high, size, visit):
    count = (high - low) // size

    @pl.loop(0, count)
    def _(group):
        visit(*[low + group * size + item for item in range(size)])

    if size > 1:

        @pl.loop(low + count * size, high)
        def _(index):
            visit(index)


def split_halves(q):
    lane = lax.broadcasted_iota(jnp.int32, q.shape, 1)
    zero = jnp.zeros_like(q)
    return jnp.concatenate([jnp.where(lane < HD, q, zero), jnp.where(lane >= HD, q, zero)], axis=0)


def in_lanes(value):
    high = value.astype(BF16)
    rest = value - high.astype(F32)
    middle = rest.astype(BF16)
    low = (rest - middle.astype(F32)).astype(BF16)
    lane = lax.broadcasted_iota(jnp.int32, value.shape, 1)
    zero = jnp.zeros_like(high)
    return jnp.where(
        lane == 0, high, jnp.where(lane == 1, middle, jnp.where(lane == 2, low, zero))
    )


def load_keys(plan, info, own_ref, prev_ref, kv_sc):
    @pl.when(pl.program_id(0) == 0)
    def _():
        kv_sc[plan.prev_rows :, :] = own_ref[...]

        @pl.when(info[1] > 0)
        def _():
            kv_sc[: plan.prev_rows, :] = prev_ref[...]


def forward_kernel(
    info,
    lam_ref,
    gain_ref,
    q_ref,
    own_ref,
    prev_ref,
    attn_ref,
    first_ref,
    second_ref,
    lse_ref,
    kv_sc,
    m_sc,
    l_sc,
    acc_sc,
    *,
    plan,
):
    bq, bk = plan.bq, plan.bk
    load_keys(plan, info, own_ref, prev_ref, kv_sc)
    start = plan.query_start(info, pl.program_id(0))
    q2 = split_halves(q_ref[...])
    m_sc[...] = jnp.full_like(m_sc, NEG)
    l_sc[...] = jnp.zeros_like(l_sc)
    acc_sc[...] = jnp.zeros_like(acc_sc)
    low, first, until, high = plan.ranges(info, start)

    def visit(index, masked):
        row = plan.key_row(info, index)
        key = kv_sc[pl.ds(row, bk), :VD]
        value = kv_sc[pl.ds(row, bk), VD:]
        scores = dot(q2, key, NT)
        if masked:
            query_pos = start + lax.broadcasted_iota(jnp.int32, (bq, 1), 0)
            begin = plan.doc_start(info, query_pos)
            key_pos = index * bk + lax.broadcasted_iota(jnp.int32, (bq, bk), 1)
            keep = (key_pos <= query_pos) & (key_pos >= begin)
            scores = jnp.concatenate(
                [jnp.where(keep, scores[:bq], NEG), jnp.where(keep, scores[bq:], NEG)], axis=0
            )
        before = m_sc[...]
        after = jnp.maximum(before, jnp.max(scores, axis=1, keepdims=True))
        weights = jnp.exp(scores - jnp.tile(after, (1, bk // VD)))
        factor = jnp.exp(before - after)
        m_sc[...] = after
        l_sc[...] = l_sc[...] * factor + jnp.sum(weights, axis=1, keepdims=True)
        acc_sc[...] = acc_sc[...] * factor + dot(weights.astype(BF16), value)

    @pl.loop(low, first)
    def _(index):
        visit(index, True)

    @pl.loop(first, until)
    def _(index):
        visit(index, False)

    @pl.loop(until, high)
    def _(index):
        visit(index, True)

    total = l_sc[...]
    maps = acc_sc[...] * (1.0 / total)
    first_map, second_map = maps[:bq], maps[bq:]
    first_ref[...] = first_map
    second_ref[...] = second_map
    difference = first_map - lam_ref[0] * second_map
    scaling = lax.rsqrt(jnp.mean(difference * difference, axis=1, keepdims=True) + EPS)
    attn_ref[...] = (difference * scaling * gain_ref[...]).astype(BF16)
    lanes = in_lanes(-(m_sc[...] + jnp.log(total)))
    lse_ref[:, :VD] = lanes[:bq]
    lse_ref[:, VD:] = lanes[bq:]


def attention_cost(plan, per_pair, extra=0):
    pairs = plan.block_len * plan.block_len * 5 // 8
    return cost(pairs * per_pair + extra, plan.block_len * VD * 32, 2 * pairs)


def attend_forward(plan, info, lam, gain, q, kv_own, kv_prev):
    rows, bq = plan.block_len, plan.bq
    grid_spec = pltpu.PrefetchScalarGridSpec(
        num_scalar_prefetch=1,
        grid=(rows // bq,),
        in_specs=[
            pl.BlockSpec(memory_space=pltpu.SMEM),
            whole_spec((1, VD)),
            row_spec(bq, VD),
            whole_spec((rows, 2 * VD)),
            whole_spec((plan.prev_rows, 2 * VD)),
        ],
        out_specs=[row_spec(bq, VD)] * 3 + [row_spec(bq, 2 * VD)],
        scratch_shapes=[
            pltpu.VMEM((plan.total, 2 * VD), BF16),
            pltpu.VMEM((2 * bq, VD), F32),
            pltpu.VMEM((2 * bq, VD), F32),
            pltpu.VMEM((2 * bq, VD), F32),
        ],
    )
    return pl.pallas_call(
        functools.partial(forward_kernel, plan=plan),
        grid_spec=grid_spec,
        out_shape=[
            jax.ShapeDtypeStruct((rows, VD), BF16),
            jax.ShapeDtypeStruct((rows, VD), F32),
            jax.ShapeDtypeStruct((rows, VD), F32),
            jax.ShapeDtypeStruct((rows, 2 * VD), BF16),
        ],
        compiler_params=pltpu.CompilerParams(vmem_limit_bytes=60 * MIB),
        cost_estimate=attention_cost(plan, 6 * VD),
        name="attend_forward",
    )(info, lam, gain, q, kv_own, kv_prev)


def difference_kernel(lam_ref, gain_ref, w_ref, *refs, heads, ends):
    count = len(ends)
    chunks, refs = refs[:count], refs[count:]
    first_refs, second_refs, refs = refs[:heads], refs[heads : 2 * heads], refs[2 * heads :]
    gm_ref, sums_ref, grad_refs = refs[0], refs[1], refs[2:]
    lam = lam_ref[0]

    @pl.when(pl.program_id(0) == 0)
    def _():
        sums_ref[...] = jnp.zeros_like(sums_ref)

    pick(chunks, ends, gm_ref)
    upstream_all = dot(gm_ref[...], w_ref[...])
    for head in range(heads):
        upstream = upstream_all[:, head * VD : (head + 1) * VD]
        first_map, second_map = first_refs[head][...], second_refs[head][...]
        difference = first_map - lam * second_map
        scaling = lax.rsqrt(jnp.mean(difference * difference, axis=1, keepdims=True) + EPS)
        normal = difference * scaling
        weighted = upstream * gain_ref[...]
        inner_mean = jnp.mean(weighted * normal, axis=1, keepdims=True)
        grad = (scaling * (weighted - normal * inner_mean)).astype(BF16)
        grad_wide = grad.astype(F32)
        first_product, second_product = grad_wide * first_map, grad_wide * second_map
        sums_ref[0:1, :] += jnp.sum(upstream * normal, axis=0, keepdims=True)
        sums_ref[1:2, :] += jnp.sum(second_product, axis=0, keepdims=True)
        out = grad_refs[head]
        out[:, :VD] = grad
        for item, product in enumerate((first_product, second_product)):
            total = jnp.sum(product, axis=1, keepdims=True)
            out[:, (item + 1) * VD : (item + 2) * VD] = in_lanes(
                jnp.broadcast_to(-total, product.shape)
            )


def difference_grads(lam, gain, weight, gm, first, second):
    own_rows = gm[0].shape[0]
    rows = 4 * own_rows
    heads = len(first)
    tile = min(256, own_rows)
    return pl.pallas_call(
        functools.partial(difference_kernel, heads=heads, ends=chunk_ends(tile, gm)),
        grid=(rows // tile,),
        in_specs=[pl.BlockSpec(memory_space=pltpu.SMEM), whole_spec((1, VD)), whole_spec(weight.shape)]
        + chunk_specs(tile, gm)
        + [row_spec(tile, VD)] * (2 * heads),
        out_specs=[row_spec(tile, D), whole_spec((8, VD))] + [row_spec(tile, 3 * VD)] * heads,
        out_shape=[jax.ShapeDtypeStruct((rows, D), BF16), jax.ShapeDtypeStruct((8, VD), F32)]
        + [jax.ShapeDtypeStruct((rows, 3 * VD), BF16)] * heads,
        compiler_params=pltpu.CompilerParams(vmem_limit_bytes=60 * MIB),
        cost_estimate=cost(2 * rows * D * heads * VD, 4 * rows * D + 14 * rows * heads * VD),
        name="difference_grads",
    )(lam, gain, weight, *gm, *first, *second)


def backward_kernel(
    info,
    lam_ref,
    q_ref,
    own_ref,
    prev_ref,
    lse_ref,
    grad_ref,
    cos_ref,
    sin_ref,
    dq_ref,
    dkv_own_ref,
    dkv_prev_ref,
    kv_sc,
    dk_sc,
    dv_sc,
    dqt_sc,
    *,
    plan,
):
    bq, bk = plan.bq, plan.bk
    step = pl.program_id(0)
    lam = lam_ref[0]

    @pl.when(step == 0)
    def _():
        lane = lax.broadcasted_iota(jnp.int32, (bk, VD), 1)
        ones = jnp.where(lane < 3, 1.0, 0.0).astype(BF16)

        def fill(source, base, rows):
            for start in range(0, rows, bk):
                to = slice(base + start, base + start + bk)
                kv_sc[to, :VD] = source[start : start + bk, :VD]
                kv_sc[to, VD : 2 * VD] = ones
                kv_sc[to, 2 * VD :] = source[start : start + bk, VD:]

        fill(own_ref, plan.prev_rows, plan.block_len)

        @pl.when(info[1] > 0)
        def _():
            fill(prev_ref, 0, plan.prev_rows)

        dk_sc[...] = jnp.zeros_like(dk_sc)
        dv_sc[...] = jnp.zeros_like(dv_sc)

    grad = grad_ref[:, :VD]
    start = plan.query_start(info, step)
    q2 = split_halves(q_ref[...])
    q_wide = jnp.concatenate(
        [q2, jnp.concatenate([lse_ref[:, :VD], lse_ref[:, VD:]], axis=0)], axis=1
    )
    ones = jnp.ones((8, VD), BF16)
    delta_first = dot(ones, grad_ref[:, VD : 2 * VD], NT)[0:1]
    delta_second = dot(ones, grad_ref[:, 2 * VD :], NT)[0:1]
    dqt_sc[...] = jnp.zeros_like(dqt_sc)
    low, _, _, high = plan.ranges(info, start)

    query_pos = start + lax.broadcasted_iota(jnp.int32, (1, bq), 1)
    begin = plan.doc_start(info, query_pos)

    def visit(*indices):
        results = []
        for index in indices:
            row = plan.key_row(info, index)
            key = kv_sc[pl.ds(row, bk), :VD]
            prob = jnp.exp(dot(kv_sc[pl.ds(row, bk), : 2 * VD], q_wide, NT))
            base = dot(kv_sc[pl.ds(row, bk), 2 * VD :], grad, NT)
            key_pos = index * bk + lax.broadcasted_iota(jnp.int32, (bk, bq), 0)
            keep = (key_pos <= query_pos) & (key_pos >= begin)
            prob_first = jnp.where(keep, prob[:, :bq], 0.0)
            prob_second = jnp.where(keep, prob[:, bq:], 0.0)
            raw = jnp.concatenate(
                [
                    (prob_first * (base + delta_first)).astype(BF16),
                    (prob_second * (base + delta_second)).astype(BF16),
                ],
                axis=1,
            )
            value_grad = dot((prob_first - lam * prob_second).astype(BF16), grad)
            results.append((row, value_grad, dot(raw, q2), dot(key, raw, TN)))
        for row, value_grad, key_grad, query_grad in results:
            dv_sc[pl.ds(row, bk), :] += value_grad
            dk_sc[pl.ds(row, bk), :] += key_grad
        dqt_sc[...] += sum(result[3] for result in results)

    in_groups(low, high, 2, visit)

    dq_t = jnp.concatenate([dqt_sc[:HD, :bq], -lam * dqt_sc[HD:, bq:]], axis=0) * SCALE
    dq_ref[...] = turn(
        dq_t.T, cos_ref[...], sin_ref[...], low_half_mask(bq), -1.0
    ).astype(BF16)

    @pl.when(step == pl.num_programs(0) - 1)
    def _():
        lane = lax.broadcasted_iota(jnp.int32, (1, VD), 1)
        side = jnp.where(lane < HD, 1.0, -lam)
        dkv_own_ref[:, :VD] = (dk_sc[plan.prev_rows :, :] * side).astype(BF16)
        dkv_own_ref[:, VD:] = dv_sc[plan.prev_rows :, :].astype(BF16)
        dkv_prev_ref[:, :VD] = (dk_sc[: plan.prev_rows, :] * side).astype(BF16)
        dkv_prev_ref[:, VD:] = dv_sc[: plan.prev_rows, :].astype(BF16)


def attend_backward(plan, info, lam, q, kv_own, kv_prev, lse, grad, cos_table, sin_table):
    rows, bq = plan.block_len, plan.bq
    grid_spec = pltpu.PrefetchScalarGridSpec(
        num_scalar_prefetch=1,
        grid=(rows // bq,),
        in_specs=[
            pl.BlockSpec(memory_space=pltpu.SMEM),
            row_spec(bq, VD),
            whole_spec((rows, 2 * VD)),
            whole_spec((plan.prev_rows, 2 * VD)),
            row_spec(bq, 2 * VD),
            row_spec(bq, 3 * VD),
            row_spec(bq, VD),
            row_spec(bq, VD),
        ],
        out_specs=[
            row_spec(bq, VD),
            whole_spec((rows, 2 * VD)),
            whole_spec((plan.prev_rows, 2 * VD)),
        ],
        scratch_shapes=[
            pltpu.VMEM((plan.total, 3 * VD), BF16),
            pltpu.VMEM((plan.total, VD), F32),
            pltpu.VMEM((plan.total, VD), F32),
            pltpu.VMEM((VD, 2 * bq), F32),
        ],
    )
    return pl.pallas_call(
        functools.partial(backward_kernel, plan=plan),
        grid_spec=grid_spec,
        out_shape=[
            jax.ShapeDtypeStruct((rows, VD), BF16),
            jax.ShapeDtypeStruct((rows, 2 * VD), BF16),
            jax.ShapeDtypeStruct((plan.prev_rows, 2 * VD), BF16),
        ],
        compiler_params=pltpu.CompilerParams(vmem_limit_bytes=60 * MIB),
        cost_estimate=attention_cost(plan, 16 * VD),
        name="attend_backward",
    )(info, lam, q, kv_own, kv_prev, lse, grad, cos_table, sin_table)


def norm_forward(values, gain_vec):
    scaling = lax.rsqrt(jnp.mean(values * values, axis=-1, keepdims=True) + EPS)
    return (values * scaling * gain_vec, scaling)


def norm_backward(values, scaling, gain_vec, upstream):
    normal = values * scaling
    weighted = upstream * gain_vec
    inner_mean = jnp.mean(weighted * normal, axis=-1, keepdims=True)
    return (scaling * (weighted - normal * inner_mean), jnp.sum(upstream * normal, axis=0))


def adamw(parameter, momentum, variance, gradient, learn_rate, decay_rate):
    momentum = BETA1 * momentum + (1.0 - BETA1) * gradient
    variance = BETA2 * variance + (1.0 - BETA2) * gradient * gradient
    corrected = momentum / (1.0 - BETA1**STEP)
    spread = jnp.sqrt(variance / (1.0 - BETA2**STEP))
    return (
        parameter - learn_rate * (corrected / (spread + ADAM_EPS) + decay_rate * parameter),
        momentum,
        variance,
    )


def send_keys(kv, ctx_count):
    if ctx_count == 2:
        return lax.ppermute(kv, "ctx", [(0, 1)])
    return lax.all_gather(kv, "ctx", axis=0, tiled=True)


def return_keys(grads, ctx_count):
    if ctx_count == 2:
        return lax.ppermute(grads, "ctx", [(1, 0)])
    return lax.psum_scatter(grads, "ctx", scatter_dimension=0, tiled=True)


def scatter_weight(grad, *others):
    grad = after(grad.astype(BF16), *others)
    return lax.psum_scatter(grad, "dp", scatter_dimension=0, tiled=True)


def sum_blocks(share, ctx_count, *others):
    if ctx_count == 2:
        other = after(lax.ppermute(share, "ctx", [(0, 1), (1, 0)]), *others)
        return share.astype(F32) + other.astype(F32)
    return after(lax.psum(share, "ctx"), *others).astype(F32)


def on_device(
    tokens,
    cotangent,
    doc_lengths,
    qkv_weight,
    out_weight,
    inner_weight,
    down_weight,
    norm_gains,
    head_gain,
    lambdas,
    qkv_momentum,
    out_momentum,
    inner_momentum,
    down_momentum,
    norm_momentum,
    head_momentum,
    lambda_momentum,
    qkv_variance,
    out_variance,
    inner_variance,
    down_variance,
    norm_variance,
    head_variance,
    lambda_variance,
):
    micro_count, own_rows, _ = tokens.shape
    head_count = lax.axis_size("head")
    ctx_count = lax.axis_size("ctx")
    block_len = own_rows * head_count
    seq_len = block_len * ctx_count
    ctx_index = lax.axis_index("ctx")
    head_index = lax.axis_index("head")
    local_heads = qkv_weight.shape[1]
    ff_local = inner_weight.shape[2]
    ndoc = doc_lengths.shape[1]
    plan = Plan(own_rows, block_len, block_len if ctx_count == 2 else seq_len, ndoc)

    def gather_weight(shard):
        return lax.all_gather(shard.astype(BF16), "dp", axis=0, tiled=True)

    def by_part(array):
        return array.transpose(1, 2, 0, 3)

    qkv_parts = row_major(by_part(qkv_weight).astype(BF16))
    qkv_low = [
        lax.all_gather(part.reshape(-1, *part.shape[2:]), "dp", axis=1, tiled=True)
        for part in (qkv_parts[:1], qkv_parts[1:])
    ]
    out_t = gather_weight(row_major(out_weight.astype(BF16).reshape(local_heads * VD, -1).T))
    inner_low = gather_weight(inner_weight.reshape(-1, 2 * ff_local))
    down_shard = row_major(down_weight.astype(BF16).T)
    down_t = gather_weight(down_shard)

    first_exp = jnp.exp(jnp.sum(lambdas[0] * lambdas[1]))
    second_exp = jnp.exp(jnp.sum(lambdas[2] * lambdas[3]))
    lambda_value = first_exp - second_exp + LAMBDA_INIT
    lam = lambda_value.reshape(1)
    head_scale = (head_gain * (1.0 - LAMBDA_INIT)).reshape(1, VD)

    chunk = jnp.arange(block_len, dtype=jnp.int32) // own_rows
    position = (
        ctx_index * block_len
        + (chunk ^ head_index) * own_rows
        + jnp.arange(block_len, dtype=jnp.int32) % own_rows
    )
    frequency = ROPE_BASE ** (
        -(jnp.arange(VD, dtype=jnp.int32) % (HD // 2)).astype(F32) / (HD // 2)
    )

    def info_of(micro):
        bounds = jnp.cumsum(doc_lengths[micro], dtype=jnp.int32)
        return jnp.concatenate([jnp.stack([head_index, ctx_index]).astype(jnp.int32), bounds])

    micros = range(micro_count)
    heads = range(local_heads)
    infos = [info_of(m) for m in micros]
    own, normed_own, normed, cot_own = [], [], [], []
    for m in micros:
        rows, cot_rows = tokens[m], cotangent[m]
        if m > 0:
            rows = after(rows, normed[0].own)
        own.append(rows.astype(F32))
        normed_own.append(norm_forward(own[m], norm_gains[0]))
        cot_own.append(cot_rows)
        normed.append(Gather(normed_own[m][0].astype(BF16), 2 if m else 1))
    position = after(position, normed[-1].own, down_shard)
    phases = position.astype(F32)[:, None] * frequency[None, :]
    cos_table, sin_table = jnp.cos(phases), jnp.sin(phases)

    normed_all, q, kv, kv_prev, cot = [], [], [], [], []

    def keep_projected(m, result):
        if len(q) == m:
            normed_all.append(result[0])
            q.append([])
            kv.append([])
            kv_prev.append([])
        q[m].extend(result[1])
        kv[m].extend(result[2])
        kv_prev[m].extend([send_keys(part, ctx_count) for part in result[2]])

    normed[0].far[0] = after(normed[0].far[0], cos_table, sin_table, *infos, *cot_own)
    result = project(normed[0].pieces(), qkv_low[:1], cos_table, sin_table)
    keep_projected(0, together(result, *slots_of(normed[1].far, 0)))
    result = project([after(normed_all[0], kv[0][-1])], qkv_low[1:], cos_table, sin_table)
    keep_projected(0, together(result, *slots_of(normed[1].far, 1)))
    cot.append(Gather(after(cot_own[0], *normed[1].far)))

    def attend(m, h, before, beside):
        out = attend_forward(
            plan, infos[m], lam, head_scale, after(q[m][h], *before), kv[m][h], kv_prev[m][h]
        )
        return together(out, *beside)

    mid = []

    def finish_attention(m):
        middle = own[m] + attended[m].value()
        value, scaling = norm_forward(middle, norm_gains[1])
        mid.append((middle, scaling, Gather(value.astype(BF16), 2)))

    maps, attn_all, attended = [], [], []
    for m in micros:
        outs = []
        for h in heads:
            if m == 0:
                before = [kv[0]] if h == 0 else [outs[-1], kv[1], out_t]
                beside = [
                    [],
                    slots_of(cot[-1].far, 0),
                    slots_of(cot[-1].far, 1),
                ][h]
            elif h == 0:
                before = [*attended[0].sent, *cot[0].pieces(), *cot[1].pieces()]
                beside = slots_of(attended[0].across) + slots_of(kv_prev[m], 1)
            else:
                before = [outs[-1], mid[0][2].own]
                beside = slots_of(mid[0][2].far, h - 1) + slots_of(kv_prev[m], h + 1)
            outs.append(attend(m, h, before, beside))
            if m == 0 and h == 0:
                pieces = after(normed[1].pieces(), outs[0])
                result = project(pieces, qkv_low, cos_table, sin_table)
                keep_projected(1, together(result, *slots_of(cot[0].far)))
                cot.append(Gather(after(cot_own[1], *cot[0].far), 2))
            if m > 0 and h == 0:
                finish_attention(0)
        maps.append([out[1:] for out in outs])
        result = output_projection([out[0] for out in outs], out_t)
        if m == 0:
            result = together(result, *slots_of(kv_prev[1], 0))
        attn_all.append(result[0])
        attended.append(Reduce(*result[1:], 2 if m else 1))

    grad_middle, gm, gain_mid = [], [], []

    def finish_feed(m, reduced):
        middle, scaling, _ = mid[m]
        grad_norm, part = norm_backward(middle, scaling, norm_gains[1], reduced.value())
        grad_middle.append((cot_own[m].astype(F32) + grad_norm).astype(BF16))
        gm.append(Gather(grad_middle[m], 2 if m else 1))
        gain_mid.append(part)

    def weight_grad(left, right, before, beside, total=None):
        result = dot(after(left, *before), right, TN)
        if total is not None:
            result = (total + result).astype(BF16)
        return together(result, *beside)

    first_gates = gate_up(
        after(mid[0][2].mate_first(), *attended[1].sent), cot[0].mate_first(), inner_low, ff_local
    )
    first_gates = together(first_gates, *slots_of(attended[1].across, 0))
    first_feed = feed(*first_gates[1:], down_t, inner_low)
    first_feed = together(first_feed, *slots_of(attended[1].across, 1))
    finish_attention(1)
    reduced_mid = [Reduce(*first_feed[3:])]
    grad_inner = weight_grad(
        first_gates[0],
        first_feed[0],
        [mid[1][2].own, *reduced_mid[0].sent],
        slots_of(mid[1][2].far, 0),
    )
    grad_down = weight_grad(
        first_gates[1], first_gates[2], [grad_inner], slots_of(mid[1][2].far, 1)
    )
    reduced_mid[0].send(*mid[1][2].far)
    second_gates = gate_up(
        after(mid[1][2].mate_first(), grad_down), cot[1].mate_first(), inner_low, ff_local
    )
    second_gates = together(second_gates, *slots_of(reduced_mid[0].across))
    finish_feed(0, reduced_mid[0])
    second_feed = feed(after(second_gates[1], gm[0].own), *second_gates[2:], down_t, inner_low)
    second_feed = together(second_feed, *slots_of(gm[0].far))
    reduced_mid.append(Reduce(*second_feed[3:], 2))
    grad_inner = weight_grad(
        second_gates[0],
        second_feed[0],
        reduced_mid[1].sent,
        slots_of(reduced_mid[1].across, 0),
        grad_inner,
    )
    grad_down = weight_grad(
        second_gates[1],
        second_gates[2],
        [grad_inner],
        slots_of(reduced_mid[1].across, 1),
        grad_down,
    )
    inner_part = scatter_weight(row_major(grad_inner))
    down_part = scatter_weight(row_major(grad_down))
    finish_feed(1, reduced_mid[1])
    ffn_pairs = [first_feed[1:3], second_feed[1:3]]

    dqs, dkvs, recvs, gm_alls, grads, sums = [], [], [], [], [], 0.0

    def start_back(m, before, beside):
        out = difference_grads(
            lam,
            head_scale,
            out_t,
            after(gm[m].pieces(), *before),
            [part[0] for part in maps[m]],
            [part[1] for part in maps[m]],
        )
        out = together(out, *beside)
        gm_alls.append(out[0])
        grads.append(out[2:])
        dqs.append([])
        dkvs.append([])
        recvs.append([])
        return out[1]

    def attend_back(m, h, before, beside):
        out = attend_backward(
            plan,
            infos[m],
            lam,
            after(q[m][h], *before),
            kv[m][h],
            kv_prev[m][h],
            maps[m][h][2],
            grads[m][h],
            cos_table,
            sin_table,
        )
        out = together(out, *beside)
        dqs[m].append(out[0])
        dkvs[m].append(out[1])
        recvs[m].append(return_keys(out[2], ctx_count))

    def unprojected(m, before, beside):
        out = unproject(after(dqs[m], *before), dkvs[m], recvs[m], qkv_low, cos_table, sin_table)
        return together(out, *beside)

    def ffn_sum(m, before):
        keep, received = ffn_pairs[m]
        return Reduce(keep, after(received, *before), 2)

    sums = start_back(0, [gm[1].own, grad_down], [])
    attend_back(0, 0, [], slots_of(gm[1].far, 0))
    attend_back(0, 1, [dqs[0][-1]], slots_of(gm[1].far, 1) + slots_of(recvs[0], 0))
    ffn = [ffn_sum(0, [dqs[0][-1]])]
    ffn.append(ffn_sum(1, [dqs[0][-1]]))
    attend_back(
        0,
        2,
        [*ffn[0].sent, *gm[1].pieces()],
        slots_of(ffn[0].across, 0) + slots_of(recvs[0], 1),
    )
    sums = sums + start_back(1, [dqs[0][-1]], slots_of(ffn[0].across, 1))
    grad_out = weight_grad(gm_alls[0], attn_all[0], [grads[1][0]], [])
    grad_out = weight_grad(gm_alls[1], attn_all[1], [grad_out], [], grad_out)
    grad_q = weight_grad(
        normed_all[0], jnp.concatenate(dqs[0], axis=1), [grad_out], []
    )
    attend_back(
        1, 0, [*ffn[1].sent, grad_q], slots_of(ffn[1].across, 0) + slots_of(recvs[0], 2)
    )
    back = [unprojected(0, [dqs[1][-1]], slots_of(ffn[1].across, 1))]
    reduced_in = [Reduce(*back[0][1:], 2)]
    attend_back(
        1,
        1,
        [back[0][0], *reduced_in[0].sent],
        slots_of(reduced_in[0].across, 0) + slots_of(recvs[1], 0),
    )
    attend_back(1, 2, [dqs[1][-1]], slots_of(reduced_in[0].across, 1) + slots_of(recvs[1], 1))
    out_part = scatter_weight(row_major(grad_out), inner_part, down_part)
    grad_kv = weight_grad(normed_all[0], back[0][0], [dqs[1][-1], out_part], [])
    grad_q = weight_grad(
        normed_all[1],
        jnp.concatenate(dqs[1], axis=1),
        [grad_kv],
        slots_of(recvs[1], 2),
        grad_q,
    )
    q_parts = [scatter_weight(row_major(grad_q), out_part)]
    back.append(unprojected(1, [grad_q], slots_of(q_parts, 0)))
    q_part = q_parts[0]
    reduced_in.append(Reduce(*back[1][1:], 2))
    grad_kv = weight_grad(
        normed_all[1],
        back[1][0],
        reduced_in[1].sent,
        [],
        grad_kv,
    )
    kv_part = scatter_weight(row_major(grad_kv), q_part)
    out_share = sum_blocks(out_part, ctx_count, *reduced_in[1].across)
    inner_share = row_major(sum_blocks(inner_part, ctx_count, grad_kv, *reduced_in[1].across))
    down_share = row_major(sum_blocks(down_part, ctx_count, grad_kv, *reduced_in[1].across))
    gain_mid = gain_mid[0] + gain_mid[1]
    outputs = [(mid[m][0] + ffn[m].value()).astype(BF16) for m in micros]

    gain_in = 0.0
    input_grads = []
    for m in micros:
        grad_in_norm, gain_part = norm_backward(
            own[m], normed_own[m][1], norm_gains[0], reduced_in[m].value()
        )
        gain_in = gain_in + gain_part
        input_grads.append((grad_middle[m].astype(F32) + grad_in_norm).astype(BF16))

    lambda_acc = -jnp.sum(sums[1])
    lambda_local = jnp.stack(
        [
            lambda_acc * first_exp * lambdas[1],
            lambda_acc * first_exp * lambdas[0],
            -lambda_acc * second_exp * lambdas[3],
            -lambda_acc * second_exp * lambdas[2],
        ]
    )
    small = jnp.concatenate(
        [
            gain_in.reshape(-1, VD),
            gain_mid.reshape(-1, VD),
            sums[:1] * (1.0 - LAMBDA_INIT),
            lambda_local.reshape(-1, VD),
        ]
    )
    small = butterfly(small)
    per = D // VD
    norm_grad = small[: 2 * per].reshape(2, D)
    head_grad = small[2 * per]
    lambda_grad = small[2 * per + 1 :].reshape(lambdas.shape)

    feed_states = [
        adamw(
            inner_weight,
            inner_momentum,
            inner_variance,
            row_major(inner_share.reshape(inner_weight.shape)),
            0.5 * D ** (-0.5),
            DECAY,
        ),
        adamw(
            down_weight, down_momentum, down_variance, row_major(down_share.T), 0.5 * FF ** (-0.5), DECAY
        ),
    ]
    out_state = adamw(
        out_weight,
        out_momentum,
        out_variance,
        row_major(out_share.T).reshape(out_weight.shape),
        0.5 * (H * VD) ** (-0.5),
        DECAY,
    )
    output, input_grad = jnp.stack(outputs), jnp.stack(input_grads)
    q_share = row_major(sum_blocks(q_part, ctx_count, *reduced_in[1].across))
    q_share = row_major(q_share.reshape(-1, local_heads, 1, VD).transpose(1, 2, 0, 3))
    kv_share = sum_blocks(
        after(kv_part, feed_states, out_state, output, q_share), ctx_count
    )
    kv_share = row_major(
        row_major(kv_share).reshape(-1, local_heads, 2, VD).transpose(1, 2, 0, 3)
    )
    qkv_share = jnp.concatenate([q_share, kv_share], axis=1)
    qkv_state = adamw(
        by_part(qkv_weight),
        by_part(qkv_momentum),
        by_part(qkv_variance),
        qkv_share,
        0.5 * D ** (-0.5),
        DECAY,
    )

    states = [
        tuple(part.transpose(2, 0, 1, 3) for part in qkv_state),
        out_state,
        *feed_states,
        adamw(norm_gains, norm_momentum, norm_variance, norm_grad, 0.4, 0.0),
        adamw(head_gain, head_momentum, head_variance, head_grad, 0.4, 0.0),
        adamw(lambdas, lambda_momentum, lambda_variance, lambda_grad, 0.1, 0.0),
    ]
    return (
        output,
        input_grad,
        *[state[0] for state in states],
        *[state[1] for state in states],
        *[state[2] for state in states],
    )


def solution(mesh):
    activation = P("dp", ("ctx", "head"), None)
    big = (P("dp", "head", None, None), P("head", None, "dp"), P("dp", None, "head"), P("head", "dp"))
    state = big + (P(), P(), P())
    return jax.shard_map(
        on_device,
        mesh=mesh,
        in_specs=(activation, activation, P("dp", None)) + state * 3,
        out_specs=(activation, activation) + state * 3,
        check_vma=False,
    )
```

```python
import functools

import jax
import jax.numpy as jnp
from jax import lax
from jax.experimental import pallas as pl
from jax.experimental.layout import Layout, with_layout_constraint
from jax.experimental.pallas import tpu as pltpu
from jax.sharding import PartitionSpec as P

D = 1536
FF = 4096
H = 12
HD = 64
STEP = 10
VD = 128


EPS = 1e-05
LAMBDA_INIT = 0.2
SCALE = 0.125
NEG = -1e30
BETA1 = 0.9
BETA2 = 0.999
ADAM_EPS = 1e-08
DECAY = 0.1
ROPE_BASE = 10000.0

MIB = 1 << 20
NT = (((1,), (1,)), ((), ()))
TN = (((0,), (0,)), ((), ()))
F32 = jnp.float32
BF16 = jnp.bfloat16
MESH = pl.DeviceIdType.MESH


def dot(left, right, dims=(((1,), (0,)), ((), ())), **kw):
    return lax.dot_general(left, right, dims, preferred_element_type=F32, **kw)


def swap(array, bit):
    size = lax.axis_size("head")
    return lax.ppermute(array, "head", [(i, i ^ bit) for i in range(size)])


def split_rows(array, count):
    size = array.shape[0] // count
    return [array[i * size : (i + 1) * size] for i in range(count)]


class Gather:
    def __init__(self, own, parts=1):
        parts = parts if own.shape[0] % 512 == 0 else 1
        self.own = own
        self.mate = swap(own, 1)
        self.far = [swap(part, 2) for part in split_rows(own, parts)]
        self.far_mate = None

    def pieces(self):
        if self.far_mate is None:
            self.far_mate = [swap(part, 1) for part in self.far]
        return [self.own, self.mate, *self.far, *self.far_mate]

    def mate_first(self):
        own, mate, *rest = self.pieces()
        count = len(self.far)
        return [mate, *rest[count:], own, *rest[:count]]


class Reduce:
    def __init__(self, keep, received, parts=1):
        rows = keep.shape[0] // 2
        parts = parts if rows % 512 == 0 else 1
        total = keep.astype(F32) + received.astype(F32)
        self.near = keep[:rows].astype(F32) + received[:rows].astype(F32)
        self.sent = [part.astype(BF16) for part in split_rows(total[rows:], parts)]
        self.send()

    def send(self, *others):
        self.across = [swap(part, 2) for part in after(self.sent, *others)]

    def value(self):
        return self.near + jnp.concatenate(self.across).astype(F32)


def after(value, *others):
    return lax.optimization_barrier((value, *others))[0]


def together(result, *slots):
    values = lax.optimization_barrier((result, *[array[i] for array, i in slots]))
    for (array, i), value in zip(slots, values[1:]):
        array[i] = value
    return values[0]


def slots_of(array, *wanted):
    return [(array, i) for i in (wanted or range(len(array))) if i < len(array)]


def row_major(array):
    return with_layout_constraint(array, Layout(tuple(range(array.ndim))))


def butterfly(array):
    for axis in ("head", "ctx", "dp"):
        size = lax.axis_size(axis)
        bit = 1
        while bit < size:
            array = array + lax.ppermute(array, axis, [(i, i ^ bit) for i in range(size)])
            bit *= 2
    return array


def chunk_specs(tile, pieces):
    specs, start = [], 0
    for piece in pieces:
        count = piece.shape[0] // tile
        specs.append(
            pl.BlockSpec(
                (tile, piece.shape[1]),
                lambda i, *_, a=start, n=count: (jnp.clip(i - a, 0, n - 1), 0),
            )
        )
        start += count
    return specs


def chunk_ends(tile, pieces):
    ends, start = [], 0
    for piece in pieces:
        start += piece.shape[0] // tile
        ends.append(start)
    return ends


def pick(refs, ends, out_ref):
    index = pl.program_id(0)
    start = 0
    for ref, end in zip(refs, ends):

        @pl.when((index >= start) & (index < end))
        def _(ref=ref):
            out_ref[...] = ref[...]

        start = end


def row_spec(tile, width):
    return pl.BlockSpec((tile, width), lambda i, *_: (i, 0))


def whole_spec(shape):
    return pl.BlockSpec(shape, lambda i, *_: (0,) * len(shape))


def mate_first_spec(tile, per, width):
    return pl.BlockSpec(
        (tile, width), lambda i, *_: ((2 * (i // per) + 1) % 5 * per + i % per, 0)
    )


def exchange_specs(tile, per, width):
    half = 2 * per
    return [
        pl.BlockSpec((tile, width), lambda i, *_: (i // half * (i - half), 0)),
        pl.BlockSpec(memory_space=pl.ANY),
    ]


def exchange_shapes(rows, width):
    return [jax.ShapeDtypeStruct((rows // 2, width), BF16)] * 2


def exchange_scratch(tile, per, width):
    half = 2 * per
    return [
        pltpu.VMEM((half, tile, width), BF16),
        pltpu.SemaphoreType.DMA((half,)),
        pltpu.SemaphoreType.DMA((half,)),
    ]


def mate_index():
    me = lax.axis_index("head")
    return me + 1 - 2 * (me % 2)


def meet_mate():
    @pl.when(pl.program_id(0) == 0)
    def _():
        barrier = pltpu.get_barrier_semaphore()
        pl.semaphore_signal(
            barrier, inc=1, device_id={"head": mate_index()}, device_id_type=MESH
        )
        pl.semaphore_wait(barrier, 1)


def exchange(value, per, keep_ref, received_ref, sent_sc, send_sem, recv_sem):
    step = pl.program_id(0)
    half = 2 * per
    tile = value.shape[0]

    def copy(slot):
        return pltpu.make_async_remote_copy(
            src_ref=sent_sc.at[slot],
            dst_ref=received_ref.at[pl.ds(pl.multiple_of(slot * tile, tile), tile)],
            send_sem=send_sem.at[slot],
            recv_sem=recv_sem.at[slot],
            device_id={"head": mate_index()},
            device_id_type=MESH,
        )

    @pl.when(step < half)
    def _():
        sent_sc[step] = value
        copy(step).start()

    @pl.when(step >= half)
    def _():
        keep_ref[...] = value

    @pl.when(step == 2 * half - 1)
    def _():
        for slot in range(half):
            copy(slot).wait()


def cost(flops, moved, transcendentals=0):
    return pl.CostEstimate(
        flops=int(flops), bytes_accessed=int(moved), transcendentals=int(transcendentals)
    )


def turn(values, cos_table, sin_table, low_half, sign):
    ahead = pltpu.roll(values, VD - HD // 2, 1)
    behind = pltpu.roll(values, HD // 2, 1)
    rotated = jnp.where(low_half, -ahead, behind)
    return values * cos_table + sign * rotated * sin_table


def low_half_mask(rows):
    lane = lax.broadcasted_iota(jnp.int32, (rows, VD), 1)
    return (lane % HD) < HD // 2


def side_by_side(w_refs):
    return jnp.concatenate(
        [w_ref[item] for w_ref in w_refs for item in range(w_ref.shape[0])], axis=1
    )


def project_kernel(*refs, heads, groups, ends):
    count = len(ends)
    chunks, w_refs, refs = refs[:count], refs[count : count + groups], refs[count + groups :]
    cos_ref, sin_ref, refs = refs[0], refs[1], refs[2:]
    if count > 1:
        x_ref, refs = refs[0], refs[1:]
        pick(chunks, ends, x_ref)
    else:
        x_ref = chunks[0]
    q_refs, kv_refs = refs[:heads], refs[heads:]
    mask = low_half_mask(x_ref.shape[0])
    cos_table, sin_table = cos_ref[...], sin_ref[...]
    out = dot(x_ref[...], side_by_side(w_refs))
    for head in range(heads):
        base = head * 3 * VD
        query = turn(out[:, base : base + VD], cos_table, sin_table, mask, 1.0) * SCALE
        key = turn(out[:, base + VD : base + 2 * VD], cos_table, sin_table, mask, 1.0)
        q_refs[head][...] = query.astype(BF16)
        kv_refs[head][:, :VD] = key.astype(BF16)
        kv_refs[head][:, VD:] = out[:, base + 2 * VD : base + 3 * VD].astype(BF16)


def project(chunks, weights, cos_table, sin_table):
    rows = cos_table.shape[0]
    heads = sum(weight.shape[0] for weight in weights) // 3
    tile = min(256, rows // 4)
    gathered = len(chunks) > 1
    out = pl.pallas_call(
        functools.partial(
            project_kernel, heads=heads, groups=len(weights), ends=chunk_ends(tile, chunks)
        ),
        grid=(rows // tile,),
        in_specs=chunk_specs(tile, chunks)
        + [whole_spec(weight.shape) for weight in weights]
        + [row_spec(tile, VD), row_spec(tile, VD)],
        out_specs=[row_spec(tile, D)] * gathered
        + [row_spec(tile, VD)] * heads
        + [row_spec(tile, 2 * VD)] * heads,
        out_shape=[jax.ShapeDtypeStruct((rows, D), BF16)] * gathered
        + [jax.ShapeDtypeStruct((rows, VD), BF16)] * heads
        + [jax.ShapeDtypeStruct((rows, 2 * VD), BF16)] * heads,
        compiler_params=pltpu.CompilerParams(vmem_limit_bytes=60 * MIB),
        cost_estimate=cost(
            6 * rows * D * heads * VD, 2 * (2 * rows * D + 3 * heads * VD * (D + rows))
        ),
        name="project",
    )(*chunks, *weights, cos_table, sin_table)
    x = out[0] if gathered else chunks[0]
    out = out[gathered:]
    return x, out[:heads], out[heads:]


def unproject_kernel(*refs, heads, groups, per):
    dq_refs, own_refs, recv_refs = refs[:heads], refs[heads : 2 * heads], refs[2 * heads : 3 * heads]
    w_refs, refs = refs[3 * heads : 3 * heads + groups], refs[3 * heads + groups :]
    cos_ref, sin_ref, kv_ref, keep_ref, received_ref, gp_sc, *scratch = refs
    meet_mate()
    mask = low_half_mask(kv_ref.shape[0])
    cos_table, sin_table = cos_ref[...], sin_ref[...]
    for head in range(heads):
        base = head * 3 * VD
        both = own_refs[head][...].astype(F32) + recv_refs[head][...].astype(F32)
        key = turn(both[:, :VD], cos_table, sin_table, mask, -1.0).astype(BF16)
        value = both[:, VD:].astype(BF16)
        gp_sc[:, base : base + VD] = dq_refs[head][...]
        gp_sc[:, base + VD : base + 2 * VD] = key
        gp_sc[:, base + 2 * VD : base + 3 * VD] = value
        kv_ref[:, head * 2 * VD : head * 2 * VD + VD] = key
        kv_ref[:, head * 2 * VD + VD : (head + 1) * 2 * VD] = value
    value = dot(gp_sc[...], side_by_side(w_refs), NT).astype(BF16)
    exchange(value, per, keep_ref, received_ref, *scratch)


def unproject(dq, dkv_own, dkv_recv, weights, cos_table, sin_table):
    rows = dq[0].shape[0]
    heads = len(dq)
    tile = min(256, rows // 4)
    per = rows // 4 // tile
    return pl.pallas_call(
        functools.partial(unproject_kernel, heads=heads, groups=len(weights), per=per),
        grid=(rows // tile,),
        in_specs=[mate_first_spec(tile, per, VD)] * heads
        + [mate_first_spec(tile, per, 2 * VD)] * (2 * heads)
        + [*[whole_spec(weight.shape) for weight in weights], mate_first_spec(tile, per, VD), mate_first_spec(tile, per, VD)],
        out_specs=[mate_first_spec(tile, per, heads * 2 * VD)] + exchange_specs(tile, per, D),
        scratch_shapes=[pltpu.VMEM((tile, heads * 3 * VD), BF16)] + exchange_scratch(tile, per, D),
        out_shape=[jax.ShapeDtypeStruct((rows, heads * 2 * VD), BF16)] + exchange_shapes(rows, D),
        compiler_params=pltpu.CompilerParams(
            vmem_limit_bytes=60 * MIB, collective_id=3, has_side_effects=True
        ),
        cost_estimate=cost(
            6 * rows * D * heads * VD,
            2 * (rows * D + 3 * D * heads * VD + 9 * rows * heads * VD),
        ),
        name="unproject",
    )(*dq, *dkv_own, *dkv_recv, *weights, cos_table, sin_table)


def output_kernel(*refs, heads, per):
    attn_refs = refs[:heads]
    w_ref, all_ref, keep_ref, received_ref, *scratch = refs[heads:]
    meet_mate()
    for head in range(heads):
        all_ref[:, head * VD : (head + 1) * VD] = attn_refs[head][...]
    value = dot(all_ref[...], w_ref[...], NT).astype(BF16)
    exchange(value, per, keep_ref, received_ref, *scratch)


def output_projection(attn, weight):
    rows = attn[0].shape[0]
    heads = len(attn)
    tile = min(256, rows // 4)
    per = rows // 4 // tile
    return pl.pallas_call(
        functools.partial(output_kernel, heads=heads, per=per),
        grid=(rows // tile,),
        in_specs=[mate_first_spec(tile, per, VD)] * heads + [whole_spec(weight.shape)],
        out_specs=[mate_first_spec(tile, per, heads * VD)] + exchange_specs(tile, per, D),
        scratch_shapes=exchange_scratch(tile, per, D),
        out_shape=[jax.ShapeDtypeStruct((rows, heads * VD), BF16)] + exchange_shapes(rows, D),
        compiler_params=pltpu.CompilerParams(
            vmem_limit_bytes=40 * MIB, collective_id=1, has_side_effects=True
        ),
        cost_estimate=cost(
            2 * rows * D * weight.shape[1], 2 * (rows * D + weight.size + 2 * rows * heads * VD)
        ),
        name="output_projection",
    )(*attn, weight)


def gate_kernel(*refs, ends, cot_ends):
    count, cot_count = len(ends), len(cot_ends)
    chunks, cot_chunks = refs[:count], refs[count : count + cot_count]
    w_ref, x_ref, cot_ref, hidden_ref, by_gate_ref, by_up_ref = refs[count + cot_count :]
    pick(chunks, ends, x_ref)
    pick(cot_chunks, cot_ends, cot_ref)
    width = hidden_ref.shape[1]
    step = min(512, width)
    x = x_ref[...]
    for base in range(0, width, step):
        cols = slice(base, base + step)
        gate = dot(x, w_ref[:, cols])
        up = dot(x, w_ref[:, width + base : width + base + step])
        share = jax.nn.sigmoid(gate)
        swish = gate * share
        hidden_ref[:, cols] = (swish * up).astype(BF16)
        by_gate_ref[:, cols] = (up * share * (1.0 + gate * (1.0 - share))).astype(BF16)
        by_up_ref[:, cols] = swish.astype(BF16)


def gate_up(chunks, cot_chunks, weights, width):
    own_rows = chunks[0].shape[0]
    rows = 4 * own_rows
    tile = min(256, own_rows)
    return pl.pallas_call(
        functools.partial(
            gate_kernel, ends=chunk_ends(tile, chunks), cot_ends=chunk_ends(tile, cot_chunks)
        ),
        grid=(rows // tile,),
        in_specs=chunk_specs(tile, chunks)
        + chunk_specs(tile, cot_chunks)
        + [whole_spec(weights.shape)],
        out_specs=[row_spec(tile, D)] * 2 + [row_spec(tile, width)] * 3,
        out_shape=[jax.ShapeDtypeStruct((rows, D), BF16)] * 2
        + [jax.ShapeDtypeStruct((rows, width), BF16)] * 3,
        compiler_params=pltpu.CompilerParams(vmem_limit_bytes=60 * MIB),
        cost_estimate=cost(
            4 * rows * D * width, 2 * (4 * rows * D + 2 * D * width + 3 * rows * width)
        ),
        name="gate_up",
    )(*chunks, *cot_chunks, weights)


def feed_kernel(
    cot_ref,
    hidden_ref,
    by_gate_ref,
    by_up_ref,
    down_ref,
    inner_ref,
    grad_ref,
    ffn_keep,
    ffn_received,
    mid_keep,
    mid_received,
    *scratch,
    per,
):
    meet_mate()
    width = hidden_ref.shape[1]
    grad_hidden = dot(cot_ref[...], down_ref[...])
    grad_ref[:, :width] = (grad_hidden * by_gate_ref[...].astype(F32)).astype(BF16)
    grad_ref[:, width:] = (grad_hidden * by_up_ref[...].astype(F32)).astype(BF16)
    middle = dot(grad_ref[...], inner_ref[...], NT).astype(BF16)
    exchange(middle, per, mid_keep, mid_received, *scratch[3:])
    output = dot(hidden_ref[...], down_ref[...], NT).astype(BF16)
    exchange(output, per, ffn_keep, ffn_received, *scratch[:3])


def feed(cot, hidden, by_gate, by_up, down, inner):
    rows, width = hidden.shape
    tile = min(256, rows // 4)
    per = rows // 4 // tile
    return pl.pallas_call(
        functools.partial(feed_kernel, per=per),
        grid=(rows // tile,),
        in_specs=[row_spec(tile, D)]
        + [row_spec(tile, width)] * 3
        + [whole_spec(down.shape), whole_spec(inner.shape)],
        out_specs=[row_spec(tile, 2 * width)]
        + exchange_specs(tile, per, D)
        + exchange_specs(tile, per, D),
        out_shape=[jax.ShapeDtypeStruct((rows, 2 * width), BF16)]
        + exchange_shapes(rows, D)
        + exchange_shapes(rows, D),
        scratch_shapes=exchange_scratch(tile, per, D) + exchange_scratch(tile, per, D),
        compiler_params=pltpu.CompilerParams(
            vmem_limit_bytes=60 * MIB, collective_id=2, has_side_effects=True
        ),
        cost_estimate=cost(
            8 * rows * D * width, 2 * (3 * rows * D + 3 * D * width + 5 * rows * width)
        ),
        name="feed",
    )(cot, hidden, by_gate, by_up, down, inner)


class Plan:
    def __init__(self, own_rows, block_len, prev_rows, ndoc):
        self.own_rows = own_rows
        self.block_len = block_len
        self.prev_rows = prev_rows
        self.ndoc = ndoc
        self.bq = min(256, own_rows)
        self.bk = min(512, own_rows)
        self.total = prev_rows + block_len

    def doc_start(self, info, pos):
        start = jnp.zeros_like(pos)
        for item in range(self.ndoc):
            start = jnp.where(pos >= info[2 + item], info[2 + item], start)
        return start

    def query_start(self, info, index):
        per = self.own_rows // self.bq
        chunk = (index // per) ^ info[0]
        return info[1] * self.block_len + chunk * self.own_rows + (index % per) * self.bq

    def key_row(self, info, index):
        per = self.own_rows // self.bk
        blocks = self.block_len // self.bk
        owner = index // blocks
        local = index % blocks
        inside = (((local // per) ^ info[0]) * per + local % per) * self.bk
        base = jnp.where(owner == info[1], self.prev_rows, owner * self.block_len)
        return pl.multiple_of(base + inside, self.bk)

    def ranges(self, info, start):
        last = start + self.bq - 1
        low = self.doc_start(info, start) // self.bk
        high = last // self.bk + 1
        open_from = (self.doc_start(info, last) + self.bk - 1) // self.bk
        first = jnp.minimum(jnp.maximum(open_from, low), high)
        until = jnp.maximum(first, jnp.minimum((start + 1) // self.bk, high))
        return low, first, until, high


def in_groups(low, high, size, visit):
    count = (high - low) // size

    @pl.loop(0, count)
    def _(group):
        visit(*[low + group * size + item for item in range(size)])

    if size > 1:

        @pl.loop(low + count * size, high)
        def _(index):
            visit(index)


def split_halves(q):
    lane = lax.broadcasted_iota(jnp.int32, q.shape, 1)
    zero = jnp.zeros_like(q)
    return jnp.concatenate([jnp.where(lane < HD, q, zero), jnp.where(lane >= HD, q, zero)], axis=0)


def in_lanes(value):
    high = value.astype(BF16)
    rest = value - high.astype(F32)
    middle = rest.astype(BF16)
    low = (rest - middle.astype(F32)).astype(BF16)
    lane = lax.broadcasted_iota(jnp.int32, value.shape, 1)
    zero = jnp.zeros_like(high)
    return jnp.where(
        lane == 0, high, jnp.where(lane == 1, middle, jnp.where(lane == 2, low, zero))
    )


def load_keys(plan, info, own_ref, prev_ref, kv_sc):
    @pl.when(pl.program_id(0) == 0)
    def _():
        kv_sc[plan.prev_rows :, :] = own_ref[...]

        @pl.when(info[1] > 0)
        def _():
            kv_sc[: plan.prev_rows, :] = prev_ref[...]


def forward_kernel(
    info,
    lam_ref,
    gain_ref,
    q_ref,
    own_ref,
    prev_ref,
    attn_ref,
    first_ref,
    second_ref,
    lse_ref,
    kv_sc,
    m_sc,
    l_sc,
    acc_sc,
    *,
    plan,
):
    bq, bk = plan.bq, plan.bk
    load_keys(plan, info, own_ref, prev_ref, kv_sc)
    start = plan.query_start(info, pl.program_id(0))
    q2 = split_halves(q_ref[...])
    m_sc[...] = jnp.full_like(m_sc, NEG)
    l_sc[...] = jnp.zeros_like(l_sc)
    acc_sc[...] = jnp.zeros_like(acc_sc)
    low, first, until, high = plan.ranges(info, start)

    def visit(index, masked):
        row = plan.key_row(info, index)
        key = kv_sc[pl.ds(row, bk), :VD]
        value = kv_sc[pl.ds(row, bk), VD:]
        scores = dot(q2, key, NT)
        if masked:
            query_pos = start + lax.broadcasted_iota(jnp.int32, (bq, 1), 0)
            begin = plan.doc_start(info, query_pos)
            key_pos = index * bk + lax.broadcasted_iota(jnp.int32, (bq, bk), 1)
            keep = (key_pos <= query_pos) & (key_pos >= begin)
            scores = jnp.concatenate(
                [jnp.where(keep, scores[:bq], NEG), jnp.where(keep, scores[bq:], NEG)], axis=0
            )
        before = m_sc[...]
        after = jnp.maximum(before, jnp.max(scores, axis=1, keepdims=True))
        weights = jnp.exp(scores - jnp.tile(after, (1, bk // VD)))
        factor = jnp.exp(before - after)
        m_sc[...] = after
        l_sc[...] = l_sc[...] * factor + jnp.sum(weights, axis=1, keepdims=True)
        acc_sc[...] = acc_sc[...] * factor + dot(weights.astype(BF16), value)

    @pl.loop(low, first)
    def _(index):
        visit(index, True)

    @pl.loop(first, until)
    def _(index):
        visit(index, False)

    @pl.loop(until, high)
    def _(index):
        visit(index, True)

    total = l_sc[...]
    maps = acc_sc[...] * (1.0 / total)
    first_map, second_map = maps[:bq], maps[bq:]
    first_ref[...] = first_map
    second_ref[...] = second_map
    difference = first_map - lam_ref[0] * second_map
    scaling = lax.rsqrt(jnp.mean(difference * difference, axis=1, keepdims=True) + EPS)
    attn_ref[...] = (difference * scaling * gain_ref[...]).astype(BF16)
    lanes = in_lanes(-(m_sc[...] + jnp.log(total)))
    lse_ref[:, :VD] = lanes[:bq]
    lse_ref[:, VD:] = lanes[bq:]


def attention_cost(plan, per_pair, extra=0):
    pairs = plan.block_len * plan.block_len * 5 // 8
    return cost(pairs * per_pair + extra, plan.block_len * VD * 32, 2 * pairs)


def attend_forward(plan, info, lam, gain, q, kv_own, kv_prev):
    rows, bq = plan.block_len, plan.bq
    grid_spec = pltpu.PrefetchScalarGridSpec(
        num_scalar_prefetch=1,
        grid=(rows // bq,),
        in_specs=[
            pl.BlockSpec(memory_space=pltpu.SMEM),
            whole_spec((1, VD)),
            row_spec(bq, VD),
            whole_spec((rows, 2 * VD)),
            whole_spec((plan.prev_rows, 2 * VD)),
        ],
        out_specs=[row_spec(bq, VD)] * 3 + [row_spec(bq, 2 * VD)],
        scratch_shapes=[
            pltpu.VMEM((plan.total, 2 * VD), BF16),
            pltpu.VMEM((2 * bq, VD), F32),
            pltpu.VMEM((2 * bq, VD), F32),
            pltpu.VMEM((2 * bq, VD), F32),
        ],
    )
    return pl.pallas_call(
        functools.partial(forward_kernel, plan=plan),
        grid_spec=grid_spec,
        out_shape=[
            jax.ShapeDtypeStruct((rows, VD), BF16),
            jax.ShapeDtypeStruct((rows, VD), F32),
            jax.ShapeDtypeStruct((rows, VD), F32),
            jax.ShapeDtypeStruct((rows, 2 * VD), BF16),
        ],
        compiler_params=pltpu.CompilerParams(vmem_limit_bytes=60 * MIB),
        cost_estimate=attention_cost(plan, 6 * VD),
        name="attend_forward",
    )(info, lam, gain, q, kv_own, kv_prev)


def difference_kernel(lam_ref, gain_ref, w_ref, *refs, heads, ends):
    count = len(ends)
    chunks, refs = refs[:count], refs[count:]
    first_refs, second_refs, refs = refs[:heads], refs[heads : 2 * heads], refs[2 * heads :]
    gm_ref, sums_ref, grad_refs = refs[0], refs[1], refs[2:]
    lam = lam_ref[0]

    @pl.when(pl.program_id(0) == 0)
    def _():
        sums_ref[...] = jnp.zeros_like(sums_ref)

    pick(chunks, ends, gm_ref)
    upstream_all = dot(gm_ref[...], w_ref[...])
    for head in range(heads):
        upstream = upstream_all[:, head * VD : (head + 1) * VD]
        first_map, second_map = first_refs[head][...], second_refs[head][...]
        difference = first_map - lam * second_map
        scaling = lax.rsqrt(jnp.mean(difference * difference, axis=1, keepdims=True) + EPS)
        normal = difference * scaling
        weighted = upstream * gain_ref[...]
        inner_mean = jnp.mean(weighted * normal, axis=1, keepdims=True)
        grad = (scaling * (weighted - normal * inner_mean)).astype(BF16)
        grad_wide = grad.astype(F32)
        first_product, second_product = grad_wide * first_map, grad_wide * second_map
        sums_ref[0:1, :] += jnp.sum(upstream * normal, axis=0, keepdims=True)
        sums_ref[1:2, :] += jnp.sum(second_product, axis=0, keepdims=True)
        out = grad_refs[head]
        out[:, :VD] = grad
        for item, product in enumerate((first_product, second_product)):
            total = jnp.sum(product, axis=1, keepdims=True)
            out[:, (item + 1) * VD : (item + 2) * VD] = in_lanes(
                jnp.broadcast_to(-total, product.shape)
            )


def difference_grads(lam, gain, weight, gm, first, second):
    own_rows = gm[0].shape[0]
    rows = 4 * own_rows
    heads = len(first)
    tile = min(256, own_rows)
    return pl.pallas_call(
        functools.partial(difference_kernel, heads=heads, ends=chunk_ends(tile, gm)),
        grid=(rows // tile,),
        in_specs=[pl.BlockSpec(memory_space=pltpu.SMEM), whole_spec((1, VD)), whole_spec(weight.shape)]
        + chunk_specs(tile, gm)
        + [row_spec(tile, VD)] * (2 * heads),
        out_specs=[row_spec(tile, D), whole_spec((8, VD))] + [row_spec(tile, 3 * VD)] * heads,
        out_shape=[jax.ShapeDtypeStruct((rows, D), BF16), jax.ShapeDtypeStruct((8, VD), F32)]
        + [jax.ShapeDtypeStruct((rows, 3 * VD), BF16)] * heads,
        compiler_params=pltpu.CompilerParams(vmem_limit_bytes=60 * MIB),
        cost_estimate=cost(2 * rows * D * heads * VD, 4 * rows * D + 14 * rows * heads * VD),
        name="difference_grads",
    )(lam, gain, weight, *gm, *first, *second)


def backward_kernel(
    info,
    lam_ref,
    q_ref,
    own_ref,
    prev_ref,
    lse_ref,
    grad_ref,
    cos_ref,
    sin_ref,
    dq_ref,
    dkv_own_ref,
    dkv_prev_ref,
    kv_sc,
    dk_sc,
    dv_sc,
    dqt_sc,
    *,
    plan,
):
    bq, bk = plan.bq, plan.bk
    step = pl.program_id(0)
    lam = lam_ref[0]

    @pl.when(step == 0)
    def _():
        lane = lax.broadcasted_iota(jnp.int32, (bk, VD), 1)
        ones = jnp.where(lane < 3, 1.0, 0.0).astype(BF16)

        def fill(source, base, rows):
            for start in range(0, rows, bk):
                to = slice(base + start, base + start + bk)
                kv_sc[to, :VD] = source[start : start + bk, :VD]
                kv_sc[to, VD : 2 * VD] = ones
                kv_sc[to, 2 * VD :] = source[start : start + bk, VD:]

        fill(own_ref, plan.prev_rows, plan.block_len)

        @pl.when(info[1] > 0)
        def _():
            fill(prev_ref, 0, plan.prev_rows)

        dk_sc[...] = jnp.zeros_like(dk_sc)
        dv_sc[...] = jnp.zeros_like(dv_sc)

    grad = grad_ref[:, :VD]
    start = plan.query_start(info, step)
    q2 = split_halves(q_ref[...])
    q_wide = jnp.concatenate(
        [q2, jnp.concatenate([lse_ref[:, :VD], lse_ref[:, VD:]], axis=0)], axis=1
    )
    ones = jnp.ones((8, VD), BF16)
    delta_first = dot(ones, grad_ref[:, VD : 2 * VD], NT)[0:1]
    delta_second = dot(ones, grad_ref[:, 2 * VD :], NT)[0:1]
    dqt_sc[...] = jnp.zeros_like(dqt_sc)
    low, _, _, high = plan.ranges(info, start)

    query_pos = start + lax.broadcasted_iota(jnp.int32, (1, bq), 1)
    begin = plan.doc_start(info, query_pos)

    def visit(*indices):
        results = []
        for index in indices:
            row = plan.key_row(info, index)
            key = kv_sc[pl.ds(row, bk), :VD]
            prob = jnp.exp(dot(kv_sc[pl.ds(row, bk), : 2 * VD], q_wide, NT))
            base = dot(kv_sc[pl.ds(row, bk), 2 * VD :], grad, NT)
            key_pos = index * bk + lax.broadcasted_iota(jnp.int32, (bk, bq), 0)
            keep = (key_pos <= query_pos) & (key_pos >= begin)
            prob_first = jnp.where(keep, prob[:, :bq], 0.0)
            prob_second = jnp.where(keep, prob[:, bq:], 0.0)
            raw = jnp.concatenate(
                [
                    (prob_first * (base + delta_first)).astype(BF16),
                    (prob_second * (base + delta_second)).astype(BF16),
                ],
                axis=1,
            )
            value_grad = dot((prob_first - lam * prob_second).astype(BF16), grad)
            results.append((row, value_grad, dot(raw, q2), dot(key, raw, TN)))
        for row, value_grad, key_grad, query_grad in results:
            dv_sc[pl.ds(row, bk), :] += value_grad
            dk_sc[pl.ds(row, bk), :] += key_grad
        dqt_sc[...] += sum(result[3] for result in results)

    in_groups(low, high, 2, visit)

    dq_t = jnp.concatenate([dqt_sc[:HD, :bq], -lam * dqt_sc[HD:, bq:]], axis=0) * SCALE
    dq_ref[...] = turn(
        dq_t.T, cos_ref[...], sin_ref[...], low_half_mask(bq), -1.0
    ).astype(BF16)

    @pl.when(step == pl.num_programs(0) - 1)
    def _():
        lane = lax.broadcasted_iota(jnp.int32, (1, VD), 1)
        side = jnp.where(lane < HD, 1.0, -lam)
        dkv_own_ref[:, :VD] = (dk_sc[plan.prev_rows :, :] * side).astype(BF16)
        dkv_own_ref[:, VD:] = dv_sc[plan.prev_rows :, :].astype(BF16)
        dkv_prev_ref[:, :VD] = (dk_sc[: plan.prev_rows, :] * side).astype(BF16)
        dkv_prev_ref[:, VD:] = dv_sc[: plan.prev_rows, :].astype(BF16)


def attend_backward(plan, info, lam, q, kv_own, kv_prev, lse, grad, cos_table, sin_table):
    rows, bq = plan.block_len, plan.bq
    grid_spec = pltpu.PrefetchScalarGridSpec(
        num_scalar_prefetch=1,
        grid=(rows // bq,),
        in_specs=[
            pl.BlockSpec(memory_space=pltpu.SMEM),
            row_spec(bq, VD),
            whole_spec((rows, 2 * VD)),
            whole_spec((plan.prev_rows, 2 * VD)),
            row_spec(bq, 2 * VD),
            row_spec(bq, 3 * VD),
            row_spec(bq, VD),
            row_spec(bq, VD),
        ],
        out_specs=[
            row_spec(bq, VD),
            whole_spec((rows, 2 * VD)),
            whole_spec((plan.prev_rows, 2 * VD)),
        ],
        scratch_shapes=[
            pltpu.VMEM((plan.total, 3 * VD), BF16),
            pltpu.VMEM((plan.total, VD), F32),
            pltpu.VMEM((plan.total, VD), F32),
            pltpu.VMEM((VD, 2 * bq), F32),
        ],
    )
    return pl.pallas_call(
        functools.partial(backward_kernel, plan=plan),
        grid_spec=grid_spec,
        out_shape=[
            jax.ShapeDtypeStruct((rows, VD), BF16),
            jax.ShapeDtypeStruct((rows, 2 * VD), BF16),
            jax.ShapeDtypeStruct((plan.prev_rows, 2 * VD), BF16),
        ],
        compiler_params=pltpu.CompilerParams(vmem_limit_bytes=60 * MIB),
        cost_estimate=attention_cost(plan, 16 * VD),
        name="attend_backward",
    )(info, lam, q, kv_own, kv_prev, lse, grad, cos_table, sin_table)


def norm_forward(values, gain_vec):
    scaling = lax.rsqrt(jnp.mean(values * values, axis=-1, keepdims=True) + EPS)
    return (values * scaling * gain_vec, scaling)


def norm_backward(values, scaling, gain_vec, upstream):
    normal = values * scaling
    weighted = upstream * gain_vec
    inner_mean = jnp.mean(weighted * normal, axis=-1, keepdims=True)
    return (scaling * (weighted - normal * inner_mean), jnp.sum(upstream * normal, axis=0))


def adamw(parameter, momentum, variance, gradient, learn_rate, decay_rate):
    momentum = BETA1 * momentum + (1.0 - BETA1) * gradient
    variance = BETA2 * variance + (1.0 - BETA2) * gradient * gradient
    corrected = momentum / (1.0 - BETA1**STEP)
    spread = jnp.sqrt(variance / (1.0 - BETA2**STEP))
    return (
        parameter - learn_rate * (corrected / (spread + ADAM_EPS) + decay_rate * parameter),
        momentum,
        variance,
    )


def send_keys(kv, ctx_count):
    if ctx_count == 2:
        return lax.ppermute(kv, "ctx", [(0, 1)])
    return lax.all_gather(kv, "ctx", axis=0, tiled=True)


def return_keys(grads, ctx_count):
    if ctx_count == 2:
        return lax.ppermute(grads, "ctx", [(1, 0)])
    return lax.psum_scatter(grads, "ctx", scatter_dimension=0, tiled=True)


def scatter_weight(grad, *others):
    grad = after(grad.astype(BF16), *others)
    return lax.psum_scatter(grad, "dp", scatter_dimension=0, tiled=True)


def exchange_blocks(share, ctx_count):
    if ctx_count == 2:
        return lax.ppermute(share, "ctx", [(0, 1), (1, 0)])
    return lax.psum(share, "ctx")


def add_blocks(share, other, ctx_count):
    if ctx_count == 2:
        return share.astype(F32) + other.astype(F32)
    return other.astype(F32)


def sum_blocks(share, ctx_count, *others):
    return add_blocks(share, after(exchange_blocks(share, ctx_count), *others), ctx_count)


def on_device(
    tokens,
    cotangent,
    doc_lengths,
    qkv_weight,
    out_weight,
    inner_weight,
    down_weight,
    norm_gains,
    head_gain,
    lambdas,
    qkv_momentum,
    out_momentum,
    inner_momentum,
    down_momentum,
    norm_momentum,
    head_momentum,
    lambda_momentum,
    qkv_variance,
    out_variance,
    inner_variance,
    down_variance,
    norm_variance,
    head_variance,
    lambda_variance,
):
    micro_count, own_rows, _ = tokens.shape
    head_count = lax.axis_size("head")
    ctx_count = lax.axis_size("ctx")
    block_len = own_rows * head_count
    seq_len = block_len * ctx_count
    ctx_index = lax.axis_index("ctx")
    head_index = lax.axis_index("head")
    local_heads = qkv_weight.shape[1]
    ff_local = inner_weight.shape[2]
    ndoc = doc_lengths.shape[1]
    plan = Plan(own_rows, block_len, block_len if ctx_count == 2 else seq_len, ndoc)

    def gather_weight(shard):
        return lax.all_gather(shard.astype(BF16), "dp", axis=0, tiled=True)

    def by_part(array):
        return array.transpose(1, 2, 0, 3)

    qkv_parts = row_major(by_part(qkv_weight).astype(BF16))
    qkv_low = [
        lax.all_gather(part.reshape(-1, *part.shape[2:]), "dp", axis=1, tiled=True)
        for part in (qkv_parts[:1], qkv_parts[1:])
    ]
    out_t = gather_weight(row_major(out_weight.astype(BF16).reshape(local_heads * VD, -1).T))
    inner_low = gather_weight(inner_weight.reshape(-1, 2 * ff_local))
    down_shard = row_major(down_weight.astype(BF16).T)
    down_t = gather_weight(down_shard)

    first_exp = jnp.exp(jnp.sum(lambdas[0] * lambdas[1]))
    second_exp = jnp.exp(jnp.sum(lambdas[2] * lambdas[3]))
    lambda_value = first_exp - second_exp + LAMBDA_INIT
    lam = lambda_value.reshape(1)
    head_scale = (head_gain * (1.0 - LAMBDA_INIT)).reshape(1, VD)

    chunk = jnp.arange(block_len, dtype=jnp.int32) // own_rows
    position = (
        ctx_index * block_len
        + (chunk ^ head_index) * own_rows
        + jnp.arange(block_len, dtype=jnp.int32) % own_rows
    )
    frequency = ROPE_BASE ** (
        -(jnp.arange(VD, dtype=jnp.int32) % (HD // 2)).astype(F32) / (HD // 2)
    )

    def info_of(micro):
        bounds = jnp.cumsum(doc_lengths[micro], dtype=jnp.int32)
        return jnp.concatenate([jnp.stack([head_index, ctx_index]).astype(jnp.int32), bounds])

    micros = range(micro_count)
    heads = range(local_heads)
    infos = [info_of(m) for m in micros]
    own, normed_own, normed, cot_own = [], [], [], []
    for m in micros:
        rows, cot_rows = tokens[m], cotangent[m]
        if m > 0:
            rows = after(rows, normed[0].own)
        own.append(rows.astype(F32))
        normed_own.append(norm_forward(own[m], norm_gains[0]))
        cot_own.append(cot_rows)
        normed.append(Gather(normed_own[m][0].astype(BF16), 2 if m else 1))
    position = after(position, normed[-1].own, down_shard)
    phases = position.astype(F32)[:, None] * frequency[None, :]
    cos_table, sin_table = jnp.cos(phases), jnp.sin(phases)

    normed_all, q, kv, kv_prev, cot = [], [], [], [], []

    def keep_projected(m, result):
        if len(q) == m:
            normed_all.append(result[0])
            q.append([])
            kv.append([])
            kv_prev.append([])
        q[m].extend(result[1])
        kv[m].extend(result[2])
        kv_prev[m].extend([send_keys(part, ctx_count) for part in result[2]])

    normed[0].far[0] = after(normed[0].far[0], cos_table, sin_table, *infos, *cot_own)
    result = project(normed[0].pieces(), qkv_low[:1], cos_table, sin_table)
    keep_projected(0, together(result, *slots_of(normed[1].far, 0)))
    result = project([after(normed_all[0], kv[0][-1])], qkv_low[1:], cos_table, sin_table)
    keep_projected(0, together(result, *slots_of(normed[1].far, 1)))
    cot.append(Gather(after(cot_own[0], *normed[1].far)))

    def attend(m, h, before, beside):
        out = attend_forward(
            plan, infos[m], lam, head_scale, after(q[m][h], *before), kv[m][h], kv_prev[m][h]
        )
        return together(out, *beside)

    mid = []

    def finish_attention(m):
        middle = own[m] + attended[m].value()
        value, scaling = norm_forward(middle, norm_gains[1])
        mid.append((middle, scaling, Gather(value.astype(BF16), 2)))

    maps, attn_all, attended = [], [], []
    for m in micros:
        outs = []
        for h in heads:
            if m == 0:
                before = [kv[0]] if h == 0 else [outs[-1], kv[1], out_t]
                beside = [
                    [],
                    slots_of(cot[-1].far, 0),
                    slots_of(cot[-1].far, 1),
                ][h]
            elif h == 0:
                before = [*attended[0].sent, *cot[0].pieces(), *cot[1].pieces()]
                beside = slots_of(attended[0].across) + slots_of(kv_prev[m], 1)
            else:
                before = [outs[-1], mid[0][2].own]
                beside = slots_of(mid[0][2].far, h - 1) + slots_of(kv_prev[m], h + 1)
            outs.append(attend(m, h, before, beside))
            if m == 0 and h == 0:
                pieces = after(normed[1].pieces(), outs[0])
                result = project(pieces, qkv_low, cos_table, sin_table)
                keep_projected(1, together(result, *slots_of(cot[0].far)))
                cot.append(Gather(after(cot_own[1], *cot[0].far), 2))
            if m > 0 and h == 0:
                finish_attention(0)
        maps.append([out[1:] for out in outs])
        result = output_projection([out[0] for out in outs], out_t)
        if m == 0:
            result = together(result, *slots_of(kv_prev[1], 0))
        attn_all.append(result[0])
        attended.append(Reduce(*result[1:], 2 if m else 1))

    grad_middle, gm, gain_mid = [], [], []

    def finish_feed(m, reduced):
        middle, scaling, _ = mid[m]
        grad_norm, part = norm_backward(middle, scaling, norm_gains[1], reduced.value())
        grad_middle.append((cot_own[m].astype(F32) + grad_norm).astype(BF16))
        gm.append(Gather(grad_middle[m], 2 if m else 1))
        gain_mid.append(part)

    def weight_grad(left, right, before, beside, total=None):
        result = dot(after(left, *before), right, TN)
        if total is not None:
            result = (total + result).astype(BF16)
        return together(result, *beside)

    first_gates = gate_up(
        after(mid[0][2].mate_first(), *attended[1].sent), cot[0].mate_first(), inner_low, ff_local
    )
    first_gates = together(first_gates, *slots_of(attended[1].across, 0))
    first_feed = feed(*first_gates[1:], down_t, inner_low)
    first_feed = together(first_feed, *slots_of(attended[1].across, 1))
    finish_attention(1)
    reduced_mid = [Reduce(*first_feed[3:])]
    grad_inner = weight_grad(
        first_gates[0],
        first_feed[0],
        [mid[1][2].own, *reduced_mid[0].sent],
        slots_of(mid[1][2].far, 0),
    )
    grad_down = weight_grad(
        first_gates[1], first_gates[2], [grad_inner], slots_of(mid[1][2].far, 1)
    )
    reduced_mid[0].send(*mid[1][2].far)
    second_gates = gate_up(
        after(mid[1][2].mate_first(), grad_down), cot[1].mate_first(), inner_low, ff_local
    )
    second_gates = together(second_gates, *slots_of(reduced_mid[0].across))
    finish_feed(0, reduced_mid[0])
    second_feed = feed(after(second_gates[1], gm[0].own), *second_gates[2:], down_t, inner_low)
    second_feed = together(second_feed, *slots_of(gm[0].far))
    reduced_mid.append(Reduce(*second_feed[3:], 2))
    grad_inner = weight_grad(
        second_gates[0],
        second_feed[0],
        reduced_mid[1].sent,
        slots_of(reduced_mid[1].across, 0),
        grad_inner,
    )
    grad_down = weight_grad(
        second_gates[1],
        second_gates[2],
        [grad_inner],
        slots_of(reduced_mid[1].across, 1),
        grad_down,
    )
    inner_part = scatter_weight(row_major(grad_inner))
    down_part = scatter_weight(row_major(grad_down))
    finish_feed(1, reduced_mid[1])
    ffn_pairs = [first_feed[1:3], second_feed[1:3]]

    dqs, dkvs, recvs, gm_alls, grads, sums = [], [], [], [], [], 0.0

    def start_back(m, before, beside):
        out = difference_grads(
            lam,
            head_scale,
            out_t,
            after(gm[m].pieces(), *before),
            [part[0] for part in maps[m]],
            [part[1] for part in maps[m]],
        )
        out = together(out, *beside)
        gm_alls.append(out[0])
        grads.append(out[2:])
        dqs.append([])
        dkvs.append([])
        recvs.append([])
        return out[1]

    def attend_back(m, h, before, beside):
        out = attend_backward(
            plan,
            infos[m],
            lam,
            after(q[m][h], *before),
            kv[m][h],
            kv_prev[m][h],
            maps[m][h][2],
            grads[m][h],
            cos_table,
            sin_table,
        )
        out = together(out, *beside)
        dqs[m].append(out[0])
        dkvs[m].append(out[1])
        recvs[m].append(return_keys(out[2], ctx_count))

    def unprojected(m, before, beside):
        out = unproject(after(dqs[m], *before), dkvs[m], recvs[m], qkv_low, cos_table, sin_table)
        return together(out, *beside)

    def ffn_sum(m, before):
        keep, received = ffn_pairs[m]
        return Reduce(keep, after(received, *before), 2)

    sums = start_back(0, [gm[1].own, grad_down], [])
    attend_back(0, 0, [], slots_of(gm[1].far, 0))
    attend_back(0, 1, [dqs[0][-1]], slots_of(gm[1].far, 1) + slots_of(recvs[0], 0))
    ffn = [ffn_sum(0, [dqs[0][-1]])]
    ffn.append(ffn_sum(1, [dqs[0][-1]]))
    attend_back(
        0,
        2,
        [*ffn[0].sent, *gm[1].pieces()],
        slots_of(ffn[0].across, 0) + slots_of(recvs[0], 1),
    )
    sums = sums + start_back(1, [dqs[0][-1]], slots_of(ffn[0].across, 1))
    grad_out = weight_grad(gm_alls[0], attn_all[0], [grads[1][0]], [])
    grad_out = weight_grad(gm_alls[1], attn_all[1], [grad_out], [], grad_out)
    grad_q = weight_grad(
        normed_all[0], jnp.concatenate(dqs[0], axis=1), [grad_out], []
    )
    down_other = [exchange_blocks(down_part, ctx_count)]
    attend_back(
        1,
        0,
        [*ffn[1].sent, grad_q],
        slots_of(ffn[1].across, 0) + slots_of(recvs[0], 2) + slots_of(down_other),
    )
    back = [unprojected(0, [dqs[1][-1]], slots_of(ffn[1].across, 1))]
    reduced_in = [Reduce(*back[0][1:], 2)]
    attend_back(
        1,
        1,
        [back[0][0], *reduced_in[0].sent],
        slots_of(reduced_in[0].across, 0) + slots_of(recvs[1], 0),
    )
    attend_back(1, 2, [dqs[1][-1]], slots_of(reduced_in[0].across, 1) + slots_of(recvs[1], 1))
    out_part = scatter_weight(row_major(grad_out), inner_part, down_part)
    grad_kv = weight_grad(normed_all[0], back[0][0], [dqs[1][-1], out_part], [])
    grad_q = weight_grad(
        normed_all[1],
        jnp.concatenate(dqs[1], axis=1),
        [grad_kv],
        slots_of(recvs[1], 2),
        grad_q,
    )
    q_parts = [scatter_weight(row_major(grad_q), out_part)]
    back.append(unprojected(1, [grad_q], slots_of(q_parts, 0)))
    q_part = q_parts[0]
    reduced_in.append(Reduce(*back[1][1:], 2))
    grad_kv = weight_grad(
        normed_all[1],
        back[1][0],
        reduced_in[1].sent,
        [],
        grad_kv,
    )
    kv_part = scatter_weight(row_major(grad_kv), q_part)
    out_share = sum_blocks(out_part, ctx_count, *reduced_in[1].across)
    inner_share = row_major(sum_blocks(inner_part, ctx_count, grad_kv))
    down_share = row_major(
        add_blocks(down_part, after(down_other[0], grad_kv), ctx_count)
    )
    gain_mid = gain_mid[0] + gain_mid[1]
    outputs = [(mid[m][0] + ffn[m].value()).astype(BF16) for m in micros]

    gain_in = 0.0
    input_grads = []
    for m in micros:
        grad_in_norm, gain_part = norm_backward(
            own[m], normed_own[m][1], norm_gains[0], reduced_in[m].value()
        )
        gain_in = gain_in + gain_part
        input_grads.append((grad_middle[m].astype(F32) + grad_in_norm).astype(BF16))

    lambda_acc = -jnp.sum(sums[1])
    lambda_local = jnp.stack(
        [
            lambda_acc * first_exp * lambdas[1],
            lambda_acc * first_exp * lambdas[0],
            -lambda_acc * second_exp * lambdas[3],
            -lambda_acc * second_exp * lambdas[2],
        ]
    )
    small = jnp.concatenate(
        [
            gain_in.reshape(-1, VD),
            gain_mid.reshape(-1, VD),
            sums[:1] * (1.0 - LAMBDA_INIT),
            lambda_local.reshape(-1, VD),
        ]
    )
    small = butterfly(small)
    per = D // VD
    norm_grad = small[: 2 * per].reshape(2, D)
    head_grad = small[2 * per]
    lambda_grad = small[2 * per + 1 :].reshape(lambdas.shape)

    feed_states = [
        adamw(
            inner_weight,
            inner_momentum,
            inner_variance,
            row_major(inner_share.reshape(inner_weight.shape)),
            0.5 * D ** (-0.5),
            DECAY,
        ),
        adamw(
            down_weight, down_momentum, down_variance, row_major(down_share.T), 0.5 * FF ** (-0.5), DECAY
        ),
    ]
    out_state = adamw(
        out_weight,
        out_momentum,
        out_variance,
        row_major(out_share.T).reshape(out_weight.shape),
        0.5 * (H * VD) ** (-0.5),
        DECAY,
    )
    output, input_grad = jnp.stack(outputs), jnp.stack(input_grads)
    q_share = row_major(sum_blocks(q_part, ctx_count, *reduced_in[1].across))
    q_share = row_major(q_share.reshape(-1, local_heads, 1, VD).transpose(1, 2, 0, 3))
    kv_share = sum_blocks(
        after(kv_part, feed_states, out_state, output, q_share), ctx_count
    )
    kv_share = row_major(
        row_major(kv_share).reshape(-1, local_heads, 2, VD).transpose(1, 2, 0, 3)
    )
    qkv_share = jnp.concatenate([q_share, kv_share], axis=1)
    qkv_state = adamw(
        by_part(qkv_weight),
        by_part(qkv_momentum),
        by_part(qkv_variance),
        qkv_share,
        0.5 * D ** (-0.5),
        DECAY,
    )

    states = [
        tuple(part.transpose(2, 0, 1, 3) for part in qkv_state),
        out_state,
        *feed_states,
        adamw(norm_gains, norm_momentum, norm_variance, norm_grad, 0.4, 0.0),
        adamw(head_gain, head_momentum, head_variance, head_grad, 0.4, 0.0),
        adamw(lambdas, lambda_momentum, lambda_variance, lambda_grad, 0.1, 0.0),
    ]
    return (
        output,
        input_grad,
        *[state[0] for state in states],
        *[state[1] for state in states],
        *[state[2] for state in states],
    )


def solution(mesh):
    activation = P("dp", ("ctx", "head"), None)
    big = (P("dp", "head", None, None), P("head", None, "dp"), P("dp", None, "head"), P("head", "dp"))
    state = big + (P(), P(), P())
    return jax.shard_map(
        on_device,
        mesh=mesh,
        in_specs=(activation, activation, P("dp", None)) + state * 3,
        out_specs=(activation, activation) + state * 3,
        check_vma=False,
    )
```

```python
import functools

import jax
import jax.numpy as jnp
from jax import lax
from jax.experimental import pallas as pl
from jax.experimental.layout import Layout, with_layout_constraint
from jax.experimental.pallas import tpu as pltpu
from jax.sharding import PartitionSpec as P

D = 1536
FF = 4096
H = 12
HD = 64
STEP = 10
VD = 128


EPS = 1e-05
LAMBDA_INIT = 0.2
SCALE = 0.125
NEG = -1e30
BETA1 = 0.9
BETA2 = 0.999
ADAM_EPS = 1e-08
DECAY = 0.1
ROPE_BASE = 10000.0

MIB = 1 << 20
NT = (((1,), (1,)), ((), ()))
TN = (((0,), (0,)), ((), ()))
F32 = jnp.float32
BF16 = jnp.bfloat16
MESH = pl.DeviceIdType.MESH


def dot(left, right, dims=(((1,), (0,)), ((), ())), **kw):
    return lax.dot_general(left, right, dims, preferred_element_type=F32, **kw)


def swap(array, bit):
    size = lax.axis_size("head")
    return lax.ppermute(array, "head", [(i, i ^ bit) for i in range(size)])


def split_rows(array, count):
    size = array.shape[0] // count
    return [array[i * size : (i + 1) * size] for i in range(count)]


class Gather:
    def __init__(self, own, parts=1):
        parts = parts if own.shape[0] % 512 == 0 else 1
        self.own = own
        self.mate = swap(own, 1)
        self.far = [swap(part, 2) for part in split_rows(own, parts)]
        self.far_mate = None

    def pieces(self):
        if self.far_mate is None:
            self.far_mate = [swap(part, 1) for part in self.far]
        return [self.own, self.mate, *self.far, *self.far_mate]

    def mate_first(self):
        own, mate, *rest = self.pieces()
        count = len(self.far)
        return [mate, *rest[count:], own, *rest[:count]]


class Reduce:
    def __init__(self, keep, received, parts=1):
        rows = keep.shape[0] // 2
        parts = parts if rows % 512 == 0 else 1
        total = keep.astype(F32) + received.astype(F32)
        self.near = keep[:rows].astype(F32) + received[:rows].astype(F32)
        self.sent = [part.astype(BF16) for part in split_rows(total[rows:], parts)]
        self.send()

    def send(self, *others):
        self.across = [swap(part, 2) for part in after(self.sent, *others)]

    def value(self):
        return self.near + jnp.concatenate(self.across).astype(F32)


def after(value, *others):
    return lax.optimization_barrier((value, *others))[0]


def together(result, *slots):
    values = lax.optimization_barrier((result, *[array[i] for array, i in slots]))
    for (array, i), value in zip(slots, values[1:]):
        array[i] = value
    return values[0]


def slots_of(array, *wanted):
    return [(array, i) for i in (wanted or range(len(array))) if i < len(array)]


def row_major(array):
    return with_layout_constraint(array, Layout(tuple(range(array.ndim))))


def butterfly(array):
    for axis in ("head", "ctx", "dp"):
        size = lax.axis_size(axis)
        bit = 1
        while bit < size:
            array = array + lax.ppermute(array, axis, [(i, i ^ bit) for i in range(size)])
            bit *= 2
    return array


def chunk_specs(tile, pieces):
    specs, start = [], 0
    for piece in pieces:
        count = piece.shape[0] // tile
        specs.append(
            pl.BlockSpec(
                (tile, piece.shape[1]),
                lambda i, *_, a=start, n=count: (jnp.clip(i - a, 0, n - 1), 0),
            )
        )
        start += count
    return specs


def chunk_ends(tile, pieces):
    ends, start = [], 0
    for piece in pieces:
        start += piece.shape[0] // tile
        ends.append(start)
    return ends


def pick(refs, ends, out_ref):
    index = pl.program_id(0)
    start = 0
    for ref, end in zip(refs, ends):

        @pl.when((index >= start) & (index < end))
        def _(ref=ref):
            out_ref[...] = ref[...]

        start = end


def row_spec(tile, width):
    return pl.BlockSpec((tile, width), lambda i, *_: (i, 0))


def whole_spec(shape):
    return pl.BlockSpec(shape, lambda i, *_: (0,) * len(shape))


def mate_first_spec(tile, per, width):
    return pl.BlockSpec(
        (tile, width), lambda i, *_: ((2 * (i // per) + 1) % 5 * per + i % per, 0)
    )


def exchange_specs(tile, per, width):
    half = 2 * per
    return [
        pl.BlockSpec((tile, width), lambda i, *_: (i // half * (i - half), 0)),
        pl.BlockSpec(memory_space=pl.ANY),
    ]


def exchange_shapes(rows, width):
    return [jax.ShapeDtypeStruct((rows // 2, width), BF16)] * 2


def exchange_scratch(tile, per, width):
    half = 2 * per
    return [
        pltpu.VMEM((half, tile, width), BF16),
        pltpu.SemaphoreType.DMA((half,)),
        pltpu.SemaphoreType.DMA((half,)),
    ]


def mate_index():
    me = lax.axis_index("head")
    return me + 1 - 2 * (me % 2)


def meet_mate():
    @pl.when(pl.program_id(0) == 0)
    def _():
        barrier = pltpu.get_barrier_semaphore()
        pl.semaphore_signal(
            barrier, inc=1, device_id={"head": mate_index()}, device_id_type=MESH
        )
        pl.semaphore_wait(barrier, 1)


def exchange(value, per, keep_ref, received_ref, sent_sc, send_sem, recv_sem):
    step = pl.program_id(0)
    half = 2 * per
    tile = value.shape[0]

    def copy(slot):
        return pltpu.make_async_remote_copy(
            src_ref=sent_sc.at[slot],
            dst_ref=received_ref.at[pl.ds(pl.multiple_of(slot * tile, tile), tile)],
            send_sem=send_sem.at[slot],
            recv_sem=recv_sem.at[slot],
            device_id={"head": mate_index()},
            device_id_type=MESH,
        )

    @pl.when(step < half)
    def _():
        sent_sc[step] = value
        copy(step).start()

    @pl.when(step >= half)
    def _():
        keep_ref[...] = value

    @pl.when(step == 2 * half - 1)
    def _():
        for slot in range(half):
            copy(slot).wait()


def cost(flops, moved, transcendentals=0):
    return pl.CostEstimate(
        flops=int(flops), bytes_accessed=int(moved), transcendentals=int(transcendentals)
    )


def turn(values, cos_table, sin_table, low_half, sign):
    ahead = pltpu.roll(values, VD - HD // 2, 1)
    behind = pltpu.roll(values, HD // 2, 1)
    rotated = jnp.where(low_half, -ahead, behind)
    return values * cos_table + sign * rotated * sin_table


def low_half_mask(rows):
    lane = lax.broadcasted_iota(jnp.int32, (rows, VD), 1)
    return (lane % HD) < HD // 2


def side_by_side(w_refs):
    return jnp.concatenate(
        [w_ref[item] for w_ref in w_refs for item in range(w_ref.shape[0])], axis=1
    )


def project_kernel(*refs, heads, groups, ends):
    count = len(ends)
    chunks, w_refs, refs = refs[:count], refs[count : count + groups], refs[count + groups :]
    cos_ref, sin_ref, refs = refs[0], refs[1], refs[2:]
    if count > 1:
        x_ref, refs = refs[0], refs[1:]
        pick(chunks, ends, x_ref)
    else:
        x_ref = chunks[0]
    q_refs, kv_refs = refs[:heads], refs[heads:]
    mask = low_half_mask(x_ref.shape[0])
    cos_table, sin_table = cos_ref[...], sin_ref[...]
    out = dot(x_ref[...], side_by_side(w_refs))
    for head in range(heads):
        base = head * 3 * VD
        query = turn(out[:, base : base + VD], cos_table, sin_table, mask, 1.0) * SCALE
        key = turn(out[:, base + VD : base + 2 * VD], cos_table, sin_table, mask, 1.0)
        q_refs[head][...] = query.astype(BF16)
        kv_refs[head][:, :VD] = key.astype(BF16)
        kv_refs[head][:, VD:] = out[:, base + 2 * VD : base + 3 * VD].astype(BF16)


def project(chunks, weights, cos_table, sin_table):
    rows = cos_table.shape[0]
    heads = sum(weight.shape[0] for weight in weights) // 3
    tile = min(256, rows // 4)
    gathered = len(chunks) > 1
    out = pl.pallas_call(
        functools.partial(
            project_kernel, heads=heads, groups=len(weights), ends=chunk_ends(tile, chunks)
        ),
        grid=(rows // tile,),
        in_specs=chunk_specs(tile, chunks)
        + [whole_spec(weight.shape) for weight in weights]
        + [row_spec(tile, VD), row_spec(tile, VD)],
        out_specs=[row_spec(tile, D)] * gathered
        + [row_spec(tile, VD)] * heads
        + [row_spec(tile, 2 * VD)] * heads,
        out_shape=[jax.ShapeDtypeStruct((rows, D), BF16)] * gathered
        + [jax.ShapeDtypeStruct((rows, VD), BF16)] * heads
        + [jax.ShapeDtypeStruct((rows, 2 * VD), BF16)] * heads,
        compiler_params=pltpu.CompilerParams(vmem_limit_bytes=60 * MIB),
        cost_estimate=cost(
            6 * rows * D * heads * VD, 2 * (2 * rows * D + 3 * heads * VD * (D + rows))
        ),
        name="project",
    )(*chunks, *weights, cos_table, sin_table)
    x = out[0] if gathered else chunks[0]
    out = out[gathered:]
    return x, out[:heads], out[heads:]


def unproject_kernel(*refs, heads, groups, per):
    dq_refs, own_refs, recv_refs = refs[:heads], refs[heads : 2 * heads], refs[2 * heads : 3 * heads]
    w_refs, refs = refs[3 * heads : 3 * heads + groups], refs[3 * heads + groups :]
    cos_ref, sin_ref, gp_ref, keep_ref, received_ref, *scratch = refs
    meet_mate()
    mask = low_half_mask(gp_ref.shape[0])
    cos_table, sin_table = cos_ref[...], sin_ref[...]
    for head in range(heads):
        base = head * 3 * VD
        both = own_refs[head][...].astype(F32) + recv_refs[head][...].astype(F32)
        query = dq_refs[head][...].astype(F32)
        gp_ref[:, base : base + VD] = turn(query, cos_table, sin_table, mask, -1.0).astype(BF16)
        gp_ref[:, base + VD : base + 2 * VD] = turn(
            both[:, :VD], cos_table, sin_table, mask, -1.0
        ).astype(BF16)
        gp_ref[:, base + 2 * VD : base + 3 * VD] = both[:, VD:].astype(BF16)
    value = dot(gp_ref[...], side_by_side(w_refs), NT).astype(BF16)
    exchange(value, per, keep_ref, received_ref, *scratch)


def unproject(dq, dkv_own, dkv_recv, weights, cos_table, sin_table):
    rows = dq[0].shape[0]
    heads = len(dq)
    tile = min(256, rows // 4)
    per = rows // 4 // tile
    return pl.pallas_call(
        functools.partial(unproject_kernel, heads=heads, groups=len(weights), per=per),
        grid=(rows // tile,),
        in_specs=[mate_first_spec(tile, per, VD)] * heads
        + [mate_first_spec(tile, per, 2 * VD)] * (2 * heads)
        + [*[whole_spec(weight.shape) for weight in weights], mate_first_spec(tile, per, VD), mate_first_spec(tile, per, VD)],
        out_specs=[mate_first_spec(tile, per, heads * 3 * VD)] + exchange_specs(tile, per, D),
        scratch_shapes=exchange_scratch(tile, per, D),
        out_shape=[jax.ShapeDtypeStruct((rows, heads * 3 * VD), BF16)] + exchange_shapes(rows, D),
        compiler_params=pltpu.CompilerParams(
            vmem_limit_bytes=60 * MIB, collective_id=3, has_side_effects=True
        ),
        cost_estimate=cost(
            6 * rows * D * heads * VD,
            2 * (rows * D + 3 * D * heads * VD + 9 * rows * heads * VD),
        ),
        name="unproject",
    )(*dq, *dkv_own, *dkv_recv, *weights, cos_table, sin_table)


def output_kernel(*refs, heads, per):
    attn_refs = refs[:heads]
    w_ref, all_ref, keep_ref, received_ref, *scratch = refs[heads:]
    meet_mate()
    for head in range(heads):
        all_ref[:, head * VD : (head + 1) * VD] = attn_refs[head][...]
    value = dot(all_ref[...], w_ref[...], NT).astype(BF16)
    exchange(value, per, keep_ref, received_ref, *scratch)


def output_projection(attn, weight):
    rows = attn[0].shape[0]
    heads = len(attn)
    tile = min(256, rows // 4)
    per = rows // 4 // tile
    return pl.pallas_call(
        functools.partial(output_kernel, heads=heads, per=per),
        grid=(rows // tile,),
        in_specs=[mate_first_spec(tile, per, VD)] * heads + [whole_spec(weight.shape)],
        out_specs=[mate_first_spec(tile, per, heads * VD)] + exchange_specs(tile, per, D),
        scratch_shapes=exchange_scratch(tile, per, D),
        out_shape=[jax.ShapeDtypeStruct((rows, heads * VD), BF16)] + exchange_shapes(rows, D),
        compiler_params=pltpu.CompilerParams(
            vmem_limit_bytes=40 * MIB, collective_id=1, has_side_effects=True
        ),
        cost_estimate=cost(
            2 * rows * D * weight.shape[1], 2 * (rows * D + weight.size + 2 * rows * heads * VD)
        ),
        name="output_projection",
    )(*attn, weight)


def gate_kernel(*refs, ends, cot_ends):
    count, cot_count = len(ends), len(cot_ends)
    chunks, cot_chunks = refs[:count], refs[count : count + cot_count]
    w_ref, x_ref, cot_ref, hidden_ref, by_gate_ref, by_up_ref = refs[count + cot_count :]
    pick(chunks, ends, x_ref)
    pick(cot_chunks, cot_ends, cot_ref)
    width = hidden_ref.shape[1]
    step = min(512, width)
    x = x_ref[...]
    for base in range(0, width, step):
        cols = slice(base, base + step)
        gate = dot(x, w_ref[:, cols])
        up = dot(x, w_ref[:, width + base : width + base + step])
        share = jax.nn.sigmoid(gate)
        swish = gate * share
        hidden_ref[:, cols] = (swish * up).astype(BF16)
        by_gate_ref[:, cols] = (up * share * (1.0 + gate * (1.0 - share))).astype(BF16)
        by_up_ref[:, cols] = swish.astype(BF16)


def gate_up(chunks, cot_chunks, weights, width):
    own_rows = chunks[0].shape[0]
    rows = 4 * own_rows
    tile = min(256, own_rows)
    return pl.pallas_call(
        functools.partial(
            gate_kernel, ends=chunk_ends(tile, chunks), cot_ends=chunk_ends(tile, cot_chunks)
        ),
        grid=(rows // tile,),
        in_specs=chunk_specs(tile, chunks)
        + chunk_specs(tile, cot_chunks)
        + [whole_spec(weights.shape)],
        out_specs=[row_spec(tile, D)] * 2 + [row_spec(tile, width)] * 3,
        out_shape=[jax.ShapeDtypeStruct((rows, D), BF16)] * 2
        + [jax.ShapeDtypeStruct((rows, width), BF16)] * 3,
        compiler_params=pltpu.CompilerParams(vmem_limit_bytes=60 * MIB),
        cost_estimate=cost(
            4 * rows * D * width, 2 * (4 * rows * D + 2 * D * width + 3 * rows * width)
        ),
        name="gate_up",
    )(*chunks, *cot_chunks, weights)


def feed_kernel(
    cot_ref,
    hidden_ref,
    by_gate_ref,
    by_up_ref,
    down_ref,
    inner_ref,
    grad_ref,
    ffn_keep,
    ffn_received,
    mid_keep,
    mid_received,
    *scratch,
    per,
):
    meet_mate()
    width = hidden_ref.shape[1]
    grad_hidden = dot(cot_ref[...], down_ref[...])
    grad_ref[:, :width] = (grad_hidden * by_gate_ref[...].astype(F32)).astype(BF16)
    grad_ref[:, width:] = (grad_hidden * by_up_ref[...].astype(F32)).astype(BF16)
    middle = dot(grad_ref[...], inner_ref[...], NT).astype(BF16)
    exchange(middle, per, mid_keep, mid_received, *scratch[3:])
    output = dot(hidden_ref[...], down_ref[...], NT).astype(BF16)
    exchange(output, per, ffn_keep, ffn_received, *scratch[:3])


def feed(cot, hidden, by_gate, by_up, down, inner):
    rows, width = hidden.shape
    tile = min(256, rows // 4)
    per = rows // 4 // tile
    return pl.pallas_call(
        functools.partial(feed_kernel, per=per),
        grid=(rows // tile,),
        in_specs=[row_spec(tile, D)]
        + [row_spec(tile, width)] * 3
        + [whole_spec(down.shape), whole_spec(inner.shape)],
        out_specs=[row_spec(tile, 2 * width)]
        + exchange_specs(tile, per, D)
        + exchange_specs(tile, per, D),
        out_shape=[jax.ShapeDtypeStruct((rows, 2 * width), BF16)]
        + exchange_shapes(rows, D)
        + exchange_shapes(rows, D),
        scratch_shapes=exchange_scratch(tile, per, D) + exchange_scratch(tile, per, D),
        compiler_params=pltpu.CompilerParams(
            vmem_limit_bytes=60 * MIB, collective_id=2, has_side_effects=True
        ),
        cost_estimate=cost(
            8 * rows * D * width, 2 * (3 * rows * D + 3 * D * width + 5 * rows * width)
        ),
        name="feed",
    )(cot, hidden, by_gate, by_up, down, inner)


class Plan:
    def __init__(self, own_rows, block_len, prev_rows, ndoc):
        self.own_rows = own_rows
        self.block_len = block_len
        self.prev_rows = prev_rows
        self.ndoc = ndoc
        self.bq = min(256, own_rows)
        self.bk = min(512, own_rows)
        self.total = prev_rows + block_len

    def doc_start(self, info, pos):
        start = jnp.zeros_like(pos)
        for item in range(self.ndoc):
            start = jnp.where(pos >= info[2 + item], info[2 + item], start)
        return start

    def query_start(self, info, index):
        per = self.own_rows // self.bq
        chunk = (index // per) ^ info[0]
        return info[1] * self.block_len + chunk * self.own_rows + (index % per) * self.bq

    def key_row(self, info, index):
        per = self.own_rows // self.bk
        blocks = self.block_len // self.bk
        owner = index // blocks
        local = index % blocks
        inside = (((local // per) ^ info[0]) * per + local % per) * self.bk
        base = jnp.where(owner == info[1], self.prev_rows, owner * self.block_len)
        return pl.multiple_of(base + inside, self.bk)

    def ranges(self, info, start):
        last = start + self.bq - 1
        low = self.doc_start(info, start) // self.bk
        high = last // self.bk + 1
        open_from = (self.doc_start(info, last) + self.bk - 1) // self.bk
        first = jnp.minimum(jnp.maximum(open_from, low), high)
        until = jnp.maximum(first, jnp.minimum((start + 1) // self.bk, high))
        return low, first, until, high


def in_groups(low, high, size, visit):
    count = (high - low) // size

    @pl.loop(0, count)
    def _(group):
        visit(*[low + group * size + item for item in range(size)])

    if size > 1:

        @pl.loop(low + count * size, high)
        def _(index):
            visit(index)


def split_halves(q):
    lane = lax.broadcasted_iota(jnp.int32, q.shape, 1)
    zero = jnp.zeros_like(q)
    return jnp.concatenate([jnp.where(lane < HD, q, zero), jnp.where(lane >= HD, q, zero)], axis=0)


def in_lanes(value):
    high = value.astype(BF16)
    rest = value - high.astype(F32)
    middle = rest.astype(BF16)
    low = (rest - middle.astype(F32)).astype(BF16)
    lane = lax.broadcasted_iota(jnp.int32, value.shape, 1)
    zero = jnp.zeros_like(high)
    return jnp.where(
        lane == 0, high, jnp.where(lane == 1, middle, jnp.where(lane == 2, low, zero))
    )


def load_keys(plan, info, own_ref, prev_ref, kv_sc):
    @pl.when(pl.program_id(0) == 0)
    def _():
        kv_sc[plan.prev_rows :, :] = own_ref[...]

        @pl.when(info[1] > 0)
        def _():
            kv_sc[: plan.prev_rows, :] = prev_ref[...]


def forward_kernel(
    info,
    lam_ref,
    gain_ref,
    q_ref,
    own_ref,
    prev_ref,
    attn_ref,
    first_ref,
    second_ref,
    lse_ref,
    kv_sc,
    m_sc,
    l_sc,
    acc_sc,
    *,
    plan,
):
    bq, bk = plan.bq, plan.bk
    load_keys(plan, info, own_ref, prev_ref, kv_sc)
    start = plan.query_start(info, pl.program_id(0))
    q2 = split_halves(q_ref[...])
    m_sc[...] = jnp.full_like(m_sc, NEG)
    l_sc[...] = jnp.zeros_like(l_sc)
    acc_sc[...] = jnp.zeros_like(acc_sc)
    low, first, until, high = plan.ranges(info, start)

    def visit(index, masked):
        row = plan.key_row(info, index)
        key = kv_sc[pl.ds(row, bk), :VD]
        value = kv_sc[pl.ds(row, bk), VD:]
        scores = dot(q2, key, NT)
        if masked:
            query_pos = start + lax.broadcasted_iota(jnp.int32, (bq, 1), 0)
            begin = plan.doc_start(info, query_pos)
            key_pos = index * bk + lax.broadcasted_iota(jnp.int32, (bq, bk), 1)
            keep = (key_pos <= query_pos) & (key_pos >= begin)
            scores = jnp.concatenate(
                [jnp.where(keep, scores[:bq], NEG), jnp.where(keep, scores[bq:], NEG)], axis=0
            )
        before = m_sc[...]
        after = jnp.maximum(before, jnp.max(scores, axis=1, keepdims=True))
        weights = jnp.exp(scores - jnp.tile(after, (1, bk // VD)))
        factor = jnp.exp(before - after)
        m_sc[...] = after
        l_sc[...] = l_sc[...] * factor + jnp.sum(weights, axis=1, keepdims=True)
        acc_sc[...] = acc_sc[...] * factor + dot(weights.astype(BF16), value)

    @pl.loop(low, first)
    def _(index):
        visit(index, True)

    @pl.loop(first, until)
    def _(index):
        visit(index, False)

    @pl.loop(until, high)
    def _(index):
        visit(index, True)

    total = l_sc[...]
    maps = acc_sc[...] * (1.0 / total)
    first_map, second_map = maps[:bq], maps[bq:]
    first_ref[...] = first_map
    second_ref[...] = second_map
    difference = first_map - lam_ref[0] * second_map
    scaling = lax.rsqrt(jnp.mean(difference * difference, axis=1, keepdims=True) + EPS)
    attn_ref[...] = (difference * scaling * gain_ref[...]).astype(BF16)
    lanes = in_lanes(-(m_sc[...] + jnp.log(total)))
    lse_ref[:, :VD] = lanes[:bq]
    lse_ref[:, VD:] = lanes[bq:]


def attention_cost(plan, per_pair, extra=0):
    pairs = plan.block_len * plan.block_len * 5 // 8
    return cost(pairs * per_pair + extra, plan.block_len * VD * 32, 2 * pairs)


def attend_forward(plan, info, lam, gain, q, kv_own, kv_prev):
    rows, bq = plan.block_len, plan.bq
    grid_spec = pltpu.PrefetchScalarGridSpec(
        num_scalar_prefetch=1,
        grid=(rows // bq,),
        in_specs=[
            pl.BlockSpec(memory_space=pltpu.SMEM),
            whole_spec((1, VD)),
            row_spec(bq, VD),
            whole_spec((rows, 2 * VD)),
            whole_spec((plan.prev_rows, 2 * VD)),
        ],
        out_specs=[row_spec(bq, VD)] * 3 + [row_spec(bq, 2 * VD)],
        scratch_shapes=[
            pltpu.VMEM((plan.total, 2 * VD), BF16),
            pltpu.VMEM((2 * bq, VD), F32),
            pltpu.VMEM((2 * bq, VD), F32),
            pltpu.VMEM((2 * bq, VD), F32),
        ],
    )
    return pl.pallas_call(
        functools.partial(forward_kernel, plan=plan),
        grid_spec=grid_spec,
        out_shape=[
            jax.ShapeDtypeStruct((rows, VD), BF16),
            jax.ShapeDtypeStruct((rows, VD), F32),
            jax.ShapeDtypeStruct((rows, VD), F32),
            jax.ShapeDtypeStruct((rows, 2 * VD), BF16),
        ],
        compiler_params=pltpu.CompilerParams(vmem_limit_bytes=60 * MIB),
        cost_estimate=attention_cost(plan, 6 * VD),
        name="attend_forward",
    )(info, lam, gain, q, kv_own, kv_prev)


def difference_kernel(lam_ref, gain_ref, w_ref, *refs, heads, ends):
    count = len(ends)
    chunks, refs = refs[:count], refs[count:]
    first_refs, second_refs, refs = refs[:heads], refs[heads : 2 * heads], refs[2 * heads :]
    gm_ref, sums_ref, grad_refs = refs[0], refs[1], refs[2:]
    lam = lam_ref[0]

    @pl.when(pl.program_id(0) == 0)
    def _():
        sums_ref[...] = jnp.zeros_like(sums_ref)

    pick(chunks, ends, gm_ref)
    upstream_all = dot(gm_ref[...], w_ref[...])
    for head in range(heads):
        upstream = upstream_all[:, head * VD : (head + 1) * VD]
        first_map, second_map = first_refs[head][...], second_refs[head][...]
        difference = first_map - lam * second_map
        scaling = lax.rsqrt(jnp.mean(difference * difference, axis=1, keepdims=True) + EPS)
        normal = difference * scaling
        weighted = upstream * gain_ref[...]
        inner_mean = jnp.mean(weighted * normal, axis=1, keepdims=True)
        grad = (scaling * (weighted - normal * inner_mean)).astype(BF16)
        grad_wide = grad.astype(F32)
        first_product, second_product = grad_wide * first_map, grad_wide * second_map
        sums_ref[0:1, :] += jnp.sum(upstream * normal, axis=0, keepdims=True)
        sums_ref[1:2, :] += jnp.sum(second_product, axis=0, keepdims=True)
        out = grad_refs[head]
        out[:, :VD] = grad
        for item, product in enumerate((first_product, second_product)):
            total = jnp.sum(product, axis=1, keepdims=True)
            out[:, (item + 1) * VD : (item + 2) * VD] = in_lanes(
                jnp.broadcast_to(-total, product.shape)
            )


def difference_grads(lam, gain, weight, gm, first, second):
    own_rows = gm[0].shape[0]
    rows = 4 * own_rows
    heads = len(first)
    tile = min(256, own_rows)
    return pl.pallas_call(
        functools.partial(difference_kernel, heads=heads, ends=chunk_ends(tile, gm)),
        grid=(rows // tile,),
        in_specs=[pl.BlockSpec(memory_space=pltpu.SMEM), whole_spec((1, VD)), whole_spec(weight.shape)]
        + chunk_specs(tile, gm)
        + [row_spec(tile, VD)] * (2 * heads),
        out_specs=[row_spec(tile, D), whole_spec((8, VD))] + [row_spec(tile, 3 * VD)] * heads,
        out_shape=[jax.ShapeDtypeStruct((rows, D), BF16), jax.ShapeDtypeStruct((8, VD), F32)]
        + [jax.ShapeDtypeStruct((rows, 3 * VD), BF16)] * heads,
        compiler_params=pltpu.CompilerParams(vmem_limit_bytes=60 * MIB),
        cost_estimate=cost(2 * rows * D * heads * VD, 4 * rows * D + 14 * rows * heads * VD),
        name="difference_grads",
    )(lam, gain, weight, *gm, *first, *second)


def backward_kernel(
    info,
    lam_ref,
    q_ref,
    own_ref,
    prev_ref,
    lse_ref,
    grad_ref,
    dq_ref,
    dkv_own_ref,
    dkv_prev_ref,
    kv_sc,
    dk_sc,
    dv_sc,
    dqt_sc,
    *,
    plan,
):
    bq, bk = plan.bq, plan.bk
    step = pl.program_id(0)
    lam = lam_ref[0]

    @pl.when(step == 0)
    def _():
        lane = lax.broadcasted_iota(jnp.int32, (bk, VD), 1)
        ones = jnp.where(lane < 3, 1.0, 0.0).astype(BF16)

        def fill(source, base, rows):
            for start in range(0, rows, bk):
                to = slice(base + start, base + start + bk)
                kv_sc[to, :VD] = source[start : start + bk, :VD]
                kv_sc[to, VD : 2 * VD] = ones
                kv_sc[to, 2 * VD :] = source[start : start + bk, VD:]

        fill(own_ref, plan.prev_rows, plan.block_len)

        @pl.when(info[1] > 0)
        def _():
            fill(prev_ref, 0, plan.prev_rows)

        dk_sc[...] = jnp.zeros_like(dk_sc)
        dv_sc[...] = jnp.zeros_like(dv_sc)

    grad = grad_ref[:, :VD]
    start = plan.query_start(info, step)
    q2 = split_halves(q_ref[...])
    q_wide = jnp.concatenate(
        [q2, jnp.concatenate([lse_ref[:, :VD], lse_ref[:, VD:]], axis=0)], axis=1
    )
    ones = jnp.ones((8, VD), BF16)
    delta_first = dot(ones, grad_ref[:, VD : 2 * VD], NT)[0:1]
    delta_second = dot(ones, grad_ref[:, 2 * VD :], NT)[0:1]
    dqt_sc[...] = jnp.zeros_like(dqt_sc)
    low, _, _, high = plan.ranges(info, start)

    query_pos = start + lax.broadcasted_iota(jnp.int32, (1, bq), 1)
    begin = plan.doc_start(info, query_pos)

    def visit(*indices):
        results = []
        for index in indices:
            row = plan.key_row(info, index)
            key = kv_sc[pl.ds(row, bk), :VD]
            prob = jnp.exp(dot(kv_sc[pl.ds(row, bk), : 2 * VD], q_wide, NT))
            base = dot(kv_sc[pl.ds(row, bk), 2 * VD :], grad, NT)
            key_pos = index * bk + lax.broadcasted_iota(jnp.int32, (bk, bq), 0)
            keep = (key_pos <= query_pos) & (key_pos >= begin)
            prob_first = jnp.where(keep, prob[:, :bq], 0.0)
            prob_second = jnp.where(keep, prob[:, bq:], 0.0)
            raw = jnp.concatenate(
                [
                    (prob_first * (base + delta_first)).astype(BF16),
                    (prob_second * (base + delta_second)).astype(BF16),
                ],
                axis=1,
            )
            value_grad = dot((prob_first - lam * prob_second).astype(BF16), grad)
            results.append((row, value_grad, dot(raw, q2), dot(key, raw, TN)))
        for row, value_grad, key_grad, query_grad in results:
            dv_sc[pl.ds(row, bk), :] += value_grad
            dk_sc[pl.ds(row, bk), :] += key_grad
        dqt_sc[...] += sum(result[3] for result in results)

    in_groups(low, high, 2, visit)

    dq_t = jnp.concatenate([dqt_sc[:HD, :bq], -lam * dqt_sc[HD:, bq:]], axis=0) * SCALE
    dq_ref[...] = dq_t.T.astype(BF16)

    @pl.when(step == pl.num_programs(0) - 1)
    def _():
        lane = lax.broadcasted_iota(jnp.int32, (1, VD), 1)
        side = jnp.where(lane < HD, 1.0, -lam)
        dkv_own_ref[:, :VD] = (dk_sc[plan.prev_rows :, :] * side).astype(BF16)
        dkv_own_ref[:, VD:] = dv_sc[plan.prev_rows :, :].astype(BF16)
        dkv_prev_ref[:, :VD] = (dk_sc[: plan.prev_rows, :] * side).astype(BF16)
        dkv_prev_ref[:, VD:] = dv_sc[: plan.prev_rows, :].astype(BF16)


def attend_backward(plan, info, lam, q, kv_own, kv_prev, lse, grad):
    rows, bq = plan.block_len, plan.bq
    grid_spec = pltpu.PrefetchScalarGridSpec(
        num_scalar_prefetch=1,
        grid=(rows // bq,),
        in_specs=[
            pl.BlockSpec(memory_space=pltpu.SMEM),
            row_spec(bq, VD),
            whole_spec((rows, 2 * VD)),
            whole_spec((plan.prev_rows, 2 * VD)),
            row_spec(bq, 2 * VD),
            row_spec(bq, 3 * VD),
        ],
        out_specs=[
            row_spec(bq, VD),
            whole_spec((rows, 2 * VD)),
            whole_spec((plan.prev_rows, 2 * VD)),
        ],
        scratch_shapes=[
            pltpu.VMEM((plan.total, 3 * VD), BF16),
            pltpu.VMEM((plan.total, VD), F32),
            pltpu.VMEM((plan.total, VD), F32),
            pltpu.VMEM((VD, 2 * bq), F32),
        ],
    )
    return pl.pallas_call(
        functools.partial(backward_kernel, plan=plan),
        grid_spec=grid_spec,
        out_shape=[
            jax.ShapeDtypeStruct((rows, VD), BF16),
            jax.ShapeDtypeStruct((rows, 2 * VD), BF16),
            jax.ShapeDtypeStruct((plan.prev_rows, 2 * VD), BF16),
        ],
        compiler_params=pltpu.CompilerParams(vmem_limit_bytes=60 * MIB),
        cost_estimate=attention_cost(plan, 16 * VD),
        name="attend_backward",
    )(info, lam, q, kv_own, kv_prev, lse, grad)


def norm_forward(values, gain_vec):
    scaling = lax.rsqrt(jnp.mean(values * values, axis=-1, keepdims=True) + EPS)
    return (values * scaling * gain_vec, scaling)


def norm_backward(values, scaling, gain_vec, upstream):
    normal = values * scaling
    weighted = upstream * gain_vec
    inner_mean = jnp.mean(weighted * normal, axis=-1, keepdims=True)
    return (scaling * (weighted - normal * inner_mean), jnp.sum(upstream * normal, axis=0))


def adamw(parameter, momentum, variance, gradient, learn_rate, decay_rate):
    momentum = BETA1 * momentum + (1.0 - BETA1) * gradient
    variance = BETA2 * variance + (1.0 - BETA2) * gradient * gradient
    corrected = momentum / (1.0 - BETA1**STEP)
    spread = jnp.sqrt(variance / (1.0 - BETA2**STEP))
    return (
        parameter - learn_rate * (corrected / (spread + ADAM_EPS) + decay_rate * parameter),
        momentum,
        variance,
    )


def send_keys(kv, ctx_count):
    if ctx_count == 2:
        return lax.ppermute(kv, "ctx", [(0, 1)])
    return lax.all_gather(kv, "ctx", axis=0, tiled=True)


def return_keys(grads, ctx_count):
    if ctx_count == 2:
        return lax.ppermute(grads, "ctx", [(1, 0)])
    return lax.psum_scatter(grads, "ctx", scatter_dimension=0, tiled=True)


def scatter_weight(grad, *others):
    grad = after(grad.astype(BF16), *others)
    return lax.psum_scatter(grad, "dp", scatter_dimension=0, tiled=True)


def exchange_blocks(share, ctx_count):
    if ctx_count == 2:
        return lax.ppermute(share, "ctx", [(0, 1), (1, 0)])
    return lax.psum(share, "ctx")


def add_blocks(share, other, ctx_count):
    if ctx_count == 2:
        return share.astype(F32) + other.astype(F32)
    return other.astype(F32)


def sum_blocks(share, ctx_count, *others):
    return add_blocks(share, after(exchange_blocks(share, ctx_count), *others), ctx_count)


def on_device(
    tokens,
    cotangent,
    doc_lengths,
    qkv_weight,
    out_weight,
    inner_weight,
    down_weight,
    norm_gains,
    head_gain,
    lambdas,
    qkv_momentum,
    out_momentum,
    inner_momentum,
    down_momentum,
    norm_momentum,
    head_momentum,
    lambda_momentum,
    qkv_variance,
    out_variance,
    inner_variance,
    down_variance,
    norm_variance,
    head_variance,
    lambda_variance,
):
    micro_count, own_rows, _ = tokens.shape
    head_count = lax.axis_size("head")
    ctx_count = lax.axis_size("ctx")
    block_len = own_rows * head_count
    seq_len = block_len * ctx_count
    ctx_index = lax.axis_index("ctx")
    head_index = lax.axis_index("head")
    local_heads = qkv_weight.shape[1]
    ff_local = inner_weight.shape[2]
    ndoc = doc_lengths.shape[1]
    plan = Plan(own_rows, block_len, block_len if ctx_count == 2 else seq_len, ndoc)

    def gather_weight(shard):
        return lax.all_gather(shard.astype(BF16), "dp", axis=0, tiled=True)

    def by_part(array):
        return array.transpose(1, 2, 0, 3)

    qkv_parts = row_major(by_part(qkv_weight).astype(BF16))
    qkv_low = [
        lax.all_gather(part.reshape(-1, *part.shape[2:]), "dp", axis=1, tiled=True)
        for part in (qkv_parts[:1], qkv_parts[1:])
    ]
    out_t = gather_weight(row_major(out_weight.astype(BF16).reshape(local_heads * VD, -1).T))
    inner_low = gather_weight(inner_weight.reshape(-1, 2 * ff_local))
    down_shard = row_major(down_weight.astype(BF16).T)
    down_t = gather_weight(down_shard)

    first_exp = jnp.exp(jnp.sum(lambdas[0] * lambdas[1]))
    second_exp = jnp.exp(jnp.sum(lambdas[2] * lambdas[3]))
    lambda_value = first_exp - second_exp + LAMBDA_INIT
    lam = lambda_value.reshape(1)
    head_scale = (head_gain * (1.0 - LAMBDA_INIT)).reshape(1, VD)

    chunk = jnp.arange(block_len, dtype=jnp.int32) // own_rows
    position = (
        ctx_index * block_len
        + (chunk ^ head_index) * own_rows
        + jnp.arange(block_len, dtype=jnp.int32) % own_rows
    )
    frequency = ROPE_BASE ** (
        -(jnp.arange(VD, dtype=jnp.int32) % (HD // 2)).astype(F32) / (HD // 2)
    )

    def info_of(micro):
        bounds = jnp.cumsum(doc_lengths[micro], dtype=jnp.int32)
        return jnp.concatenate([jnp.stack([head_index, ctx_index]).astype(jnp.int32), bounds])

    micros = range(micro_count)
    heads = range(local_heads)
    infos = [info_of(m) for m in micros]
    own, normed_own, normed, cot_own = [], [], [], []
    for m in micros:
        rows, cot_rows = tokens[m], cotangent[m]
        if m > 0:
            rows = after(rows, normed[0].own)
        own.append(rows.astype(F32))
        normed_own.append(norm_forward(own[m], norm_gains[0]))
        cot_own.append(cot_rows)
        normed.append(Gather(normed_own[m][0].astype(BF16), 2 if m else 1))
    position = after(position, normed[-1].own, down_shard)
    phases = position.astype(F32)[:, None] * frequency[None, :]
    cos_table, sin_table = jnp.cos(phases), jnp.sin(phases)

    normed_all, q, kv, kv_prev, cot = [], [], [], [], []

    def keep_projected(m, result):
        if len(q) == m:
            normed_all.append(result[0])
            q.append([])
            kv.append([])
            kv_prev.append([])
        q[m].extend(result[1])
        kv[m].extend(result[2])
        kv_prev[m].extend([send_keys(part, ctx_count) for part in result[2]])

    normed[0].far[0] = after(normed[0].far[0], cos_table, sin_table, *infos, *cot_own)
    result = project(normed[0].pieces(), qkv_low[:1], cos_table, sin_table)
    keep_projected(0, together(result, *slots_of(normed[1].far, 0)))
    result = project([after(normed_all[0], kv[0][-1])], qkv_low[1:], cos_table, sin_table)
    keep_projected(0, together(result, *slots_of(normed[1].far, 1)))
    cot.append(Gather(after(cot_own[0], *normed[1].far)))

    def attend(m, h, before, beside):
        out = attend_forward(
            plan, infos[m], lam, head_scale, after(q[m][h], *before), kv[m][h], kv_prev[m][h]
        )
        return together(out, *beside)

    mid = []

    def finish_attention(m):
        middle = own[m] + attended[m].value()
        value, scaling = norm_forward(middle, norm_gains[1])
        mid.append((middle, scaling, Gather(value.astype(BF16), 2)))

    maps, attn_all, attended = [], [], []
    for m in micros:
        outs = []
        for h in heads:
            if m == 0:
                before = [kv[0]] if h == 0 else [outs[-1], kv[1], out_t]
                beside = [
                    [],
                    slots_of(cot[-1].far, 0),
                    slots_of(cot[-1].far, 1),
                ][h]
            elif h == 0:
                before = [*attended[0].sent, *cot[0].pieces(), *cot[1].pieces()]
                beside = slots_of(attended[0].across) + slots_of(kv_prev[m], 1)
            else:
                before = [outs[-1], mid[0][2].own]
                beside = slots_of(mid[0][2].far, h - 1) + slots_of(kv_prev[m], h + 1)
            outs.append(attend(m, h, before, beside))
            if m == 0 and h == 0:
                pieces = after(normed[1].pieces(), outs[0])
                result = project(pieces, qkv_low, cos_table, sin_table)
                keep_projected(1, together(result, *slots_of(cot[0].far)))
                cot.append(Gather(after(cot_own[1], *cot[0].far), 2))
            if m > 0 and h == 0:
                finish_attention(0)
        maps.append([out[1:] for out in outs])
        result = output_projection([out[0] for out in outs], out_t)
        if m == 0:
            result = together(result, *slots_of(kv_prev[1], 0))
        attn_all.append(result[0])
        attended.append(Reduce(*result[1:], 2 if m else 1))

    grad_middle, gm, gain_mid = [], [], []

    def finish_feed(m, reduced):
        middle, scaling, _ = mid[m]
        grad_norm, part = norm_backward(middle, scaling, norm_gains[1], reduced.value())
        grad_middle.append((cot_own[m].astype(F32) + grad_norm).astype(BF16))
        gm.append(Gather(grad_middle[m], 2 if m else 1))
        gain_mid.append(part)

    def weight_grad(left, right, before, beside, total=None):
        result = dot(after(left, *before), right, TN)
        if total is not None:
            result = (total + result).astype(BF16)
        return together(result, *beside)

    first_gates = gate_up(
        after(mid[0][2].mate_first(), *attended[1].sent), cot[0].mate_first(), inner_low, ff_local
    )
    first_gates = together(first_gates, *slots_of(attended[1].across, 0))
    first_feed = feed(*first_gates[1:], down_t, inner_low)
    first_feed = together(first_feed, *slots_of(attended[1].across, 1))
    finish_attention(1)
    reduced_mid = [Reduce(*first_feed[3:])]
    grad_inner = weight_grad(
        first_gates[0],
        first_feed[0],
        [mid[1][2].own, *reduced_mid[0].sent],
        slots_of(mid[1][2].far, 0),
    )
    grad_down = weight_grad(
        first_gates[1], first_gates[2], [grad_inner], slots_of(mid[1][2].far, 1)
    )
    reduced_mid[0].send(*mid[1][2].far)
    second_gates = gate_up(
        after(mid[1][2].mate_first(), grad_down), cot[1].mate_first(), inner_low, ff_local
    )
    second_gates = together(second_gates, *slots_of(reduced_mid[0].across))
    finish_feed(0, reduced_mid[0])
    second_feed = feed(after(second_gates[1], gm[0].own), *second_gates[2:], down_t, inner_low)
    second_feed = together(second_feed, *slots_of(gm[0].far))
    reduced_mid.append(Reduce(*second_feed[3:], 2))
    grad_inner = weight_grad(
        second_gates[0],
        second_feed[0],
        reduced_mid[1].sent,
        slots_of(reduced_mid[1].across, 0),
        grad_inner,
    )
    grad_down = weight_grad(
        second_gates[1],
        second_gates[2],
        [grad_inner],
        slots_of(reduced_mid[1].across, 1),
        grad_down,
    )
    inner_part = scatter_weight(row_major(grad_inner))
    down_part = scatter_weight(row_major(grad_down))
    finish_feed(1, reduced_mid[1])
    ffn_pairs = [first_feed[1:3], second_feed[1:3]]

    dqs, dkvs, recvs, gm_alls, grads, sums = [], [], [], [], [], 0.0

    def start_back(m, before, beside):
        out = difference_grads(
            lam,
            head_scale,
            out_t,
            after(gm[m].pieces(), *before),
            [part[0] for part in maps[m]],
            [part[1] for part in maps[m]],
        )
        out = together(out, *beside)
        gm_alls.append(out[0])
        grads.append(out[2:])
        dqs.append([])
        dkvs.append([])
        recvs.append([])
        return out[1]

    def attend_back(m, h, before, beside):
        out = attend_backward(
            plan,
            infos[m],
            lam,
            after(q[m][h], *before),
            kv[m][h],
            kv_prev[m][h],
            maps[m][h][2],
            grads[m][h],
        )
        out = together(out, *beside)
        dqs[m].append(out[0])
        dkvs[m].append(out[1])
        recvs[m].append(return_keys(out[2], ctx_count))

    def unprojected(m, before, beside):
        out = unproject(after(dqs[m], *before), dkvs[m], recvs[m], qkv_low, cos_table, sin_table)
        return together(out, *beside)

    def ffn_sum(m, before):
        keep, received = ffn_pairs[m]
        return Reduce(keep, after(received, *before), 2)

    sums = start_back(0, [gm[1].own, grad_down], [])
    attend_back(0, 0, [], slots_of(gm[1].far, 0))
    attend_back(0, 1, [dqs[0][-1]], slots_of(gm[1].far, 1) + slots_of(recvs[0], 0))
    ffn = [ffn_sum(0, [dqs[0][-1]])]
    ffn.append(ffn_sum(1, [dqs[0][-1]]))
    attend_back(
        0,
        2,
        [*ffn[0].sent, *gm[1].pieces()],
        slots_of(ffn[0].across, 0) + slots_of(recvs[0], 1),
    )
    sums = sums + start_back(1, [dqs[0][-1]], slots_of(ffn[0].across, 1))
    grad_out = weight_grad(gm_alls[0], attn_all[0], [grads[1][0]], [])
    grad_out = weight_grad(gm_alls[1], attn_all[1], [grad_out], [], grad_out)
    down_other = [exchange_blocks(down_part, ctx_count)]
    attend_back(
        1,
        0,
        [*ffn[1].sent, grad_out],
        slots_of(ffn[1].across, 0) + slots_of(recvs[0], 2) + slots_of(down_other),
    )
    back = [unprojected(0, [dqs[1][-1]], slots_of(ffn[1].across, 1))]
    reduced_in = [Reduce(*back[0][1:], 2)]
    attend_back(
        1,
        1,
        [back[0][0], *reduced_in[0].sent],
        slots_of(reduced_in[0].across, 0) + slots_of(recvs[1], 0),
    )
    attend_back(1, 2, [dqs[1][-1]], slots_of(reduced_in[0].across, 1) + slots_of(recvs[1], 1))
    out_part = scatter_weight(row_major(grad_out), inner_part, down_part)
    grad_qkv = weight_grad(
        normed_all[0], back[0][0], [dqs[1][-1], out_part], slots_of(recvs[1], 2)
    )
    back.append(unprojected(1, [grad_qkv], []))
    reduced_in.append(Reduce(*back[1][1:], 2))
    grad_qkv = weight_grad(normed_all[1], back[1][0], reduced_in[1].sent, [], grad_qkv)
    last_part = scatter_weight(row_major(grad_qkv), out_part)
    out_share = sum_blocks(out_part, ctx_count, *reduced_in[1].across)
    inner_share = row_major(sum_blocks(inner_part, ctx_count, grad_qkv))
    down_share = row_major(
        add_blocks(down_part, after(down_other[0], grad_qkv), ctx_count)
    )
    gain_mid = gain_mid[0] + gain_mid[1]
    outputs = [(mid[m][0] + ffn[m].value()).astype(BF16) for m in micros]

    gain_in = 0.0
    input_grads = []
    for m in micros:
        grad_in_norm, gain_part = norm_backward(
            own[m], normed_own[m][1], norm_gains[0], reduced_in[m].value()
        )
        gain_in = gain_in + gain_part
        input_grads.append((grad_middle[m].astype(F32) + grad_in_norm).astype(BF16))

    lambda_acc = -jnp.sum(sums[1])
    lambda_local = jnp.stack(
        [
            lambda_acc * first_exp * lambdas[1],
            lambda_acc * first_exp * lambdas[0],
            -lambda_acc * second_exp * lambdas[3],
            -lambda_acc * second_exp * lambdas[2],
        ]
    )
    small = jnp.concatenate(
        [
            gain_in.reshape(-1, VD),
            gain_mid.reshape(-1, VD),
            sums[:1] * (1.0 - LAMBDA_INIT),
            lambda_local.reshape(-1, VD),
        ]
    )
    small = butterfly(small)
    per = D // VD
    norm_grad = small[: 2 * per].reshape(2, D)
    head_grad = small[2 * per]
    lambda_grad = small[2 * per + 1 :].reshape(lambdas.shape)

    feed_states = [
        adamw(
            inner_weight,
            inner_momentum,
            inner_variance,
            row_major(inner_share.reshape(inner_weight.shape)),
            0.5 * D ** (-0.5),
            DECAY,
        ),
        adamw(
            down_weight, down_momentum, down_variance, row_major(down_share.T), 0.5 * FF ** (-0.5), DECAY
        ),
    ]
    out_state = adamw(
        out_weight,
        out_momentum,
        out_variance,
        row_major(out_share.T).reshape(out_weight.shape),
        0.5 * (H * VD) ** (-0.5),
        DECAY,
    )
    output, input_grad = jnp.stack(outputs), jnp.stack(input_grads)
    qkv_share = sum_blocks(
        after(last_part, feed_states, out_state, output, input_grad), ctx_count
    )
    qkv_share = row_major(
        row_major(qkv_share).reshape(-1, local_heads, 3, VD).transpose(1, 2, 0, 3)
    )
    qkv_state = adamw(
        by_part(qkv_weight),
        by_part(qkv_momentum),
        by_part(qkv_variance),
        qkv_share,
        0.5 * D ** (-0.5),
        DECAY,
    )

    states = [
        tuple(part.transpose(2, 0, 1, 3) for part in qkv_state),
        out_state,
        *feed_states,
        adamw(norm_gains, norm_momentum, norm_variance, norm_grad, 0.4, 0.0),
        adamw(head_gain, head_momentum, head_variance, head_grad, 0.4, 0.0),
        adamw(lambdas, lambda_momentum, lambda_variance, lambda_grad, 0.1, 0.0),
    ]
    return (
        output,
        input_grad,
        *[state[0] for state in states],
        *[state[1] for state in states],
        *[state[2] for state in states],
    )


def solution(mesh):
    activation = P("dp", ("ctx", "head"), None)
    big = (P("dp", "head", None, None), P("head", None, "dp"), P("dp", None, "head"), P("head", "dp"))
    state = big + (P(), P(), P())
    return jax.shard_map(
        on_device,
        mesh=mesh,
        in_specs=(activation, activation, P("dp", None)) + state * 3,
        out_specs=(activation, activation) + state * 3,
        check_vma=False,
    )
```
